32 devices in a mesh: section: 2 (over core), expert: 4 (over y, x), seq: 4 (over z).
Axes of the slice: x: 2, y: 2, z: 4, core: 2. Of those that a mesh axis runs over, the one named last changes fastest.
Arguments:
- inputs: bfloat16 [2, 4, 1024, 768], P(None, 'expert', 'seq'), may hold values from -6 to 6
- cotangent: bfloat16 [2, 4, 1024, 768], P(None, 'expert', 'seq'), may hold values from -6 to 6
- query_key_value_weight: bfloat16 [2, 768, 2304], P('section', ('expert', 'seq')), may hold values from -0.21875 to 0.21875
- w_attn_out: bfloat16 [2, 768, 768], P('section', ('expert', 'seq')), may hold values from -0.625 to 0.625
- w_router: bfloat16 [2, 768, 16], P('section', ('expert', 'seq')), may hold values from -0.4375 to 0.4375
- norm_gains: bfloat16 [2, 2, 768], P('section', None, ('expert', 'seq')), may hold values from 0.5 to 1.5
- rel_table: bfloat16 [2, 64, 12], P('section', ('expert', 'seq')), may hold values from -4 to 324
- w_expert_in: bfloat16 [2, 16, 768, 3072], P('section', ('expert', 'seq')), may hold values from -0.21875 to 0.21875
- w_expert_out: bfloat16 [2, 16, 3072, 768], P('section', ('expert', 'seq')), may hold values from -0.109375 to 0.109375
- routes: int32 [2, 2, 4, 1024, 2], P('section', None, 'expert', 'seq'), may hold values from 0 to 15, all different within a row; in each aligned block of 256 rows (0 to 255, 256 to 511, ..., all dimensions but the last counted through in order) at most 64 rows name the same one
Outputs:
- activations: bfloat16 [2, 2, 4, 1024, 768], P('section', None, 'expert', 'seq')
- input_grads: float32 [2, 2, 4, 1024, 768], P('section', None, 'expert', 'seq')
- grad_qkv: float32 [2, 768, 2304], P('section', ('expert', 'seq'))
- grad_attn_out: float32 [2, 768, 768], P('section', ('expert', 'seq'))
- grad_router: float32 [2, 768, 16], P('section', ('expert', 'seq'))
- grad_gains: float32 [2, 2, 768], P('section', None, ('expert', 'seq'))
- grad_table: float32 [2, 64, 12], P('section', ('expert', 'seq'))
- grad_expert_in: float32 [2, 16, 768, 3072], P('section', ('expert', 'seq'))
- grad_expert_out: float32 [2, 16, 3072, 768], P('section', ('expert', 'seq'))
The draws below stay inside these ranges and needn't reach their ends.
Inputs may be any that keep to these rules, and one draw needn't show every extreme that they name: `routes`: in each aligned block of 256 tokens (one device's piece of one sequence of one micro-batch) no expert is named by more than 64 tokens, a bound that some block reaches; a token's two experts differ.
All inputs are finite; a program needn't handle non-finite values.
Results may differ from the reference program's by a relative error of at most 0.025.
Values may be sent and summed in bfloat16 or wider, within the bound.
A program may use at most 384 MiB of HBM per device.

```python
import math
import jax
import jax.numpy as jnp
import numpy as np
from jax import lax

D = 768
H = 12
HD = 64
FF = 3072
TOK_PIECE = 256
M = 2
BUCKETS = 64
LEN = 1024
SEQS = 4
EXPERTS = 16
CAP = 64
BW = 16


def draw_rel_table(key, part):
    table_shape = (2, BUCKETS, H)
    return jax.random.truncated_normal(key, -4.0, 4.0, table_shape, jnp.float32).astype(jnp.bfloat16)


def block_scale(rng, dims, cuts, smallest, top_value):
    factor_of = 1.0
    for position, blocks in cuts:
        steps = jax.random.uniform(jax.random.fold_in(jax.random.fold_in(rng, 6), position), (blocks,), jnp.float32, smallest / len(cuts), top_value / len(cuts))
        factor_of = factor_of * jnp.repeat(jnp.exp(steps), dims[position] // blocks).reshape((-1,) + (1,) * (len(dims) - 1 - position))
    return factor_of


def assign_block(key, own, number, rows, count, top, bound, skew):
    order = jax.random.permutation(key, count)
    heavy_load, usual = portions_of(count, rows * top, bound, skew, True), portions_of(count, rows * top, bound, skew, False)
    places = jnp.arange(count)

    def named(tallies, turn):
        used = int((tallies > 0).sum())
        fixed = max(1, used // 4)
        passed = fixed + (places - fixed + turn * (used - fixed)) % max(1, count - fixed)
        return jnp.zeros((count,), jnp.int32).at[order[jnp.where(places < fixed, places, passed)]].set(jnp.asarray(tallies, jnp.int32))

    tallies = jnp.where(number % 4 == 0, named(heavy_load, number // 4), named(usual, number - number // 4 - 1))
    mixed = jax.random.permutation(jax.random.fold_in(own, 3), count)
    source_of, receiver = mixed[0:count // 2 * 2:2], mixed[1:count // 2 * 2:2]
    margin = jnp.minimum(tallies[source_of] - 1, bound - tallies[receiver]) // 2
    margin = jnp.where((source_of == order[0]) | (receiver == order[0]) | (tallies[receiver] == 0), 0, jnp.maximum(margin, 0))
    passed = jax.random.randint(jax.random.fold_in(own, 4), (count // 2,), 0, 1 << 20) % (margin + 1)
    tallies = tallies.at[source_of].add(-passed).at[receiver].add(passed)
    items = jnp.searchsorted(jnp.cumsum(tallies), jnp.arange(rows * top), side="right").astype(jnp.int32)
    table = items.reshape(top, rows).T
    table = table[jax.random.permutation(jax.random.fold_in(own, 1), rows)]
    turn = jax.random.randint(jax.random.fold_in(own, 2), (rows, 1), 0, top)
    return jnp.take_along_axis(table, (jnp.arange(top)[None, :] + turn) % top, axis=1)


def portions_of(count, total, limit, lean, full):
    portions = [(1 << 20) // math.isqrt(standing ** lean) + 1 for standing in range(1, count + 1)]
    largest = limit if full else min(limit, max(-(-total // count), total * portions[0] // sum(portions)))
    least = 1 if total - largest >= count - 1 else 0
    given, spare = [largest] + [least] * (count - 1), total - largest - least * (count - 1)
    while spare > 0:
        movable = [i for i in range(1, count) if given[i] < largest] or [i for i in range(1, count) if given[i] < limit]
        mass, budget = sum([portions[i] for i in movable]), spare
        for i in movable:
            extra = min(limit - given[i], max(1, budget * portions[i] // mass), spare)
            given[i] = given[i] + extra
            spare = spare - extra
    return np.array(given)


def noise(own_key, shape, spread, reach, pieces=(), kind=jnp.bfloat16):
    entries = spread * jax.random.normal(own_key, shape, jnp.float32)
    if pieces:
        entries = entries * block_scale(own_key, shape, pieces, -0.22, 0.18)
    return jnp.clip(entries, -reach, reach).astype(kind)


def setup_inputs(seed: int = 0) -> dict:
    key_list = jax.random.split(jax.random.key(seed), 11)
    inputs = noise(key_list[0], (M, SEQS, LEN, D), 1.0, 6.0, ((1, 4), (2, 4)))
    cotangent = noise(key_list[1], (M, SEQS, LEN, D), 1.0, 6.0, ((1, 4), (2, 4)))
    query_key_value_weight = noise(key_list[2], (2, D, 3 * D), D ** -0.5, 0.21875, ((0, 2), (1, 16)))
    w_attn_out = noise(key_list[3], (2, D, D), (D // 8) ** -0.5, 0.625, ((0, 2), (1, 16)))
    w_router = noise(key_list[4], (2, D, EXPERTS), (D // 4) ** -0.5, 0.4375, ((0, 2), (1, 16)))
    norm_gains = jnp.clip(1.0 + 0.1 * jax.random.normal(key_list[5], (2, 2, D), jnp.float32), 0.5, 1.5).astype(jnp.bfloat16)
    rel_table = draw_rel_table(jax.random.fold_in(key_list[10], 71), 0)
    w_expert_in = noise(key_list[7], (2, EXPERTS, D, FF), D ** -0.5, 0.21875, ((0, 2), (1, 16)))
    w_expert_out = noise(key_list[8], (2, EXPERTS, FF, D), FF ** -0.5, 0.109375, ((0, 2), (1, 16)))
    routes_keys = jax.random.split(jax.random.fold_in(key_list[9], 1), 2 * M * SEQS * LEN // TOK_PIECE)
    routes_turns = jax.random.permutation(jax.random.fold_in(key_list[9], 3), 2 * M * SEQS * LEN // TOK_PIECE)
    routes = jax.vmap(lambda own, number: assign_block(jax.random.fold_in(key_list[9], 2), own, number, TOK_PIECE, EXPERTS, 2, CAP, 2))(routes_keys, routes_turns).reshape((2, M, SEQS, LEN, 2))
    return dict(inputs=inputs, cotangent=cotangent, query_key_value_weight=query_key_value_weight, w_attn_out=w_attn_out, w_router=w_router, norm_gains=norm_gains, rel_table=rel_table, w_expert_in=w_expert_in, w_expert_out=w_expert_out, routes=routes)


highest_precision = lax.Precision.HIGHEST

@jax.custom_vjp
def lower_precision(v):
    return lax.optimization_barrier(v.astype(jnp.bfloat16)).astype(jnp.float32)

@jax.custom_vjp
def lower_precision_backward(v):
    return v

def low_keep(v):
    return (lower_precision(v), None)

def low_pass(kept, grad):
    return (grad,)

def back_keep(v):
    return (v, None)

def back_low(kept, grad):
    return (lower_precision(grad),)
lower_precision.defvjp(low_keep, low_pass)
lower_precision_backward.defvjp(back_keep, back_low)

def rms_norm(values, gain):
    return values * lax.rsqrt(lax.optimization_barrier(jnp.mean(values * values, axis=-1, keepdims=True)) + 1e-06) * gain

def attend_one(queries, keys_in, values_in, rel_bias):
    positions = jnp.arange(LEN, dtype=jnp.int32)
    distance = positions[:, None] - positions[None, :]
    causal = distance >= 0
    bucket = jnp.where(causal, distance, 0) // BW
    offsets = jnp.transpose(rel_bias[bucket], (2, 0, 1))
    scores = jnp.einsum('qhd,khd->hqk', queries, keys_in, precision=highest_precision) * HD ** (-0.5) + offsets
    scores = lower_precision_backward(jnp.where(causal[None], scores, -1e+30))
    row_max = lax.optimization_barrier(jnp.max(scores, axis=2, keepdims=True))
    expo_values = jnp.exp(scores - row_max)
    probs_all = expo_values / lax.optimization_barrier(jnp.sum(expo_values, axis=2, keepdims=True))
    return jnp.einsum('hqk,khd->qhd', lower_precision(probs_all), values_in, precision=highest_precision)

def slot_table(route_rows):
    flat_routes = route_rows.reshape(-1)
    filler = flat_routes.shape[0]
    slot_total = M * SEQS * LEN // TOK_PIECE * CAP

    def members(expert):
        return jnp.nonzero(flat_routes == expert, size=slot_total, fill_value=filler)[0].astype(jnp.int32)
    return lax.map(members, jnp.arange(EXPERTS, dtype=jnp.int32))

def layer(residual_stream, weights, route_rows, slot_ids):
    query_key_value_weight, output_weight, w_gate, gains_pair, rel_bias, w_in, w_down = weights
    sequence_count = residual_stream.shape[0]
    normalized_input = lower_precision(rms_norm(residual_stream, gains_pair[0]))
    mixed_stream = lower_precision(lower_precision_backward(jnp.einsum('naw,wr->nar', normalized_input, query_key_value_weight, precision=highest_precision)))
    queries = mixed_stream[..., :D].reshape(sequence_count, LEN, H, HD)
    keys_all = mixed_stream[..., D:2 * D].reshape(sequence_count, LEN, H, HD)
    values_all = mixed_stream[..., 2 * D:].reshape(sequence_count, LEN, H, HD)

    def attend_members(members):
        return attend_one(members[0], members[1], members[2], rel_bias)
    attention_result = lax.map(jax.checkpoint(attend_members), (queries, keys_all, values_all))
    attention_result = lower_precision(lower_precision_backward(attention_result.reshape(sequence_count, LEN, D)))
    middle_stream = residual_stream + lower_precision_backward(jnp.einsum('naw,wr->nar', attention_result, output_weight, precision=highest_precision))
    normed_two = lower_precision(rms_norm(middle_stream, gains_pair[1]))
    flat_rows = normed_two.reshape(-1, D)
    logits = lower_precision_backward(jnp.dot(flat_rows, w_gate, precision=highest_precision))
    chosen = jnp.take_along_axis(logits, route_rows, axis=1)
    first_gate = jax.nn.sigmoid(chosen[:, 0] - chosen[:, 1])
    gate_flat = jnp.stack([first_gate, 1.0 - first_gate], axis=1).reshape(-1)
    padded = jnp.concatenate([flat_rows, jnp.zeros((1, D), flat_rows.dtype)], axis=0)

    def run_expert(members):
        assignment, weight_in, weight_down = members
        chosen_rows = lower_precision_backward(padded[assignment // 2])
        hidden = lower_precision_backward(jnp.dot(chosen_rows, weight_in, precision=highest_precision))
        activation = lower_precision(jax.nn.gelu(hidden, approximate=False))
        return lower_precision(lower_precision_backward(jnp.dot(activation, weight_down, precision=highest_precision)))
    produced = lax.map(jax.checkpoint(run_expert), (slot_ids, w_in, w_down))
    gate_padded = jnp.concatenate([gate_flat, jnp.zeros((1,), gate_flat.dtype)])
    weighted = produced * gate_padded[slot_ids][..., None]
    combined = jnp.zeros((flat_rows.shape[0] + 1, D), flat_rows.dtype)
    combined = combined.at[(slot_ids // 2).reshape(-1)].add(weighted.reshape(-1, D))
    return middle_stream + combined[:-1].reshape(sequence_count, LEN, D)

def reference(inputs, cotangent, query_key_value_weight, w_attn_out, w_router, norm_gains, rel_table, w_expert_in, w_expert_out, routes):
    sequence_count = M * SEQS
    weights = tuple((weight.astype(jnp.float32) for weight in (query_key_value_weight, w_attn_out, w_router, norm_gains, rel_table, w_expert_in, w_expert_out)))
    route_list = [routes[section_id].reshape(-1, 2).astype(jnp.int32) for section_id in range(2)]
    slot_list = [slot_table(route_rows) for route_rows in route_list]

    def forward(residual_stream, probe, params):
        first_out = layer(residual_stream, tuple((param[0] for param in params)), route_list[0], slot_list[0])
        second_in = lower_precision(lower_precision_backward(first_out)) + probe
        second_out = layer(second_in, tuple((param[1] for param in params)), route_list[1], slot_list[1])
        return (first_out, second_out)
    residual_stream = inputs.astype(jnp.float32).reshape(sequence_count, LEN, D)
    probe = jnp.zeros_like(residual_stream)
    (first_out, second_out), pullback = jax.vjp(forward, residual_stream, probe, weights)
    down_grad = cotangent.astype(jnp.float32).reshape(sequence_count, LEN, D)
    stream_grad, probe_grad, grads = pullback((jnp.zeros_like(first_out), down_grad))
    out_shape = (2, M, SEQS, LEN, D)
    activations = jnp.stack([first_out, second_out]).astype(jnp.bfloat16).reshape(out_shape)
    input_grads = jnp.stack([stream_grad, probe_grad]).reshape(out_shape)
    return (activations, input_grads, grads[0], grads[1], grads[2], grads[3], grads[4], grads[5], grads[6])
```

```python
import functools

import jax
import jax.numpy as jnp
from jax import lax
from jax.experimental import pallas as pl
from jax.experimental.pallas import tpu as pltpu
from jax.sharding import Mesh
from jax.sharding import PartitionSpec as P

F32 = jnp.float32
BF16 = jnp.bfloat16
EPS = 1e-06
MASKED = -1e30
GROUP = 4
RANKS = ("expert", "zhi", "zlo")
VMEM_LIMIT = 60 << 20

NN = (((1,), (0,)), ((), ()))
NT = (((1,), (1,)), ((), ()))
TN = (((0,), (0,)), ((), ()))


def mm(left, right, dims=NN):
    return lax.dot_general(left, right, dims, preferred_element_type=F32)


def inverse_rms(values):
    return lax.rsqrt(jnp.mean(values * values, axis=-1, keepdims=True) + EPS)


def whole(array):
    rank = len(array.shape)
    return pl.BlockSpec(array.shape, lambda *unused: (0,) * rank)


def call(body, name, outs, args, scalars=None, scratch=(), flops=0):
    specs = [pl.BlockSpec(memory_space=pltpu.SMEM)] if scalars is not None else []
    specs += [pl.BlockSpec(memory_space=pltpu.VMEM)] * len(args)
    operands = ([scalars] if scalars is not None else []) + list(args)
    moved = sum(a.size * a.dtype.itemsize for a in list(args) + list(outs))
    return pl.pallas_call(
        body,
        name=name,
        in_specs=specs,
        out_specs=[pl.BlockSpec(memory_space=pltpu.VMEM)] * len(outs),
        out_shape=list(outs),
        scratch_shapes=list(scratch),
        compiler_params=pltpu.CompilerParams(vmem_limit_bytes=VMEM_LIMIT),
        cost_estimate=pl.CostEstimate(flops=flops, bytes_accessed=moved, transcendentals=0),
    )(*operands)


def shape(dims, dtype):
    return jax.ShapeDtypeStruct(tuple(dims), dtype)


def bucket_onehot(buckets, span, spacing):
    width = 2 * span * GROUP
    column = lax.broadcasted_iota(jnp.int32, (buckets, width), 1)
    delta = column // (2 * span)
    distance = column - delta * (2 * span) - span + span * delta
    bucket = jnp.where(distance >= 0, distance // spacing, -1)
    row = lax.broadcasted_iota(jnp.int32, (buckets, width), 0)
    return (bucket == row).astype(BF16)


def fill_bias(first_head, heads, table, vectors, bias, span, spacing):
    buckets, head_count = table.shape
    hot = bucket_onehot(buckets, span, spacing)
    rows = mm(table[...], hot, TN)
    column = lax.broadcasted_iota(jnp.int32, (1, 2 * span * GROUP), 1)
    rows = jnp.where(column < span, MASKED, rows)
    vectors[0:head_count, :] = rows
    for head in range(heads):
        picked = vectors[pl.ds(first_head + head, 1), :]
        for delta in range(GROUP):
            piece = picked[:, delta * 2 * span : (delta + 1) * 2 * span]
            spread = jnp.broadcast_to(piece, (span, 2 * span))
            rolled = pltpu.roll(spread, span, 1, stride=1, stride_axis=0)
            bias[head * GROUP + delta] = rolled[:, :span]


def attention_forward(sizes, ids, own, flip, side, side_flip, gain, weight, table,
                      out, mixed, gathered, stats, vectors, bias, turned):
    span, heads, size, spacing = sizes
    width = heads * size
    fill_bias(ids[4] * heads, heads, table, vectors, bias, span, spacing)
    for slot, piece in enumerate((own, flip, side, side_flip)):
        gathered[pl.ds(pl.multiple_of(ids[slot] * span, span), span), :] = piece[...]
    for part in range(GROUP):
        rows = slice(part * span, (part + 1) * span)
        values = gathered[rows, :].astype(F32)
        normed = (values * inverse_rms(values) * gain[...].astype(F32)).astype(BF16)
        mixed[rows, :] = mm(normed, weight[...]).astype(BF16)
    for head in range(heads):
        columns = slice(head * size, (head + 1) * size)
        query_t = (mixed[:, columns].astype(F32) * size ** (-0.5)).T.astype(BF16)
        key = mixed[:, width + head * size : width + (head + 1) * size]
        value_t = mixed[:, 2 * width + head * size : 2 * width + (head + 1) * size].astype(F32).T.astype(BF16)
        for part in range(GROUP):
            mine = slice(part * span, (part + 1) * span)
            blocks = []
            for other in range(part + 1):
                raw = mm(key[other * span : (other + 1) * span], query_t[:, mine])
                blocks.append(raw + bias[head * GROUP + part - other])
            top = functools.reduce(jnp.maximum, [jnp.max(b, axis=0, keepdims=True) for b in blocks])
            total = jnp.zeros_like(top)
            gained = jnp.zeros((size, span), F32)
            for other, block in enumerate(blocks):
                raised = jnp.exp(block - top)
                total = total + jnp.sum(raised, axis=0, keepdims=True)
                gained = gained + mm(value_t[:, other * span : (other + 1) * span], raised.astype(BF16))
            turned[columns, mine] = gained / total
            stats[head : head + 1, mine] = top + jnp.log(total)
    for part in range(GROUP):
        mine = slice(part * span, (part + 1) * span)
        out[part] = turned[:, mine].T.astype(BF16)


def route_masks(routes, experts):
    lane = lax.broadcasted_iota(jnp.int32, (routes.shape[0], experts), 1)
    return [(routes[:, k : k + 1] == lane).astype(F32) for k in range(2)]


def pick_rows(slot, slots):
    lane = lax.broadcasted_iota(jnp.int32, (slot.shape[0], slots), 1).astype(F32)
    return (lane == slot).astype(BF16)


def fill_slots(aux_t, slots, k):
    row = lax.broadcasted_iota(jnp.int32, (slots, aux_t.shape[1]), 0).astype(F32)
    return (row == aux_t[k : k + 1, :]).astype(BF16)


def after_attention(capacity, attended, own, w_out, gain, router, routes,
                    outgoing, middle, normed_two, aux):
    tokens = own.shape[0]
    experts = router.shape[1]
    slots = experts * capacity
    width = attended.shape[2]
    total = own[...].astype(F32)
    for group in range(GROUP):
        total = total + mm(attended[group], w_out[group * width : (group + 1) * width, :])
    middle[...] = total
    normed = (total * inverse_rms(total) * gain[...].astype(F32)).astype(BF16)
    normed_two[...] = normed
    logits = mm(normed, router[...])
    masks = route_masks(routes, experts)
    members = (masks[0] + masks[1]).astype(BF16)
    row = lax.broadcasted_iota(jnp.int32, (tokens, tokens), 0)
    column = lax.broadcasted_iota(jnp.int32, (tokens, tokens), 1)
    earlier = mm((row > column).astype(BF16), members)
    chosen = [jnp.sum(logits * mask, axis=1, keepdims=True) for mask in masks]
    first = jax.nn.sigmoid(chosen[0] - chosen[1])
    places = [
        routes[:, k : k + 1].astype(F32) * capacity + jnp.sum(earlier * masks[k], axis=1, keepdims=True)
        for k in range(2)
    ]
    lane = lax.broadcasted_iota(jnp.int32, (tokens, 128), 1)
    packed = jnp.zeros((tokens, 128), F32)
    for index, entry in enumerate((places[0], places[1], first, 1.0 - first)):
        packed = jnp.where(lane == index, entry, packed)
    aux[...] = packed
    packed_t = packed.T
    hot = fill_slots(packed_t, slots, 0) + fill_slots(packed_t, slots, 1)
    outgoing[...] = mm(hot, normed).astype(BF16)


def expert_forward(rows, w_in, w_down, activation, slope, produced, total):
    step = pl.program_id(0)

    @pl.when(step == 0)
    def clear():
        total[...] = jnp.zeros_like(total)

    chunk = rows.shape[0] // 4
    for part in range(4):
        mine = slice(part * chunk, (part + 1) * chunk)
        hidden = mm(rows[mine, :], w_in[...])
        half = 0.5 * (1.0 + lax.erf(hidden * 0.7071067811865476))
        bell = jnp.exp(-0.5 * hidden * hidden) * 0.3989422804014327
        raised = (hidden * half).astype(BF16)
        activation[mine, :] = raised
        slope[mine, :] = (half + hidden * bell).astype(BF16)
        total[mine, :] += mm(raised, w_down[...])

    @pl.when(step == pl.num_programs(0) - 1)
    def finish():
        produced[...] = total[...].astype(BF16)


def expert_backward(arrived_grad, w_in, w_down, slope, hidden_grad, rows_grad, total):
    step = pl.program_id(0)

    @pl.when(step == 0)
    def clear():
        total[...] = jnp.zeros_like(total)

    chunk = arrived_grad.shape[0] // 4
    for part in range(4):
        mine = slice(part * chunk, (part + 1) * chunk)
        lifted = mm(arrived_grad[mine, :], w_down[...], NT) * slope[mine, :].astype(F32)
        lowered = lifted.astype(BF16)
        hidden_grad[mine, :] = lowered
        total[mine, :] += mm(lowered, w_in[...], NT)

    @pl.when(step == pl.num_programs(0) - 1)
    def finish():
        rows_grad[...] = total[...].astype(BF16)


def tile_of(hidden):
    return 768 if hidden % 768 == 0 else hidden


def run_expert_forward(rows, w_in, w_down):
    count, features = rows.shape
    hidden = w_in.shape[1]
    tile = tile_of(hidden)
    return pl.pallas_call(
        expert_forward,
        name="expert_forward",
        grid=(hidden // tile,),
        in_specs=[
            whole(rows),
            pl.BlockSpec((features, tile), lambda j: (0, j)),
            pl.BlockSpec((tile, features), lambda j: (j, 0)),
        ],
        out_specs=[
            pl.BlockSpec((count, tile), lambda j: (0, j)),
            pl.BlockSpec((count, tile), lambda j: (0, j)),
            pl.BlockSpec((count, features), lambda j: (0, 0)),
        ],
        out_shape=[shape((count, hidden), BF16), shape((count, hidden), BF16), shape((count, features), BF16)],
        scratch_shapes=[pltpu.VMEM((count, features), F32)],
        compiler_params=pltpu.CompilerParams(vmem_limit_bytes=VMEM_LIMIT),
        cost_estimate=pl.CostEstimate(
            flops=4 * count * features * hidden, bytes_accessed=30 << 20, transcendentals=2 * count * hidden
        ),
    )(rows, w_in, w_down)


def run_expert_backward(arrived_grad, w_in, w_down, slope):
    count, features = arrived_grad.shape
    hidden = w_in.shape[1]
    tile = tile_of(hidden)
    return pl.pallas_call(
        expert_backward,
        name="expert_backward",
        grid=(hidden // tile,),
        in_specs=[
            whole(arrived_grad),
            pl.BlockSpec((features, tile), lambda j: (0, j)),
            pl.BlockSpec((tile, features), lambda j: (j, 0)),
            pl.BlockSpec((count, tile), lambda j: (0, j)),
        ],
        out_specs=[
            pl.BlockSpec((count, tile), lambda j: (0, j)),
            pl.BlockSpec((count, features), lambda j: (0, 0)),
        ],
        out_shape=[shape((count, hidden), BF16), shape((count, features), BF16)],
        scratch_shapes=[pltpu.VMEM((count, features), F32)],
        compiler_params=pltpu.CompilerParams(vmem_limit_bytes=VMEM_LIMIT),
        cost_estimate=pl.CostEstimate(
            flops=4 * count * features * hidden, bytes_accessed=30 << 20, transcendentals=0
        ),
    )(arrived_grad, w_in, w_down, slope)


def weight_partials(scalars, rows, hidden_grad, activation, arrived_grad, grad_in, grad_down):
    @pl.when(scalars[0] == 1)
    def wanted():
        grad_in[...] = mm(rows[...], hidden_grad[...], TN).astype(BF16)
        grad_down[...] = mm(activation[...], arrived_grad[...], TN).astype(BF16)


def run_weight_partials(wanted, rows, hidden_grad, activation, arrived_grad):
    count, features = rows.shape
    hidden = hidden_grad.shape[1]
    tile = tile_of(hidden)
    return pl.pallas_call(
        weight_partials,
        name="weight_partials",
        grid_spec=pltpu.PrefetchScalarGridSpec(
            num_scalar_prefetch=1,
            grid=(hidden // tile,),
            in_specs=[
                pl.BlockSpec((count, features), lambda j, s: (0, 0)),
                pl.BlockSpec((count, tile), lambda j, s: (0, j * s[0])),
                pl.BlockSpec((count, tile), lambda j, s: (0, j * s[0])),
                pl.BlockSpec((count, features), lambda j, s: (0, 0)),
            ],
            out_specs=[
                pl.BlockSpec((features, tile), lambda j, s: (0, j * s[0])),
                pl.BlockSpec((tile, features), lambda j, s: (j * s[0], 0)),
            ],
        ),
        out_shape=[shape((features, hidden), BF16), shape((hidden, features), BF16)],
        compiler_params=pltpu.CompilerParams(vmem_limit_bytes=VMEM_LIMIT),
        cost_estimate=pl.CostEstimate(
            flops=4 * count * features * hidden, bytes_accessed=30 << 20, transcendentals=0
        ),
    )(wanted, rows, hidden_grad, activation, arrived_grad)


def weight_totals(scalars, rows, hidden_grad, activation, arrived_grad,
                  rows_1, hidden_grad_1, activation_1, arrived_grad_1,
                  sent_in, sent_down, grad_in, grad_down):
    def build(left, right, left_down, right_down):
        grad_in[...] = mm(left[...], right[...], TN) + sent_in[...].astype(F32)
        grad_down[...] = mm(left_down[...], right_down[...], TN) + sent_down[...].astype(F32)

    @pl.when(scalars[0] == 0)
    def first():
        build(rows, hidden_grad, activation, arrived_grad)

    @pl.when(scalars[0] == 1)
    def second():
        build(rows_1, hidden_grad_1, activation_1, arrived_grad_1)


def run_weight_totals(core, first, second, sent_in, sent_down):
    count, features = first[0].shape
    hidden = first[1].shape[1]
    tile = tile_of(hidden) // 2

    def operand_specs(which):
        def column(j, s):
            return (0, jnp.where(s[0] == which, j, 0))

        return [
            pl.BlockSpec((count, features), lambda j, s: (0, 0)),
            pl.BlockSpec((count, tile), column),
            pl.BlockSpec((count, tile), column),
            pl.BlockSpec((count, features), lambda j, s: (0, 0)),
        ]

    across = pl.BlockSpec((features, tile), lambda j, s: (0, j))
    down = pl.BlockSpec((tile, features), lambda j, s: (j, 0))
    return pl.pallas_call(
        weight_totals,
        name="weight_totals",
        grid_spec=pltpu.PrefetchScalarGridSpec(
            num_scalar_prefetch=1,
            grid=(hidden // tile,),
            in_specs=operand_specs(0) + operand_specs(1) + [across, down],
            out_specs=[across, down],
        ),
        out_shape=[shape((features, hidden), F32), shape((hidden, features), F32)],
        compiler_params=pltpu.CompilerParams(vmem_limit_bytes=VMEM_LIMIT),
        cost_estimate=pl.CostEstimate(
            flops=4 * count * features * hidden, bytes_accessed=60 << 20, transcendentals=0
        ),
    )(core, *first, *second, sent_in, sent_down)


def combine(returned, aux, middle, result, difference):
    slots = returned.shape[0]
    packed = aux[...]
    outs = [mm(pick_rows(packed[:, k : k + 1], slots), returned[...]) for k in range(2)]
    total = middle[...] + packed[:, 2:3] * outs[0] + packed[:, 3:4] * outs[1]
    result[...] = total.astype(BF16)
    difference[...] = outs[0] - outs[1]


def spread_grads(upstream, aux, outgoing):
    slots = outgoing.shape[0]
    packed = aux[...]
    packed_t = packed.T
    values = upstream[...].astype(F32)
    total = jnp.zeros(outgoing.shape, F32)
    for k in range(2):
        total = total + mm(fill_slots(packed_t, slots, k), (values * packed[:, 2 + k : 3 + k]).astype(BF16))
    outgoing[...] = total.astype(BF16)


def bucket_sums(block_sums, buckets):
    heads, deltas, sides, count, unused = block_sums.shape
    dims = (deltas, sides, count, count, buckets)
    delta, side, key, query, bucket = [lax.broadcasted_iota(jnp.int32, dims, axis) for axis in range(5)]
    hot = (delta * count + query - key - side == bucket).astype(F32)
    return jnp.einsum("hdskq,dskqb->hb", block_sums, hot, precision=lax.Precision.HIGHEST)


def norm_backward(values, gain, grad):
    scale = inverse_rms(values)
    unit = values * scale
    lifted = grad * gain
    back = scale * (lifted - unit * jnp.mean(lifted * unit, axis=-1, keepdims=True))
    return back, jnp.sum(grad * unit, axis=0, keepdims=True)


def before_attention(returned, aux, upstream, difference, middle, normed_two, attended, gain,
                     router, w_out, routes, middle_grad, attended_grad, out_grad, router_grad, gain_grad):
    slots = returned.shape[0]
    experts = router.shape[1]
    width = attended.shape[2]
    packed = aux[...]
    hot = pick_rows(packed[:, 0:1], slots) + pick_rows(packed[:, 1:2], slots)
    token_grad = mm(hot, returned[...])
    flow = upstream[...].astype(F32)
    shift = jnp.sum(flow * difference[...], axis=1, keepdims=True) * packed[:, 2:3] * packed[:, 3:4]
    masks = route_masks(routes, experts)
    logits_grad = (shift * (masks[0] - masks[1])).astype(BF16)
    router_grad[...] = mm(normed_two[...], logits_grad, TN)
    token_grad = token_grad + mm(logits_grad, router[...], NT)
    back, gain_part = norm_backward(middle[...], gain[...].astype(F32), token_grad)
    gain_grad[...] = gain_part
    total = flow + back
    middle_grad[...] = total
    branch = total.astype(BF16)
    for group in range(GROUP):
        mine = slice(group * width, (group + 1) * width)
        out_grad[mine, :] = mm(attended[group], branch, TN)
        attended_grad[group] = mm(branch, w_out[mine, :], NT).astype(BF16)


def attention_backward(sizes, ids, mixed, stats, attended, grads, gathered, gain, weight, table,
                       kept, sent, qkv_grad, gain_grad, table_grad,
                       vectors, bias, mixed_grad, sums, key_total, value_total, turned, strips):
    span, heads, size, spacing = sizes
    width = heads * size
    count = span // spacing
    row = lax.broadcasted_iota(jnp.int32, (span, span), 0)
    column = lax.broadcasted_iota(jnp.int32, (span, span), 1)
    later = (column % spacing) >= (row % spacing)
    fill_bias(ids[4] * heads, heads, table, vectors, bias, span, spacing)
    for head in range(heads):
        columns = slice(head * size, (head + 1) * size)
        key_columns = slice(width + head * size, width + (head + 1) * size)
        value_columns = slice(2 * width + head * size, 2 * width + (head + 1) * size)
        query = (mixed[:, columns].astype(F32) * size ** (-0.5)).astype(BF16)
        query_t = query.astype(F32).T.astype(BF16)
        key = mixed[:, key_columns]
        key_t = key.astype(F32).T.astype(BF16)
        value = mixed[:, value_columns]
        key_total[...] = jnp.zeros_like(key_total)
        value_total[...] = jnp.zeros_like(value_total)
        sums[...] = jnp.zeros_like(sums)
        for part in range(GROUP):
            mine = slice(part * span, (part + 1) * span)
            grad = grads[part, :, columns]
            grad_wide = grad.astype(F32)
            grad_t = grad_wide.T
            outcome_t = attended[part, :, columns].astype(F32).T
            delta_row = jnp.sum(grad_t * outcome_t, axis=0, keepdims=True)
            grad_t = grad_t.astype(BF16)
            level = stats[head : head + 1, mine]
            query_total = jnp.zeros((size, span), F32)
            for other in range(part + 1):
                theirs = slice(other * span, (other + 1) * span)
                raw = mm(key[theirs], query_t[:, mine])
                prob = jnp.exp(raw + (bias[head * GROUP + part - other] - level))
                prob_grad = mm(value[theirs], grad_t)
                low = (prob * (prob_grad - delta_row)).astype(BF16)
                sums[part - other] += low.astype(F32)
                query_total = query_total + mm(key_t[:, theirs], low)
                key_total[theirs, :] += mm(low, query[mine])
                value_total[theirs, :] += mm(prob.astype(BF16), grad)
            turned[:, mine] = query_total * size ** (-0.5)
        mixed_grad[:, columns] = turned[...].T.astype(BF16)
        mixed_grad[:, key_columns] = key_total[...].astype(BF16)
        mixed_grad[:, value_columns] = value_total[...].astype(BF16)
        for delta in range(GROUP):
            upper = jnp.where(later, sums[delta], 0.0)
            for side, block in enumerate((upper, sums[delta] - upper)):
                start = ((head * GROUP + delta) * 2 + side) * count
                strips[start : start + count, :] = jnp.sum(block.reshape(count, spacing, span), axis=1)
    lane = lax.broadcasted_iota(jnp.int32, (span, count), 0) // spacing
    hot = (lane == lax.broadcasted_iota(jnp.int32, (span, count), 1)).astype(F32)
    table_grad[...] = lax.dot_general(
        strips[...], hot, NN, precision=lax.Precision.HIGHEST, preferred_element_type=F32
    )
    gain_total = jnp.zeros(gain_grad.shape, F32)
    weight_total = jnp.zeros(qkv_grad.shape, F32)
    for part in range(GROUP):
        place = ids[5 + part]
        rows = pl.ds(pl.multiple_of(place * span, span), span)
        values = gathered[rows, :].astype(F32)
        unit = values * inverse_rms(values)
        normed = (unit * gain[...].astype(F32)).astype(BF16)
        lowered = mixed_grad[rows, :]
        weight_total = weight_total + mm(normed, lowered, TN)
        back = mm(lowered, weight[...], NT)
        gain_total = gain_total + jnp.sum(back * unit, axis=0, keepdims=True)
        target = kept if part < 2 else sent
        target[part % 2] = back.astype(BF16)
    qkv_grad[...] = weight_total
    gain_grad[...] = gain_total


def first_norm_grad(kept, arrived, own, gain, middle_grad, wide, low):
    grad = kept[...].astype(F32) + arrived[...].astype(F32)
    back, unused = norm_backward(own[...].astype(F32), gain[...].astype(F32), grad)
    total = middle_grad[...] + back
    wide[...] = total
    low[...] = total.astype(BF16)


FLIP = [(0, 1), (1, 0)]


def flip(block):
    return lax.ppermute(block, "section", FLIP)


def beside(block):
    return lax.ppermute(block, "zlo", FLIP)


def scatter_pairs(turn):
    return [
        (core * 4 + a * 2 + b, b * 4 + (core ^ turn) * 2 + a)
        for core in range(2)
        for a in range(2)
        for b in range(2)
    ]


def to_working(block, turn):
    return lax.ppermute(block, ("section", "zhi", "zlo"), scatter_pairs(turn))


def to_home(block, turn):
    pairs = [(after, before) for before, after in scatter_pairs(turn)]
    return lax.ppermute(block, ("section", "zhi", "zlo"), pairs)


def exchange(block, experts, capacity):
    features = block.shape[-1]
    moved = lax.all_to_all(
        block.reshape(experts, capacity, features), RANKS, split_axis=0, concat_axis=0, tiled=True
    )
    return moved.reshape(experts * capacity, features)


def regroup(block):
    return lax.all_to_all(block, ("zlo", "section"), split_axis=0, concat_axis=0, tiled=True)


def per_device(inputs, cotangent, qkv_shard, out_shard, router_shard, gain_shard, table_shard,
               w_expert_in, w_expert_out, routes):
    core = lax.axis_index("section")
    zhi = lax.axis_index("zhi")
    zlo = lax.axis_index("zlo")
    span, features = inputs.shape[2:]
    ranks = lax.axis_size(RANKS)
    shard_rows = qkv_shard.shape[1]
    experts = router_shard.shape[2]
    table_rows, head_count = table_shard.shape[1:]
    buckets = table_rows * ranks
    heads = head_count // GROUP
    size = features // head_count
    width = heads * size
    spacing = GROUP * span // buckets
    capacity = max(2, 4 * span // experts)
    slots = experts * capacity
    group = 2 * zlo + core
    sizes = (span, heads, size, spacing)
    ids = jnp.stack([
        group, 2 * zlo + 1 - core, 2 * (1 - zlo) + core, 2 * (1 - zlo) + 1 - core, group,
        core, 2 + core, 1 - core, 3 - core,
    ]).astype(jnp.int32)
    core_id = core.astype(jnp.int32).reshape(1)

    own = to_working(lax.dynamic_index_in_dim(inputs, core, 0, keepdims=False)[0], 0)
    given = to_working(lax.dynamic_index_in_dim(cotangent, core, 0, keepdims=False)[0], 0)
    route_parts = [
        to_working(lax.dynamic_index_in_dim(routes[0], core ^ turn, 0, keepdims=False)[0], turn)
        for turn in range(2)
    ]
    section_routes = [
        jnp.where(zhi == section, route_parts[0], route_parts[1]) for section in range(2)
    ]

    small = jnp.concatenate([
        router_shard[0],
        gain_shard[0].T,
        jnp.pad(table_shard[0], ((0, shard_rows - table_rows), (0, 0))),
    ], axis=1)
    small = jnp.pad(small, ((0, 0), (0, -small.shape[1] % 128)))
    packed = jnp.concatenate([qkv_shard[0], out_shard[0], small], axis=1)
    full = lax.all_gather(packed, RANKS, axis=0, tiled=True)
    qkv_full = full[:, : 3 * features].reshape(features, 3, GROUP, width)

    def columns_of(which):
        return lax.dynamic_index_in_dim(qkv_full, which, 2, keepdims=False).reshape(features, 3 * width)

    rest = full[:, 3 * features :]
    mine = (columns_of(group), rest)
    theirs = (flip(columns_of(2 * zlo + 1 - core)), flip(rest))
    w_in = w_expert_in[0, 0]
    w_down = w_expert_out[0, 0]
    w_in_other = flip(w_in)
    w_down_other = flip(w_down)

    weights = []
    for section in range(2):
        is_own = core == section
        qkv = jnp.where(is_own, mine[0], theirs[0])
        others = jnp.where(is_own, mine[1], theirs[1])
        w_out = others[:, :features]
        router = others[:, features : features + experts]
        gains = others[:, features + experts : features + experts + 2].T
        table = others[:, features + experts + 2 : features + experts + 2 + head_count]
        table = table.reshape(ranks, shard_rows, head_count)[:, :table_rows].reshape(buckets, head_count)
        weights.append((
            qkv, w_out, router, gains[0:1], gains[1:2], table,
            jnp.where(is_own, w_in, w_in_other), jnp.where(is_own, w_down, w_down_other),
        ))

    bias_scratch = [
        pltpu.VMEM((-(-head_count // 8) * 8, 2 * span * GROUP), F32),
        pltpu.VMEM((heads * GROUP, span, span), F32),
    ]
    length = GROUP * span
    blocks = span // spacing
    states = []
    results = []
    stream = own
    for section in range(2):
        qkv, w_out, router, gain_one, gain_two, table, expert_in, expert_down = weights[section]
        route_rows = section_routes[section]
        side = beside(stream)
        pieces = (stream, flip(stream), side, flip(side))
        outcome, mixed, gathered, stats = call(
            functools.partial(attention_forward, sizes), "attention_forward",
            [shape((GROUP, span, width), BF16), shape((length, 3 * width), BF16),
             shape((length, features), BF16), shape((8, length), F32)],
            [*pieces, gain_one, qkv, table], scalars=ids,
            scratch=[*bias_scratch, pltpu.VMEM((width, length), F32)], flops=4 << 30,
        )
        attended = regroup(outcome)
        outgoing, middle, normed_two, aux = call(
            functools.partial(after_attention, capacity), "after_attention",
            [shape((slots, features), BF16), shape((span, features), F32),
             shape((span, features), BF16), shape((span, 128), F32)],
            [attended, stream, w_out, gain_two, router, route_rows], flops=1 << 30,
        )
        arrived = exchange(outgoing, experts, capacity)
        activation, slope, produced = run_expert_forward(arrived, expert_in, expert_down)
        returned = exchange(produced, experts, capacity)
        result, difference = call(
            combine, "combine", [shape((span, features), BF16), shape((span, features), F32)],
            [returned, aux, middle], flops=1 << 30,
        )
        states.append((stream, outcome, mixed, gathered, stats, attended, middle, normed_two, aux,
                       arrived, activation, slope, difference))
        results.append(result)
        stream = result

    home = [
        to_home(jnp.where((zhi ^ turn) == 0, results[0], results[1]), turn) for turn in range(2)
    ]
    section_outputs = jnp.stack([
        jnp.where(core == 0, home[0], home[1]), jnp.where(core == 0, home[1], home[0])
    ])

    upstream = given
    small_grads = [None, None]
    qkv_grads = [None, None]
    expert_states = [None, None]
    partials = [None, None]
    stream_grads = [None, None]
    for section in (1, 0):
        qkv, w_out, router, gain_one, gain_two, table, expert_in, expert_down = weights[section]
        (stream, outcome, mixed, gathered, stats, attended, middle, normed_two, aux,
         arrived, activation, slope, difference) = states[section]
        route_rows = section_routes[section]
        (spread,) = call(spread_grads, "spread_grads", [shape((slots, features), BF16)],
                         [upstream, aux], flops=1 << 30)
        arrived_grad = exchange(spread, experts, capacity)
        hidden_grad, rows_grad = run_expert_backward(arrived_grad, expert_in, expert_down, slope)
        returned = exchange(rows_grad, experts, capacity)
        expert_states[section] = (arrived, hidden_grad, activation, arrived_grad)
        wanted = (core != section).astype(jnp.int32).reshape(1)
        partials[section] = [
            lax.ppermute(part, "section", [(1 - section, section)])
            for part in run_weight_partials(wanted, *expert_states[section])
        ]
        middle_grad, attended_grad, out_grad, router_grad, gain_two_grad = call(
            before_attention, "before_attention",
            [shape((span, features), F32), shape((GROUP, span, width), BF16),
             shape((features, features), F32), shape((features, experts), F32), shape((1, features), F32)],
            [returned, aux, upstream, difference, middle, normed_two, attended, gain_two, router, w_out,
             route_rows], flops=2 << 30,
        )
        small_grads[section] = jnp.concatenate([out_grad, router_grad, gain_two_grad.T], axis=1)
        grads = regroup(attended_grad)
        kept, sent, qkv_grad, gain_one_grad, table_grad = call(
            functools.partial(attention_backward, sizes), "attention_backward",
            [shape((2, span, features), BF16), shape((2, span, features), BF16),
             shape((features, 3 * width), F32), shape((1, features), F32), shape((heads * GROUP * 2 * blocks, blocks), F32)],
            [mixed, stats, outcome, grads, gathered, gain_one, qkv, table], scalars=ids,
            scratch=[*bias_scratch, pltpu.VMEM((length, 3 * width), BF16),
                     pltpu.VMEM((GROUP, span, span), F32), pltpu.VMEM((length, size), F32),
                     pltpu.VMEM((length, size), F32), pltpu.VMEM((size, length), F32),
                     pltpu.VMEM((heads * GROUP * 2 * blocks, span), F32)],
            flops=8 << 30,
        )
        pair = kept.astype(F32) + flip(sent).astype(F32)
        stay = lax.dynamic_index_in_dim(pair, zlo, 0, keepdims=False)
        leave = lax.dynamic_index_in_dim(pair, 1 - zlo, 0, keepdims=False).astype(BF16)
        wide, low = call(
            first_norm_grad, "first_norm_grad", [shape((span, features), F32), shape((span, features), BF16)],
            [stay, beside(leave), stream, gain_one, middle_grad],
        )
        table_total = bucket_sums(table_grad.reshape(heads, GROUP, 2, blocks, blocks), buckets)
        per_block = buckets // (ranks // 2)
        block_rows = features // (ranks // 2)
        table_column = jnp.pad(
            table_total.T.reshape(ranks // 2, per_block, heads),
            ((0, 0), (0, block_rows - per_block), (0, 0)),
        ).reshape(features, heads)
        packed_grad = jnp.concatenate([qkv_grad, gain_one_grad.T, table_column], axis=1)
        packed_grad = jnp.pad(packed_grad, ((0, 0), (0, -packed_grad.shape[1] % 128)))
        qkv_grads[section] = packed_grad.astype(BF16)
        stream_grads[section] = low
        upstream = low

    def spread_sum(block, axes, parts):
        rows, columns = block.shape
        moved = lax.all_to_all(
            block.reshape(parts, rows // parts, columns), axes, split_axis=0, concat_axis=0, tiled=True
        )
        return jnp.sum(moved.astype(F32), axis=0)

    def of_core(pair, which):
        return jnp.where(which == 0, pair[0], pair[1])

    shared = of_core(small_grads, core) + flip(of_core(small_grads, 1 - core).astype(BF16)).astype(F32)
    shared = jnp.pad(shared, ((0, 0), (0, -shared.shape[1] % 128))).astype(BF16)
    shared = spread_sum(shared, RANKS, ranks)
    grad_out = shared[:, :features]
    grad_router = shared[:, features : features + experts]
    grad_gain_two = shared[:, features + experts]

    reduced = jnp.stack([spread_sum(block, ("expert", "zhi"), ranks // 2) for block in qkv_grads])
    half = reduced.shape[1] // 2
    columns = reduced.shape[2]
    heads_of = reduced.reshape(2, 2, half, columns)
    gains_part = reduced[:, :, 3 * width].reshape(2, 2, half)
    per_row = buckets // ranks
    table_part = reduced[:, : 2 * per_row, 3 * width + 1 : 3 * width + 1 + heads].reshape(2, 2, per_row, heads)
    heads_of = heads_of.at[:, :, :, 3 * width + 1 :].set(0.0)
    heads_of = heads_of.at[:, :, :per_row, 3 * width + 1 : 3 * width + 1 + heads].set(table_part)
    sending = jnp.transpose(heads_of, (1, 0, 2, 3)).reshape(GROUP, half, columns)
    gathered_grad = regroup(sending)
    split = gathered_grad[:, :, : 3 * width].reshape(GROUP, half, 3, width)
    grad_qkv = jnp.transpose(split, (1, 2, 0, 3)).reshape(half, 3 * features)
    grad_gain_one = jnp.sum(gathered_grad[:, :, 3 * width], axis=0)
    grad_table = jnp.transpose(
        gathered_grad[:, :per_row, 3 * width + 1 : 3 * width + 1 + heads], (1, 0, 2)
    ).reshape(per_row, head_count)
    grad_gains = jnp.stack([grad_gain_one, grad_gain_two])

    home = [
        to_home(jnp.where((zhi ^ turn) == 0, stream_grads[0], stream_grads[1]), turn) for turn in range(2)
    ]
    section_grads = jnp.stack([
        jnp.where(core == 0, home[0], home[1]), jnp.where(core == 0, home[1], home[0])
    ]).astype(F32)

    sent_in = jnp.where(core == 0, partials[0][0], partials[1][0])
    sent_down = jnp.where(core == 0, partials[0][1], partials[1][1])
    grad_in, grad_down = run_weight_totals(core_id, expert_states[0], expert_states[1], sent_in, sent_down)
    return (
        section_outputs[None, :, None],
        section_grads[None, :, None],
        grad_qkv[None],
        grad_out[None],
        grad_router[None],
        grad_gains[None],
        grad_table[None],
        grad_in[None, None],
        grad_down[None, None],
    )


def solution(mesh):
    sections, ranks, pieces = mesh.devices.shape
    work = Mesh(
        mesh.devices.reshape(sections, ranks, pieces // 2, 2), ("section", "expert", "zhi", "zlo")
    )
    piece = ("zhi", "zlo")
    in_specs = (
        P(None, "expert", piece, None),
        P(None, "expert", piece, None),
        P("section", RANKS, None),
        P("section", RANKS, None),
        P("section", RANKS, None),
        P("section", None, RANKS),
        P("section", RANKS, None),
        P("section", RANKS, None, None),
        P("section", RANKS, None, None),
        P("section", None, "expert", piece, None),
    )
    out_specs = (
        P("section", None, "expert", piece, None),
        P("section", None, "expert", piece, None),
        P("section", RANKS, None),
        P("section", RANKS, None),
        P("section", RANKS, None),
        P("section", None, RANKS),
        P("section", RANKS, None),
        P("section", RANKS, None, None),
        P("section", RANKS, None, None),
    )
    return jax.shard_map(per_device, mesh=work, in_specs=in_specs, out_specs=out_specs, check_vma=False)
```

```python
import functools

import jax
import jax.numpy as jnp
from jax import lax
from jax.experimental import pallas as pl
from jax.experimental.pallas import tpu as pltpu
from jax.sharding import Mesh
from jax.sharding import PartitionSpec as P

F32 = jnp.float32
BF16 = jnp.bfloat16
EPS = 1e-06
MASKED = -1e30
GROUP = 4
RANKS = ("expert", "zhi", "zlo")
VMEM_LIMIT = 60 << 20

NN = (((1,), (0,)), ((), ()))
NT = (((1,), (1,)), ((), ()))
TN = (((0,), (0,)), ((), ()))


def mm(left, right, dims=NN):
    return lax.dot_general(left, right, dims, preferred_element_type=F32)


def inverse_rms(values):
    return lax.rsqrt(jnp.mean(values * values, axis=-1, keepdims=True) + EPS)


def whole(array):
    rank = len(array.shape)
    return pl.BlockSpec(array.shape, lambda *unused: (0,) * rank)


def ordered(body, skipped):
    def inner(*refs):
        return body(*refs[skipped:])

    return inner if skipped else body


def call(body, name, outs, args, scalars=None, scratch=(), flops=0, after=()):
    specs = [pl.BlockSpec(memory_space=pl.ANY)] * len(after)
    specs += [pl.BlockSpec(memory_space=pltpu.SMEM)] if scalars is not None else []
    specs += [pl.BlockSpec(memory_space=pltpu.VMEM)] * len(args)
    operands = list(after) + ([scalars] if scalars is not None else []) + list(args)
    moved = sum(a.size * a.dtype.itemsize for a in list(args) + list(outs))
    body = ordered(body, len(after))
    return pl.pallas_call(
        body,
        name=name,
        in_specs=specs,
        out_specs=[pl.BlockSpec(memory_space=pltpu.VMEM)] * len(outs),
        out_shape=list(outs),
        scratch_shapes=list(scratch),
        compiler_params=pltpu.CompilerParams(vmem_limit_bytes=VMEM_LIMIT),
        cost_estimate=pl.CostEstimate(flops=flops, bytes_accessed=moved, transcendentals=0),
    )(*operands)


def shape(dims, dtype):
    return jax.ShapeDtypeStruct(tuple(dims), dtype)


def bucket_onehot(buckets, span, spacing):
    width = 2 * span * GROUP
    column = lax.broadcasted_iota(jnp.int32, (buckets, width), 1)
    delta = column // (2 * span)
    distance = column - delta * (2 * span) - span + span * delta
    bucket = jnp.where(distance >= 0, distance // spacing, -1)
    row = lax.broadcasted_iota(jnp.int32, (buckets, width), 0)
    return (bucket == row).astype(BF16)


def fill_bias(first_head, heads, table, vectors, bias, span, spacing):
    buckets, head_count = table.shape
    hot = bucket_onehot(buckets, span, spacing)
    rows = mm(table[...], hot, TN)
    column = lax.broadcasted_iota(jnp.int32, (1, 2 * span * GROUP), 1)
    rows = jnp.where(column < span, MASKED, rows)
    vectors[0:head_count, :] = rows
    for head in range(heads):
        picked = vectors[pl.ds(first_head + head, 1), :]
        for delta in range(GROUP):
            piece = picked[:, delta * 2 * span : (delta + 1) * 2 * span]
            spread = jnp.broadcast_to(piece, (span, 2 * span))
            rolled = pltpu.roll(spread, span, 1, stride=1, stride_axis=0)
            bias[head * GROUP + delta] = rolled[:, :span]


def attention_forward(sizes, ids, own, flip, side, side_flip, gain, weight, table,
                      out, mixed, gathered, stats, vectors, bias):
    span, heads, size, spacing, unused = sizes
    width = heads * size
    fill_bias(ids[4] * heads, heads, table, vectors, bias, span, spacing)
    for slot, piece in enumerate((own, flip, side, side_flip)):
        gathered[pl.ds(pl.multiple_of(ids[slot] * span, span), span), :] = piece[...]
    for part in range(GROUP):
        rows = slice(part * span, (part + 1) * span)
        values = gathered[rows, :].astype(F32)
        normed = (values * inverse_rms(values) * gain[...].astype(F32)).astype(BF16)
        mixed[rows, :] = mm(normed, weight[:, : 3 * width]).astype(BF16)
    for head in range(heads):
        columns = slice(head * size, (head + 1) * size)
        query_t = (mixed[:, columns].astype(F32) * size ** (-0.5)).T.astype(BF16)
        key = mixed[:, width + head * size : width + (head + 1) * size]
        value_t = mixed[:, 2 * width + head * size : 2 * width + (head + 1) * size].astype(F32).T.astype(BF16)
        for part in range(GROUP):
            mine = slice(part * span, (part + 1) * span)
            blocks = []
            for other in range(part + 1):
                raw = mm(key[other * span : (other + 1) * span], query_t[:, mine])
                blocks.append(raw + bias[head * GROUP + part - other])
            top = functools.reduce(jnp.maximum, [jnp.max(b, axis=0, keepdims=True) for b in blocks])
            total = jnp.zeros_like(top)
            gained = jnp.zeros((size, span), F32)
            for other, block in enumerate(blocks):
                raised = jnp.exp(block - top)
                total = total + jnp.sum(raised, axis=0, keepdims=True)
                gained = gained + mm(value_t[:, other * span : (other + 1) * span], raised.astype(BF16))
            out[part, columns, :] = (gained / total).astype(BF16)
            stats[head : head + 1, mine] = top + jnp.log(total)


def route_masks(routes, experts):
    lane = lax.broadcasted_iota(jnp.int32, (routes.shape[0], experts), 1)
    return [(routes[:, k : k + 1] == lane).astype(F32) for k in range(2)]


def pick_rows(slot, slots):
    lane = lax.broadcasted_iota(jnp.int32, (slot.shape[0], slots), 1).astype(F32)
    return (lane == slot).astype(BF16)


def fill_slots(aux_t, slots, k):
    row = lax.broadcasted_iota(jnp.int32, (slots, aux_t.shape[1]), 0).astype(F32)
    return (row == aux_t[k : k + 1, :]).astype(BF16)


def after_attention(capacity, attended, own, w_out, gain, router, routes,
                    outgoing, middle, normed_two, aux):
    tokens = own.shape[0]
    experts = router.shape[1]
    slots = experts * capacity
    width = attended.shape[1]
    total = own[...].astype(F32)
    for group in range(GROUP):
        total = total + mm(attended[group], w_out[group * width : (group + 1) * width, :], TN)
    middle[...] = total
    normed = (total * inverse_rms(total) * gain[...].astype(F32)).astype(BF16)
    normed_two[...] = normed
    logits = mm(normed, router[...])
    masks = route_masks(routes, experts)
    members = (masks[0] + masks[1]).astype(BF16)
    row = lax.broadcasted_iota(jnp.int32, (tokens, tokens), 0)
    column = lax.broadcasted_iota(jnp.int32, (tokens, tokens), 1)
    earlier = mm((row > column).astype(BF16), members)
    chosen = [jnp.sum(logits * mask, axis=1, keepdims=True) for mask in masks]
    first = jax.nn.sigmoid(chosen[0] - chosen[1])
    places = [
        routes[:, k : k + 1].astype(F32) * capacity + jnp.sum(earlier * masks[k], axis=1, keepdims=True)
        for k in range(2)
    ]
    lane = lax.broadcasted_iota(jnp.int32, (tokens, 128), 1)
    packed = jnp.zeros((tokens, 128), F32)
    for index, entry in enumerate((places[0], places[1], first, 1.0 - first)):
        packed = jnp.where(lane == index, entry, packed)
    aux[...] = packed
    packed_t = packed.T
    hot = fill_slots(packed_t, slots, 0) + fill_slots(packed_t, slots, 1)
    outgoing[...] = mm(hot, normed).astype(BF16)


def expert_forward(rows, w_in, w_down, activation, slope, produced, total):
    step = pl.program_id(0)

    @pl.when(step == 0)
    def clear():
        total[...] = jnp.zeros_like(total)

    chunk = rows.shape[0] // 4
    for part in range(4):
        mine = slice(part * chunk, (part + 1) * chunk)
        hidden = mm(rows[mine, :], w_in[...])
        half = 0.5 * (1.0 + lax.erf(hidden * 0.7071067811865476))
        bell = jnp.exp(-0.5 * hidden * hidden) * 0.3989422804014327
        raised = (hidden * half).astype(BF16)
        activation[mine, :] = raised
        slope[mine, :] = (half + hidden * bell).astype(BF16)
        total[mine, :] += mm(raised, w_down[...])

    @pl.when(step == pl.num_programs(0) - 1)
    def finish():
        produced[...] = total[...].astype(BF16)


def expert_backward(arrived_grad, w_in, w_down, slope, hidden_grad, rows_grad, total):
    step = pl.program_id(0)

    @pl.when(step == 0)
    def clear():
        total[...] = jnp.zeros_like(total)

    chunk = arrived_grad.shape[0] // 4
    for part in range(4):
        mine = slice(part * chunk, (part + 1) * chunk)
        lifted = mm(arrived_grad[mine, :], w_down[...], NT) * slope[mine, :].astype(F32)
        lowered = lifted.astype(BF16)
        hidden_grad[mine, :] = lowered
        total[mine, :] += mm(lowered, w_in[...], NT)

    @pl.when(step == pl.num_programs(0) - 1)
    def finish():
        rows_grad[...] = total[...].astype(BF16)


def tile_of(hidden):
    return 768 if hidden % 768 == 0 else hidden


def run_expert_forward(rows, w_in, w_down):
    count, features = rows.shape
    hidden = w_in.shape[1]
    tile = tile_of(hidden)
    return pl.pallas_call(
        expert_forward,
        name="expert_forward",
        grid=(hidden // tile,),
        in_specs=[
            whole(rows),
            pl.BlockSpec((features, tile), lambda j: (0, j)),
            pl.BlockSpec((tile, features), lambda j: (j, 0)),
        ],
        out_specs=[
            pl.BlockSpec((count, tile), lambda j: (0, j)),
            pl.BlockSpec((count, tile), lambda j: (0, j)),
            pl.BlockSpec((count, features), lambda j: (0, 0)),
        ],
        out_shape=[shape((count, hidden), BF16), shape((count, hidden), BF16), shape((count, features), BF16)],
        scratch_shapes=[pltpu.VMEM((count, features), F32)],
        compiler_params=pltpu.CompilerParams(vmem_limit_bytes=VMEM_LIMIT),
        cost_estimate=pl.CostEstimate(
            flops=4 * count * features * hidden, bytes_accessed=30 << 20, transcendentals=2 * count * hidden
        ),
    )(rows, w_in, w_down)


def run_expert_backward(arrived_grad, w_in, w_down, slope):
    count, features = arrived_grad.shape
    hidden = w_in.shape[1]
    tile = tile_of(hidden)
    return pl.pallas_call(
        expert_backward,
        name="expert_backward",
        grid=(hidden // tile,),
        in_specs=[
            whole(arrived_grad),
            pl.BlockSpec((features, tile), lambda j: (0, j)),
            pl.BlockSpec((tile, features), lambda j: (j, 0)),
            pl.BlockSpec((count, tile), lambda j: (0, j)),
        ],
        out_specs=[
            pl.BlockSpec((count, tile), lambda j: (0, j)),
            pl.BlockSpec((count, features), lambda j: (0, 0)),
        ],
        out_shape=[shape((count, hidden), BF16), shape((count, features), BF16)],
        scratch_shapes=[pltpu.VMEM((count, features), F32)],
        compiler_params=pltpu.CompilerParams(vmem_limit_bytes=VMEM_LIMIT),
        cost_estimate=pl.CostEstimate(
            flops=4 * count * features * hidden, bytes_accessed=30 << 20, transcendentals=0
        ),
    )(arrived_grad, w_in, w_down, slope)


def weight_partials(scalars, rows, hidden_grad, activation, arrived_grad, grad_in, grad_down):
    @pl.when(scalars[0] == 1)
    def wanted():
        grad_in[...] = mm(rows[...], hidden_grad[...], TN).astype(BF16)
        grad_down[...] = mm(activation[...], arrived_grad[...], TN).astype(BF16)


def run_weight_partials(wanted, rows, hidden_grad, activation, arrived_grad):
    count, features = rows.shape
    hidden = hidden_grad.shape[1]
    tile = tile_of(hidden)
    return pl.pallas_call(
        weight_partials,
        name="weight_partials",
        grid_spec=pltpu.PrefetchScalarGridSpec(
            num_scalar_prefetch=1,
            grid=(hidden // tile,),
            in_specs=[
                pl.BlockSpec((count, features), lambda j, s: (0, 0)),
                pl.BlockSpec((count, tile), lambda j, s: (0, j * s[0])),
                pl.BlockSpec((count, tile), lambda j, s: (0, j * s[0])),
                pl.BlockSpec((count, features), lambda j, s: (0, 0)),
            ],
            out_specs=[
                pl.BlockSpec((features, tile), lambda j, s: (0, j * s[0])),
                pl.BlockSpec((tile, features), lambda j, s: (j * s[0], 0)),
            ],
        ),
        out_shape=[shape((features, hidden), BF16), shape((hidden, features), BF16)],
        compiler_params=pltpu.CompilerParams(vmem_limit_bytes=VMEM_LIMIT),
        cost_estimate=pl.CostEstimate(
            flops=4 * count * features * hidden, bytes_accessed=30 << 20, transcendentals=0
        ),
    )(wanted, rows, hidden_grad, activation, arrived_grad)


def weight_totals(scalars, left, right, sent, left_1, right_1, sent_1, after, total):
    @pl.when(scalars[0] == 0)
    def first():
        total[...] = mm(left[...], right[...], TN) + sent[...].astype(F32)

    @pl.when(scalars[0] == 1)
    def second():
        total[...] = mm(left_1[...], right_1[...], TN) + sent_1[...].astype(F32)


def run_weight_totals(core, first, second, tiled_left, after):
    count, features = first[1 if tiled_left else 0].shape
    hidden = first[0 if tiled_left else 1].shape[1]
    tile = tile_of(hidden)

    def specs(which):
        def step(j, s):
            return jnp.where(s[0] == which, j, 0)

        full = pl.BlockSpec((count, features), lambda j, s: (0, 0))
        part = pl.BlockSpec((count, tile), lambda j, s: (0, step(j, s)))
        if tiled_left:
            return [part, full, pl.BlockSpec((tile, features), lambda j, s: (step(j, s), 0))]
        return [full, part, pl.BlockSpec((features, tile), lambda j, s: (0, step(j, s)))]

    if tiled_left:
        out_spec = pl.BlockSpec((tile, features), lambda j, s: (j, 0))
        dims = (hidden, features)
    else:
        out_spec = pl.BlockSpec((features, tile), lambda j, s: (0, j))
        dims = (features, hidden)
    return pl.pallas_call(
        weight_totals,
        name="weight_totals",
        grid_spec=pltpu.PrefetchScalarGridSpec(
            num_scalar_prefetch=1, grid=(hidden // tile,),
            in_specs=specs(0) + specs(1) + [pl.BlockSpec(memory_space=pl.ANY)], out_specs=out_spec,
        ),
        out_shape=shape(dims, F32),
        compiler_params=pltpu.CompilerParams(vmem_limit_bytes=VMEM_LIMIT),
        cost_estimate=pl.CostEstimate(
            flops=2 * count * features * hidden, bytes_accessed=30 << 20, transcendentals=0
        ),
    )(core, *first, *second, after)


def combine(returned, aux, middle, result, difference):
    slots = returned.shape[0]
    packed = aux[...]
    outs = [mm(pick_rows(packed[:, k : k + 1], slots), returned[...]) for k in range(2)]
    total = middle[...] + packed[:, 2:3] * outs[0] + packed[:, 3:4] * outs[1]
    result[...] = total.astype(BF16)
    difference[...] = outs[0] - outs[1]


def spread_grads(upstream, aux, outgoing):
    slots = outgoing.shape[0]
    packed = aux[...]
    packed_t = packed.T
    values = upstream[...].astype(F32)
    total = jnp.zeros(outgoing.shape, F32)
    for k in range(2):
        total = total + mm(fill_slots(packed_t, slots, k), (values * packed[:, 2 + k : 3 + k]).astype(BF16))
    outgoing[...] = total.astype(BF16)


def norm_backward(values, gain, grad):
    scale = inverse_rms(values)
    unit = values * scale
    lifted = grad * gain
    back = scale * (lifted - unit * jnp.mean(lifted * unit, axis=-1, keepdims=True))
    return back, jnp.sum(grad * unit, axis=0, keepdims=True)


def before_attention(returned, aux, upstream, difference, middle, normed_two, attended, gain,
                     router, w_out, routes, middle_grad, attended_grad, shared_grad):
    slots = returned.shape[0]
    experts = router.shape[1]
    width = attended.shape[1]
    features = w_out.shape[1]
    packed = aux[...]
    hot = pick_rows(packed[:, 0:1], slots) + pick_rows(packed[:, 1:2], slots)
    token_grad = mm(hot, returned[...])
    flow = upstream[...].astype(F32)
    shift = jnp.sum(flow * difference[...], axis=1, keepdims=True) * packed[:, 2:3] * packed[:, 3:4]
    masks = route_masks(routes, experts)
    logits_grad = (shift * (masks[0] - masks[1])).astype(BF16)
    token_grad = token_grad + mm(logits_grad, router[...], NT)
    back, gain_part = norm_backward(middle[...], gain[...].astype(F32), token_grad)
    total = flow + back
    middle_grad[...] = total
    branch = total.astype(BF16)
    for group in range(GROUP):
        mine = slice(group * width, (group + 1) * width)
        shared_grad[mine, :features] = mm(attended[group], branch).astype(BF16)
        attended_grad[group] = mm(w_out[mine, :], branch, NT).astype(BF16)
    tail = shared_grad.shape[1] - features
    gain_column = jnp.broadcast_to(gain_part, (8, features)).T
    lane = lax.broadcasted_iota(jnp.int32, (features, tail), 1)
    shared_grad[:, features:] = jnp.where(lane == experts, gain_column[:, 0:1], 0.0).astype(BF16)
    shared_grad[:, features : features + experts] = mm(normed_two[...], logits_grad, TN).astype(BF16)


def attention_backward(sizes, ids, mixed, stats, attended, grads, gathered, gain, weight, table,
                       stay, leave, sent, shared_grad,
                       vectors, bias, mixed_grad, sums, key_total, value_total, turned, strips):
    span, heads, size, spacing, ranks = sizes
    width = heads * size
    count = span // spacing
    buckets = table.shape[0]
    features = weight.shape[0]
    row = lax.broadcasted_iota(jnp.int32, (span, span), 0)
    column = lax.broadcasted_iota(jnp.int32, (span, span), 1)
    later = (column % spacing) >= (row % spacing)
    lane = lax.broadcasted_iota(jnp.int32, (span, 128), 0) // spacing
    backwards = (count - 1 - lane == lax.broadcasted_iota(jnp.int32, (span, 128), 1)).astype(F32)
    strips[...] = jnp.zeros_like(strips)
    fill_bias(ids[4] * heads, heads, table, vectors, bias, span, spacing)
    for head in range(heads):
        columns = slice(head * size, (head + 1) * size)
        key_columns = slice(width + head * size, width + (head + 1) * size)
        value_columns = slice(2 * width + head * size, 2 * width + (head + 1) * size)
        query = (mixed[:, columns].astype(F32) * size ** (-0.5)).astype(BF16)
        query_t = query.astype(F32).T.astype(BF16)
        key = mixed[:, key_columns]
        key_t = key.astype(F32).T.astype(BF16)
        value = mixed[:, value_columns]
        key_total[...] = jnp.zeros_like(key_total)
        value_total[...] = jnp.zeros_like(value_total)
        sums[...] = jnp.zeros_like(sums)
        for part in range(GROUP):
            mine = slice(part * span, (part + 1) * span)
            grad_t = grads[part, columns, :]
            delta_row = jnp.sum(
                grad_t.astype(F32) * attended[part, columns, :].astype(F32), axis=0, keepdims=True
            )
            level = stats[head : head + 1, mine]
            query_total = jnp.zeros((size, span), F32)
            for other in range(part + 1):
                theirs = slice(other * span, (other + 1) * span)
                raw = mm(key[theirs], query_t[:, mine])
                prob = jnp.exp(raw + (bias[head * GROUP + part - other] - level))
                prob_grad = mm(value[theirs], grad_t)
                low = (prob * (prob_grad - delta_row)).astype(BF16)
                sums[part - other] += low.astype(F32)
                query_total = query_total + mm(key_t[:, theirs], low)
                key_total[theirs, :] += mm(low, query[mine])
                value_total[theirs, :] += mm(prob.astype(BF16), grad_t, NT)
            turned[:, mine] = query_total * size ** (-0.5)
        mixed_grad[:, columns] = turned[...].T.astype(BF16)
        mixed_grad[:, key_columns] = key_total[...].astype(BF16)
        mixed_grad[:, value_columns] = value_total[...].astype(BF16)
        for delta in range(GROUP):
            upper = jnp.where(later, sums[delta], 0.0)
            for side, block in enumerate((upper, sums[delta] - upper)):
                tiles = lax.dot_general(
                    jnp.sum(block.reshape(count, spacing, span), axis=1), backwards, NN,
                    precision=lax.Precision.HIGHEST, preferred_element_type=F32,
                )
                turned_tiles = pltpu.roll(tiles, 0, 1, stride=1, stride_axis=0)
                place = (delta * 2 + side) * 128
                strips[head : head + 1, place : place + 128] = jnp.sum(turned_tiles, axis=0, keepdims=True)
    entry = lax.broadcasted_iota(jnp.int32, (GROUP * 2 * 128, 128), 0)
    bucket = (entry // 256) * count + count - 1 - entry % 128 - (entry // 128) % 2
    hot = (bucket == lax.broadcasted_iota(jnp.int32, (GROUP * 2 * 128, 128), 1)) & (entry % 128 < 2 * count)
    table_rows = lax.dot_general(
        strips[...], hot.astype(F32), NN, precision=lax.Precision.HIGHEST, preferred_element_type=F32
    )
    gain_total = jnp.zeros((1, features), F32)
    weight_total = jnp.zeros((features, 3 * width), F32)
    for part in range(GROUP):
        place = ids[5 + part]
        rows = pl.ds(pl.multiple_of(place * span, span), span)
        values = gathered[rows, :].astype(F32)
        unit = values * inverse_rms(values)
        normed = (unit * gain[...].astype(F32)).astype(BF16)
        lowered = mixed_grad[rows, :]
        weight_total = weight_total + mm(normed, lowered, TN)
        back = mm(lowered, weight[:, : 3 * width], NT)
        gain_total = gain_total + jnp.sum(back * unit, axis=0, keepdims=True)
        if part == 0:
            stay[...] = back.astype(BF16)
        elif part == 1:
            leave[...] = back.astype(BF16)
        else:
            sent[part - 2] = back.astype(BF16)
    owned = buckets // ranks
    bucket = lax.broadcasted_iota(jnp.int32, (128, features), 0)
    target = (bucket // owned) * (features // ranks) + bucket % owned
    spot = (target == lax.broadcasted_iota(jnp.int32, (128, features), 1)) & (bucket < buckets)
    placed = lax.dot_general(
        table_rows, spot.astype(F32), NN, precision=lax.Precision.HIGHEST, preferred_element_type=F32
    )
    extra = jnp.concatenate([placed, jnp.broadcast_to(gain_total, (8, features))], axis=0)
    shared_grad[...] = jnp.zeros_like(shared_grad)
    shared_grad[:, : 3 * width] = weight_total.astype(BF16)
    shared_grad[:, 3 * width : 3 * width + 16] = extra.T.astype(BF16)


def first_norm_grad(stay, partner, arrived, own, gain, middle_grad, low):
    grad = stay[...].astype(F32) + partner[0].astype(F32) + arrived[...].astype(F32)
    back, unused = norm_backward(own[...].astype(F32), gain[...].astype(F32), grad)
    low[...] = (middle_grad[...] + back).astype(BF16)


FLIP = [(0, 1), (1, 0)]


def flip(block):
    return lax.ppermute(block, "section", FLIP)


def beside(block):
    return lax.ppermute(block, "zlo", FLIP)


def scatter_pairs(turn):
    return [
        (core * 4 + a * 2 + b, b * 4 + (core ^ turn) * 2 + a)
        for core in range(2)
        for a in range(2)
        for b in range(2)
    ]


def to_working(block, turn):
    return lax.ppermute(block, ("section", "zhi", "zlo"), scatter_pairs(turn))


def to_home(block, section, batch):
    turn = section ^ batch
    pairs = [(after, before) for before, after in scatter_pairs(turn) if before // 4 == section]
    return lax.ppermute(block, ("section", "zhi", "zlo"), pairs)


def home_pair(blocks, core):
    return jnp.stack([
        jnp.where(core == 0, to_home(blocks[0], 0, batch), to_home(blocks[1], 1, batch))
        for batch in range(2)
    ])


def exchange(block, experts, capacity):
    features = block.shape[-1]
    moved = lax.all_to_all(
        block.reshape(experts, capacity, features), RANKS, split_axis=0, concat_axis=0, tiled=True
    )
    return moved.reshape(experts * capacity, features)


def spread_sum(block, axes, parts):
    rows, columns = block.shape
    moved = lax.all_to_all(
        block.reshape(parts, rows // parts, columns), axes, split_axis=0, concat_axis=0, tiled=True
    )
    return jnp.sum(moved.astype(F32), axis=0)


def regroup(block):
    return lax.all_to_all(block, ("zlo", "section"), split_axis=0, concat_axis=0, tiled=True)


def gather_columns(blocks, out, staged, local_sem, send_sem, recv_sem, stage_send, stage_recv):
    core = lax.axis_index("section")
    expert = lax.axis_index("expert")
    zhi = lax.axis_index("zhi")
    zlo = lax.axis_index("zlo")
    place = 2 * zhi + zlo
    other = 1 - core
    beside_x = expert + 1 - 2 * (expert % 2)
    beside_y = (expert + 2) % 4
    places = [place, place + 1 - 2 * zlo, (place + 2) % 4, 3 - place]

    def at(section, rank_expert, rank_place):
        return out.at[section, rank_expert * 4 + rank_place]

    barrier = pltpu.get_barrier_semaphore()
    peers = [{"section": other}, {"expert": beside_x}, {"expert": beside_y}]
    peers += [{"zhi": spot // 2, "zlo": spot % 2} for spot in places[1:]]
    for peer in peers:
        pl.semaphore_signal(barrier, inc=1, device_id=peer, device_id_type=pl.DeviceIdType.MESH)
    pl.semaphore_wait(barrier, len(peers))

    started = []

    def send(source, target, index, section, owner, spot, peer):
        copy = pltpu.make_async_remote_copy(
            src_ref=source, dst_ref=target, send_sem=send_sem.at[index],
            recv_sem=recv_sem.at[section, owner * 4 + spot], device_id=peer,
            device_id_type=pl.DeviceIdType.MESH,
        )
        copy.start()
        started.append(copy)

    def arrived(section, owner, spot):
        pltpu.make_async_remote_copy(
            src_ref=at(section, owner, spot), dst_ref=at(section, owner, spot), send_sem=send_sem.at[0],
            recv_sem=recv_sem.at[section, owner * 4 + spot], device_id={"section": other},
            device_id_type=pl.DeviceIdType.MESH,
        ).wait_recv()

    trades = []
    for parity in range(2):
        trade = pltpu.make_async_remote_copy(
            src_ref=blocks.at[2 * parity + other], dst_ref=staged.at[parity], send_sem=stage_send.at[parity],
            recv_sem=stage_recv.at[parity], device_id={"section": other},
            device_id_type=pl.DeviceIdType.MESH,
        )
        trade.start()
        trades.append(trade)

    index = 0
    for which in range(2):
        section = core if which == 0 else other
        if which == 1:
            for trade in trades:
                trade.wait()

        def block_for(parity):
            return blocks.at[2 * parity + core] if which == 0 else staged.at[parity]

        for step, spot in enumerate(places[1:]):
            send(block_for(spot % 2), at(section, expert, place), index, section, expert, place,
                 {"zhi": spot // 2, "zlo": spot % 2})
            index += 1
        for peer in (beside_x, beside_y):
            send(block_for(zlo), at(section, expert, place), index, section, expert, place, {"expert": peer})
            index += 1
        local = pltpu.make_async_copy(block_for(zlo), at(section, expert, place), local_sem)
        local.start()
        local.wait()
    sections = (core, other)
    for spot in places[1:]:
        for section in sections:
            arrived(section, expert, spot)
            for peer in (beside_x, beside_y):
                send(at(section, expert, spot), at(section, expert, spot), index, section, expert, spot,
                     {"expert": peer})
                index += 1
    for section in sections:
        for step, spot in enumerate(places):
            arrived(section, beside_x, spot)
            arrived(section, beside_y, spot)
            source, peer = ((beside_x, beside_y), (beside_y, beside_x))[step % 2]
            send(at(section, source, spot), at(section, source, spot), index, section, source, spot,
                 {"expert": peer})
            index += 1
    diagonal = 3 - expert
    for section in sections:
        for spot in places:
            arrived(section, diagonal, spot)
    for copy in started:
        copy.wait_send()


def run_gather_columns(blocks, ranks):
    groups, rows, columns = blocks.shape
    return pl.pallas_call(
        gather_columns,
        name="gather_columns",
        in_specs=[pl.BlockSpec(memory_space=pltpu.VMEM)],
        out_specs=pl.BlockSpec(memory_space=pltpu.VMEM),
        out_shape=shape((2, ranks, rows, columns), blocks.dtype),
        scratch_shapes=[
            pltpu.VMEM((2, rows, columns), blocks.dtype),
            pltpu.SemaphoreType.DMA,
            pltpu.SemaphoreType.DMA((30,)),
            pltpu.SemaphoreType.DMA((2, ranks)),
            pltpu.SemaphoreType.DMA((2,)),
            pltpu.SemaphoreType.DMA((2,)),
        ],
        compiler_params=pltpu.CompilerParams(
            collective_id=0, has_side_effects=True, vmem_limit_bytes=16 << 20
        ),
        cost_estimate=pl.CostEstimate(flops=0, bytes_accessed=40 << 20, transcendentals=0),
    )(blocks)


def per_device(inputs, cotangent, qkv_shard, out_shard, router_shard, gain_shard, table_shard,
               w_expert_in, w_expert_out, routes):
    core = lax.axis_index("section")
    zhi = lax.axis_index("zhi")
    zlo = lax.axis_index("zlo")
    span, features = inputs.shape[2:]
    ranks = lax.axis_size(RANKS)
    shard_rows = qkv_shard.shape[1]
    experts = router_shard.shape[2]
    table_rows, head_count = table_shard.shape[1:]
    buckets = table_rows * ranks
    heads = head_count // GROUP
    size = features // head_count
    width = heads * size
    spacing = GROUP * span // buckets
    capacity = max(2, 4 * span // experts)
    slots = experts * capacity
    group = 2 * zlo + core
    sizes = (span, heads, size, spacing, ranks)
    ids = jnp.stack([
        group, 2 * zlo + 1 - core, 2 * (1 - zlo) + core, 2 * (1 - zlo) + 1 - core, group,
        group, 2 * (1 - zlo) + core, 2 * zlo + 1 - core, 2 * (1 - zlo) + 1 - core,
    ]).astype(jnp.int32)
    core_id = core.astype(jnp.int32).reshape(1)

    own = to_working(lax.dynamic_index_in_dim(inputs, core, 0, keepdims=False)[0], 0)
    given = to_working(lax.dynamic_index_in_dim(cotangent, core, 0, keepdims=False)[0], 0)
    route_parts = [
        to_working(lax.dynamic_index_in_dim(routes[0], core ^ turn, 0, keepdims=False)[0], turn)
        for turn in range(2)
    ]
    section_routes = [
        jnp.where(zhi == section, route_parts[0], route_parts[1]) for section in range(2)
    ]

    small = jnp.concatenate([
        router_shard[0],
        gain_shard[0].T,
        jnp.pad(table_shard[0], ((0, shard_rows - table_rows), (0, 0))),
    ], axis=1)
    by_group = jnp.transpose(
        qkv_shard[0].reshape(shard_rows, 3, GROUP, width), (2, 0, 1, 3)
    ).reshape(GROUP, shard_rows, 3 * width)
    by_group = jnp.concatenate(
        [by_group, jnp.broadcast_to(small[None], (GROUP, *small.shape))], axis=2
    )
    by_group = jnp.pad(by_group, ((0, 0), (0, 0), (0, -by_group.shape[2] % 128)))
    columns = by_group.shape[2]
    if lax.axis_size("expert") == 4:
        early = run_gather_columns(by_group, ranks).reshape(2, features, columns)
        early = [early[0], early[1]]
    else:
        whole_early = lax.all_gather(by_group, RANKS, axis=1, tiled=True)
        kept = lax.dynamic_index_in_dim(whole_early, group, 0, keepdims=False)
        traded = flip(lax.dynamic_index_in_dim(whole_early, 2 * zlo + 1 - core, 0, keepdims=False))
        early = [
            jnp.where(core == section, kept, traded).reshape(features, columns) for section in range(2)
        ]
    w_out_own = lax.all_gather(out_shard[0], RANKS, axis=0, tiled=True)
    w_in = w_expert_in[0, 0]
    w_down = w_expert_out[0, 0]
    w_in_other = flip(w_in)
    w_down_other = flip(w_down)

    weights = []
    for section in range(2):
        is_own = core == section
        others = early[section][:, 3 * width :]
        router = others[:, :experts]
        gains = others[:, experts : experts + 2].T
        table = others[:, experts + 2 : experts + 2 + head_count]
        table = table.reshape(ranks, shard_rows, head_count)[:, :table_rows].reshape(buckets, head_count)
        weights.append((
            early[section], router, gains[0:1], gains[1:2], table,
            jnp.where(is_own, w_in, w_in_other), jnp.where(is_own, w_down, w_down_other),
        ))

    bias_scratch = [
        pltpu.VMEM((-(-head_count // 8) * 8, 2 * span * GROUP), F32),
        pltpu.VMEM((heads * GROUP, span, span), F32),
    ]
    length = GROUP * span
    blocks = span // spacing
    states = []
    results = []
    stream = own
    for section in range(2):
        qkv, router, gain_one, gain_two, table, expert_in, expert_down = weights[section]
        route_rows = section_routes[section]
        side = beside(stream)
        pieces = (stream, flip(stream), side, flip(side))
        outcome, mixed, gathered, stats = call(
            functools.partial(attention_forward, sizes), "attention_forward",
            [shape((GROUP, width, span), BF16), shape((length, 3 * width), BF16),
             shape((length, features), BF16), shape((8, length), F32)],
            [*pieces, gain_one, qkv, table], scalars=ids, scratch=bias_scratch, flops=4 << 30,
        )
        attended = regroup(outcome)
        if section == 0:
            attended, w_out_own = lax.optimization_barrier((attended, w_out_own))
            w_out_other = flip(w_out_own)
            w_outs = [jnp.where(core == which, w_out_own, w_out_other) for which in range(2)]
        w_out = w_outs[section]
        outgoing, middle, normed_two, aux = call(
            functools.partial(after_attention, capacity), "after_attention",
            [shape((slots, features), BF16), shape((span, features), F32),
             shape((span, features), BF16), shape((span, 128), F32)],
            [attended, stream, w_out, gain_two, router, route_rows], flops=1 << 30,
        )
        arrived = exchange(outgoing, experts, capacity)
        activation, slope, produced = run_expert_forward(arrived, expert_in, expert_down)
        returned = exchange(produced, experts, capacity)
        result, difference = call(
            combine, "combine", [shape((span, features), BF16), shape((span, features), F32)],
            [returned, aux, middle], flops=1 << 30,
        )
        states.append((stream, outcome, mixed, gathered, stats, attended, middle, normed_two, aux,
                       arrived, activation, slope, difference))
        results.append(result)
        stream = result

    section_outputs = home_pair(results, core)

    upstream = given
    shared_grads = [None, None]
    shared_partner = [None, None]
    shared_qkv = [None, None]
    qkv_grads = [None, None]
    expert_states = [None, None]
    partials = [None, None]
    stream_grads = [None, None]
    for section in (1, 0):
        qkv, router, gain_one, gain_two, table, expert_in, expert_down = weights[section]
        w_out = w_outs[section]
        (stream, outcome, mixed, gathered, stats, attended, middle, normed_two, aux,
         arrived, activation, slope, difference) = states[section]
        route_rows = section_routes[section]
        (spread,) = call(spread_grads, "spread_grads", [shape((slots, features), BF16)],
                         [upstream, aux], flops=1 << 30)
        arrived_grad = exchange(spread, experts, capacity)
        if section == 0:
            waiting, arrived_grad = lax.optimization_barrier((shared_qkv[1], arrived_grad))
            qkv_grads[1] = spread_sum(waiting, ("expert", "zhi"), ranks // 2)
        hidden_grad, rows_grad = run_expert_backward(arrived_grad, expert_in, expert_down, slope)
        returned = exchange(rows_grad, experts, capacity)
        expert_states[section] = (arrived, hidden_grad, activation, arrived_grad)
        wanted = (core != section).astype(jnp.int32).reshape(1)
        shares = run_weight_partials(wanted, *expert_states[section])
        partials[section] = [lax.ppermute(part, "section", [(1 - section, section)]) for part in shares]
        middle_grad, attended_grad, shared_grads[section] = call(
            before_attention, "before_attention",
            [shape((span, features), F32), shape((GROUP, width, span), BF16),
             shape((features, features + -(-(experts + 1) // 128) * 128), BF16)],
            [returned, aux, upstream, difference, middle, normed_two, attended, gain_two, router, w_out,
             route_rows], flops=2 << 30, after=shares[:1],
        )
        shared_partner[section] = lax.ppermute(shared_grads[section], "section", [(1 - section, section)])
        grads = regroup(attended_grad)
        stay, leave, sent, shared_qkv[section] = call(
            functools.partial(attention_backward, sizes), "attention_backward",
            [shape((span, features), BF16), shape((span, features), BF16), shape((2, span, features), BF16),
             shape((features, -(-(3 * width + 16) // 128) * 128), BF16)],
            [mixed, stats, outcome, grads, gathered, gain_one, qkv, table], scalars=ids,
            scratch=[*bias_scratch, pltpu.VMEM((length, 3 * width), BF16),
                     pltpu.VMEM((GROUP, span, span), F32), pltpu.VMEM((length, size), F32),
                     pltpu.VMEM((length, size), F32), pltpu.VMEM((size, length), F32),
                     pltpu.VMEM((8, GROUP * 2 * 128), F32)],
            flops=8 << 30,
        )
        partner = flip(sent)
        leave = leave + partner[1]
        filler = ()
        if section == 0:
            leave, waiting = lax.optimization_barrier((leave, shared_qkv[0]))
            qkv_grads[0] = spread_sum(waiting, ("expert", "zhi"), ranks // 2)
            grad_in = run_weight_totals(
                core_id, *[(expert_states[which][0], expert_states[which][1], partials[which][0])
                           for which in range(2)], False, sent)
            filler = (grad_in,)
        arrived_share = beside(leave)
        (low,) = call(
            first_norm_grad, "first_norm_grad", [shape((span, features), BF16)],
            [stay, partner, arrived_share, stream, gain_one, middle_grad], after=filler,
        )
        stream_grads[section] = low
        upstream = low

    shared = jnp.where(
        core == 0,
        shared_grads[0].astype(F32) + shared_partner[0].astype(F32),
        shared_grads[1].astype(F32) + shared_partner[1].astype(F32),
    ).astype(BF16)
    shared = spread_sum(shared, RANKS, ranks)
    grad_out = shared[:, :features]
    grad_router = shared[:, features : features + experts]
    grad_gain_two = shared[:, features + experts]

    columns = qkv_grads[0].shape[1]
    halves = [block.reshape(2, shard_rows, columns) for block in qkv_grads]
    sending = jnp.stack([halves[0][0], halves[1][0], halves[0][1], halves[1][1]])
    owned = regroup(sending)
    split = owned[:, :, : 3 * width].reshape(GROUP, shard_rows, 3, width)
    grad_qkv = jnp.transpose(split, (1, 2, 0, 3)).reshape(shard_rows, 3 * features)
    grad_table = jnp.transpose(
        owned[:, :table_rows, 3 * width : 3 * width + heads], (1, 0, 2)
    ).reshape(table_rows, head_count)
    grad_gain_one = jnp.sum(owned[:, :, 3 * width + 8], axis=0)
    grad_gains = jnp.stack([grad_gain_one, grad_gain_two])

    section_grads = home_pair(stream_grads, core).astype(F32)

    grad_down = run_weight_totals(
        core_id, *[(expert_states[which][2], expert_states[which][3], partials[which][1])
                   for which in range(2)], True, stream_grads[0])
    return (
        section_outputs[None, :, None],
        section_grads[None, :, None],
        grad_qkv[None],
        grad_out[None],
        grad_router[None],
        grad_gains[None],
        grad_table[None],
        grad_in[None, None],
        grad_down[None, None],
    )


def solution(mesh):
    sections, ranks, pieces = mesh.devices.shape
    work = Mesh(
        mesh.devices.reshape(sections, ranks, pieces // 2, 2), ("section", "expert", "zhi", "zlo")
    )
    piece = ("zhi", "zlo")
    in_specs = (
        P(None, "expert", piece, None),
        P(None, "expert", piece, None),
        P("section", RANKS, None),
        P("section", RANKS, None),
        P("section", RANKS, None),
        P("section", None, RANKS),
        P("section", RANKS, None),
        P("section", RANKS, None, None),
        P("section", RANKS, None, None),
        P("section", None, "expert", piece, None),
    )
    out_specs = (
        P("section", None, "expert", piece, None),
        P("section", None, "expert", piece, None),
        P("section", RANKS, None),
        P("section", RANKS, None),
        P("section", RANKS, None),
        P("section", None, RANKS),
        P("section", RANKS, None),
        P("section", RANKS, None, None),
        P("section", RANKS, None, None),
    )
    return jax.shard_map(per_device, mesh=work, in_specs=in_specs, out_specs=out_specs, check_vma=False)
```

```python
import functools

import jax
import jax.numpy as jnp
from jax import lax
from jax.experimental import pallas as pl
from jax.experimental.pallas import tpu as pltpu
from jax.sharding import Mesh
from jax.sharding import PartitionSpec as P

F32 = jnp.float32
BF16 = jnp.bfloat16
EPS = 1e-06
MASKED = -1e30
GROUP = 4
RANKS = ("expert", "zhi", "zlo")
VMEM_LIMIT = 60 << 20

NN = (((1,), (0,)), ((), ()))
NT = (((1,), (1,)), ((), ()))
TN = (((0,), (0,)), ((), ()))


def mm(left, right, dims=NN):
    return lax.dot_general(left, right, dims, preferred_element_type=F32)


def inverse_rms(values):
    return lax.rsqrt(jnp.mean(values * values, axis=-1, keepdims=True) + EPS)


def whole(array):
    rank = len(array.shape)
    return pl.BlockSpec(array.shape, lambda *unused: (0,) * rank)


def ordered(body, skipped):
    def inner(*refs):
        return body(*refs[skipped:])

    return inner if skipped else body


def call(body, name, outs, args, scalars=None, scratch=(), flops=0, after=()):
    specs = [pl.BlockSpec(memory_space=pl.ANY)] * len(after)
    specs += [pl.BlockSpec(memory_space=pltpu.SMEM)] if scalars is not None else []
    specs += [pl.BlockSpec(memory_space=pltpu.VMEM)] * len(args)
    operands = list(after) + ([scalars] if scalars is not None else []) + list(args)
    moved = sum(a.size * a.dtype.itemsize for a in list(args) + list(outs))
    body = ordered(body, len(after))
    return pl.pallas_call(
        body,
        name=name,
        in_specs=specs,
        out_specs=[pl.BlockSpec(memory_space=pltpu.VMEM)] * len(outs),
        out_shape=list(outs),
        scratch_shapes=list(scratch),
        compiler_params=pltpu.CompilerParams(vmem_limit_bytes=VMEM_LIMIT),
        cost_estimate=pl.CostEstimate(flops=flops, bytes_accessed=moved, transcendentals=0),
    )(*operands)


def shape(dims, dtype):
    return jax.ShapeDtypeStruct(tuple(dims), dtype)


def bucket_onehot(buckets, span, spacing):
    width = 2 * span * GROUP
    column = lax.broadcasted_iota(jnp.int32, (buckets, width), 1)
    delta = column // (2 * span)
    distance = column - delta * (2 * span) - span + span * delta
    bucket = jnp.where(distance >= 0, distance // spacing, -1)
    row = lax.broadcasted_iota(jnp.int32, (buckets, width), 0)
    return (bucket == row).astype(BF16)


def fill_bias(first_head, heads, table, vectors, bias, span, spacing):
    buckets, head_count = table.shape
    hot = bucket_onehot(buckets, span, spacing)
    rows = mm(table[...], hot, TN)
    column = lax.broadcasted_iota(jnp.int32, (1, 2 * span * GROUP), 1)
    rows = jnp.where(column < span, MASKED, rows)
    vectors[0:head_count, :] = rows
    for head in range(heads):
        picked = vectors[pl.ds(first_head + head, 1), :]
        for delta in range(GROUP):
            piece = picked[:, delta * 2 * span : (delta + 1) * 2 * span]
            spread = jnp.broadcast_to(piece, (span, 2 * span))
            rolled = pltpu.roll(spread, span, 1, stride=1, stride_axis=0)
            bias[head * GROUP + delta] = rolled[:, :span]


def attention_forward(sizes, ids, own, flip, side, side_flip, gain, weight, table,
                      out, mixed, gathered, stats, vectors, bias):
    span, heads, size, spacing, unused = sizes
    width = heads * size
    fill_bias(ids[4] * heads, heads, table, vectors, bias, span, spacing)
    for slot, piece in enumerate((own, flip, side, side_flip)):
        gathered[pl.ds(pl.multiple_of(ids[slot] * span, span), span), :] = piece[...]
    for part in range(GROUP):
        rows = slice(part * span, (part + 1) * span)
        values = gathered[rows, :].astype(F32)
        normed = (values * inverse_rms(values) * gain[...].astype(F32)).astype(BF16)
        mixed[rows, :] = mm(normed, weight[:, : 3 * width]).astype(BF16)
    for head in range(heads):
        columns = slice(head * size, (head + 1) * size)
        query_t = (mixed[:, columns].astype(F32) * size ** (-0.5)).T.astype(BF16)
        key = mixed[:, width + head * size : width + (head + 1) * size]
        value_t = mixed[:, 2 * width + head * size : 2 * width + (head + 1) * size].astype(F32).T.astype(BF16)
        for part in range(GROUP):
            mine = slice(part * span, (part + 1) * span)
            blocks = []
            for other in range(part + 1):
                raw = mm(key[other * span : (other + 1) * span], query_t[:, mine])
                blocks.append(raw + bias[head * GROUP + part - other])
            top = functools.reduce(jnp.maximum, [jnp.max(b, axis=0, keepdims=True) for b in blocks])
            total = jnp.zeros_like(top)
            gained = jnp.zeros((size, span), F32)
            for other, block in enumerate(blocks):
                raised = jnp.exp(block - top)
                total = total + jnp.sum(raised, axis=0, keepdims=True)
                gained = gained + mm(value_t[:, other * span : (other + 1) * span], raised.astype(BF16))
            out[part, columns, :] = (gained / total).astype(BF16)
            stats[head : head + 1, mine] = top + jnp.log(total)


def route_masks(routes, experts):
    lane = lax.broadcasted_iota(jnp.int32, (routes.shape[0], experts), 1)
    return [(routes[:, k : k + 1] == lane).astype(F32) for k in range(2)]


def pick_rows(slot, slots):
    lane = lax.broadcasted_iota(jnp.int32, (slot.shape[0], slots), 1).astype(F32)
    return (lane == slot).astype(BF16)


def fill_slots(aux_t, slots, k):
    row = lax.broadcasted_iota(jnp.int32, (slots, aux_t.shape[1]), 0).astype(F32)
    return (row == aux_t[k : k + 1, :]).astype(BF16)


def after_attention(capacity, attended, own, w_out, gain, router, routes,
                    outgoing, middle, normed_two, aux):
    tokens = own.shape[0]
    experts = router.shape[1]
    slots = experts * capacity
    width = attended.shape[1]
    total = own[...].astype(F32)
    for group in range(GROUP):
        total = total + mm(attended[group], w_out[group * width : (group + 1) * width, :], TN)
    middle[...] = total
    normed = (total * inverse_rms(total) * gain[...].astype(F32)).astype(BF16)
    normed_two[...] = normed
    logits = mm(normed, router[...])
    masks = route_masks(routes, experts)
    members = (masks[0] + masks[1]).astype(BF16)
    row = lax.broadcasted_iota(jnp.int32, (tokens, tokens), 0)
    column = lax.broadcasted_iota(jnp.int32, (tokens, tokens), 1)
    earlier = mm((row > column).astype(BF16), members)
    chosen = [jnp.sum(logits * mask, axis=1, keepdims=True) for mask in masks]
    first = jax.nn.sigmoid(chosen[0] - chosen[1])
    places = [
        routes[:, k : k + 1].astype(F32) * capacity + jnp.sum(earlier * masks[k], axis=1, keepdims=True)
        for k in range(2)
    ]
    lane = lax.broadcasted_iota(jnp.int32, (tokens, 128), 1)
    packed = jnp.zeros((tokens, 128), F32)
    for index, entry in enumerate((places[0], places[1], first, 1.0 - first)):
        packed = jnp.where(lane == index, entry, packed)
    aux[...] = packed
    packed_t = packed.T
    hot = fill_slots(packed_t, slots, 0) + fill_slots(packed_t, slots, 1)
    outgoing[...] = mm(hot, normed).astype(BF16)


def expert_forward(rows, w_in, w_down, activation, slope, produced, total):
    step = pl.program_id(0)

    @pl.when(step == 0)
    def clear():
        total[...] = jnp.zeros_like(total)

    chunk = rows.shape[0] // 4
    for part in range(4):
        mine = slice(part * chunk, (part + 1) * chunk)
        hidden = mm(rows[mine, :], w_in[...])
        half = 0.5 * (1.0 + lax.erf(hidden * 0.7071067811865476))
        bell = jnp.exp(-0.5 * hidden * hidden) * 0.3989422804014327
        raised = (hidden * half).astype(BF16)
        activation[mine, :] = raised
        slope[mine, :] = (half + hidden * bell).astype(BF16)
        total[mine, :] += mm(raised, w_down[...])

    @pl.when(step == pl.num_programs(0) - 1)
    def finish():
        produced[...] = total[...].astype(BF16)


def expert_backward(arrived_grad, w_in, w_down, slope, hidden_grad, rows_grad, total):
    step = pl.program_id(0)

    @pl.when(step == 0)
    def clear():
        total[...] = jnp.zeros_like(total)

    chunk = arrived_grad.shape[0] // 4
    for part in range(4):
        mine = slice(part * chunk, (part + 1) * chunk)
        lifted = mm(arrived_grad[mine, :], w_down[...], NT) * slope[mine, :].astype(F32)
        lowered = lifted.astype(BF16)
        hidden_grad[mine, :] = lowered
        total[mine, :] += mm(lowered, w_in[...], NT)

    @pl.when(step == pl.num_programs(0) - 1)
    def finish():
        rows_grad[...] = total[...].astype(BF16)


def tile_of(hidden):
    return 768 if hidden % 768 == 0 else hidden


def run_expert_forward(rows, w_in, w_down):
    count, features = rows.shape
    hidden = w_in.shape[1]
    tile = tile_of(hidden)
    return pl.pallas_call(
        expert_forward,
        name="expert_forward",
        grid=(hidden // tile,),
        in_specs=[
            whole(rows),
            pl.BlockSpec((features, tile), lambda j: (0, j)),
            pl.BlockSpec((tile, features), lambda j: (j, 0)),
        ],
        out_specs=[
            pl.BlockSpec((count, tile), lambda j: (0, j)),
            pl.BlockSpec((count, tile), lambda j: (0, j)),
            pl.BlockSpec((count, features), lambda j: (0, 0)),
        ],
        out_shape=[shape((count, hidden), BF16), shape((count, hidden), BF16), shape((count, features), BF16)],
        scratch_shapes=[pltpu.VMEM((count, features), F32)],
        compiler_params=pltpu.CompilerParams(vmem_limit_bytes=VMEM_LIMIT),
        cost_estimate=pl.CostEstimate(
            flops=4 * count * features * hidden, bytes_accessed=30 << 20, transcendentals=2 * count * hidden
        ),
    )(rows, w_in, w_down)


def run_expert_backward(arrived_grad, w_in, w_down, slope):
    count, features = arrived_grad.shape
    hidden = w_in.shape[1]
    tile = tile_of(hidden)
    return pl.pallas_call(
        expert_backward,
        name="expert_backward",
        grid=(hidden // tile,),
        in_specs=[
            whole(arrived_grad),
            pl.BlockSpec((features, tile), lambda j: (0, j)),
            pl.BlockSpec((tile, features), lambda j: (j, 0)),
            pl.BlockSpec((count, tile), lambda j: (0, j)),
        ],
        out_specs=[
            pl.BlockSpec((count, tile), lambda j: (0, j)),
            pl.BlockSpec((count, features), lambda j: (0, 0)),
        ],
        out_shape=[shape((count, hidden), BF16), shape((count, features), BF16)],
        scratch_shapes=[pltpu.VMEM((count, features), F32)],
        compiler_params=pltpu.CompilerParams(vmem_limit_bytes=VMEM_LIMIT),
        cost_estimate=pl.CostEstimate(
            flops=4 * count * features * hidden, bytes_accessed=30 << 20, transcendentals=0
        ),
    )(arrived_grad, w_in, w_down, slope)


def weight_partials(scalars, rows, hidden_grad, activation, arrived_grad, grad_in, grad_down):
    @pl.when(scalars[0] == 1)
    def wanted():
        grad_in[...] = mm(rows[...], hidden_grad[...], TN).astype(BF16)
        grad_down[...] = mm(activation[...], arrived_grad[...], TN).astype(BF16)


def run_weight_partials(wanted, rows, hidden_grad, activation, arrived_grad):
    count, features = rows.shape
    hidden = hidden_grad.shape[1]
    tile = tile_of(hidden)
    return pl.pallas_call(
        weight_partials,
        name="weight_partials",
        grid_spec=pltpu.PrefetchScalarGridSpec(
            num_scalar_prefetch=1,
            grid=(hidden // tile,),
            in_specs=[
                pl.BlockSpec((count, features), lambda j, s: (0, 0)),
                pl.BlockSpec((count, tile), lambda j, s: (0, j * s[0])),
                pl.BlockSpec((count, tile), lambda j, s: (0, j * s[0])),
                pl.BlockSpec((count, features), lambda j, s: (0, 0)),
            ],
            out_specs=[
                pl.BlockSpec((features, tile), lambda j, s: (0, j * s[0])),
                pl.BlockSpec((tile, features), lambda j, s: (j * s[0], 0)),
            ],
        ),
        out_shape=[shape((features, hidden), BF16), shape((hidden, features), BF16)],
        compiler_params=pltpu.CompilerParams(vmem_limit_bytes=VMEM_LIMIT),
        cost_estimate=pl.CostEstimate(
            flops=4 * count * features * hidden, bytes_accessed=30 << 20, transcendentals=0
        ),
    )(wanted, rows, hidden_grad, activation, arrived_grad)


def weight_totals(scalars, left, right, sent, left_1, right_1, sent_1, after, total):
    @pl.when(scalars[0] == 0)
    def first():
        total[...] = mm(left[...], right[...], TN) + sent[...].astype(F32)

    @pl.when(scalars[0] == 1)
    def second():
        total[...] = mm(left_1[...], right_1[...], TN) + sent_1[...].astype(F32)


def run_weight_totals(core, first, second, tiled_left, after):
    count, features = first[1 if tiled_left else 0].shape
    hidden = first[0 if tiled_left else 1].shape[1]
    tile = tile_of(hidden)

    def specs(which):
        def step(j, s):
            return jnp.where(s[0] == which, j, 0)

        full = pl.BlockSpec((count, features), lambda j, s: (0, 0))
        part = pl.BlockSpec((count, tile), lambda j, s: (0, step(j, s)))
        if tiled_left:
            return [part, full, pl.BlockSpec((tile, features), lambda j, s: (step(j, s), 0))]
        return [full, part, pl.BlockSpec((features, tile), lambda j, s: (0, step(j, s)))]

    if tiled_left:
        out_spec = pl.BlockSpec((tile, features), lambda j, s: (j, 0))
        dims = (hidden, features)
    else:
        out_spec = pl.BlockSpec((features, tile), lambda j, s: (0, j))
        dims = (features, hidden)
    return pl.pallas_call(
        weight_totals,
        name="weight_totals",
        grid_spec=pltpu.PrefetchScalarGridSpec(
            num_scalar_prefetch=1, grid=(hidden // tile,),
            in_specs=specs(0) + specs(1) + [pl.BlockSpec(memory_space=pl.ANY)], out_specs=out_spec,
        ),
        out_shape=shape(dims, F32),
        compiler_params=pltpu.CompilerParams(vmem_limit_bytes=VMEM_LIMIT),
        cost_estimate=pl.CostEstimate(
            flops=2 * count * features * hidden, bytes_accessed=30 << 20, transcendentals=0
        ),
    )(core, *first, *second, after)


def combine(returned, aux, middle, result, difference):
    slots = returned.shape[0]
    packed = aux[...]
    outs = [mm(pick_rows(packed[:, k : k + 1], slots), returned[...]) for k in range(2)]
    total = middle[...] + packed[:, 2:3] * outs[0] + packed[:, 3:4] * outs[1]
    result[...] = total.astype(BF16)
    difference[...] = outs[0] - outs[1]


def spread_grads(upstream, aux, outgoing):
    slots = outgoing.shape[0]
    packed = aux[...]
    packed_t = packed.T
    values = upstream[...].astype(F32)
    total = jnp.zeros(outgoing.shape, F32)
    for k in range(2):
        total = total + mm(fill_slots(packed_t, slots, k), (values * packed[:, 2 + k : 3 + k]).astype(BF16))
    outgoing[...] = total.astype(BF16)


def norm_backward(values, gain, grad):
    scale = inverse_rms(values)
    unit = values * scale
    lifted = grad * gain
    back = scale * (lifted - unit * jnp.mean(lifted * unit, axis=-1, keepdims=True))
    return back, jnp.sum(grad * unit, axis=0, keepdims=True)


def before_attention(returned, aux, upstream, difference, middle, normed_two, attended, gain,
                     router, w_out, routes, middle_grad, attended_grad, shared_grad):
    slots = returned.shape[0]
    experts = router.shape[1]
    width = attended.shape[1]
    features = w_out.shape[1]
    packed = aux[...]
    hot = pick_rows(packed[:, 0:1], slots) + pick_rows(packed[:, 1:2], slots)
    token_grad = mm(hot, returned[...])
    flow = upstream[...].astype(F32)
    shift = jnp.sum(flow * difference[...], axis=1, keepdims=True) * packed[:, 2:3] * packed[:, 3:4]
    masks = route_masks(routes, experts)
    logits_grad = (shift * (masks[0] - masks[1])).astype(BF16)
    token_grad = token_grad + mm(logits_grad, router[...], NT)
    back, gain_part = norm_backward(middle[...], gain[...].astype(F32), token_grad)
    total = flow + back
    middle_grad[...] = total
    branch = total.astype(BF16)
    for group in range(GROUP):
        mine = slice(group * width, (group + 1) * width)
        shared_grad[mine, :features] = mm(attended[group], branch).astype(BF16)
        attended_grad[group] = mm(w_out[mine, :], branch, NT).astype(BF16)
    tail = shared_grad.shape[1] - features
    gain_column = jnp.broadcast_to(gain_part, (8, features)).T
    lane = lax.broadcasted_iota(jnp.int32, (features, tail), 1)
    shared_grad[:, features:] = jnp.where(lane == experts, gain_column[:, 0:1], 0.0).astype(BF16)
    shared_grad[:, features : features + experts] = mm(normed_two[...], logits_grad, TN).astype(BF16)


def attention_backward(sizes, ids, mixed, stats, attended, grads, gathered, gain, weight, table,
                       stay, leave, sent, shared_grad,
                       vectors, bias, mixed_grad, sums, key_total, value_total, turned, strips):
    span, heads, size, spacing, ranks = sizes
    width = heads * size
    count = span // spacing
    buckets = table.shape[0]
    features = weight.shape[0]
    row = lax.broadcasted_iota(jnp.int32, (span, span), 0)
    column = lax.broadcasted_iota(jnp.int32, (span, span), 1)
    later = (column % spacing) >= (row % spacing)
    lane = lax.broadcasted_iota(jnp.int32, (span, 128), 0) // spacing
    backwards = (count - 1 - lane == lax.broadcasted_iota(jnp.int32, (span, 128), 1)).astype(F32)
    strips[...] = jnp.zeros_like(strips)
    fill_bias(ids[4] * heads, heads, table, vectors, bias, span, spacing)
    for head in range(heads):
        columns = slice(head * size, (head + 1) * size)
        key_columns = slice(width + head * size, width + (head + 1) * size)
        value_columns = slice(2 * width + head * size, 2 * width + (head + 1) * size)
        query = (mixed[:, columns].astype(F32) * size ** (-0.5)).astype(BF16)
        query_t = query.astype(F32).T.astype(BF16)
        key = mixed[:, key_columns]
        key_t = key.astype(F32).T.astype(BF16)
        value = mixed[:, value_columns]
        key_total[...] = jnp.zeros_like(key_total)
        value_total[...] = jnp.zeros_like(value_total)
        sums[...] = jnp.zeros_like(sums)
        for part in range(GROUP):
            mine = slice(part * span, (part + 1) * span)
            grad_t = grads[part, columns, :]
            delta_row = jnp.sum(
                grad_t.astype(F32) * attended[part, columns, :].astype(F32), axis=0, keepdims=True
            )
            level = stats[head : head + 1, mine]
            query_total = jnp.zeros((size, span), F32)
            for other in range(part + 1):
                theirs = slice(other * span, (other + 1) * span)
                raw = mm(key[theirs], query_t[:, mine])
                prob = jnp.exp(raw + (bias[head * GROUP + part - other] - level))
                prob_grad = mm(value[theirs], grad_t)
                low = (prob * (prob_grad - delta_row)).astype(BF16)
                sums[part - other] += low.astype(F32)
                query_total = query_total + mm(key_t[:, theirs], low)
                key_total[theirs, :] += mm(low, query[mine])
                value_total[theirs, :] += mm(prob.astype(BF16), grad_t, NT)
            turned[:, mine] = query_total * size ** (-0.5)
        mixed_grad[:, columns] = turned[...].T.astype(BF16)
        mixed_grad[:, key_columns] = key_total[...].astype(BF16)
        mixed_grad[:, value_columns] = value_total[...].astype(BF16)
        for delta in range(GROUP):
            upper = jnp.where(later, sums[delta], 0.0)
            for side, block in enumerate((upper, sums[delta] - upper)):
                tiles = lax.dot_general(
                    jnp.sum(block.reshape(count, spacing, span), axis=1), backwards, NN,
                    precision=lax.Precision.HIGHEST, preferred_element_type=F32,
                )
                turned_tiles = pltpu.roll(tiles, 0, 1, stride=1, stride_axis=0)
                place = (delta * 2 + side) * 128
                strips[head : head + 1, place : place + 128] = jnp.sum(turned_tiles, axis=0, keepdims=True)
    entry = lax.broadcasted_iota(jnp.int32, (GROUP * 2 * 128, 128), 0)
    bucket = (entry // 256) * count + count - 1 - entry % 128 - (entry // 128) % 2
    hot = (bucket == lax.broadcasted_iota(jnp.int32, (GROUP * 2 * 128, 128), 1)) & (entry % 128 < 2 * count)
    table_rows = lax.dot_general(
        strips[...], hot.astype(F32), NN, precision=lax.Precision.HIGHEST, preferred_element_type=F32
    )
    gain_total = jnp.zeros((1, features), F32)
    weight_total = jnp.zeros((features, 3 * width), F32)
    for part in range(GROUP):
        place = ids[5 + part]
        rows = pl.ds(pl.multiple_of(place * span, span), span)
        values = gathered[rows, :].astype(F32)
        unit = values * inverse_rms(values)
        normed = (unit * gain[...].astype(F32)).astype(BF16)
        lowered = mixed_grad[rows, :]
        weight_total = weight_total + mm(normed, lowered, TN)
        back = mm(lowered, weight[:, : 3 * width], NT)
        gain_total = gain_total + jnp.sum(back * unit, axis=0, keepdims=True)
        if part == 0:
            stay[...] = back.astype(BF16)
        elif part == 1:
            leave[...] = back.astype(BF16)
        else:
            sent[part - 2] = back.astype(BF16)
    owned = buckets // ranks
    bucket = lax.broadcasted_iota(jnp.int32, (128, features), 0)
    target = (bucket // owned) * (features // ranks) + bucket % owned
    spot = (target == lax.broadcasted_iota(jnp.int32, (128, features), 1)) & (bucket < buckets)
    placed = lax.dot_general(
        table_rows, spot.astype(F32), NN, precision=lax.Precision.HIGHEST, preferred_element_type=F32
    )
    extra = jnp.concatenate([placed, jnp.broadcast_to(gain_total, (8, features))], axis=0)
    shared_grad[...] = jnp.zeros_like(shared_grad)
    shared_grad[:, : 3 * width] = weight_total.astype(BF16)
    shared_grad[:, 3 * width : 3 * width + 16] = extra.T.astype(BF16)


def first_norm_grad(stay, partner, arrived, own, gain, middle_grad, low):
    grad = stay[...].astype(F32) + partner[0].astype(F32) + arrived[...].astype(F32)
    back, unused = norm_backward(own[...].astype(F32), gain[...].astype(F32), grad)
    low[...] = (middle_grad[...] + back).astype(BF16)


FLIP = [(0, 1), (1, 0)]


def flip(block):
    return lax.ppermute(block, "section", FLIP)


def beside(block):
    return lax.ppermute(block, "zlo", FLIP)


def scatter_pairs(turn):
    return [
        (core * 4 + a * 2 + b, b * 4 + (core ^ turn) * 2 + a)
        for core in range(2)
        for a in range(2)
        for b in range(2)
    ]


def to_working(block, turn):
    return lax.ppermute(block, ("section", "zhi", "zlo"), scatter_pairs(turn))


def to_home(block, section, batch):
    turn = section ^ batch
    pairs = [(after, before) for before, after in scatter_pairs(turn) if before // 4 == section]
    return lax.ppermute(block, ("section", "zhi", "zlo"), pairs)


def home_pair(blocks, core):
    return jnp.stack([
        jnp.where(core == 0, to_home(blocks[0], 0, batch), to_home(blocks[1], 1, batch))
        for batch in range(2)
    ])


def exchange(block, experts, capacity):
    features = block.shape[-1]
    moved = lax.all_to_all(
        block.reshape(experts, capacity, features), RANKS, split_axis=0, concat_axis=0, tiled=True
    )
    return moved.reshape(experts * capacity, features)


def spread_sum(block, axes, parts):
    rows, columns = block.shape
    moved = lax.all_to_all(
        block.reshape(parts, rows // parts, columns), axes, split_axis=0, concat_axis=0, tiled=True
    )
    return jnp.sum(moved.astype(F32), axis=0)


def regroup(block):
    return lax.all_to_all(block, ("zlo", "section"), split_axis=0, concat_axis=0, tiled=True)


def gather_columns(blocks, out, staged, local_sem, send_sem, recv_sem, stage_send, stage_recv):
    core = lax.axis_index("section")
    expert = lax.axis_index("expert")
    zhi = lax.axis_index("zhi")
    zlo = lax.axis_index("zlo")
    place = 2 * zhi + zlo
    other = 1 - core
    beside_x = expert + 1 - 2 * (expert % 2)
    beside_y = (expert + 2) % 4
    places = [place, place + 1 - 2 * zlo, (place + 2) % 4, 3 - place]

    def at(section, rank_expert, rank_place):
        return out.at[section, rank_expert * 4 + rank_place]

    barrier = pltpu.get_barrier_semaphore()
    peers = [{"section": other}, {"expert": beside_x}, {"expert": beside_y}]
    peers += [{"zhi": spot // 2, "zlo": spot % 2} for spot in places[1:]]
    for peer in peers:
        pl.semaphore_signal(barrier, inc=1, device_id=peer, device_id_type=pl.DeviceIdType.MESH)
    pl.semaphore_wait(barrier, len(peers))

    started = []

    def send(source, target, index, section, owner, spot, peer):
        copy = pltpu.make_async_remote_copy(
            src_ref=source, dst_ref=target, send_sem=send_sem.at[index],
            recv_sem=recv_sem.at[section, owner * 4 + spot], device_id=peer,
            device_id_type=pl.DeviceIdType.MESH,
        )
        copy.start()
        started.append(copy)

    def arrived(section, owner, spot):
        pltpu.make_async_remote_copy(
            src_ref=at(section, owner, spot), dst_ref=at(section, owner, spot), send_sem=send_sem.at[0],
            recv_sem=recv_sem.at[section, owner * 4 + spot], device_id={"section": other},
            device_id_type=pl.DeviceIdType.MESH,
        ).wait_recv()

    trades = []
    for parity in range(2):
        trade = pltpu.make_async_remote_copy(
            src_ref=blocks.at[2 * parity + other], dst_ref=staged.at[parity], send_sem=stage_send.at[parity],
            recv_sem=stage_recv.at[parity], device_id={"section": other},
            device_id_type=pl.DeviceIdType.MESH,
        )
        trade.start()
        trades.append(trade)

    index = 0
    for which in range(2):
        section = core if which == 0 else other
        if which == 1:
            for trade in trades:
                trade.wait()

        def block_for(parity):
            return blocks.at[2 * parity + core] if which == 0 else staged.at[parity]

        for step, spot in enumerate(places[1:]):
            send(block_for(spot % 2), at(section, expert, place), index, section, expert, place,
                 {"zhi": spot // 2, "zlo": spot % 2})
            index += 1
        for peer in (beside_x, beside_y):
            send(block_for(zlo), at(section, expert, place), index, section, expert, place, {"expert": peer})
            index += 1
        local = pltpu.make_async_copy(block_for(zlo), at(section, expert, place), local_sem)
        local.start()
        local.wait()
    sections = (core, other)
    for spot in places[1:]:
        for section in sections:
            arrived(section, expert, spot)
            for peer in (beside_x, beside_y):
                send(at(section, expert, spot), at(section, expert, spot), index, section, expert, spot,
                     {"expert": peer})
                index += 1
    for section in sections:
        for step, spot in enumerate(places):
            arrived(section, beside_x, spot)
            arrived(section, beside_y, spot)
            source, peer = ((beside_x, beside_y), (beside_y, beside_x))[step % 2]
            send(at(section, source, spot), at(section, source, spot), index, section, source, spot,
                 {"expert": peer})
            index += 1
    diagonal = 3 - expert
    for section in sections:
        for spot in places:
            arrived(section, diagonal, spot)
    for copy in started:
        copy.wait_send()


def run_gather_columns(blocks, ranks):
    groups, rows, columns = blocks.shape
    return pl.pallas_call(
        gather_columns,
        name="gather_columns",
        in_specs=[pl.BlockSpec(memory_space=pltpu.VMEM)],
        out_specs=pl.BlockSpec(memory_space=pltpu.VMEM),
        out_shape=shape((2, ranks, rows, columns), blocks.dtype),
        scratch_shapes=[
            pltpu.VMEM((2, rows, columns), blocks.dtype),
            pltpu.SemaphoreType.DMA,
            pltpu.SemaphoreType.DMA((30,)),
            pltpu.SemaphoreType.DMA((2, ranks)),
            pltpu.SemaphoreType.DMA((2,)),
            pltpu.SemaphoreType.DMA((2,)),
        ],
        compiler_params=pltpu.CompilerParams(
            collective_id=0, has_side_effects=True, vmem_limit_bytes=16 << 20
        ),
        cost_estimate=pl.CostEstimate(flops=0, bytes_accessed=40 << 20, transcendentals=0),
    )(blocks)


OFFSETS = [(step, place) for place in (0, 3, 1, 2) for step in range(4)]
SENDS = (4, 5, 6, 7, 12, 13, 14, 15, 8, 9, 10, 11, 1, 2, 3)
BATCH = 4
REMOTE = pl.DeviceIdType.MESH


def across(index, step):
    return (index, index + 1 - 2 * (index % 2), (index + 2) % 4, 3 - index)[step]


def expert_layer(mode, section, *refs):
    forward = mode != "backward"
    backward = mode != "forward"
    refs = list(refs)

    def take(count):
        taken = refs[:count]
        del refs[:count]
        return taken

    weights = take(4)
    outgoing = take(2 if mode == "both" else 1)
    if mode == "backward":
        saved_rows, saved_activation, saved_slope, unused, unused_1 = take(5)
    returned = take(len(outgoing))
    if mode == "forward":
        kept_rows, kept_activation, kept_slope = take(3)
    else:
        grad_in, grad_down = take(2)
    arrived = take(len(outgoing))
    finished = take(len(outgoing))
    w_in, w_down, activation, slope, totals = take(5)
    send_sem, recv_sem, back_send, back_recv, load_sem = take(5)
    if backward:
        parts, staged, part_send, part_recv, out_sem = take(5)

    core = lax.axis_index("section")
    expert = lax.axis_index("expert")
    place = 2 * lax.axis_index("zhi") + lax.axis_index("zlo")
    me = expert * 4 + place
    hidden = w_in.shape[1]
    slot_rows, features = arrived[0].shape[1:]
    rows_in_batch = BATCH * slot_rows
    tile = tile_of(hidden)
    tiles = hidden // tile
    peers = []
    ranks = []
    for step, move in OFFSETS:
        to_expert, to_place = across(expert, step), across(place, move)
        ranks.append(to_expert * 4 + to_place)
        peers.append({"expert": to_expert, "zhi": to_place // 2, "zlo": to_place % 2})

    loads = []

    def load(source, target, index):
        copy = pltpu.make_async_copy(source, target, load_sem.at[index])
        copy.start()
        loads.append(copy)

    @pl.when(core == section)
    def own_weights():
        pltpu.make_async_copy(weights[0], w_in, load_sem.at[0]).start()
        pltpu.make_async_copy(weights[1], w_down, load_sem.at[1]).start()

    @pl.when(core != section)
    def other_weights():
        pltpu.make_async_copy(weights[2], w_in, load_sem.at[0]).start()
        pltpu.make_async_copy(weights[3], w_down, load_sem.at[1]).start()

    if mode == "backward":
        load(saved_activation, activation, 2)
        load(saved_slope, slope, 3)

    barrier = pltpu.get_barrier_semaphore()
    for peer in peers[1:] + ([{"section": 1 - core}] if backward else []):
        pl.semaphore_signal(barrier, inc=1, device_id=peer, device_id_type=REMOTE)
    pl.semaphore_wait(barrier, 16 if backward else 15)

    def remote(source, target, send, recv, peer):
        return pltpu.make_async_remote_copy(
            src_ref=source, dst_ref=target, send_sem=send, recv_sem=recv, device_id=peer, device_id_type=REMOTE
        )

    sent = []
    for slot in SENDS:
        for kind, block in enumerate(outgoing):
            copy = remote(block.at[ranks[slot]], arrived[kind].at[slot], send_sem.at[kind, slot],
                          recv_sem.at[kind, slot], peers[slot])
            copy.start()
            sent.append(copy)
    for kind, block in enumerate(outgoing):
        arrived[kind][0] = block[me]

    pltpu.make_async_copy(weights[0], w_in, load_sem.at[0]).wait()
    pltpu.make_async_copy(weights[1], w_down, load_sem.at[1]).wait()
    for copy in loads:
        copy.wait()

    saves = []
    for batch in range(len(OFFSETS) // BATCH):
        slots = range(batch * BATCH, (batch + 1) * BATCH)
        mine = slice(batch * rows_in_batch, (batch + 1) * rows_in_batch)
        for slot in slots:
            for kind in range(len(outgoing)):
                if slot:
                    remote(arrived[kind].at[slot], arrived[kind].at[slot], send_sem.at[kind, slot],
                           recv_sem.at[kind, slot], peers[slot]).wait_recv()

        def block_of(kind):
            return arrived[kind][slots[0] : slots[-1] + 1].reshape(rows_in_batch, features)

        def one_tile(index, unused):
            spot = pl.ds(pl.multiple_of(index * tile, tile), tile)
            if forward:
                values = mm(block_of(0), w_in[:, spot])
                half = 0.5 * (1.0 + lax.erf(values * 0.7071067811865476))
                bell = jnp.exp(-0.5 * values * values) * 0.3989422804014327
                raised = (values * half).astype(BF16)
                steep = half + values * bell
                activation[mine, spot] = raised
                if mode == "forward":
                    slope[mine, spot] = steep.astype(BF16)
                totals[0] += mm(raised, w_down[spot, :])
            else:
                steep = slope[mine, spot].astype(F32)
            if backward:
                lowered = (mm(block_of(len(outgoing) - 1), w_down[spot, :], NT) * steep).astype(BF16)
                slope[mine, spot] = lowered
                totals[len(outgoing) - 1] += mm(lowered, w_in[:, spot], NT)
            return unused

        totals[...] = jnp.zeros_like(totals)
        lax.fori_loop(0, tiles, one_tile, 0)
        for kind in range(len(outgoing)):
            finished[kind][slots[0] : slots[-1] + 1] = (
                totals[kind].astype(BF16).reshape(BATCH, slot_rows, features)
            )
        for slot in slots:
            for kind in range(len(outgoing)):
                if slot:
                    copy = remote(finished[kind].at[slot], returned[kind].at[me], back_send.at[kind, slot],
                                  back_recv.at[kind, slot], peers[slot])
                    copy.start()
                    sent.append(copy)
                else:
                    returned[kind][me] = finished[kind][0]
        if mode == "forward":
            for index, (source, target) in enumerate(((activation, kept_activation), (slope, kept_slope))):
                copy = pltpu.make_async_copy(
                    source.at[mine, :], target.at[mine, :], load_sem.at[2 + 2 * batch + index]
                )
                copy.start()
                saves.append(copy)
    if mode == "forward":
        kept_rows[...] = arrived[0][...]

    if backward:
        count = slot_rows * len(OFFSETS)
        grads = arrived[len(outgoing) - 1]
        inputs = arrived[0] if forward else saved_rows
        partner = {"section": 1 - core}

        def share_copy(index):
            return remote(parts.at[index], parts.at[index], part_send.at[index], part_recv.at[index], partner)

        def out_copy(index):
            spot = pl.ds(index // 2 * tile, tile)
            target = grad_down.at[spot, :] if index % 2 else grad_in.at[:, spot]
            return pltpu.make_async_copy(staged.at[index % 2], target, out_sem.at[index])

        for index in range(2 * tiles):
            spot = pl.ds(index // 2 * tile, tile)
            if index % 2:
                value = mm(activation[:, spot], grads[...].reshape(count, features), TN)
            else:
                value = mm(inputs[...].reshape(count, features), slope[:, spot], TN)

            @pl.when(core != section)
            def give():
                parts[index] = value.astype(BF16)
                share_copy(index).start()

            @pl.when(core == section)
            def keep():
                share_copy(index).wait_recv()
                if index >= 2:
                    out_copy(index - 2).wait()
                staged[index % 2] = value + parts[index].astype(F32)
                out_copy(index).start()

    for slot in range(1, len(OFFSETS)):
        for kind in range(len(outgoing)):
            remote(finished[kind].at[slot], returned[kind].at[ranks[slot]], back_send.at[kind, slot],
                   back_recv.at[kind, slot], peers[slot]).wait_recv()
    for copy in sent:
        copy.wait_send()
    for copy in saves:
        copy.wait()
    if backward:
        @pl.when(core != section)
        def given():
            for index in range(2 * tiles):
                share_copy(index).wait_send()

        @pl.when(core == section)
        def stored():
            for index in range(2 * tiles - 2, 2 * tiles):
                out_copy(index).wait()


def run_expert_layer(mode, section, weights, outgoing, saved=(), grads=()):
    ranks, slot_rows, features = outgoing[0].shape
    hidden = weights[0].shape[1]
    count = ranks * slot_rows
    tile = tile_of(hidden)
    kinds = len(outgoing)
    anywhere = pl.BlockSpec(memory_space=pl.ANY)
    local = pl.BlockSpec(memory_space=pltpu.VMEM)
    block = shape((ranks, slot_rows, features), BF16)
    wide = shape((count, hidden), BF16)
    in_specs = [anywhere] * 4 + [local] * kinds
    operands = [*weights, *outgoing]
    out_shape = [block] * kinds
    out_specs = [local] * kinds
    aliases = {}
    if mode == "forward":
        out_shape += [block, wide, wide]
        out_specs += [local, anywhere, anywhere]
    else:
        out_shape += [shape((features, hidden), F32), shape((hidden, features), F32)]
        out_specs += [anywhere, anywhere]
    if mode == "backward":
        aliases = {len(operands) + 3: kinds, len(operands) + 4: kinds + 1}
        operands += [*saved, *grads]
        in_specs += [local, anywhere, anywhere, anywhere, anywhere]
    scratch = [pltpu.VMEM(block.shape, BF16)] * (2 * kinds) + [
        pltpu.VMEM((features, hidden), BF16), pltpu.VMEM((hidden, features), BF16),
        pltpu.VMEM((count, hidden), BF16), pltpu.VMEM((count, hidden), BF16),
        pltpu.VMEM((kinds, BATCH * slot_rows, features), F32),
        pltpu.SemaphoreType.DMA((kinds, ranks)), pltpu.SemaphoreType.DMA((kinds, ranks)),
        pltpu.SemaphoreType.DMA((kinds, ranks)), pltpu.SemaphoreType.DMA((kinds, ranks)),
        pltpu.SemaphoreType.DMA((10,)),
    ]
    if mode != "forward":
        pieces = 2 * hidden // tile
        scratch += [
            pltpu.VMEM((pieces, features, tile), BF16), pltpu.VMEM((2, features, tile), F32),
            pltpu.SemaphoreType.DMA((pieces,)), pltpu.SemaphoreType.DMA((pieces,)),
            pltpu.SemaphoreType.DMA((pieces,)),
        ]
    return pl.pallas_call(
        functools.partial(expert_layer, mode, section),
        name="expert_layer_" + mode,
        in_specs=in_specs,
        out_specs=out_specs,
        out_shape=out_shape,
        scratch_shapes=scratch,
        input_output_aliases=aliases,
        compiler_params=pltpu.CompilerParams(
            collective_id={"forward": 1, "both": 2, "backward": 3}[mode], has_side_effects=True,
            vmem_limit_bytes=VMEM_LIMIT,
        ),
        cost_estimate=pl.CostEstimate(
            flops=8 * kinds * count * features * hidden, bytes_accessed=160 << 20, transcendentals=0
        ),
    )(*operands)


def per_device(inputs, cotangent, qkv_shard, out_shard, router_shard, gain_shard, table_shard,
               w_expert_in, w_expert_out, routes):
    core = lax.axis_index("section")
    zhi = lax.axis_index("zhi")
    zlo = lax.axis_index("zlo")
    span, features = inputs.shape[2:]
    ranks = lax.axis_size(RANKS)
    shard_rows = qkv_shard.shape[1]
    experts = router_shard.shape[2]
    table_rows, head_count = table_shard.shape[1:]
    buckets = table_rows * ranks
    heads = head_count // GROUP
    size = features // head_count
    width = heads * size
    spacing = GROUP * span // buckets
    capacity = max(2, 4 * span // experts)
    slots = experts * capacity
    group = 2 * zlo + core
    sizes = (span, heads, size, spacing, ranks)
    ids = jnp.stack([
        group, 2 * zlo + 1 - core, 2 * (1 - zlo) + core, 2 * (1 - zlo) + 1 - core, group,
        group, 2 * (1 - zlo) + core, 2 * zlo + 1 - core, 2 * (1 - zlo) + 1 - core,
    ]).astype(jnp.int32)
    core_id = core.astype(jnp.int32).reshape(1)

    own = to_working(lax.dynamic_index_in_dim(inputs, core, 0, keepdims=False)[0], 0)
    given = to_working(lax.dynamic_index_in_dim(cotangent, core, 0, keepdims=False)[0], 0)
    route_parts = [
        to_working(lax.dynamic_index_in_dim(routes[0], core ^ turn, 0, keepdims=False)[0], turn)
        for turn in range(2)
    ]
    section_routes = [
        jnp.where(zhi == section, route_parts[0], route_parts[1]) for section in range(2)
    ]

    small = jnp.concatenate([
        router_shard[0],
        gain_shard[0].T,
        jnp.pad(table_shard[0], ((0, shard_rows - table_rows), (0, 0))),
    ], axis=1)
    by_group = jnp.transpose(
        qkv_shard[0].reshape(shard_rows, 3, GROUP, width), (2, 0, 1, 3)
    ).reshape(GROUP, shard_rows, 3 * width)
    by_group = jnp.concatenate(
        [by_group, jnp.broadcast_to(small[None], (GROUP, *small.shape))], axis=2
    )
    by_group = jnp.pad(by_group, ((0, 0), (0, 0), (0, -by_group.shape[2] % 128)))
    columns = by_group.shape[2]
    if lax.axis_size("expert") == 4:
        early = run_gather_columns(by_group, ranks).reshape(2, features, columns)
        early = [early[0], early[1]]
    else:
        whole_early = lax.all_gather(by_group, RANKS, axis=1, tiled=True)
        kept = lax.dynamic_index_in_dim(whole_early, group, 0, keepdims=False)
        traded = flip(lax.dynamic_index_in_dim(whole_early, 2 * zlo + 1 - core, 0, keepdims=False))
        early = [
            jnp.where(core == section, kept, traded).reshape(features, columns) for section in range(2)
        ]
    w_out_own = lax.all_gather(out_shard[0], RANKS, axis=0, tiled=True)
    w_in = w_expert_in[0, 0]
    w_down = w_expert_out[0, 0]
    w_in_other = flip(w_in)
    w_down_other = flip(w_down)

    fused = lax.axis_size("expert") == 4 and features == tile_of(w_in.shape[1])
    expert_weights = (w_in, w_down, w_in_other, w_down_other)

    def by_rank(block):
        return block.reshape(ranks, capacity, features)

    def by_slot(block):
        return block.reshape(slots, features)

    weights = []
    for section in range(2):
        is_own = core == section
        others = early[section][:, 3 * width :]
        router = others[:, :experts]
        gains = others[:, experts : experts + 2].T
        table = others[:, experts + 2 : experts + 2 + head_count]
        table = table.reshape(ranks, shard_rows, head_count)[:, :table_rows].reshape(buckets, head_count)
        weights.append((
            early[section], router, gains[0:1], gains[1:2], table,
            None if fused else jnp.where(is_own, w_in, w_in_other),
            None if fused else jnp.where(is_own, w_down, w_down_other),
        ))

    bias_scratch = [
        pltpu.VMEM((-(-head_count // 8) * 8, 2 * span * GROUP), F32),
        pltpu.VMEM((heads * GROUP, span, span), F32),
    ]
    length = GROUP * span
    blocks = span // spacing
    states = []
    results = []
    stream = own
    for section in range(2):
        qkv, router, gain_one, gain_two, table, expert_in, expert_down = weights[section]
        route_rows = section_routes[section]
        side = beside(stream)
        pieces = (stream, flip(stream), side, flip(side))
        outcome, mixed, gathered, stats = call(
            functools.partial(attention_forward, sizes), "attention_forward",
            [shape((GROUP, width, span), BF16), shape((length, 3 * width), BF16),
             shape((length, features), BF16), shape((8, length), F32)],
            [*pieces, gain_one, qkv, table], scalars=ids, scratch=bias_scratch, flops=4 << 30,
        )
        attended = regroup(outcome)
        if section == 0:
            attended, w_out_own = lax.optimization_barrier((attended, w_out_own))
            w_out_other = flip(w_out_own)
            w_outs = [jnp.where(core == which, w_out_own, w_out_other) for which in range(2)]
        w_out = w_outs[section]
        outgoing, middle, normed_two, aux = call(
            functools.partial(after_attention, capacity), "after_attention",
            [shape((slots, features), BF16), shape((span, features), F32),
             shape((span, features), BF16), shape((span, 128), F32)],
            [attended, stream, w_out, gain_two, router, route_rows], flops=1 << 30,
        )
        if fused and section == 0:
            returned, arrived, activation, slope = run_expert_layer(
                "forward", section, expert_weights, [by_rank(outgoing)])
            returned = by_slot(returned)
        elif fused:
            (spread,) = call(spread_grads, "spread_grads", [shape((slots, features), BF16)],
                             [given, aux], flops=1 << 30)
            returned, returned_grad, grad_in, grad_down = run_expert_layer(
                "both", section, expert_weights, [by_rank(outgoing), by_rank(spread)])
            returned = by_slot(returned)
            arrived = activation = slope = None
        else:
            arrived = exchange(outgoing, experts, capacity)
            activation, slope, produced = run_expert_forward(arrived, expert_in, expert_down)
            returned = exchange(produced, experts, capacity)
        result, difference = call(
            combine, "combine", [shape((span, features), BF16), shape((span, features), F32)],
            [returned, aux, middle], flops=1 << 30,
        )
        states.append((stream, outcome, mixed, gathered, stats, attended, middle, normed_two, aux,
                       arrived, activation, slope, difference))
        results.append(result)
        stream = result

    section_outputs = home_pair(results, core)

    upstream = given
    shared_grads = [None, None]
    shared_partner = [None, None]
    shared_qkv = [None, None]
    qkv_grads = [None, None]
    expert_states = [None, None]
    partials = [None, None]
    stream_grads = [None, None]
    for section in (1, 0):
        qkv, router, gain_one, gain_two, table, expert_in, expert_down = weights[section]
        w_out = w_outs[section]
        (stream, outcome, mixed, gathered, stats, attended, middle, normed_two, aux,
         arrived, activation, slope, difference) = states[section]
        route_rows = section_routes[section]
        shares = ()
        if fused and section == 1:
            returned = by_slot(returned_grad)
        else:
            (spread,) = call(spread_grads, "spread_grads", [shape((slots, features), BF16)],
                             [upstream, aux], flops=1 << 30)
        if fused and section == 0:
            returned, grad_in, grad_down = run_expert_layer(
                "backward", section, expert_weights, [by_rank(spread)], [arrived, activation, slope],
                [grad_in, grad_down])
            returned = by_slot(returned)
        elif not fused:
            arrived_grad = exchange(spread, experts, capacity)
            hidden_grad, rows_grad = run_expert_backward(arrived_grad, expert_in, expert_down, slope)
            returned = exchange(rows_grad, experts, capacity)
            expert_states[section] = (arrived, hidden_grad, activation, arrived_grad)
            wanted = (core != section).astype(jnp.int32).reshape(1)
            shares = run_weight_partials(wanted, *expert_states[section])
            partials[section] = [lax.ppermute(part, "section", [(1 - section, section)]) for part in shares]
        if section == 0:
            waiting, returned = lax.optimization_barrier((shared_qkv[1], returned))
            qkv_grads[1] = spread_sum(waiting, ("expert", "zhi"), ranks // 2)
        middle_grad, attended_grad, shared_grads[section] = call(
            before_attention, "before_attention",
            [shape((span, features), F32), shape((GROUP, width, span), BF16),
             shape((features, features + -(-(experts + 1) // 128) * 128), BF16)],
            [returned, aux, upstream, difference, middle, normed_two, attended, gain_two, router, w_out,
             route_rows], flops=2 << 30, after=shares[:1],
        )
        shared_partner[section] = lax.ppermute(shared_grads[section], "section", [(1 - section, section)])
        grads = regroup(attended_grad)
        stay, leave, sent, shared_qkv[section] = call(
            functools.partial(attention_backward, sizes), "attention_backward",
            [shape((span, features), BF16), shape((span, features), BF16), shape((2, span, features), BF16),
             shape((features, -(-(3 * width + 16) // 128) * 128), BF16)],
            [mixed, stats, outcome, grads, gathered, gain_one, qkv, table], scalars=ids,
            scratch=[*bias_scratch, pltpu.VMEM((length, 3 * width), BF16),
                     pltpu.VMEM((GROUP, span, span), F32), pltpu.VMEM((length, size), F32),
                     pltpu.VMEM((length, size), F32), pltpu.VMEM((size, length), F32),
                     pltpu.VMEM((8, GROUP * 2 * 128), F32)],
            flops=8 << 30,
        )
        partner = flip(sent)
        leave = leave + partner[1]
        filler = ()
        if section == 0:
            leave, waiting = lax.optimization_barrier((leave, shared_qkv[0]))
            qkv_grads[0] = spread_sum(waiting, ("expert", "zhi"), ranks // 2)
            if not fused:
                grad_in = run_weight_totals(
                    core_id, *[(expert_states[which][0], expert_states[which][1], partials[which][0])
                               for which in range(2)], False, sent)
                filler = (grad_in,)
        arrived_share = beside(leave)
        (low,) = call(
            first_norm_grad, "first_norm_grad", [shape((span, features), BF16)],
            [stay, partner, arrived_share, stream, gain_one, middle_grad], after=filler,
        )
        stream_grads[section] = low
        upstream = low

    shared = jnp.where(
        core == 0,
        shared_grads[0].astype(F32) + shared_partner[0].astype(F32),
        shared_grads[1].astype(F32) + shared_partner[1].astype(F32),
    ).astype(BF16)
    shared = spread_sum(shared, RANKS, ranks)
    grad_out = shared[:, :features]
    grad_router = shared[:, features : features + experts]
    grad_gain_two = shared[:, features + experts]

    columns = qkv_grads[0].shape[1]
    halves = [block.reshape(2, shard_rows, columns) for block in qkv_grads]
    sending = jnp.stack([halves[0][0], halves[1][0], halves[0][1], halves[1][1]])
    owned = regroup(sending)
    split = owned[:, :, : 3 * width].reshape(GROUP, shard_rows, 3, width)
    grad_qkv = jnp.transpose(split, (1, 2, 0, 3)).reshape(shard_rows, 3 * features)
    grad_table = jnp.transpose(
        owned[:, :table_rows, 3 * width : 3 * width + heads], (1, 0, 2)
    ).reshape(table_rows, head_count)
    grad_gain_one = jnp.sum(owned[:, :, 3 * width + 8], axis=0)
    grad_gains = jnp.stack([grad_gain_one, grad_gain_two])

    section_grads = home_pair(stream_grads, core).astype(F32)

    if not fused:
        grad_down = run_weight_totals(
            core_id, *[(expert_states[which][2], expert_states[which][3], partials[which][1])
                       for which in range(2)], True, stream_grads[0])
    return (
        section_outputs[None, :, None],
        section_grads[None, :, None],
        grad_qkv[None],
        grad_out[None],
        grad_router[None],
        grad_gains[None],
        grad_table[None],
        grad_in[None, None],
        grad_down[None, None],
    )


def solution(mesh):
    sections, ranks, pieces = mesh.devices.shape
    work = Mesh(
        mesh.devices.reshape(sections, ranks, pieces // 2, 2), ("section", "expert", "zhi", "zlo")
    )
    piece = ("zhi", "zlo")
    in_specs = (
        P(None, "expert", piece, None),
        P(None, "expert", piece, None),
        P("section", RANKS, None),
        P("section", RANKS, None),
        P("section", RANKS, None),
        P("section", None, RANKS),
        P("section", RANKS, None),
        P("section", RANKS, None, None),
        P("section", RANKS, None, None),
        P("section", None, "expert", piece, None),
    )
    out_specs = (
        P("section", None, "expert", piece, None),
        P("section", None, "expert", piece, None),
        P("section", RANKS, None),
        P("section", RANKS, None),
        P("section", RANKS, None),
        P("section", None, RANKS),
        P("section", RANKS, None),
        P("section", RANKS, None, None),
        P("section", RANKS, None, None),
    )
    return jax.shard_map(per_device, mesh=work, in_specs=in_specs, out_specs=out_specs, check_vma=False)
```

```python
import functools

import jax
import jax.numpy as jnp
from jax import lax
from jax.experimental import pallas as pl
from jax.experimental.pallas import tpu as pltpu
from jax.sharding import Mesh
from jax.sharding import PartitionSpec as P

F32 = jnp.float32
BF16 = jnp.bfloat16
EPS = 1e-06
MASKED = -1e30
GROUP = 4
RANKS = ("expert", "zhi", "zlo")
VMEM_LIMIT = 60 << 20

NN = (((1,), (0,)), ((), ()))
NT = (((1,), (1,)), ((), ()))
TN = (((0,), (0,)), ((), ()))


def mm(left, right, dims=NN):
    return lax.dot_general(left, right, dims, preferred_element_type=F32)


def inverse_rms(values):
    return lax.rsqrt(jnp.mean(values * values, axis=-1, keepdims=True) + EPS)


def whole(array):
    rank = len(array.shape)
    return pl.BlockSpec(array.shape, lambda *unused: (0,) * rank)


def ordered(body, skipped):
    def inner(*refs):
        return body(*refs[skipped:])

    return inner if skipped else body


REMOTE = pl.DeviceIdType.MESH


def remote(source, target, send, recv, peer):
    return pltpu.make_async_remote_copy(
        src_ref=source, dst_ref=target, send_sem=send, recv_sem=recv, device_id=peer, device_id_type=REMOTE
    )


def across(index, step):
    return (index, index + 1 - 2 * (index % 2), (index + 2) % 4, 3 - index)[step]


def greet(peers):
    barrier = pltpu.get_barrier_semaphore()
    for peer in peers:
        pl.semaphore_signal(barrier, inc=1, device_id=peer, device_id_type=REMOTE)
    pl.semaphore_wait(barrier, len(peers))


def call(body, name, outs, args, scalars=None, scratch=(), flops=0, after=(), collective=None, anywhere=(),
         out_anywhere=()):
    specs = [pl.BlockSpec(memory_space=pl.ANY)] * len(after)
    specs += [pl.BlockSpec(memory_space=pltpu.SMEM)] if scalars is not None else []
    specs += [
        pl.BlockSpec(memory_space=pl.ANY if index in anywhere else pltpu.VMEM) for index in range(len(args))
    ]
    operands = list(after) + ([scalars] if scalars is not None else []) + list(args)
    moved = sum(a.size * a.dtype.itemsize for a in list(args) + list(outs))
    body = ordered(body, len(after))
    return pl.pallas_call(
        body,
        name=name,
        in_specs=specs,
        out_specs=[
            pl.BlockSpec(memory_space=pl.ANY if index in out_anywhere else pltpu.VMEM)
            for index in range(len(outs))
        ],
        out_shape=list(outs),
        scratch_shapes=list(scratch),
        compiler_params=pltpu.CompilerParams(
            vmem_limit_bytes=VMEM_LIMIT, collective_id=collective, has_side_effects=collective is not None
        ),
        cost_estimate=pl.CostEstimate(flops=flops, bytes_accessed=moved, transcendentals=0),
    )(*operands)


def shape(dims, dtype):
    return jax.ShapeDtypeStruct(tuple(dims), dtype)


def bucket_onehot(buckets, span, spacing):
    width = 2 * span * GROUP
    column = lax.broadcasted_iota(jnp.int32, (buckets, width), 1)
    delta = column // (2 * span)
    distance = column - delta * (2 * span) - span + span * delta
    bucket = jnp.where(distance >= 0, distance // spacing, -1)
    row = lax.broadcasted_iota(jnp.int32, (buckets, width), 0)
    return (bucket == row).astype(BF16)


def fill_bias(first_head, heads, table, vectors, bias, span, spacing):
    buckets, head_count = table.shape
    hot = bucket_onehot(buckets, span, spacing)
    rows = mm(table[...], hot, TN)
    column = lax.broadcasted_iota(jnp.int32, (1, 2 * span * GROUP), 1)
    rows = jnp.where(column < span, MASKED, rows)
    vectors[0:head_count, :] = rows
    for head in range(heads):
        picked = vectors[pl.ds(first_head + head, 1), :]
        for delta in range(GROUP):
            piece = picked[:, delta * 2 * span : (delta + 1) * 2 * span]
            spread = jnp.broadcast_to(piece, (span, 2 * span))
            rolled = pltpu.roll(spread, span, 1, stride=1, stride_axis=0)
            bias[head * GROUP + delta] = rolled[:, :span]


def attention_forward(sizes, ids, own, flip, side, side_flip, gain, weight, table,
                      out, mixed, gathered, stats, vectors, bias):
    span, heads, size, spacing, unused = sizes
    width = heads * size
    fill_bias(ids[4] * heads, heads, table, vectors, bias, span, spacing)
    for slot, piece in enumerate((own, flip, side, side_flip)):
        gathered[pl.ds(pl.multiple_of(ids[slot] * span, span), span), :] = piece[...]
    for part in range(GROUP):
        rows = slice(part * span, (part + 1) * span)
        values = gathered[rows, :].astype(F32)
        normed = (values * inverse_rms(values) * gain[...].astype(F32)).astype(BF16)
        mixed[rows, :] = mm(normed, weight[:, : 3 * width]).astype(BF16)
    for head in range(heads):
        columns = slice(head * size, (head + 1) * size)
        query_t = (mixed[:, columns].astype(F32) * size ** (-0.5)).T.astype(BF16)
        key = mixed[:, width + head * size : width + (head + 1) * size]
        value_t = mixed[:, 2 * width + head * size : 2 * width + (head + 1) * size].astype(F32).T.astype(BF16)
        for part in range(GROUP):
            mine = slice(part * span, (part + 1) * span)
            blocks = []
            for other in range(part + 1):
                raw = mm(key[other * span : (other + 1) * span], query_t[:, mine])
                blocks.append(raw + bias[head * GROUP + part - other])
            top = functools.reduce(jnp.maximum, [jnp.max(b, axis=0, keepdims=True) for b in blocks])
            total = jnp.zeros_like(top)
            gained = jnp.zeros((size, span), F32)
            for other, block in enumerate(blocks):
                raised = jnp.exp(block - top)
                total = total + jnp.sum(raised, axis=0, keepdims=True)
                gained = gained + mm(value_t[:, other * span : (other + 1) * span], raised.astype(BF16))
            out[part, columns, :] = (gained / total).astype(BF16)
            stats[head : head + 1, mine] = top + jnp.log(total)


def route_masks(routes, experts):
    lane = lax.broadcasted_iota(jnp.int32, (routes.shape[0], experts), 1)
    return [(routes[:, k : k + 1] == lane).astype(F32) for k in range(2)]


def pick_rows(slot, slots):
    lane = lax.broadcasted_iota(jnp.int32, (slot.shape[0], slots), 1).astype(F32)
    return (lane == slot).astype(BF16)


def fill_slots(aux_t, slots, k):
    row = lax.broadcasted_iota(jnp.int32, (slots, aux_t.shape[1]), 0).astype(F32)
    return (row == aux_t[k : k + 1, :]).astype(BF16)


def after_attention(capacity, attended, own, w_out, gain, router, routes,
                    outgoing, middle, normed_two, aux):
    tokens = own.shape[0]
    experts = router.shape[1]
    slots = experts * capacity
    width = attended.shape[1]
    total = own[...].astype(F32)
    for group in range(GROUP):
        total = total + mm(attended[group], w_out[group * width : (group + 1) * width, :], TN)
    middle[...] = total
    normed = (total * inverse_rms(total) * gain[...].astype(F32)).astype(BF16)
    normed_two[...] = normed
    logits = mm(normed, router[...])
    masks = route_masks(routes, experts)
    members = (masks[0] + masks[1]).astype(BF16)
    row = lax.broadcasted_iota(jnp.int32, (tokens, tokens), 0)
    column = lax.broadcasted_iota(jnp.int32, (tokens, tokens), 1)
    earlier = mm((row > column).astype(BF16), members)
    chosen = [jnp.sum(logits * mask, axis=1, keepdims=True) for mask in masks]
    first = jax.nn.sigmoid(chosen[0] - chosen[1])
    places = [
        routes[:, k : k + 1].astype(F32) * capacity + jnp.sum(earlier * masks[k], axis=1, keepdims=True)
        for k in range(2)
    ]
    lane = lax.broadcasted_iota(jnp.int32, (tokens, 128), 1)
    packed = jnp.zeros((tokens, 128), F32)
    for index, entry in enumerate((places[0], places[1], first, 1.0 - first)):
        packed = jnp.where(lane == index, entry, packed)
    aux[...] = packed
    packed_t = packed.T
    hot = fill_slots(packed_t, slots, 0) + fill_slots(packed_t, slots, 1)
    outgoing[...] = mm(hot, normed).astype(BF16)


def expert_forward(rows, w_in, w_down, activation, slope, produced, total):
    step = pl.program_id(0)

    @pl.when(step == 0)
    def clear():
        total[...] = jnp.zeros_like(total)

    chunk = rows.shape[0] // 4
    for part in range(4):
        mine = slice(part * chunk, (part + 1) * chunk)
        hidden = mm(rows[mine, :], w_in[...])
        half = 0.5 * (1.0 + lax.erf(hidden * 0.7071067811865476))
        bell = jnp.exp(-0.5 * hidden * hidden) * 0.3989422804014327
        raised = (hidden * half).astype(BF16)
        activation[mine, :] = raised
        slope[mine, :] = (half + hidden * bell).astype(BF16)
        total[mine, :] += mm(raised, w_down[...])

    @pl.when(step == pl.num_programs(0) - 1)
    def finish():
        produced[...] = total[...].astype(BF16)


def expert_backward(arrived_grad, w_in, w_down, slope, hidden_grad, rows_grad, total):
    step = pl.program_id(0)

    @pl.when(step == 0)
    def clear():
        total[...] = jnp.zeros_like(total)

    chunk = arrived_grad.shape[0] // 4
    for part in range(4):
        mine = slice(part * chunk, (part + 1) * chunk)
        lifted = mm(arrived_grad[mine, :], w_down[...], NT) * slope[mine, :].astype(F32)
        lowered = lifted.astype(BF16)
        hidden_grad[mine, :] = lowered
        total[mine, :] += mm(lowered, w_in[...], NT)

    @pl.when(step == pl.num_programs(0) - 1)
    def finish():
        rows_grad[...] = total[...].astype(BF16)


def tile_of(hidden):
    return 768 if hidden % 768 == 0 else hidden


def run_expert_forward(rows, w_in, w_down):
    count, features = rows.shape
    hidden = w_in.shape[1]
    tile = tile_of(hidden)
    return pl.pallas_call(
        expert_forward,
        name="expert_forward",
        grid=(hidden // tile,),
        in_specs=[
            whole(rows),
            pl.BlockSpec((features, tile), lambda j: (0, j)),
            pl.BlockSpec((tile, features), lambda j: (j, 0)),
        ],
        out_specs=[
            pl.BlockSpec((count, tile), lambda j: (0, j)),
            pl.BlockSpec((count, tile), lambda j: (0, j)),
            pl.BlockSpec((count, features), lambda j: (0, 0)),
        ],
        out_shape=[shape((count, hidden), BF16), shape((count, hidden), BF16), shape((count, features), BF16)],
        scratch_shapes=[pltpu.VMEM((count, features), F32)],
        compiler_params=pltpu.CompilerParams(vmem_limit_bytes=VMEM_LIMIT),
        cost_estimate=pl.CostEstimate(
            flops=4 * count * features * hidden, bytes_accessed=30 << 20, transcendentals=2 * count * hidden
        ),
    )(rows, w_in, w_down)


def run_expert_backward(arrived_grad, w_in, w_down, slope):
    count, features = arrived_grad.shape
    hidden = w_in.shape[1]
    tile = tile_of(hidden)
    return pl.pallas_call(
        expert_backward,
        name="expert_backward",
        grid=(hidden // tile,),
        in_specs=[
            whole(arrived_grad),
            pl.BlockSpec((features, tile), lambda j: (0, j)),
            pl.BlockSpec((tile, features), lambda j: (j, 0)),
            pl.BlockSpec((count, tile), lambda j: (0, j)),
        ],
        out_specs=[
            pl.BlockSpec((count, tile), lambda j: (0, j)),
            pl.BlockSpec((count, features), lambda j: (0, 0)),
        ],
        out_shape=[shape((count, hidden), BF16), shape((count, features), BF16)],
        scratch_shapes=[pltpu.VMEM((count, features), F32)],
        compiler_params=pltpu.CompilerParams(vmem_limit_bytes=VMEM_LIMIT),
        cost_estimate=pl.CostEstimate(
            flops=4 * count * features * hidden, bytes_accessed=30 << 20, transcendentals=0
        ),
    )(arrived_grad, w_in, w_down, slope)


def weight_partials(scalars, rows, hidden_grad, activation, arrived_grad, grad_in, grad_down):
    @pl.when(scalars[0] == 1)
    def wanted():
        grad_in[...] = mm(rows[...], hidden_grad[...], TN).astype(BF16)
        grad_down[...] = mm(activation[...], arrived_grad[...], TN).astype(BF16)


def run_weight_partials(wanted, rows, hidden_grad, activation, arrived_grad):
    count, features = rows.shape
    hidden = hidden_grad.shape[1]
    tile = tile_of(hidden)
    return pl.pallas_call(
        weight_partials,
        name="weight_partials",
        grid_spec=pltpu.PrefetchScalarGridSpec(
            num_scalar_prefetch=1,
            grid=(hidden // tile,),
            in_specs=[
                pl.BlockSpec((count, features), lambda j, s: (0, 0)),
                pl.BlockSpec((count, tile), lambda j, s: (0, j * s[0])),
                pl.BlockSpec((count, tile), lambda j, s: (0, j * s[0])),
                pl.BlockSpec((count, features), lambda j, s: (0, 0)),
            ],
            out_specs=[
                pl.BlockSpec((features, tile), lambda j, s: (0, j * s[0])),
                pl.BlockSpec((tile, features), lambda j, s: (j * s[0], 0)),
            ],
        ),
        out_shape=[shape((features, hidden), BF16), shape((hidden, features), BF16)],
        compiler_params=pltpu.CompilerParams(vmem_limit_bytes=VMEM_LIMIT),
        cost_estimate=pl.CostEstimate(
            flops=4 * count * features * hidden, bytes_accessed=30 << 20, transcendentals=0
        ),
    )(wanted, rows, hidden_grad, activation, arrived_grad)


def weight_totals(scalars, left, right, sent, left_1, right_1, sent_1, after, total):
    @pl.when(scalars[0] == 0)
    def first():
        total[...] = mm(left[...], right[...], TN) + sent[...].astype(F32)

    @pl.when(scalars[0] == 1)
    def second():
        total[...] = mm(left_1[...], right_1[...], TN) + sent_1[...].astype(F32)


def run_weight_totals(core, first, second, tiled_left, after):
    count, features = first[1 if tiled_left else 0].shape
    hidden = first[0 if tiled_left else 1].shape[1]
    tile = tile_of(hidden)

    def specs(which):
        def step(j, s):
            return jnp.where(s[0] == which, j, 0)

        full = pl.BlockSpec((count, features), lambda j, s: (0, 0))
        part = pl.BlockSpec((count, tile), lambda j, s: (0, step(j, s)))
        if tiled_left:
            return [part, full, pl.BlockSpec((tile, features), lambda j, s: (step(j, s), 0))]
        return [full, part, pl.BlockSpec((features, tile), lambda j, s: (0, step(j, s)))]

    if tiled_left:
        out_spec = pl.BlockSpec((tile, features), lambda j, s: (j, 0))
        dims = (hidden, features)
    else:
        out_spec = pl.BlockSpec((features, tile), lambda j, s: (0, j))
        dims = (features, hidden)
    return pl.pallas_call(
        weight_totals,
        name="weight_totals",
        grid_spec=pltpu.PrefetchScalarGridSpec(
            num_scalar_prefetch=1, grid=(hidden // tile,),
            in_specs=specs(0) + specs(1) + [pl.BlockSpec(memory_space=pl.ANY)], out_specs=out_spec,
        ),
        out_shape=shape(dims, F32),
        compiler_params=pltpu.CompilerParams(vmem_limit_bytes=VMEM_LIMIT),
        cost_estimate=pl.CostEstimate(
            flops=2 * count * features * hidden, bytes_accessed=30 << 20, transcendentals=0
        ),
    )(core, *first, *second, after)


def combine(returned, aux, middle, result, difference):
    slots = returned.shape[0]
    packed = aux[...]
    outs = [mm(pick_rows(packed[:, k : k + 1], slots), returned[...]) for k in range(2)]
    total = middle[...] + packed[:, 2:3] * outs[0] + packed[:, 3:4] * outs[1]
    result[...] = total.astype(BF16)
    difference[...] = outs[0] - outs[1]


def spread_grads(upstream, aux, outgoing):
    slots = outgoing.shape[0]
    packed = aux[...]
    packed_t = packed.T
    values = upstream[...].astype(F32)
    total = jnp.zeros(outgoing.shape, F32)
    for k in range(2):
        total = total + mm(fill_slots(packed_t, slots, k), (values * packed[:, 2 + k : 3 + k]).astype(BF16))
    outgoing[...] = total.astype(BF16)


def norm_backward(values, gain, grad):
    scale = inverse_rms(values)
    unit = values * scale
    lifted = grad * gain
    back = scale * (lifted - unit * jnp.mean(lifted * unit, axis=-1, keepdims=True))
    return back, jnp.sum(grad * unit, axis=0, keepdims=True)


def before_attention(returned, aux, upstream, difference, middle, normed_two, attended, gain,
                     router, w_out, routes, *refs):
    if len(refs) > 3:
        grad_in, grad_down, middle_grad, attended_grad, shared_grad, out_in, out_down, held, in_sem, out_sem = refs
        tile = held.shape[2]
        tiles = held.shape[0] // 2
        places = [(slice(None), pl.ds(index * tile, tile)) for index in range(tiles)]
        places = [(grad_in.at[p], out_in.at[p]) for p in places] + [
            (grad_down.at[pl.ds(index * tile, tile)], out_down.at[pl.ds(index * tile, tile)])
            for index in range(tiles)
        ]
        fetches = [
            pltpu.make_async_copy(pair[0], held.at[index], in_sem.at[index]) for index, pair in enumerate(places)
        ]
        stores = [
            pltpu.make_async_copy(held.at[index], pair[1], out_sem.at[index]) for index, pair in enumerate(places)
        ]
        for fetch in fetches:
            fetch.start()
    else:
        middle_grad, attended_grad, shared_grad = refs
        fetches = stores = ()
    slots = returned.shape[0]
    experts = router.shape[1]
    width = attended.shape[1]
    features = w_out.shape[1]
    packed = aux[...]
    hot = pick_rows(packed[:, 0:1], slots) + pick_rows(packed[:, 1:2], slots)
    token_grad = mm(hot, returned[...])
    flow = upstream[...].astype(F32)
    shift = jnp.sum(flow * difference[...], axis=1, keepdims=True) * packed[:, 2:3] * packed[:, 3:4]
    masks = route_masks(routes, experts)
    logits_grad = (shift * (masks[0] - masks[1])).astype(BF16)
    token_grad = token_grad + mm(logits_grad, router[...], NT)
    back, gain_part = norm_backward(middle[...], gain[...].astype(F32), token_grad)
    total = flow + back
    middle_grad[...] = total
    branch = total.astype(BF16)
    for fetch, store in zip(fetches, stores):
        fetch.wait()
        store.start()
    for group in range(GROUP):
        mine = slice(group * width, (group + 1) * width)
        shared_grad[mine, :features] = mm(attended[group], branch).astype(BF16)
        attended_grad[group] = mm(w_out[mine, :], branch, NT).astype(BF16)
    tail = shared_grad.shape[1] - features
    gain_column = jnp.broadcast_to(gain_part, (8, features)).T
    lane = lax.broadcasted_iota(jnp.int32, (features, tail), 1)
    shared_grad[:, features:] = jnp.where(lane == experts, gain_column[:, 0:1], 0.0).astype(BF16)
    shared_grad[:, features : features + experts] = mm(normed_two[...], logits_grad, TN).astype(BF16)
    for store in stores:
        store.wait()


def attention_backward(sizes, ids, mixed, stats, attended, grads, gathered, gain, weight, table,
                       stay, leave, sent, shared_grad,
                       vectors, bias, mixed_grad, sums, key_total, value_total, turned, strips):
    span, heads, size, spacing, ranks = sizes
    width = heads * size
    count = span // spacing
    buckets = table.shape[0]
    features = weight.shape[0]
    row = lax.broadcasted_iota(jnp.int32, (span, span), 0)
    column = lax.broadcasted_iota(jnp.int32, (span, span), 1)
    later = (column % spacing) >= (row % spacing)
    lane = lax.broadcasted_iota(jnp.int32, (span, 128), 0) // spacing
    backwards = (count - 1 - lane == lax.broadcasted_iota(jnp.int32, (span, 128), 1)).astype(F32)
    strips[...] = jnp.zeros_like(strips)
    fill_bias(ids[4] * heads, heads, table, vectors, bias, span, spacing)
    for head in range(heads):
        columns = slice(head * size, (head + 1) * size)
        key_columns = slice(width + head * size, width + (head + 1) * size)
        value_columns = slice(2 * width + head * size, 2 * width + (head + 1) * size)
        query = (mixed[:, columns].astype(F32) * size ** (-0.5)).astype(BF16)
        query_t = query.astype(F32).T.astype(BF16)
        key = mixed[:, key_columns]
        key_t = key.astype(F32).T.astype(BF16)
        value = mixed[:, value_columns]
        key_total[...] = jnp.zeros_like(key_total)
        value_total[...] = jnp.zeros_like(value_total)
        sums[...] = jnp.zeros_like(sums)
        for part in range(GROUP):
            mine = slice(part * span, (part + 1) * span)
            grad_t = grads[part, columns, :]
            delta_row = jnp.sum(
                grad_t.astype(F32) * attended[part, columns, :].astype(F32), axis=0, keepdims=True
            )
            level = stats[head : head + 1, mine]
            query_total = jnp.zeros((size, span), F32)
            for other in range(part + 1):
                theirs = slice(other * span, (other + 1) * span)
                raw = mm(key[theirs], query_t[:, mine])
                prob = jnp.exp(raw + (bias[head * GROUP + part - other] - level))
                prob_grad = mm(value[theirs], grad_t)
                low = (prob * (prob_grad - delta_row)).astype(BF16)
                sums[part - other] += low.astype(F32)
                query_total = query_total + mm(key_t[:, theirs], low)
                key_total[theirs, :] += mm(low, query[mine])
                value_total[theirs, :] += mm(prob.astype(BF16), grad_t, NT)
            turned[:, mine] = query_total * size ** (-0.5)
        mixed_grad[:, columns] = turned[...].T.astype(BF16)
        mixed_grad[:, key_columns] = key_total[...].astype(BF16)
        mixed_grad[:, value_columns] = value_total[...].astype(BF16)
        for delta in range(GROUP):
            upper = jnp.where(later, sums[delta], 0.0)
            for side, block in enumerate((upper, sums[delta] - upper)):
                tiles = lax.dot_general(
                    jnp.sum(block.reshape(count, spacing, span), axis=1), backwards, NN,
                    precision=lax.Precision.HIGHEST, preferred_element_type=F32,
                )
                turned_tiles = pltpu.roll(tiles, 0, 1, stride=1, stride_axis=0)
                place = (delta * 2 + side) * 128
                strips[head : head + 1, place : place + 128] = jnp.sum(turned_tiles, axis=0, keepdims=True)
    entry = lax.broadcasted_iota(jnp.int32, (GROUP * 2 * 128, 128), 0)
    bucket = (entry // 256) * count + count - 1 - entry % 128 - (entry // 128) % 2
    hot = (bucket == lax.broadcasted_iota(jnp.int32, (GROUP * 2 * 128, 128), 1)) & (entry % 128 < 2 * count)
    table_rows = lax.dot_general(
        strips[...], hot.astype(F32), NN, precision=lax.Precision.HIGHEST, preferred_element_type=F32
    )
    gain_total = jnp.zeros((1, features), F32)
    weight_total = jnp.zeros((features, 3 * width), F32)
    for part in range(GROUP):
        place = ids[5 + part]
        rows = pl.ds(pl.multiple_of(place * span, span), span)
        values = gathered[rows, :].astype(F32)
        unit = values * inverse_rms(values)
        normed = (unit * gain[...].astype(F32)).astype(BF16)
        lowered = mixed_grad[rows, :]
        weight_total = weight_total + mm(normed, lowered, TN)
        back = mm(lowered, weight[:, : 3 * width], NT)
        gain_total = gain_total + jnp.sum(back * unit, axis=0, keepdims=True)
        if part == 0:
            stay[...] = back.astype(BF16)
        elif part == 1:
            leave[...] = back.astype(BF16)
        else:
            sent[part - 2] = back.astype(BF16)
    owned = buckets // ranks
    bucket = lax.broadcasted_iota(jnp.int32, (128, features), 0)
    target = (bucket // owned) * (features // ranks) + bucket % owned
    spot = (target == lax.broadcasted_iota(jnp.int32, (128, features), 1)) & (bucket < buckets)
    placed = lax.dot_general(
        table_rows, spot.astype(F32), NN, precision=lax.Precision.HIGHEST, preferred_element_type=F32
    )
    extra = jnp.concatenate([placed, jnp.broadcast_to(gain_total, (8, features))], axis=0)
    shared_grad[...] = jnp.zeros_like(shared_grad)
    shared_grad[:, : 3 * width] = weight_total.astype(BF16)
    shared_grad[:, 3 * width : 3 * width + 16] = extra.T.astype(BF16)


def first_norm_grad(stay, partner, arrived, own, gain, middle_grad, low):
    grad = stay[...].astype(F32) + partner[0].astype(F32) + arrived[...].astype(F32)
    back, unused = norm_backward(own[...].astype(F32), gain[...].astype(F32), grad)
    low[...] = (middle_grad[...] + back).astype(BF16)


def settle(home_sections, final, stay, leave, sent, own, gain, middle_grad, *refs):
    refs = list(refs)

    def take(count):
        taken = refs[:count]
        del refs[:count]
        return taken

    going = take(len(home_sections))
    qkv = take(2 if final else 0)
    low, home = take(2)
    owned = take(1 if final else 0)
    partner_share, side_share, leaving, pair_send, pair_recv, home_send, home_recv = take(7)
    core = lax.axis_index("section")
    expert = lax.axis_index("expert")
    zhi = lax.axis_index("zhi")
    zlo = lax.axis_index("zlo")
    place = 2 * zhi + zlo
    line = []
    for move in range(4):
        spot = across(place, move)
        for turn in range(2):
            if move or turn:
                line.append({"section": 1 - core if turn else core, "zhi": spot // 2, "zlo": spot % 2})
    plane = [across(expert, step) for step in range(1, 4)]
    greet(line + ([{"expert": spot} for spot in plane] if final else []))

    partner_copy = remote(sent, partner_share, pair_send.at[0], pair_recv.at[0], {"section": 1 - core})
    partner_copy.start()
    aligned = (zlo == zhi) & (zlo == core)

    def home_copy(block, section, index):
        return remote(block, home.at[zhi], home_send.at[index], home_recv.at[zhi],
                      {"section": section, "zhi": zlo, "zlo": core})

    def send_home(block, section, index):
        here = aligned & (core == section)

        @pl.when(here)
        def keep():
            home[zhi] = block[...]

        @pl.when(jnp.logical_not(here))
        def give():
            home_copy(block, section, index).start()

    for index, (block, section) in enumerate(zip(going, home_sections)):
        send_home(block, section, index)
    if final:
        shares, totals, pieces, plane_send, plane_recv, line_send, line_recv = take(7)
        copies = []
        for section in range(2):
            for step, spot in enumerate(plane):
                copy = remote(qkv[section].at[pl.ds(4 * spot, 4)], shares.at[section, step],
                              plane_send.at[section, step], plane_recv.at[section, step], {"expert": spot})
                copy.start()
                copies.append(copy)
    partner_copy.wait()
    leaving[...] = leave[...] + partner_share[1]
    side_copy = remote(leaving, side_share, pair_send.at[1], pair_recv.at[1], {"zlo": 1 - zlo})
    side_copy.start()
    grad = stay[...].astype(F32) + partner_share[0].astype(F32)
    side_copy.wait()
    grad = grad + side_share[...].astype(F32)
    back, unused = norm_backward(own[...].astype(F32), gain[...].astype(F32), grad)
    low[...] = (middle_grad[...] + back).astype(BF16)
    sent_home = list(zip(going, home_sections))
    if final:
        send_home(low, 0, len(going))
        sent_home.append((low, 0))
        for copy in copies:
            copy.wait()
        for section in range(2):
            total = qkv[section][pl.ds(4 * expert, 4)].astype(F32)
            for step in range(3):
                total = total + shares[section, step].astype(F32)
            totals[section] = total.astype(BF16)
        line_copies = []
        for turn in range(2):
            section = 1 - core if turn else core
            for move in range(4):
                spot = across(place, move)
                if move or turn:
                    copy = remote(totals.at[section, spot], pieces.at[2 * place + core],
                                  line_send.at[turn, move], line_recv.at[turn, move],
                                  {"section": section, "zhi": spot // 2, "zlo": spot % 2})
                    copy.start()
                    line_copies.append((copy, turn, spot))
        pieces[2 * place + core] = totals[core, place]
        for turn in range(2):
            for move in range(4):
                if move or turn:
                    source = pieces.at[2 * across(place, move) + (1 - core if turn else core)]
                    remote(source, source, line_send.at[turn, move], line_recv.at[turn, move],
                           {"section": 1 - core}).wait_recv()
        for group in range(GROUP):
            owned[0][group] = pieces[group].astype(F32) + pieces[GROUP + group].astype(F32)
        for copy, unused, unused_1 in line_copies:
            copy.wait_send()
    for batch in range(2):
        @pl.when(jnp.logical_not(aligned & (zhi == batch)))
        def landed():
            remote(home.at[batch], home.at[batch], home_send.at[0], home_recv.at[batch],
                   {"section": 1 - core}).wait_recv()
    for index, (block, section) in enumerate(sent_home):
        @pl.when(jnp.logical_not(aligned & (core == section)))
        def left():
            home_copy(block, section, index).wait_send()


FLIP = [(0, 1), (1, 0)]


def flip(block):
    return lax.ppermute(block, "section", FLIP)


def beside(block):
    return lax.ppermute(block, "zlo", FLIP)


def scatter_pairs(turn):
    return [
        (core * 4 + a * 2 + b, b * 4 + (core ^ turn) * 2 + a)
        for core in range(2)
        for a in range(2)
        for b in range(2)
    ]


def to_working(block, turn):
    return lax.ppermute(block, ("section", "zhi", "zlo"), scatter_pairs(turn))


def to_home(block, section, batch):
    turn = section ^ batch
    pairs = [(after, before) for before, after in scatter_pairs(turn) if before // 4 == section]
    return lax.ppermute(block, ("section", "zhi", "zlo"), pairs)


def home_pair(blocks, core):
    return jnp.stack([
        jnp.where(core == 0, to_home(blocks[0], 0, batch), to_home(blocks[1], 1, batch))
        for batch in range(2)
    ])


def exchange(block, experts, capacity):
    features = block.shape[-1]
    moved = lax.all_to_all(
        block.reshape(experts, capacity, features), RANKS, split_axis=0, concat_axis=0, tiled=True
    )
    return moved.reshape(experts * capacity, features)


def spread_sum(block, axes, parts):
    rows, columns = block.shape
    moved = lax.all_to_all(
        block.reshape(parts, rows // parts, columns), axes, split_axis=0, concat_axis=0, tiled=True
    )
    return jnp.sum(moved.astype(F32), axis=0)


def regroup(block):
    return lax.all_to_all(block, ("zlo", "section"), split_axis=0, concat_axis=0, tiled=True)


def gather_columns(blocks, out, staged, local_sem, send_sem, recv_sem, stage_send, stage_recv):
    core = lax.axis_index("section")
    expert = lax.axis_index("expert")
    zhi = lax.axis_index("zhi")
    zlo = lax.axis_index("zlo")
    place = 2 * zhi + zlo
    other = 1 - core
    beside_x = expert + 1 - 2 * (expert % 2)
    beside_y = (expert + 2) % 4
    places = [place, place + 1 - 2 * zlo, (place + 2) % 4, 3 - place]

    def at(section, rank_expert, rank_place):
        return out.at[section, rank_expert * 4 + rank_place]

    barrier = pltpu.get_barrier_semaphore()
    peers = [{"section": other}, {"expert": beside_x}, {"expert": beside_y}]
    peers += [{"zhi": spot // 2, "zlo": spot % 2} for spot in places[1:]]
    for peer in peers:
        pl.semaphore_signal(barrier, inc=1, device_id=peer, device_id_type=pl.DeviceIdType.MESH)
    pl.semaphore_wait(barrier, len(peers))

    started = []

    def send(source, target, index, section, owner, spot, peer):
        copy = pltpu.make_async_remote_copy(
            src_ref=source, dst_ref=target, send_sem=send_sem.at[index],
            recv_sem=recv_sem.at[section, owner * 4 + spot], device_id=peer,
            device_id_type=pl.DeviceIdType.MESH,
        )
        copy.start()
        started.append(copy)

    def arrived(section, owner, spot):
        pltpu.make_async_remote_copy(
            src_ref=at(section, owner, spot), dst_ref=at(section, owner, spot), send_sem=send_sem.at[0],
            recv_sem=recv_sem.at[section, owner * 4 + spot], device_id={"section": other},
            device_id_type=pl.DeviceIdType.MESH,
        ).wait_recv()

    trades = []
    for parity in range(2):
        trade = pltpu.make_async_remote_copy(
            src_ref=blocks.at[2 * parity + other], dst_ref=staged.at[parity], send_sem=stage_send.at[parity],
            recv_sem=stage_recv.at[parity], device_id={"section": other},
            device_id_type=pl.DeviceIdType.MESH,
        )
        trade.start()
        trades.append(trade)

    index = 0
    for which in range(2):
        section = core if which == 0 else other
        if which == 1:
            for trade in trades:
                trade.wait()

        def block_for(parity):
            return blocks.at[2 * parity + core] if which == 0 else staged.at[parity]

        for step, spot in enumerate(places[1:]):
            send(block_for(spot % 2), at(section, expert, place), index, section, expert, place,
                 {"zhi": spot // 2, "zlo": spot % 2})
            index += 1
        for peer in (beside_x, beside_y):
            send(block_for(zlo), at(section, expert, place), index, section, expert, place, {"expert": peer})
            index += 1
        local = pltpu.make_async_copy(block_for(zlo), at(section, expert, place), local_sem)
        local.start()
        local.wait()
    sections = (core, other)
    for spot in places[1:]:
        for section in sections:
            arrived(section, expert, spot)
            for peer in (beside_x, beside_y):
                send(at(section, expert, spot), at(section, expert, spot), index, section, expert, spot,
                     {"expert": peer})
                index += 1
    for section in sections:
        for step, spot in enumerate(places):
            arrived(section, beside_x, spot)
            arrived(section, beside_y, spot)
            source, peer = ((beside_x, beside_y), (beside_y, beside_x))[step % 2]
            send(at(section, source, spot), at(section, source, spot), index, section, source, spot,
                 {"expert": peer})
            index += 1
    diagonal = 3 - expert
    for section in sections:
        for spot in places:
            arrived(section, diagonal, spot)
    for copy in started:
        copy.wait_send()


def run_gather_columns(blocks, ranks):
    groups, rows, columns = blocks.shape
    return pl.pallas_call(
        gather_columns,
        name="gather_columns",
        in_specs=[pl.BlockSpec(memory_space=pltpu.VMEM)],
        out_specs=pl.BlockSpec(memory_space=pltpu.VMEM),
        out_shape=shape((2, ranks, rows, columns), blocks.dtype),
        scratch_shapes=[
            pltpu.VMEM((2, rows, columns), blocks.dtype),
            pltpu.SemaphoreType.DMA,
            pltpu.SemaphoreType.DMA((30,)),
            pltpu.SemaphoreType.DMA((2, ranks)),
            pltpu.SemaphoreType.DMA((2,)),
            pltpu.SemaphoreType.DMA((2,)),
        ],
        compiler_params=pltpu.CompilerParams(
            collective_id=0, has_side_effects=True, vmem_limit_bytes=16 << 20
        ),
        cost_estimate=pl.CostEstimate(flops=0, bytes_accessed=40 << 20, transcendentals=0),
    )(blocks)


OFFSETS = [(step, place) for place in (0, 3, 1, 2) for step in range(4)]
SENDS = (4, 5, 6, 7, 12, 13, 14, 15, 8, 9, 10, 11, 1, 2, 3)
BATCH = 4


def expert_layer(mode, section, *refs):
    forward = mode != "backward"
    backward = mode != "forward"
    refs = list(refs)

    def take(count):
        taken = refs[:count]
        del refs[:count]
        return taken

    weights = take(4)
    outgoing = take(2 if mode == "both" else 1)
    if mode == "backward":
        saved_rows, saved_activation, saved_slope, unused, unused_1 = take(5)
    returned = take(len(outgoing))
    if mode == "forward":
        kept_rows, kept_activation, kept_slope = take(3)
    else:
        grad_in, grad_down = take(2)
    arrived = take(len(outgoing))
    finished = take(len(outgoing))
    w_in, w_down, activation, slope, totals = take(5)
    send_sem, recv_sem, back_send, back_recv, load_sem = take(5)
    if backward:
        parts, staged, part_send, part_recv, out_sem = take(5)

    core = lax.axis_index("section")
    expert = lax.axis_index("expert")
    place = 2 * lax.axis_index("zhi") + lax.axis_index("zlo")
    me = expert * 4 + place
    hidden = w_in.shape[1]
    slot_rows, features = arrived[0].shape[1:]
    rows_in_batch = BATCH * slot_rows
    tile = tile_of(hidden)
    tiles = hidden // tile
    peers = []
    ranks = []
    for step, move in OFFSETS:
        to_expert, to_place = across(expert, step), across(place, move)
        ranks.append(to_expert * 4 + to_place)
        peers.append({"expert": to_expert, "zhi": to_place // 2, "zlo": to_place % 2})

    loads = []

    def load(source, target, index):
        copy = pltpu.make_async_copy(source, target, load_sem.at[index])
        copy.start()
        loads.append(copy)

    @pl.when(core == section)
    def own_weights():
        pltpu.make_async_copy(weights[0], w_in, load_sem.at[0]).start()
        pltpu.make_async_copy(weights[1], w_down, load_sem.at[1]).start()

    @pl.when(core != section)
    def other_weights():
        pltpu.make_async_copy(weights[2], w_in, load_sem.at[0]).start()
        pltpu.make_async_copy(weights[3], w_down, load_sem.at[1]).start()

    if mode == "backward":
        load(saved_activation, activation, 2)
        load(saved_slope, slope, 3)

    greet(peers[1:] + ([{"section": 1 - core}] if backward else []))

    sent = []
    for slot in SENDS:
        for kind, block in enumerate(outgoing):
            copy = remote(block.at[ranks[slot]], arrived[kind].at[slot], send_sem.at[kind, slot],
                          recv_sem.at[kind, slot], peers[slot])
            copy.start()
            sent.append(copy)
    for kind, block in enumerate(outgoing):
        arrived[kind][0] = block[me]

    pltpu.make_async_copy(weights[0], w_in, load_sem.at[0]).wait()
    pltpu.make_async_copy(weights[1], w_down, load_sem.at[1]).wait()
    for copy in loads:
        copy.wait()

    saves = []
    for batch in range(len(OFFSETS) // BATCH):
        slots = range(batch * BATCH, (batch + 1) * BATCH)
        mine = slice(batch * rows_in_batch, (batch + 1) * rows_in_batch)
        for slot in slots:
            for kind in range(len(outgoing)):
                if slot:
                    remote(arrived[kind].at[slot], arrived[kind].at[slot], send_sem.at[kind, slot],
                           recv_sem.at[kind, slot], peers[slot]).wait_recv()

        def block_of(kind):
            return arrived[kind][slots[0] : slots[-1] + 1].reshape(rows_in_batch, features)

        def one_tile(index, unused):
            spot = pl.ds(pl.multiple_of(index * tile, tile), tile)
            if forward:
                values = mm(block_of(0), w_in[:, spot])
                half = 0.5 * (1.0 + lax.erf(values * 0.7071067811865476))
                bell = jnp.exp(-0.5 * values * values) * 0.3989422804014327
                raised = (values * half).astype(BF16)
                steep = half + values * bell
                activation[mine, spot] = raised
                if mode == "forward":
                    slope[mine, spot] = steep.astype(BF16)
                totals[0] += mm(raised, w_down[spot, :])
            else:
                steep = slope[mine, spot].astype(F32)
            if backward:
                lowered = (mm(block_of(len(outgoing) - 1), w_down[spot, :], NT) * steep).astype(BF16)
                slope[mine, spot] = lowered
                totals[len(outgoing) - 1] += mm(lowered, w_in[:, spot], NT)
            return unused

        totals[...] = jnp.zeros_like(totals)
        lax.fori_loop(0, tiles, one_tile, 0)
        for kind in range(len(outgoing)):
            finished[kind][slots[0] : slots[-1] + 1] = (
                totals[kind].astype(BF16).reshape(BATCH, slot_rows, features)
            )
        for slot in slots:
            for kind in range(len(outgoing)):
                if slot:
                    copy = remote(finished[kind].at[slot], returned[kind].at[me], back_send.at[kind, slot],
                                  back_recv.at[kind, slot], peers[slot])
                    copy.start()
                    sent.append(copy)
                else:
                    returned[kind][me] = finished[kind][0]
        if mode == "forward":
            for index, (source, target) in enumerate(((activation, kept_activation), (slope, kept_slope))):
                copy = pltpu.make_async_copy(
                    source.at[mine, :], target.at[mine, :], load_sem.at[2 + 2 * batch + index]
                )
                copy.start()
                saves.append(copy)
    if mode == "forward":
        kept_rows[...] = arrived[0][...]

    if backward:
        count = slot_rows * len(OFFSETS)
        grads = arrived[len(outgoing) - 1]
        inputs = arrived[0] if forward else saved_rows
        partner = {"section": 1 - core}

        def share_copy(index):
            return remote(parts.at[index], parts.at[index], part_send.at[index], part_recv.at[index], partner)

        def out_copy(index):
            spot = pl.ds(index // 2 * tile, tile)
            target = grad_down.at[spot, :] if index % 2 else grad_in.at[:, spot]
            return pltpu.make_async_copy(staged.at[index % 2], target, out_sem.at[index])

        for index in range(2 * tiles):
            spot = pl.ds(index // 2 * tile, tile)
            if index % 2:
                value = mm(activation[:, spot], grads[...].reshape(count, features), TN)
            else:
                value = mm(inputs[...].reshape(count, features), slope[:, spot], TN)

            @pl.when(core != section)
            def give():
                parts[index] = value.astype(BF16)
                share_copy(index).start()

            @pl.when(core == section)
            def keep():
                share_copy(index).wait_recv()
                if index >= 2:
                    out_copy(index - 2).wait()
                staged[index % 2] = value + parts[index].astype(F32)
                out_copy(index).start()

    for slot in range(1, len(OFFSETS)):
        for kind in range(len(outgoing)):
            remote(finished[kind].at[slot], returned[kind].at[ranks[slot]], back_send.at[kind, slot],
                   back_recv.at[kind, slot], peers[slot]).wait_recv()
    for copy in sent:
        copy.wait_send()
    for copy in saves:
        copy.wait()
    if backward:
        @pl.when(core != section)
        def given():
            for index in range(2 * tiles):
                share_copy(index).wait_send()

        @pl.when(core == section)
        def stored():
            for index in range(2 * tiles - 2, 2 * tiles):
                out_copy(index).wait()


def run_expert_layer(mode, section, weights, outgoing, saved=(), grads=()):
    ranks, slot_rows, features = outgoing[0].shape
    hidden = weights[0].shape[1]
    count = ranks * slot_rows
    tile = tile_of(hidden)
    kinds = len(outgoing)
    anywhere = pl.BlockSpec(memory_space=pl.ANY)
    local = pl.BlockSpec(memory_space=pltpu.VMEM)
    block = shape((ranks, slot_rows, features), BF16)
    wide = shape((count, hidden), BF16)
    in_specs = [anywhere] * 4 + [local] * kinds
    operands = [*weights, *outgoing]
    out_shape = [block] * kinds
    out_specs = [local] * kinds
    aliases = {}
    if mode == "forward":
        out_shape += [block, wide, wide]
        out_specs += [local, anywhere, anywhere]
    else:
        out_shape += [shape((features, hidden), F32), shape((hidden, features), F32)]
        out_specs += [anywhere, anywhere]
    if mode == "backward":
        aliases = {len(operands) + 3: kinds, len(operands) + 4: kinds + 1}
        operands += [*saved, *grads]
        in_specs += [local, anywhere, anywhere, anywhere, anywhere]
    scratch = [pltpu.VMEM(block.shape, BF16)] * (2 * kinds) + [
        pltpu.VMEM((features, hidden), BF16), pltpu.VMEM((hidden, features), BF16),
        pltpu.VMEM((count, hidden), BF16), pltpu.VMEM((count, hidden), BF16),
        pltpu.VMEM((kinds, BATCH * slot_rows, features), F32),
        pltpu.SemaphoreType.DMA((kinds, ranks)), pltpu.SemaphoreType.DMA((kinds, ranks)),
        pltpu.SemaphoreType.DMA((kinds, ranks)), pltpu.SemaphoreType.DMA((kinds, ranks)),
        pltpu.SemaphoreType.DMA((10,)),
    ]
    if mode != "forward":
        pieces = 2 * hidden // tile
        scratch += [
            pltpu.VMEM((pieces, features, tile), BF16), pltpu.VMEM((2, features, tile), F32),
            pltpu.SemaphoreType.DMA((pieces,)), pltpu.SemaphoreType.DMA((pieces,)),
            pltpu.SemaphoreType.DMA((pieces,)),
        ]
    return pl.pallas_call(
        functools.partial(expert_layer, mode, section),
        name="expert_layer_" + mode,
        in_specs=in_specs,
        out_specs=out_specs,
        out_shape=out_shape,
        scratch_shapes=scratch,
        input_output_aliases=aliases,
        compiler_params=pltpu.CompilerParams(
            collective_id={"forward": 1, "both": 2, "backward": 3}[mode], has_side_effects=True,
            vmem_limit_bytes=VMEM_LIMIT,
        ),
        cost_estimate=pl.CostEstimate(
            flops=8 * kinds * count * features * hidden, bytes_accessed=160 << 20, transcendentals=0
        ),
    )(*operands)


def run_settle(final, main, going, home_sections, qkv, collective):
    span, features = main[0].shape
    dma = pltpu.SemaphoreType.DMA
    block = pltpu.VMEM((span, features), BF16)
    outs = [shape((span, features), BF16), shape((2, span, features), BF16)]
    scratch = [
        pltpu.VMEM((2, span, features), BF16), block, block, dma((2,)), dma((2,)), dma((2,)), dma((2,)),
    ]
    if final:
        ranks, rows, columns = qkv[0].shape
        outs.append(shape((GROUP, rows, columns), F32))
        scratch += [
            pltpu.VMEM((2, 3, 4, rows, columns), BF16), pltpu.VMEM((2, 4, rows, columns), BF16),
            pltpu.VMEM((2 * GROUP, rows, columns), BF16), dma((2, 3)), dma((2, 3)), dma((2, 4)), dma((2, 4)),
        ]
    return call(
        functools.partial(settle, tuple(home_sections), final), "settle_last" if final else "settle",
        outs, [*main, *going, *qkv], scratch=scratch, collective=collective,
    )


def per_device(inputs, cotangent, qkv_shard, out_shard, router_shard, gain_shard, table_shard,
               w_expert_in, w_expert_out, routes):
    core = lax.axis_index("section")
    zhi = lax.axis_index("zhi")
    zlo = lax.axis_index("zlo")
    span, features = inputs.shape[2:]
    ranks = lax.axis_size(RANKS)
    shard_rows = qkv_shard.shape[1]
    experts = router_shard.shape[2]
    table_rows, head_count = table_shard.shape[1:]
    buckets = table_rows * ranks
    heads = head_count // GROUP
    size = features // head_count
    width = heads * size
    spacing = GROUP * span // buckets
    capacity = max(2, 4 * span // experts)
    slots = experts * capacity
    group = 2 * zlo + core
    sizes = (span, heads, size, spacing, ranks)
    ids = jnp.stack([
        group, 2 * zlo + 1 - core, 2 * (1 - zlo) + core, 2 * (1 - zlo) + 1 - core, group,
        group, 2 * (1 - zlo) + core, 2 * zlo + 1 - core, 2 * (1 - zlo) + 1 - core,
    ]).astype(jnp.int32)
    core_id = core.astype(jnp.int32).reshape(1)

    own = to_working(lax.dynamic_index_in_dim(inputs, core, 0, keepdims=False)[0], 0)
    given = to_working(lax.dynamic_index_in_dim(cotangent, core, 0, keepdims=False)[0], 0)
    route_parts = [
        to_working(lax.dynamic_index_in_dim(routes[0], core ^ turn, 0, keepdims=False)[0], turn)
        for turn in range(2)
    ]
    section_routes = [
        jnp.where(zhi == section, route_parts[0], route_parts[1]) for section in range(2)
    ]

    small = jnp.concatenate([
        router_shard[0],
        gain_shard[0].T,
        jnp.pad(table_shard[0], ((0, shard_rows - table_rows), (0, 0))),
    ], axis=1)
    by_group = jnp.transpose(
        qkv_shard[0].reshape(shard_rows, 3, GROUP, width), (2, 0, 1, 3)
    ).reshape(GROUP, shard_rows, 3 * width)
    by_group = jnp.concatenate(
        [by_group, jnp.broadcast_to(small[None], (GROUP, *small.shape))], axis=2
    )
    by_group = jnp.pad(by_group, ((0, 0), (0, 0), (0, -by_group.shape[2] % 128)))
    columns = by_group.shape[2]
    if lax.axis_size("expert") == 4:
        early = run_gather_columns(by_group, ranks).reshape(2, features, columns)
        early = [early[0], early[1]]
    else:
        whole_early = lax.all_gather(by_group, RANKS, axis=1, tiled=True)
        kept = lax.dynamic_index_in_dim(whole_early, group, 0, keepdims=False)
        traded = flip(lax.dynamic_index_in_dim(whole_early, 2 * zlo + 1 - core, 0, keepdims=False))
        early = [
            jnp.where(core == section, kept, traded).reshape(features, columns) for section in range(2)
        ]
    w_out_own = lax.all_gather(out_shard[0], RANKS, axis=0, tiled=True)
    w_in = w_expert_in[0, 0]
    w_down = w_expert_out[0, 0]
    w_in_other = flip(w_in)
    w_down_other = flip(w_down)

    fused = lax.axis_size("expert") == 4 and features == tile_of(w_in.shape[1])
    expert_weights = (w_in, w_down, w_in_other, w_down_other)

    def by_rank(block):
        return block.reshape(ranks, capacity, features)

    def by_slot(block):
        return block.reshape(slots, features)

    weights = []
    for section in range(2):
        is_own = core == section
        others = early[section][:, 3 * width :]
        router = others[:, :experts]
        gains = others[:, experts : experts + 2].T
        table = others[:, experts + 2 : experts + 2 + head_count]
        table = table.reshape(ranks, shard_rows, head_count)[:, :table_rows].reshape(buckets, head_count)
        weights.append((
            early[section], router, gains[0:1], gains[1:2], table,
            None if fused else jnp.where(is_own, w_in, w_in_other),
            None if fused else jnp.where(is_own, w_down, w_down_other),
        ))

    bias_scratch = [
        pltpu.VMEM((-(-head_count // 8) * 8, 2 * span * GROUP), F32),
        pltpu.VMEM((heads * GROUP, span, span), F32),
    ]
    length = GROUP * span
    blocks = span // spacing
    states = []
    results = []
    stream = own
    for section in range(2):
        qkv, router, gain_one, gain_two, table, expert_in, expert_down = weights[section]
        route_rows = section_routes[section]
        side = beside(stream)
        pieces = (stream, flip(stream), side, flip(side))
        outcome, mixed, gathered, stats = call(
            functools.partial(attention_forward, sizes), "attention_forward",
            [shape((GROUP, width, span), BF16), shape((length, 3 * width), BF16),
             shape((length, features), BF16), shape((8, length), F32)],
            [*pieces, gain_one, qkv, table], scalars=ids, scratch=bias_scratch, flops=4 << 30,
        )
        attended = regroup(outcome)
        if section == 0:
            attended, w_out_own = lax.optimization_barrier((attended, w_out_own))
            w_out_other = flip(w_out_own)
            w_outs = [jnp.where(core == which, w_out_own, w_out_other) for which in range(2)]
        w_out = w_outs[section]
        outgoing, middle, normed_two, aux = call(
            functools.partial(after_attention, capacity), "after_attention",
            [shape((slots, features), BF16), shape((span, features), F32),
             shape((span, features), BF16), shape((span, 128), F32)],
            [attended, stream, w_out, gain_two, router, route_rows], flops=1 << 30,
        )
        if fused and section == 0:
            returned, arrived, activation, slope = run_expert_layer(
                "forward", section, expert_weights, [by_rank(outgoing)])
            returned = by_slot(returned)
        elif fused:
            (spread,) = call(spread_grads, "spread_grads", [shape((slots, features), BF16)],
                             [given, aux], flops=1 << 30)
            returned, returned_grad, grad_in, grad_down = run_expert_layer(
                "both", section, expert_weights, [by_rank(outgoing), by_rank(spread)])
            returned = by_slot(returned)
            arrived = activation = slope = None
        else:
            arrived = exchange(outgoing, experts, capacity)
            activation, slope, produced = run_expert_forward(arrived, expert_in, expert_down)
            returned = exchange(produced, experts, capacity)
        result, difference = call(
            combine, "combine", [shape((span, features), BF16), shape((span, features), F32)],
            [returned, aux, middle], flops=1 << 30,
        )
        states.append((stream, outcome, mixed, gathered, stats, attended, middle, normed_two, aux,
                       arrived, activation, slope, difference))
        results.append(result)
        stream = result

    if not fused:
        section_outputs = home_pair(results, core)

    upstream = given
    shared_grads = [None, None]
    shared_partner = [None, None]
    shared_qkv = [None, None]
    qkv_grads = [None, None]
    expert_states = [None, None]
    partials = [None, None]
    stream_grads = [None, None]
    for section in (1, 0):
        qkv, router, gain_one, gain_two, table, expert_in, expert_down = weights[section]
        w_out = w_outs[section]
        (stream, outcome, mixed, gathered, stats, attended, middle, normed_two, aux,
         arrived, activation, slope, difference) = states[section]
        route_rows = section_routes[section]
        shares = ()
        if fused and section == 1:
            returned = by_slot(returned_grad)
        else:
            (spread,) = call(spread_grads, "spread_grads", [shape((slots, features), BF16)],
                             [upstream, aux], flops=1 << 30)
        if fused and section == 0:
            returned, grad_in, grad_down = run_expert_layer(
                "backward", section, expert_weights, [by_rank(spread)], [arrived, activation, slope],
                [grad_in, grad_down])
            returned = by_slot(returned)
        elif not fused:
            arrived_grad = exchange(spread, experts, capacity)
            hidden_grad, rows_grad = run_expert_backward(arrived_grad, expert_in, expert_down, slope)
            returned = exchange(rows_grad, experts, capacity)
            expert_states[section] = (arrived, hidden_grad, activation, arrived_grad)
            wanted = (core != section).astype(jnp.int32).reshape(1)
            shares = run_weight_partials(wanted, *expert_states[section])
            partials[section] = [lax.ppermute(part, "section", [(1 - section, section)]) for part in shares]
        if section == 0 and not fused:
            waiting, returned = lax.optimization_barrier((shared_qkv[1], returned))
            qkv_grads[1] = spread_sum(waiting, ("expert", "zhi"), ranks // 2)
        outs = [shape((span, features), F32), shape((GROUP, width, span), BF16),
                shape((features, features + -(-(experts + 1) // 128) * 128), BF16)]
        operands = [returned, aux, upstream, difference, middle, normed_two, attended, gain_two, router, w_out,
                    route_rows]
        scratch = []
        if fused and section == 0:
            outs += [shape(grad_in.shape, F32), shape(grad_down.shape, F32)]
            operands += [grad_in, grad_down]
            pieces = 2 * grad_in.shape[1] // features
            scratch = [pltpu.VMEM((pieces, features, features), F32),
                       pltpu.SemaphoreType.DMA((pieces,)), pltpu.SemaphoreType.DMA((pieces,))]
        middle_grad, attended_grad, shared_grads[section], *published = call(
            before_attention, "before_attention", outs, operands, scratch=scratch, flops=2 << 30,
            after=shares[:1], anywhere=(11, 12), out_anywhere=(3, 4),
        )
        if published:
            grad_in, grad_down = published
        shared_partner[section] = lax.ppermute(shared_grads[section], "section", [(1 - section, section)])
        grads = regroup(attended_grad)
        stay, leave, sent, shared_qkv[section] = call(
            functools.partial(attention_backward, sizes), "attention_backward",
            [shape((span, features), BF16), shape((span, features), BF16), shape((2, span, features), BF16),
             shape((features, -(-(3 * width + 16) // 128) * 128), BF16)],
            [mixed, stats, outcome, grads, gathered, gain_one, qkv, table], scalars=ids,
            scratch=[*bias_scratch, pltpu.VMEM((length, 3 * width), BF16),
                     pltpu.VMEM((GROUP, span, span), F32), pltpu.VMEM((length, size), F32),
                     pltpu.VMEM((length, size), F32), pltpu.VMEM((size, length), F32),
                     pltpu.VMEM((8, GROUP * 2 * 128), F32)],
            flops=8 << 30,
        )
        if fused:
            low, *settled = run_settle(
                section == 0, [stay, leave, sent, stream, gain_one, middle_grad],
                [stream_grads[1]] if section == 0 else results, [1] if section == 0 else [0, 1],
                [block.reshape(ranks, shard_rows, -1) for block in shared_qkv] if section == 0 else [],
                10 if section == 0 else 11,
            )
            if section == 1:
                section_outputs = settled[0]
            else:
                section_grads, owned = settled
        else:
            partner = flip(sent)
            leave = leave + partner[1]
            filler = ()
            if section == 0:
                leave, waiting = lax.optimization_barrier((leave, shared_qkv[0]))
                qkv_grads[0] = spread_sum(waiting, ("expert", "zhi"), ranks // 2)
                grad_in = run_weight_totals(
                    core_id, *[(expert_states[which][0], expert_states[which][1], partials[which][0])
                               for which in range(2)], False, sent)
                filler = (grad_in,)
            arrived_share = beside(leave)
            (low,) = call(
                first_norm_grad, "first_norm_grad", [shape((span, features), BF16)],
                [stay, partner, arrived_share, stream, gain_one, middle_grad], after=filler,
            )
        stream_grads[section] = low
        upstream = low

    shared = jnp.where(
        core == 0,
        shared_grads[0].astype(F32) + shared_partner[0].astype(F32),
        shared_grads[1].astype(F32) + shared_partner[1].astype(F32),
    ).astype(BF16)
    shared = spread_sum(shared, RANKS, ranks)
    grad_out = shared[:, :features]
    grad_router = shared[:, features : features + experts]
    grad_gain_two = shared[:, features + experts]

    if not fused:
        columns = qkv_grads[0].shape[1]
        halves = [block.reshape(2, shard_rows, columns) for block in qkv_grads]
        owned = regroup(jnp.stack([halves[0][0], halves[1][0], halves[0][1], halves[1][1]]))
        section_grads = home_pair(stream_grads, core)
    split = owned[:, :, : 3 * width].reshape(GROUP, shard_rows, 3, width)
    grad_qkv = jnp.transpose(split, (1, 2, 0, 3)).reshape(shard_rows, 3 * features)
    grad_table = jnp.transpose(
        owned[:, :table_rows, 3 * width : 3 * width + heads], (1, 0, 2)
    ).reshape(table_rows, head_count)
    grad_gain_one = jnp.sum(owned[:, :, 3 * width + 8], axis=0)
    grad_gains = jnp.stack([grad_gain_one, grad_gain_two])

    section_grads = section_grads.astype(F32)

    if not fused:
        grad_down = run_weight_totals(
            core_id, *[(expert_states[which][2], expert_states[which][3], partials[which][1])
                       for which in range(2)], True, stream_grads[0])
    return (
        section_outputs[None, :, None],
        section_grads[None, :, None],
        grad_qkv[None],
        grad_out[None],
        grad_router[None],
        grad_gains[None],
        grad_table[None],
        grad_in[None, None],
        grad_down[None, None],
    )


def solution(mesh):
    sections, ranks, pieces = mesh.devices.shape
    work = Mesh(
        mesh.devices.reshape(sections, ranks, pieces // 2, 2), ("section", "expert", "zhi", "zlo")
    )
    piece = ("zhi", "zlo")
    in_specs = (
        P(None, "expert", piece, None),
        P(None, "expert", piece, None),
        P("section", RANKS, None),
        P("section", RANKS, None),
        P("section", RANKS, None),
        P("section", None, RANKS),
        P("section", RANKS, None),
        P("section", RANKS, None, None),
        P("section", RANKS, None, None),
        P("section", None, "expert", piece, None),
    )
    out_specs = (
        P("section", None, "expert", piece, None),
        P("section", None, "expert", piece, None),
        P("section", RANKS, None),
        P("section", RANKS, None),
        P("section", RANKS, None),
        P("section", None, RANKS),
        P("section", RANKS, None),
        P("section", RANKS, None, None),
        P("section", RANKS, None, None),
    )
    return jax.shard_map(per_device, mesh=work, in_specs=in_specs, out_specs=out_specs, check_vma=False)
```

```python
import functools

import jax
import jax.numpy as jnp
from jax import lax
from jax.experimental import pallas as pl
from jax.experimental.pallas import tpu as pltpu
from jax.sharding import Mesh
from jax.sharding import PartitionSpec as P

F32 = jnp.float32
BF16 = jnp.bfloat16
EPS = 1e-06
SECTION, EXPERT, ZHI, ZLO = "section", "expert", "zhi", "zlo"
FORWARD, BACKWARD, BOTH = "forward", "backward", "both"
MASKED = -1e30
GROUP = 4
RANKS = (EXPERT, ZHI, ZLO)
VMEM_LIMIT = 60 << 20

NN = (((1,), (0,)), ((), ()))
NT = (((1,), (1,)), ((), ()))
TN = (((0,), (0,)), ((), ()))


def mm(left, right, dims=NN):
    return lax.dot_general(left, right, dims, preferred_element_type=F32)


def inverse_rms(values):
    return lax.rsqrt(jnp.mean(values * values, axis=-1, keepdims=True) + EPS)


def whole(array):
    rank = len(array.shape)
    return pl.BlockSpec(array.shape, lambda *unused: (0,) * rank)


def ordered(body, skipped):
    def inner(*refs):
        return body(*refs[skipped:])

    return inner if skipped else body


def fetched(body, picked, skipped):
    def inner(*refs):
        refs = list(refs)
        semaphores = refs.pop()
        blocks = refs[-len(picked) :]
        del refs[-len(picked) :]
        copies = []
        for place, index in enumerate(sorted(picked)):
            source = refs[skipped + index].at[pl.ds(picked[index], 1)]
            copy = pltpu.make_async_copy(source, blocks[place], semaphores.at[place])
            copy.start()
            copies.append(copy)
            refs[skipped + index] = blocks[place]
        for copy in copies:
            copy.wait()
        return body(*refs)

    return inner


REMOTE = pl.DeviceIdType.MESH


def remote(source, target, send, recv, peer):
    return pltpu.make_async_remote_copy(
        src_ref=source, dst_ref=target, send_sem=send, recv_sem=recv, device_id=peer, device_id_type=REMOTE
    )


def across(index, step):
    return (index, index + 1 - 2 * (index % 2), (index + 2) % 4, 3 - index)[step]


def greet(peers):
    barrier = pltpu.get_barrier_semaphore()
    for peer in peers:
        pl.semaphore_signal(barrier, inc=1, device_id=peer, device_id_type=REMOTE)
    pl.semaphore_wait(barrier, len(peers))


def call(body, name, outs, args, scalars=None, scratch=(), flops=0, after=(), collective=None, anywhere=(),
         out_anywhere=(), picks=()):
    specs = [pl.BlockSpec(memory_space=pl.ANY)] * len(after)
    specs += [pl.BlockSpec(memory_space=pltpu.SMEM)] if scalars is not None else []
    picked = dict(picks)
    specs += [
        pl.BlockSpec(memory_space=pl.ANY if index in anywhere or index in picked else pltpu.VMEM)
        for index in range(len(args))
    ]
    operands = list(after) + ([scalars] if scalars is not None else []) + list(args)
    moved = sum(a.size * a.dtype.itemsize for a in list(args) + list(outs))
    body = ordered(body, len(after))
    if picked:
        body = fetched(body, picked, int(scalars is not None))
        scratch = list(scratch) + [
            pltpu.VMEM((1, *args[index].shape[1:]), args[index].dtype) for index in sorted(picked)
        ] + [pltpu.SemaphoreType.DMA((len(picked),))]
    return pl.pallas_call(
        body,
        name=name,
        in_specs=specs,
        out_specs=[
            pl.BlockSpec(memory_space=pl.ANY if index in out_anywhere else pltpu.VMEM)
            for index in range(len(outs))
        ],
        out_shape=list(outs),
        scratch_shapes=list(scratch),
        compiler_params=pltpu.CompilerParams(
            vmem_limit_bytes=VMEM_LIMIT, collective_id=collective, has_side_effects=collective is not None
        ),
        cost_estimate=pl.CostEstimate(flops=flops, bytes_accessed=moved, transcendentals=0),
    )(*operands)


def shape(dims, dtype):
    return jax.ShapeDtypeStruct(tuple(dims), dtype)


def bucket_onehot(buckets, span, spacing):
    width = 2 * span * GROUP
    column = lax.broadcasted_iota(jnp.int32, (buckets, width), 1)
    delta = column // (2 * span)
    distance = column - delta * (2 * span) - span + span * delta
    bucket = jnp.where(distance >= 0, distance // spacing, -1)
    row = lax.broadcasted_iota(jnp.int32, (buckets, width), 0)
    return (bucket == row).astype(BF16)


def fill_bias(first_head, heads, table, vectors, bias, span, spacing):
    buckets, head_count = table.shape
    hot = bucket_onehot(buckets, span, spacing)
    rows = mm(table, hot, TN)
    column = lax.broadcasted_iota(jnp.int32, (1, 2 * span * GROUP), 1)
    rows = jnp.where(column < span, MASKED, rows)
    vectors[0:head_count, :] = rows
    for head in range(heads):
        picked = vectors[pl.ds(first_head + head, 1), :]
        for delta in range(GROUP):
            piece = picked[:, delta * 2 * span : (delta + 1) * 2 * span]
            spread = jnp.broadcast_to(piece, (span, 2 * span))
            rolled = pltpu.roll(spread, span, 1, stride=1, stride_axis=0)
            bias[head * GROUP + delta] = rolled[:, :span]


def attention_forward(sizes, ids, own, flip, side, side_flip, gain, weight, table,
                      out, mixed, gathered, stats, vectors, bias):
    span, heads, size, spacing, unused = sizes
    width = heads * size
    fill_bias(ids[4] * heads, heads, table[...], vectors, bias, span, spacing)
    for slot, piece in enumerate((own, flip, side, side_flip)):
        gathered[pl.ds(pl.multiple_of(ids[slot] * span, span), span), :] = piece[...]
    for part in range(GROUP):
        project(gathered, slice(part * span, (part + 1) * span), gain[...], weight[:, : 3 * width], mixed)
    for head in range(heads):
        attend_head(sizes, head, mixed, bias, out, stats)


def project(gathered, rows, gain, weight, mixed):
    values = gathered[rows, :].astype(F32)
    normed = (values * inverse_rms(values) * gain.astype(F32)).astype(BF16)
    mixed[rows, :] = mm(normed, weight).astype(BF16)


def attend_head(sizes, head, mixed, bias, out, stats):
    span, heads, size = sizes[:3]
    width = heads * size
    columns = slice(head * size, (head + 1) * size)
    query_t = (mixed[:, columns].astype(F32) * size ** (-0.5)).T.astype(BF16)
    key = mixed[:, width + head * size : width + (head + 1) * size]
    value_t = mixed[:, 2 * width + head * size : 2 * width + (head + 1) * size].astype(F32).T.astype(BF16)
    for part in range(GROUP):
        mine = slice(part * span, (part + 1) * span)
        blocks = []
        for other in range(part + 1):
            raw = mm(key[other * span : (other + 1) * span], query_t[:, mine])
            blocks.append(raw + bias[head * GROUP + part - other])
        top = functools.reduce(jnp.maximum, [jnp.max(b, axis=0, keepdims=True) for b in blocks])
        total = jnp.zeros_like(top)
        gained = jnp.zeros((size, span), F32)
        for other, block in enumerate(blocks):
            raised = jnp.exp(block - top)
            total = total + jnp.sum(raised, axis=0, keepdims=True)
            gained = gained + mm(value_t[:, other * span : (other + 1) * span], raised.astype(BF16))
        out[part, columns, :] = (gained / total).astype(BF16)
        stats[head : head + 1, mine] = top + jnp.log(total)


def route_masks(columns, experts):
    lane = lax.broadcasted_iota(jnp.int32, (columns[0].shape[0], experts), 1).astype(F32)
    return [(column == lane).astype(F32) for column in columns]


def route_columns(routes):
    return [routes[:, k : k + 1].astype(F32) for k in range(2)]


def slot_places(columns, masks, capacity):
    tokens = columns[0].shape[0]
    members = (masks[0] + masks[1]).astype(BF16)
    row = lax.broadcasted_iota(jnp.int32, (tokens, tokens), 0)
    column = lax.broadcasted_iota(jnp.int32, (tokens, tokens), 1)
    earlier = mm((row > column).astype(BF16), members)
    return [
        columns[k] * capacity + jnp.sum(earlier * masks[k], axis=1, keepdims=True) for k in range(2)
    ]


def dispatch(total, gain, router, masks, places, slots, outgoing, normed_two, aux):
    tokens = total.shape[0]
    normed = (total * inverse_rms(total) * gain.astype(F32)).astype(BF16)
    normed_two[...] = normed
    logits = mm(normed, router)
    chosen = [jnp.sum(logits * mask, axis=1, keepdims=True) for mask in masks]
    first = jax.nn.sigmoid(chosen[0] - chosen[1])
    lane = lax.broadcasted_iota(jnp.int32, (tokens, 128), 1)
    packed = jnp.zeros((tokens, 128), F32)
    for index, entry in enumerate((places[0], places[1], first, 1.0 - first)):
        packed = jnp.where(lane == index, entry, packed)
    aux[...] = packed
    packed_t = packed.T
    hot = fill_slots(packed_t, slots, 0) + fill_slots(packed_t, slots, 1)
    outgoing[...] = mm(hot, normed).astype(BF16)
    return packed


def pick_rows(slot, slots):
    lane = lax.broadcasted_iota(jnp.int32, (slot.shape[0], slots), 1).astype(F32)
    return (lane == slot).astype(BF16)


def fill_slots(aux_t, slots, k):
    row = lax.broadcasted_iota(jnp.int32, (slots, aux_t.shape[1]), 0).astype(F32)
    return (row == aux_t[k : k + 1, :]).astype(BF16)


def after_attention(capacity, attended, own, w_out, gain, router, routes,
                    outgoing, middle, normed_two, aux):
    experts = router.shape[1]
    width = attended.shape[1]
    total = own[...].astype(F32)
    for group in range(GROUP):
        total = total + mm(attended[group], w_out[group * width : (group + 1) * width, :], TN)
    middle[...] = total
    columns = route_columns(routes)
    masks = route_masks(columns, experts)
    places = slot_places(columns, masks, capacity)
    dispatch(total, gain[...], router[...], masks, places, experts * capacity, outgoing, normed_two, aux)


def expert_forward(rows, w_in, w_down, activation, slope, produced, total):
    step = pl.program_id(0)

    @pl.when(step == 0)
    def clear():
        total[...] = jnp.zeros_like(total)

    chunk = rows.shape[0] // 4
    for part in range(4):
        mine = slice(part * chunk, (part + 1) * chunk)
        hidden = mm(rows[mine, :], w_in[...])
        half = 0.5 * (1.0 + lax.erf(hidden * 0.7071067811865476))
        bell = jnp.exp(-0.5 * hidden * hidden) * 0.3989422804014327
        raised = (hidden * half).astype(BF16)
        activation[mine, :] = raised
        slope[mine, :] = (half + hidden * bell).astype(BF16)
        total[mine, :] += mm(raised, w_down[...])

    @pl.when(step == pl.num_programs(0) - 1)
    def finish():
        produced[...] = total[...].astype(BF16)


def expert_backward(arrived_grad, w_in, w_down, slope, hidden_grad, rows_grad, total):
    step = pl.program_id(0)

    @pl.when(step == 0)
    def clear():
        total[...] = jnp.zeros_like(total)

    chunk = arrived_grad.shape[0] // 4
    for part in range(4):
        mine = slice(part * chunk, (part + 1) * chunk)
        lifted = mm(arrived_grad[mine, :], w_down[...], NT) * slope[mine, :].astype(F32)
        lowered = lifted.astype(BF16)
        hidden_grad[mine, :] = lowered
        total[mine, :] += mm(lowered, w_in[...], NT)

    @pl.when(step == pl.num_programs(0) - 1)
    def finish():
        rows_grad[...] = total[...].astype(BF16)


def tile_of(hidden):
    return 768 if hidden % 768 == 0 else hidden


def run_expert_forward(rows, w_in, w_down):
    count, features = rows.shape
    hidden = w_in.shape[1]
    tile = tile_of(hidden)
    return pl.pallas_call(
        expert_forward,
        name="expert_forward",
        grid=(hidden // tile,),
        in_specs=[
            whole(rows),
            pl.BlockSpec((features, tile), lambda j: (0, j)),
            pl.BlockSpec((tile, features), lambda j: (j, 0)),
        ],
        out_specs=[
            pl.BlockSpec((count, tile), lambda j: (0, j)),
            pl.BlockSpec((count, tile), lambda j: (0, j)),
            pl.BlockSpec((count, features), lambda j: (0, 0)),
        ],
        out_shape=[shape((count, hidden), BF16), shape((count, hidden), BF16), shape((count, features), BF16)],
        scratch_shapes=[pltpu.VMEM((count, features), F32)],
        compiler_params=pltpu.CompilerParams(vmem_limit_bytes=VMEM_LIMIT),
        cost_estimate=pl.CostEstimate(
            flops=4 * count * features * hidden, bytes_accessed=30 << 20, transcendentals=2 * count * hidden
        ),
    )(rows, w_in, w_down)


def run_expert_backward(arrived_grad, w_in, w_down, slope):
    count, features = arrived_grad.shape
    hidden = w_in.shape[1]
    tile = tile_of(hidden)
    return pl.pallas_call(
        expert_backward,
        name="expert_backward",
        grid=(hidden // tile,),
        in_specs=[
            whole(arrived_grad),
            pl.BlockSpec((features, tile), lambda j: (0, j)),
            pl.BlockSpec((tile, features), lambda j: (j, 0)),
            pl.BlockSpec((count, tile), lambda j: (0, j)),
        ],
        out_specs=[
            pl.BlockSpec((count, tile), lambda j: (0, j)),
            pl.BlockSpec((count, features), lambda j: (0, 0)),
        ],
        out_shape=[shape((count, hidden), BF16), shape((count, features), BF16)],
        scratch_shapes=[pltpu.VMEM((count, features), F32)],
        compiler_params=pltpu.CompilerParams(vmem_limit_bytes=VMEM_LIMIT),
        cost_estimate=pl.CostEstimate(
            flops=4 * count * features * hidden, bytes_accessed=30 << 20, transcendentals=0
        ),
    )(arrived_grad, w_in, w_down, slope)


def weight_partials(scalars, rows, hidden_grad, activation, arrived_grad, grad_in, grad_down):
    @pl.when(scalars[0] == 1)
    def wanted():
        grad_in[...] = mm(rows[...], hidden_grad[...], TN).astype(BF16)
        grad_down[...] = mm(activation[...], arrived_grad[...], TN).astype(BF16)


def run_weight_partials(wanted, rows, hidden_grad, activation, arrived_grad):
    count, features = rows.shape
    hidden = hidden_grad.shape[1]
    tile = tile_of(hidden)
    return pl.pallas_call(
        weight_partials,
        name="weight_partials",
        grid_spec=pltpu.PrefetchScalarGridSpec(
            num_scalar_prefetch=1,
            grid=(hidden // tile,),
            in_specs=[
                pl.BlockSpec((count, features), lambda j, s: (0, 0)),
                pl.BlockSpec((count, tile), lambda j, s: (0, j * s[0])),
                pl.BlockSpec((count, tile), lambda j, s: (0, j * s[0])),
                pl.BlockSpec((count, features), lambda j, s: (0, 0)),
            ],
            out_specs=[
                pl.BlockSpec((features, tile), lambda j, s: (0, j * s[0])),
                pl.BlockSpec((tile, features), lambda j, s: (j * s[0], 0)),
            ],
        ),
        out_shape=[shape((features, hidden), BF16), shape((hidden, features), BF16)],
        compiler_params=pltpu.CompilerParams(vmem_limit_bytes=VMEM_LIMIT),
        cost_estimate=pl.CostEstimate(
            flops=4 * count * features * hidden, bytes_accessed=30 << 20, transcendentals=0
        ),
    )(wanted, rows, hidden_grad, activation, arrived_grad)


def weight_totals(scalars, left, right, sent, left_1, right_1, sent_1, after, total):
    @pl.when(scalars[0] == 0)
    def first():
        total[...] = mm(left[...], right[...], TN) + sent[...].astype(F32)

    @pl.when(scalars[0] == 1)
    def second():
        total[...] = mm(left_1[...], right_1[...], TN) + sent_1[...].astype(F32)


def run_weight_totals(core, first, second, tiled_left, after):
    count, features = first[1 if tiled_left else 0].shape
    hidden = first[0 if tiled_left else 1].shape[1]
    tile = tile_of(hidden)

    def specs(which):
        def step(j, s):
            return jnp.where(s[0] == which, j, 0)

        full = pl.BlockSpec((count, features), lambda j, s: (0, 0))
        part = pl.BlockSpec((count, tile), lambda j, s: (0, step(j, s)))
        if tiled_left:
            return [part, full, pl.BlockSpec((tile, features), lambda j, s: (step(j, s), 0))]
        return [full, part, pl.BlockSpec((features, tile), lambda j, s: (0, step(j, s)))]

    if tiled_left:
        out_spec = pl.BlockSpec((tile, features), lambda j, s: (j, 0))
        dims = (hidden, features)
    else:
        out_spec = pl.BlockSpec((features, tile), lambda j, s: (0, j))
        dims = (features, hidden)
    return pl.pallas_call(
        weight_totals,
        name="weight_totals",
        grid_spec=pltpu.PrefetchScalarGridSpec(
            num_scalar_prefetch=1, grid=(hidden // tile,),
            in_specs=specs(0) + specs(1) + [pl.BlockSpec(memory_space=pl.ANY)], out_specs=out_spec,
        ),
        out_shape=shape(dims, F32),
        compiler_params=pltpu.CompilerParams(vmem_limit_bytes=VMEM_LIMIT),
        cost_estimate=pl.CostEstimate(
            flops=2 * count * features * hidden, bytes_accessed=30 << 20, transcendentals=0
        ),
    )(core, *first, *second, after)


def combined(returned, packed, middle):
    slots = returned.shape[0]
    outs = [mm(pick_rows(packed[:, k : k + 1], slots), returned) for k in range(2)]
    return middle + packed[:, 2:3] * outs[0] + packed[:, 3:4] * outs[1], outs[0] - outs[1]


def combine(returned, aux, middle, result, difference):
    total, gap = combined(returned[...], aux[...], middle[...])
    result[...] = total.astype(BF16)
    difference[...] = gap


def spread_values(values, packed, slots):
    packed_t = packed.T
    total = jnp.zeros((slots, values.shape[1]), F32)
    for k in range(2):
        total = total + mm(fill_slots(packed_t, slots, k), (values * packed[:, 2 + k : 3 + k]).astype(BF16))
    return total.astype(BF16)


def spread_grads(upstream, aux, outgoing):
    outgoing[...] = spread_values(upstream[...].astype(F32), aux[...], outgoing.shape[0])


def norm_backward(values, gain, grad):
    scale = inverse_rms(values)
    unit = values * scale
    lifted = grad * gain
    back = scale * (lifted - unit * jnp.mean(lifted * unit, axis=-1, keepdims=True))
    return back, jnp.sum(grad * unit, axis=0, keepdims=True)


def publisher(grad_in, grad_down, out_in, out_down, held, in_sem, out_sem):
    tile = held.shape[2]
    tiles = held.shape[0] // 2
    across_tiles = [(slice(None), pl.ds(index * tile, tile)) for index in range(tiles)]
    down_tiles = [pl.ds(index * tile, tile) for index in range(tiles)]
    places = [(grad_in.at[p], out_in.at[p]) for p in across_tiles]
    places += [(grad_down.at[p], out_down.at[p]) for p in down_tiles]
    fetches = [
        pltpu.make_async_copy(pair[0], held.at[index], in_sem.at[index]) for index, pair in enumerate(places)
    ]
    stores = [
        pltpu.make_async_copy(held.at[index], pair[1], out_sem.at[index]) for index, pair in enumerate(places)
    ]
    for fetch in fetches:
        fetch.start()
    return fetches, stores


def token_backward(returned, packed, flow, difference, middle, normed_two, attended, gain, router, out_block,
                   columns, middle_grad, attended_grad, shared_grad, fetches=(), stores=()):
    slots, features = returned.shape
    experts = router.shape[1]
    width = attended.shape[1]

    def publish(quarter):
        share = len(fetches) // 4
        for index in range(quarter * share, (quarter + 1) * share):
            fetches[index].wait()
            stores[index].start()

    hot = pick_rows(packed[:, 0:1], slots) + pick_rows(packed[:, 1:2], slots)
    token_grad = mm(hot, returned)
    publish(0)
    shift = jnp.sum(flow * difference, axis=1, keepdims=True) * packed[:, 2:3] * packed[:, 3:4]
    masks = route_masks(columns, experts)
    logits_grad = (shift * (masks[0] - masks[1])).astype(BF16)
    token_grad = token_grad + mm(logits_grad, router, NT)
    back, gain_part = norm_backward(middle, gain.astype(F32), token_grad)
    total = flow + back
    middle_grad[...] = total
    branch = total.astype(BF16)
    publish(1)
    for group in range(GROUP):
        mine = slice(group * width, (group + 1) * width)
        attended_grad[group] = mm(out_block(group), branch, NT).astype(BF16)
        shared_grad[mine, :features] = mm(attended[group], branch).astype(BF16)
        if group == 1:
            publish(2)
    publish(3)
    tail = shared_grad.shape[1] - features
    gain_column = jnp.broadcast_to(gain_part, (8, features)).T
    lane = lax.broadcasted_iota(jnp.int32, (features, tail), 1)
    shared_grad[:, features:] = jnp.where(lane == experts, gain_column[:, 0:1], 0.0).astype(BF16)
    shared_grad[:, features : features + experts] = mm(normed_two, logits_grad, TN).astype(BF16)
    for store in stores:
        store.wait()


def before_attention(returned, aux, upstream, difference, middle, normed_two, attended, gain,
                     router, w_out, routes, middle_grad, attended_grad, shared_grad):
    width = attended.shape[1]
    token_backward(
        returned[...], aux[...], upstream[...].astype(F32), difference[...], middle[...], normed_two[...],
        attended, gain[...], router[...], lambda group: w_out[group * width : (group + 1) * width, :],
        route_columns(routes), middle_grad, attended_grad, shared_grad,
    )


def before_attention_fused(sizes, returned, aux, upstream, difference, middle, normed_two, attended,
                           early, w_outs, routes, grad_in, grad_down,
                           middle_grad, attended_grad, shared_grad, out_in, out_down, held, in_sem, out_sem):
    fetches, stores = publisher(grad_in, grad_down, out_in, out_down, held, in_sem, out_sem)
    router, unused, gain_two, unused_1 = unpack_small(sizes, early, 0)
    token_backward(
        returned[...], aux[...], upstream[...].astype(F32), difference[...], middle[...], normed_two[...],
        attended, gain_two, router, lambda group: out_rows(sizes, w_outs, 0, group),
        route_columns(routes[0].T), middle_grad, attended_grad, shared_grad, fetches, stores,
    )


def back_head(sizes, head, mixed, stats, attended, grads, bias, work):
    mixed_grad, sums, key_total, value_total, turned, strips = work
    span, heads, size, spacing = sizes[:4]
    width = heads * size
    count = span // spacing
    row = lax.broadcasted_iota(jnp.int32, (span, span), 0)
    column = lax.broadcasted_iota(jnp.int32, (span, span), 1)
    later = (column % spacing) >= (row % spacing)
    lane = lax.broadcasted_iota(jnp.int32, (span, 128), 0) // spacing
    backwards = (count - 1 - lane == lax.broadcasted_iota(jnp.int32, (span, 128), 1)).astype(F32)
    columns = slice(head * size, (head + 1) * size)
    key_columns = slice(width + head * size, width + (head + 1) * size)
    value_columns = slice(2 * width + head * size, 2 * width + (head + 1) * size)
    query = (mixed[:, columns].astype(F32) * size ** (-0.5)).astype(BF16)
    query_t = query.astype(F32).T.astype(BF16)
    key = mixed[:, key_columns]
    key_t = key.astype(F32).T.astype(BF16)
    value = mixed[:, value_columns]
    key_total[...] = jnp.zeros_like(key_total)
    value_total[...] = jnp.zeros_like(value_total)
    sums[...] = jnp.zeros_like(sums)
    for part in range(GROUP):
        mine = slice(part * span, (part + 1) * span)
        grad_t = grads[part, columns, :]
        delta_row = jnp.sum(
            grad_t.astype(F32) * attended[part, columns, :].astype(F32), axis=0, keepdims=True
        )
        level = stats[head : head + 1, mine]
        query_total = jnp.zeros((size, span), F32)
        for other in range(part + 1):
            theirs = slice(other * span, (other + 1) * span)
            raw = mm(key[theirs], query_t[:, mine])
            prob = jnp.exp(raw + (bias[head * GROUP + part - other] - level))
            prob_grad = mm(value[theirs], grad_t)
            low = (prob * (prob_grad - delta_row)).astype(BF16)
            sums[part - other] += low.astype(F32)
            query_total = query_total + mm(key_t[:, theirs], low)
            key_total[theirs, :] += mm(low, query[mine])
            value_total[theirs, :] += mm(prob.astype(BF16), grad_t, NT)
        turned[:, mine] = query_total * size ** (-0.5)
    mixed_grad[:, columns] = turned[...].T.astype(BF16)
    mixed_grad[:, key_columns] = key_total[...].astype(BF16)
    mixed_grad[:, value_columns] = value_total[...].astype(BF16)
    for delta in range(GROUP):
        upper = jnp.where(later, sums[delta], 0.0)
        for side, block in enumerate((upper, sums[delta] - upper)):
            tiles = lax.dot_general(
                jnp.sum(block.reshape(count, spacing, span), axis=1), backwards, NN,
                precision=lax.Precision.HIGHEST, preferred_element_type=F32,
            )
            turned_tiles = pltpu.roll(tiles, 0, 1, stride=1, stride_axis=0)
            place = (delta * 2 + side) * 128
            strips[head : head + 1, place : place + 128] = jnp.sum(turned_tiles, axis=0, keepdims=True)


def back_piece(sizes, gathered, rows, gain, weight, mixed_grad):
    values = gathered[rows, :].astype(F32)
    back = mm(mixed_grad[rows, :], weight, NT)
    return back, jnp.sum(back * values * inverse_rms(values), axis=0, keepdims=True)


def weight_share(sizes, gathered, gain, mixed_grad):
    span, heads, size = sizes[:3]
    total = jnp.zeros((gathered.shape[1], 3 * heads * size), F32)
    for part in range(GROUP):
        rows = slice(part * span, (part + 1) * span)
        values = gathered[rows, :].astype(F32)
        normed = (values * inverse_rms(values) * gain.astype(F32)).astype(BF16)
        total = total + mm(normed, mixed_grad[rows, :], TN)
    return total


def extra_columns(sizes, buckets, features, strips, gain_total):
    span, heads, size, spacing, ranks = sizes
    count = span // spacing
    entry = lax.broadcasted_iota(jnp.int32, (GROUP * 2 * 128, 128), 0)
    bucket = (entry // 256) * count + count - 1 - entry % 128 - (entry // 128) % 2
    hot = (bucket == lax.broadcasted_iota(jnp.int32, (GROUP * 2 * 128, 128), 1)) & (entry % 128 < 2 * count)
    table_rows = lax.dot_general(
        strips[...], hot.astype(F32), NN, precision=lax.Precision.HIGHEST, preferred_element_type=F32
    )
    owned = buckets // ranks
    bucket = lax.broadcasted_iota(jnp.int32, (128, features), 0)
    target = (bucket // owned) * (features // ranks) + bucket % owned
    spot = (target == lax.broadcasted_iota(jnp.int32, (128, features), 1)) & (bucket < buckets)
    placed = lax.dot_general(
        table_rows, spot.astype(F32), NN, precision=lax.Precision.HIGHEST, preferred_element_type=F32
    )
    extra = jnp.concatenate([placed, jnp.broadcast_to(gain_total, (8, features))], axis=0)
    return extra.T.astype(BF16)


def attention_backward(sizes, ids, mixed, stats, attended, grads, gathered, gain, weight, table,
                       stay, leave, sent, shared_grad, vectors, bias, *work):
    span, heads, size, spacing, ranks = sizes
    width = heads * size
    mixed_grad, strips = work[0], work[5]
    strips[...] = jnp.zeros_like(strips)
    fill_bias(ids[4] * heads, heads, table[...], vectors, bias, span, spacing)
    for head in range(heads):
        back_head(sizes, head, mixed, stats, attended, grads, bias, work)
    gain_total = 0.0
    for part in range(GROUP):
        rows = pl.ds(pl.multiple_of(ids[5 + part] * span, span), span)
        back, gain_part = back_piece(sizes, gathered, rows, gain[...], weight[:, : 3 * width], mixed_grad)
        gain_total = gain_total + gain_part
        if part == 0:
            stay[...] = back.astype(BF16)
        elif part == 1:
            leave[...] = back.astype(BF16)
        else:
            sent[part - 2] = back.astype(BF16)
    shared_grad[...] = jnp.zeros_like(shared_grad)
    shared_grad[:, : 3 * width] = weight_share(sizes, gathered, gain[...], mixed_grad).astype(BF16)
    shared_grad[:, 3 * width : 3 * width + 16] = extra_columns(
        sizes, table.shape[0], weight.shape[0], strips, gain_total
    )


def first_norm_grad(stay, partner, arrived, own, gain, middle_grad, low):
    grad = stay[...].astype(F32) + partner[0].astype(F32) + arrived[...].astype(F32)
    back, unused = norm_backward(own[...].astype(F32), gain[...].astype(F32), grad)
    low[...] = (middle_grad[...] + back).astype(BF16)


FLIP = [(0, 1), (1, 0)]


def flip(block):
    return lax.ppermute(block, SECTION, FLIP)


def beside(block):
    return lax.ppermute(block, ZLO, FLIP)


def scatter_pairs(turn):
    return [
        (core * 4 + a * 2 + b, b * 4 + (core ^ turn) * 2 + a)
        for core in range(2)
        for a in range(2)
        for b in range(2)
    ]


def to_working(block, turn):
    return lax.ppermute(block, (SECTION, ZHI, ZLO), scatter_pairs(turn))


def to_home(block, section, batch):
    turn = section ^ batch
    pairs = [(after, before) for before, after in scatter_pairs(turn) if before // 4 == section]
    return lax.ppermute(block, (SECTION, ZHI, ZLO), pairs)


def home_pair(blocks, core):
    return jnp.stack([
        jnp.where(core == 0, to_home(blocks[0], 0, batch), to_home(blocks[1], 1, batch))
        for batch in range(2)
    ])


def exchange(block, experts, capacity):
    features = block.shape[-1]
    moved = lax.all_to_all(
        block.reshape(experts, capacity, features), RANKS, split_axis=0, concat_axis=0, tiled=True
    )
    return moved.reshape(experts * capacity, features)


def spread_sum(block, axes, parts):
    rows, columns = block.shape
    moved = lax.all_to_all(
        block.reshape(parts, rows // parts, columns), axes, split_axis=0, concat_axis=0, tiled=True
    )
    return jnp.sum(moved.astype(F32), axis=0)


def regroup(block):
    return lax.all_to_all(block, (ZLO, SECTION), split_axis=0, concat_axis=0, tiled=True)


OFFSETS = [(step, place) for place in (0, 3, 1, 2) for step in range(4)]
SENDS = (12, 13, 14, 15, 4, 5, 6, 7, 8, 9, 10, 11, 1, 2, 3)
BATCH = 4
BATCH_ORDER = (0, 3, 2, 1)


def expert_layer(mode, section, *refs):
    forward = mode != BACKWARD
    backward = mode != FORWARD
    refs = list(refs)

    def take(count):
        taken = refs[:count]
        del refs[:count]
        return taken

    weights = take(4)
    outgoing = take(2 if mode == BOTH else 1)
    if mode == BACKWARD:
        saved_rows, saved_activation, saved_slope, unused, unused_1 = take(5)
    returned = take(len(outgoing))
    if mode == FORWARD:
        kept_rows, kept_activation, kept_slope = take(3)
    else:
        grad_in, grad_down = take(2)
    arrived = take(len(outgoing))
    finished = take(len(outgoing))
    w_in, w_down, activation, slope, totals = take(5)
    send_sem, recv_sem, back_send, back_recv, load_sem = take(5)
    if backward:
        parts, staged, part_send, part_recv, out_sem = take(5)

    core = lax.axis_index(SECTION)
    expert = lax.axis_index(EXPERT)
    place = 2 * lax.axis_index(ZHI) + lax.axis_index(ZLO)
    me = expert * 4 + place
    hidden = w_in.shape[1]
    slot_rows, features = arrived[0].shape[1:]
    rows_in_batch = BATCH * slot_rows
    tile = tile_of(hidden)
    tiles = hidden // tile
    peers = []
    ranks = []
    for step, move in OFFSETS:
        to_expert, to_place = across(expert, step), across(place, move)
        ranks.append(to_expert * 4 + to_place)
        peers.append(dict(expert=to_expert, zhi=to_place // 2, zlo=to_place % 2))

    loads = []

    def load(source, target, index):
        copy = pltpu.make_async_copy(source, target, load_sem.at[index])
        copy.start()
        loads.append(copy)

    @pl.when(core == section)
    def own_weights():
        pltpu.make_async_copy(weights[0], w_in, load_sem.at[0]).start()
        pltpu.make_async_copy(weights[1], w_down, load_sem.at[1]).start()

    @pl.when(core != section)
    def other_weights():
        pltpu.make_async_copy(weights[2], w_in, load_sem.at[0]).start()
        pltpu.make_async_copy(weights[3], w_down, load_sem.at[1]).start()

    if mode == BACKWARD:
        load(saved_activation, activation, 2)
        load(saved_slope, slope, 3)

    greet(peers[1:] + ([dict(section=1 - core)] if backward else []))

    sent = []
    for slot in SENDS:
        for kind, block in enumerate(outgoing):
            copy = remote(block.at[ranks[slot]], arrived[kind].at[slot], send_sem.at[kind, slot],
                          recv_sem.at[kind, slot], peers[slot])
            copy.start()
            sent.append(copy)
    for kind, block in enumerate(outgoing):
        arrived[kind][0] = block[me]

    pltpu.make_async_copy(weights[0], w_in, load_sem.at[0]).wait()
    pltpu.make_async_copy(weights[1], w_down, load_sem.at[1]).wait()
    for copy in loads:
        copy.wait()

    saves = []
    for batch in BATCH_ORDER:
        slots = range(batch * BATCH, (batch + 1) * BATCH)
        mine = slice(batch * rows_in_batch, (batch + 1) * rows_in_batch)
        for slot in slots:
            for kind in range(len(outgoing)):
                if slot:
                    remote(arrived[kind].at[slot], arrived[kind].at[slot], send_sem.at[kind, slot],
                           recv_sem.at[kind, slot], peers[slot]).wait_recv()

        def block_of(kind):
            return arrived[kind][slots[0] : slots[-1] + 1].reshape(rows_in_batch, features)

        def one_tile(index, unused):
            spot = pl.ds(pl.multiple_of(index * tile, tile), tile)
            if forward:
                values = mm(block_of(0), w_in[:, spot])
                half = 0.5 * (1.0 + lax.erf(values * 0.7071067811865476))
                bell = jnp.exp(-0.5 * values * values) * 0.3989422804014327
                raised = (values * half).astype(BF16)
                steep = half + values * bell
                activation[mine, spot] = raised
                if mode == FORWARD:
                    slope[mine, spot] = steep.astype(BF16)
                totals[0] += mm(raised, w_down[spot, :])
            else:
                steep = slope[mine, spot].astype(F32)
            if backward:
                lowered = (mm(block_of(len(outgoing) - 1), w_down[spot, :], NT) * steep).astype(BF16)
                slope[mine, spot] = lowered
                totals[len(outgoing) - 1] += mm(lowered, w_in[:, spot], NT)
            return unused

        totals[...] = jnp.zeros_like(totals)
        lax.fori_loop(0, tiles, one_tile, 0)
        for kind in range(len(outgoing)):
            finished[kind][slots[0] : slots[-1] + 1] = (
                totals[kind].astype(BF16).reshape(BATCH, slot_rows, features)
            )
        for slot in slots:
            for kind in range(len(outgoing)):
                if slot:
                    copy = remote(finished[kind].at[slot], returned[kind].at[me], back_send.at[kind, slot],
                                  back_recv.at[kind, slot], peers[slot])
                    copy.start()
                    sent.append(copy)
                else:
                    returned[kind][me] = finished[kind][0]
        if mode == FORWARD:
            for index, (source, target) in enumerate(((activation, kept_activation), (slope, kept_slope))):
                copy = pltpu.make_async_copy(
                    source.at[mine, :], target.at[mine, :], load_sem.at[2 + 2 * batch + index]
                )
                copy.start()
                saves.append(copy)
    if mode == FORWARD:
        kept_rows[...] = arrived[0][...]

    if backward:
        count = slot_rows * len(OFFSETS)
        grads = arrived[len(outgoing) - 1]
        inputs = arrived[0] if forward else saved_rows
        partner = dict(section=1 - core)

        def share_copy(index):
            return remote(parts.at[index], parts.at[index], part_send.at[index], part_recv.at[index], partner)

        def out_copy(index):
            spot = pl.ds(index // 2 * tile, tile)
            target = grad_down.at[spot, :] if index % 2 else grad_in.at[:, spot]
            return pltpu.make_async_copy(staged.at[index % 2], target, out_sem.at[index])

        for index in range(2 * tiles):
            spot = pl.ds(index // 2 * tile, tile)
            if index % 2:
                value = mm(activation[:, spot], grads[...].reshape(count, features), TN)
            else:
                value = mm(inputs[...].reshape(count, features), slope[:, spot], TN)

            @pl.when(core != section)
            def give():
                parts[index] = value.astype(BF16)
                share_copy(index).start()

            @pl.when(core == section)
            def keep():
                share_copy(index).wait_recv()
                if index >= 2:
                    out_copy(index - 2).wait()
                staged[index % 2] = value + parts[index].astype(F32)
                out_copy(index).start()

    for slot in range(1, len(OFFSETS)):
        for kind in range(len(outgoing)):
            remote(finished[kind].at[slot], returned[kind].at[ranks[slot]], back_send.at[kind, slot],
                   back_recv.at[kind, slot], peers[slot]).wait_recv()
    for copy in sent:
        copy.wait_send()
    for copy in saves:
        copy.wait()
    if backward:
        @pl.when(core != section)
        def given():
            for index in range(2 * tiles):
                share_copy(index).wait_send()

        @pl.when(core == section)
        def stored():
            for index in range(2 * tiles - 2, 2 * tiles):
                out_copy(index).wait()


def run_expert_layer(mode, section, weights, outgoing, saved=(), grads=()):
    ranks, slot_rows, features = outgoing[0].shape
    hidden = weights[0].shape[1]
    count = ranks * slot_rows
    tile = tile_of(hidden)
    kinds = len(outgoing)
    anywhere = pl.BlockSpec(memory_space=pl.ANY)
    local = pl.BlockSpec(memory_space=pltpu.VMEM)
    block = shape((ranks, slot_rows, features), BF16)
    wide = shape((count, hidden), BF16)
    in_specs = [anywhere] * 4 + [local] * kinds
    operands = [*weights, *outgoing]
    out_shape = [block] * kinds
    out_specs = [local] * kinds
    aliases = {}
    if mode == FORWARD:
        out_shape += [block, wide, wide]
        out_specs += [local, anywhere, anywhere]
    else:
        out_shape += [shape((features, hidden), F32), shape((hidden, features), F32)]
        out_specs += [anywhere, anywhere]
    if mode == BACKWARD:
        aliases = {len(operands) + 3: kinds, len(operands) + 4: kinds + 1}
        operands += [*saved, *grads]
        in_specs += [local, anywhere, anywhere, anywhere, anywhere]
    scratch = [pltpu.VMEM(block.shape, BF16)] * (2 * kinds) + [
        pltpu.VMEM((features, hidden), BF16), pltpu.VMEM((hidden, features), BF16),
        pltpu.VMEM((count, hidden), BF16), pltpu.VMEM((count, hidden), BF16),
        pltpu.VMEM((kinds, BATCH * slot_rows, features), F32),
        pltpu.SemaphoreType.DMA((kinds, ranks)), pltpu.SemaphoreType.DMA((kinds, ranks)),
        pltpu.SemaphoreType.DMA((kinds, ranks)), pltpu.SemaphoreType.DMA((kinds, ranks)),
        pltpu.SemaphoreType.DMA((10,)),
    ]
    if mode != FORWARD:
        pieces = 2 * hidden // tile
        scratch += [
            pltpu.VMEM((pieces, features, tile), BF16), pltpu.VMEM((2, features, tile), F32),
            pltpu.SemaphoreType.DMA((pieces,)), pltpu.SemaphoreType.DMA((pieces,)),
            pltpu.SemaphoreType.DMA((pieces,)),
        ]
    return pl.pallas_call(
        functools.partial(expert_layer, mode, section),
        name="expert_layer_" + mode,
        in_specs=in_specs,
        out_specs=out_specs,
        out_shape=out_shape,
        scratch_shapes=scratch,
        input_output_aliases=aliases,
        compiler_params=pltpu.CompilerParams(
            collective_id={FORWARD: 1, BOTH: 2, BACKWARD: 3}[mode], has_side_effects=True,
            vmem_limit_bytes=VMEM_LIMIT,
        ),
        cost_estimate=pl.CostEstimate(
            flops=8 * kinds * count * features * hidden, bytes_accessed=160 << 20, transcendentals=0
        ),
    )(*operands)


class Sizes:
    def __init__(self, **sizes):
        self.__dict__.update(sizes)
        self.width = self.heads * self.size
        self.length = GROUP * self.span
        self.slots = self.experts * self.capacity
        self.attention = (self.span, self.heads, self.size, self.spacing, self.ranks)
        self.base = 3 * self.width // 128 * 128
        self.offset = 3 * self.width - self.base
        self.table_lane = self.offset + self.experts + 2


def unpack_small(sizes, early, section):
    tail = early[section, :, :, sizes.base :]
    tail = tail.reshape(sizes.features, tail.shape[2])
    tail_t = tail.astype(F32).T
    first = sizes.offset + sizes.experts
    bucket = lax.broadcasted_iota(jnp.int32, (sizes.buckets, sizes.features), 0)
    target = bucket // sizes.table_rows * sizes.shard_rows + bucket % sizes.table_rows
    spot = target == lax.broadcasted_iota(jnp.int32, (sizes.buckets, sizes.features), 1)
    table = mm(spot.astype(BF16), tail).astype(BF16)
    router = tail[:, sizes.offset : first]
    return router, tail_t[first : first + 1, :], tail_t[first + 1 : first + 2, :], table


def qkv_columns(sizes, early, section):
    return early[section, :, :, : 3 * sizes.width].reshape(sizes.features, 3 * sizes.width)


def out_rows(sizes, w_outs, section, group):
    per_group = sizes.ranks // GROUP
    rows = w_outs[section, group * per_group : (group + 1) * per_group]
    return rows.reshape(sizes.width, sizes.features)


def whereabouts():
    core, zhi, zlo = (lax.axis_index(name) for name in (SECTION, ZHI, ZLO))
    return core, zhi, zlo, 2 * zhi + zlo, 2 * zlo + core


def line_peers(core, place):
    peers = []
    for move in range(4):
        spot = across(place, move)
        for turn in range(2):
            if move or turn:
                peers.append(dict(section=1 - core if turn else core, zhi=spot // 2, zlo=spot % 2))
    return peers


class Regroup:
    def __init__(self, block, target, send, recv):
        core, unused, zlo, unused_1, mine = whereabouts()
        self.copies = []
        for index, (turn, move) in enumerate(((0, 1), (1, 1), (1, 0))):
            to_core = 1 - core if turn else core
            to_zlo = 1 - zlo if move else zlo
            copy = remote(block.at[2 * to_zlo + to_core], target.at[mine], send.at[index], recv.at[index],
                          dict(section=to_core, zlo=to_zlo))
            copy.start()
            self.copies.append(copy)
        target[mine] = block[mine]

    def wait(self):
        for copy in self.copies:
            copy.wait()


class WeightGather:
    def __init__(self, blocks, shard, early, w_outs, staged, sems):
        (self.early_send, self.early_recv, self.stage_send, self.stage_recv, self.local_sem,
         self.out_send, self.out_recv) = sems
        self.blocks, self.shard, self.early, self.w_outs, self.staged = blocks, shard, early, w_outs, staged
        self.core, unused, self.zlo, self.place, unused_1 = whereabouts()
        self.other = 1 - self.core
        self.expert = lax.axis_index(EXPERT)
        self.beside_x = across(self.expert, 1)
        self.beside_y = across(self.expert, 2)
        self.places = [across(self.place, move) for move in range(4)]
        self.sections = (self.core, self.other)
        self.started = []
        self.early_count = self.out_count = 0

    def at(self, section, owner, spot):
        return self.early.at[section, owner * 4 + spot]

    def send(self, source, section, owner, spot, peer):
        copy = remote(source, self.at(section, owner, spot), self.early_send.at[self.early_count],
                      self.early_recv.at[section, owner * 4 + spot], peer)
        self.early_count += 1
        copy.start()
        self.started.append(copy)

    def arrived(self, section, owner, spot):
        block = self.at(section, owner, spot)
        remote(block, block, self.early_send.at[0], self.early_recv.at[section, owner * 4 + spot],
               dict(section=self.other)).wait_recv()

    def out_at(self, section, owner, spot):
        return self.w_outs.at[section, owner * 4 + spot]

    def send_out(self, source, owner, spot, peer):
        copy = remote(source, self.out_at(self.core, owner, spot), self.out_send.at[self.out_count],
                      self.out_recv.at[self.core, owner * 4 + spot], peer)
        self.out_count += 1
        copy.start()
        self.started.append(copy)

    def out_arrived(self, section, owner, spot):
        block = self.out_at(section, owner, spot)
        remote(block, block, self.out_send.at[0], self.out_recv.at[section, owner * 4 + spot],
               dict(section=self.other)).wait_recv()

    def trade(self):
        self.trades = []
        for parity in range(2):
            copy = remote(self.blocks.at[2 * parity + self.other], self.staged.at[parity],
                          self.stage_send.at[parity], self.stage_recv.at[parity], dict(section=self.other))
            copy.start()
            self.trades.append(copy)

    def start(self):
        for which, section in enumerate(self.sections):
            if which:
                for copy in self.trades:
                    copy.wait()

            def block_for(parity):
                return self.staged.at[parity] if which else self.blocks.at[2 * parity + self.core]

            for spot in self.places[1:]:
                self.send(block_for(spot % 2), section, self.expert, self.place,
                          dict(zhi=spot // 2, zlo=spot % 2))
            for peer in (self.beside_x, self.beside_y):
                self.send(block_for(self.zlo), section, self.expert, self.place, dict(expert=peer))
            local = pltpu.make_async_copy(
                block_for(self.zlo), self.at(section, self.expert, self.place), self.local_sem
            )
            local.start()
            local.wait()

    def along_z(self):
        for spot in self.places[1:]:
            for section in self.sections:
                self.arrived(section, self.expert, spot)
                for peer in (self.beside_x, self.beside_y):
                    self.send(self.at(section, self.expert, spot), section, self.expert, spot, dict(expert=peer))

    def over_plane(self):
        for section in self.sections:
            for step, spot in enumerate(self.places):
                self.arrived(section, self.beside_x, spot)
                self.arrived(section, self.beside_y, spot)
                source, peer = ((self.beside_x, self.beside_y), (self.beside_y, self.beside_x))[step % 2]
                self.send(self.at(section, source, spot), section, source, spot, dict(expert=peer))

    def finish_early(self):
        diagonal = 3 - self.expert
        for section in self.sections:
            for spot in self.places:
                self.arrived(section, diagonal, spot)

    def out_start(self):
        for spot in self.places[1:]:
            self.send_out(self.shard, self.expert, self.place, dict(zhi=spot // 2, zlo=spot % 2))
        for peer in (self.beside_x, self.beside_y):
            self.send_out(self.shard, self.expert, self.place, dict(expert=peer))
        self.send_out(self.shard, self.expert, self.place, dict(section=self.other))
        local = pltpu.make_async_copy(
            self.shard, self.out_at(self.core, self.expert, self.place), self.local_sem
        )
        local.start()
        local.wait()

    def out_pass(self, owner, spot, peers):
        block = self.out_at(self.core, owner, spot)
        self.out_arrived(self.core, owner, spot)
        for peer in peers + [dict(section=self.other)]:
            self.send_out(block, owner, spot, peer)

    def out_along_z(self):
        for spot in self.places[1:]:
            self.out_pass(self.expert, spot, [dict(expert=self.beside_x), dict(expert=self.beside_y)])

    def out_over_plane(self):
        for step, spot in enumerate(self.places):
            self.out_pass(self.beside_x, spot, [dict(expert=self.beside_y)] if step % 2 == 0 else [])
            self.out_pass(self.beside_y, spot, [dict(expert=self.beside_x)] if step % 2 else [])

    def out_finish(self):
        for spot in self.places:
            self.out_pass(3 - self.expert, spot, [])

    def out_all(self):
        for owner in range(4):
            for spot in range(4):
                self.out_arrived(self.other, owner, spot)

    def close(self):
        for copy in self.started:
            copy.wait_send()


def attend(section, sizes, *refs):
    refs = list(refs)

    def take(count):
        taken = refs[:count]
        del refs[:count]
        return taken

    if section == 0:
        home_rows, home_routes, blocks, shard = take(4)
    else:
        returned, aux_before, middle_before, early, w_outs, routes, given = take(7)
    outcome, mixed, gathered, stats, outgoing, middle, normed_two, aux, attended = take(9)
    if section == 0:
        early, w_outs, routes = take(3)
    else:
        result, difference, spread = take(3)
    vectors, bias, pair_send, pair_recv, group_send, group_recv = take(6)
    span = sizes.span
    core, zhi, zlo, place, group = whereabouts()
    expert = lax.axis_index(EXPERT)

    def rows_of(piece):
        return pl.ds(pl.multiple_of(piece * span, span), span)

    own, flipped = group, 2 * zlo + 1 - core
    side, side_flipped = 2 * (1 - zlo) + core, 2 * (1 - zlo) + 1 - core
    partner, beside_z = dict(section=1 - core), dict(zlo=1 - zlo)
    greet(line_peers(core, place)
          + ([dict(expert=across(expert, 1)), dict(expert=across(expert, 2))] if section == 0 else []))

    pair_copies = []

    def pass_piece(piece, index, peer):
        block = gathered.at[rows_of(piece)]
        copy = remote(block, block, pair_send.at[index], pair_recv.at[index], peer)
        copy.start()
        pair_copies.append(copy)

    def await_piece(piece, index):
        block = gathered.at[rows_of(piece)]
        remote(block, block, pair_send.at[index], pair_recv.at[index], partner).wait_recv()

    if section == 0:
        staged, home_send, home_recv = take(3)
        gather = WeightGather(blocks, shard, early, w_outs, staged, take(7))
        gather.trade()
        aligned = (zlo == zhi) & (zlo == core)

        def to_work(source, target, index, slot, turn):
            peer = dict(section=zlo, zhi=1 - core if turn else core, zlo=zhi)
            return remote(source, target, home_send.at[index], home_recv.at[slot], peer)

        rows_copy = to_work(home_rows, gathered.at[rows_of(place)], 0, 0, 0)
        route_copies = [
            to_work(home_routes.at[1 - core if turn else core], routes.at[core], 1 + turn, 1 + core, turn)
            for turn in range(2)
        ]

        @pl.when(aligned)
        def keep():
            gathered[rows_of(place), :] = home_rows[...]
            routes[core] = home_routes[core]

        @pl.when(jnp.logical_not(aligned))
        def give():
            rows_copy.start()
            route_copies[0].start()

        route_copies[1].start()
        gather.start()

        @pl.when(jnp.logical_not(aligned))
        def landed():
            rows_copy.wait_recv()

        pass_piece(own, 0, beside_z)
        pass_piece(own, 1, partner)
        gather.along_z()
        gather.over_plane()
        gather.out_start()
        await_piece(side, 0)
        pass_piece(side, 2, partner)
        gather.finish_early()
    else:
        total, gap = combined(returned[...], aux_before[...], middle_before[...])
        result[...] = total.astype(BF16)
        gathered[rows_of(own), :] = total.astype(BF16)
        difference[...] = gap
        pass_piece(own, 0, beside_z)
        pass_piece(own, 1, partner)

    router, gain_one, gain_two, table = unpack_small(sizes, early, section)
    fill_bias(group * sizes.heads + sizes.table_lane, sizes.heads, table, vectors, bias, span, sizes.spacing)
    weight = qkv_columns(sizes, early, section)
    project(gathered, rows_of(own), gain_one, weight, mixed)
    await_piece(flipped, 1)
    project(gathered, rows_of(flipped), gain_one, weight, mixed)
    if section:
        await_piece(side, 0)
        pass_piece(side, 2, partner)
    project(gathered, rows_of(side), gain_one, weight, mixed)
    await_piece(side_flipped, 2)
    project(gathered, rows_of(side_flipped), gain_one, weight, mixed)
    for head in range(sizes.heads):
        if section == 0 and head < 3:
            (gather.out_along_z, gather.out_over_plane, gather.out_finish)[head]()
        attend_head(sizes.attention, head, mixed, bias, outcome, stats)
    if section == 0:
        for stage in (gather.out_along_z, gather.out_over_plane, gather.out_finish)[sizes.heads :]:
            stage()
        for which in range(2):
            @pl.when(jnp.logical_not(aligned & (core == which)))
            def routed():
                remote(routes.at[which], routes.at[which], home_send.at[1], home_recv.at[1 + which],
                       partner).wait_recv()
    trade = Regroup(outcome, attended, group_send, group_recv)
    columns_t = routes[section].T
    columns = [columns_t[:, k : k + 1] for k in range(2)]
    masks = route_masks(columns, sizes.experts)
    places = slot_places(columns, masks, sizes.capacity)
    if section == 0:
        gather.out_all()
    total = gathered[rows_of(own), :].astype(F32)
    trade.wait()
    for member in range(GROUP):
        total = total + mm(attended[member], out_rows(sizes, w_outs, section, member), TN)
    middle[...] = total
    packed = dispatch(total, gain_two, router, masks, places, sizes.slots, outgoing, normed_two, aux)
    if section:
        spread[...] = spread_values(given[...].astype(F32), packed, sizes.slots)
    for copy in pair_copies:
        copy.wait_send()
    if section == 0:
        gather.close()

        @pl.when(jnp.logical_not(aligned))
        def given_away():
            rows_copy.wait_send()
            route_copies[0].wait_send()

        route_copies[1].wait_send()


def run_attend(section, sizes, operands, collective):
    dma = pltpu.SemaphoreType.DMA
    span, features, width = sizes.span, sizes.features, sizes.width
    outs = [
        shape((GROUP, width, span), BF16), shape((sizes.length, 3 * width), BF16),
        shape((sizes.length, features), BF16), shape((8, sizes.length), F32),
        shape((sizes.slots, features), BF16), shape((span, features), F32), shape((span, features), BF16),
        shape((span, 128), F32), shape((GROUP, width, span), BF16),
    ]
    scratch = [
        pltpu.VMEM((128, 2 * span * GROUP), F32), pltpu.VMEM((sizes.heads * GROUP, span, span), F32),
        dma((3,)), dma((3,)), dma((3,)), dma((3,)),
    ]
    if section == 0:
        unused, rows, columns = operands[2].shape
        outs += [
            shape((2, sizes.ranks, rows, columns), BF16), shape((2, sizes.ranks, rows, features), BF16),
            shape((2, 8, span), F32),
        ]
        scratch += [
            pltpu.VMEM((2, rows, columns), BF16), dma((3,)), dma((3,)),
            dma((30,)), dma((2, sizes.ranks)), dma((2,)), dma((2,)), dma, dma((34,)), dma((2, sizes.ranks)),
        ]
    else:
        outs += [shape((span, features), BF16), shape((span, features), F32), shape((sizes.slots, features), BF16)]
    return call(
        functools.partial(attend, section, sizes), "attend", outs, operands, scratch=scratch,
        flops=6 << 30, collective=collective,
    )


def unpack(sizes, home, owned, shared, stream_grads, grad_qkv, grad_out, grad_router, grad_gains, grad_table):
    width, features, experts = sizes.width, sizes.features, sizes.experts
    stream_grads[...] = home[...].astype(F32)
    grad_qkv[...] = jnp.concatenate(
        [owned[member, :, part * width : (part + 1) * width] for part in range(3) for member in range(GROUP)],
        axis=1,
    )
    grad_out[...] = shared[:, :features]
    tail = shared[:, features:]
    grad_router[...] = tail[:, :experts]
    ends = [owned[member, :, sizes.base :] for member in range(GROUP)]
    grad_table[...] = jnp.concatenate(
        [end[: sizes.table_rows, sizes.offset : sizes.offset + sizes.heads] for end in ends], axis=1
    )
    spot = sizes.offset + 8
    grad_gains[0:1, :] = (ends[0] + ends[1] + ends[2] + ends[3]).T[spot : spot + 1, :]
    grad_gains[1:2, :] = tail.T[experts : experts + 1, :]


class Homes:
    def __init__(self, home, send, recv):
        self.home, self.send_sem, self.recv_sem = home, send, recv
        self.core, self.zhi, self.zlo, unused, unused_1 = whereabouts()
        self.aligned = (self.zlo == self.zhi) & (self.zlo == self.core)
        self.sent = []

    def copy(self, block, section, index):
        return remote(block, self.home.at[self.zhi], self.send_sem.at[index], self.recv_sem.at[self.zhi],
                      dict(section=section, zhi=self.zlo, zlo=self.core))

    def send(self, block, section):
        index = len(self.sent)
        here = self.aligned & (self.core == section)
        self.sent.append((block, section))

        @pl.when(here)
        def keep():
            self.home[self.zhi] = block[...]

        @pl.when(jnp.logical_not(here))
        def give():
            self.copy(block, section, index).start()

    def close(self):
        for batch in range(2):
            @pl.when(jnp.logical_not(self.aligned & (self.zhi == batch)))
            def landed():
                block = self.home.at[batch]
                remote(block, block, self.send_sem.at[0], self.recv_sem.at[batch],
                       dict(section=1 - self.core)).wait_recv()
        for index, (block, section) in enumerate(self.sent):
            @pl.when(jnp.logical_not(self.aligned & (self.core == section)))
            def left():
                self.copy(block, section, index).wait_send()


class PlaneSum:
    def __init__(self, source, shares, send, recv):
        self.source, self.shares = source, shares
        self.expert = lax.axis_index(EXPERT)
        self.copies = []
        for step in range(1, 4):
            spot = across(self.expert, step)
            copy = remote(source.at[pl.ds(4 * spot, 4)], shares.at[step - 1], send.at[step - 1],
                          recv.at[step - 1], dict(expert=spot))
            copy.start()
            self.copies.append(copy)

    def total(self):
        for copy in self.copies:
            copy.wait()
        total = self.source[pl.ds(4 * self.expert, 4)].astype(F32)
        for step in range(3):
            total = total + self.shares[step].astype(F32)
        return total.astype(BF16)


def attend_back(section, sizes, *refs):
    refs = list(refs)

    def take(count):
        taken = refs[:count]
        del refs[:count]
        return taken

    last = section == 0
    early, mixed, stats, outcome, gathered = take(5)
    if last:
        middle_grad, attended_grad, first_low, *shared, other_qkv = take(6)
        home, owned, owned_shared, = take(3)
    else:
        (returned, returned_grad, aux, middle, given, normed_two, attended, w_outs, routes,
         first_result, next_aux) = take(11)
        shared_grad, low, qkv_grad, home, spread = take(5)
    vectors, bias, *work = take(8)
    (grads, kept, leaving, sent, partner_share, side_share, group_send, group_recv, pair_send, pair_recv,
     home_send, home_recv) = take(12)
    mixed_grad, strips = work[0], work[5]
    span, features, width = sizes.span, sizes.features, sizes.width
    core, zhi, zlo, place, group = whereabouts()
    expert = lax.axis_index(EXPERT)
    if last:
        (low, qkv_grad, other_shares, qkv_shares, shared_in, shared_sum, shared_shares, line_totals, pieces,
         shared_totals, shared_parts, other_send, other_recv, plane_send, plane_recv, in_send, in_recv,
         shared_send, shared_recv, line_send, line_recv, spread_send, spread_recv) = take(23)
    else:
        middle_grad, attended_grad, second_result = take(3)
    greet(line_peers(core, place) + ([dict(expert=across(expert, step)) for step in range(1, 4)] if last else []))
    homes = Homes(home, home_send, home_recv)
    router, gain_one, gain_two, table = unpack_small(sizes, early, 0)
    if not last:
        homes.send(first_result, 0)
        total, difference = combined(returned[...], aux[...], middle[...])
        second_result[...] = total.astype(BF16)
        token_backward(
            returned_grad[...], aux[...], given[...].astype(F32), difference, middle[...], normed_two[...],
            attended, gain_two, router, lambda member: out_rows(sizes, w_outs, 0, member),
            route_columns(routes[section].T), middle_grad, attended_grad, shared_grad,
        )
    trade = Regroup(attended_grad, grads, group_send, group_recv)
    if last:
        partner = dict(section=1 - core)
        for which in range(2):
            @pl.when(core != which)
            def pass_share():
                remote(shared[which], shared_in, in_send, in_recv, partner).start()

        other_sum = PlaneSum(other_qkv, other_shares, other_send, other_recv)
        homes.send(first_low, 1)
    else:
        homes.send(second_result, 1)
    strips[...] = jnp.zeros_like(strips)
    fill_bias(group * sizes.heads + sizes.table_lane, sizes.heads, table, vectors, bias, span, sizes.spacing)
    if last:
        remote(shared[0], shared_in, in_send, in_recv, partner).wait_recv()
        for which in range(2):
            @pl.when(core == which)
            def add_share():
                shared_sum[...] = shared[which][...] + shared_in[...]

        plane_shared = PlaneSum(shared_sum, shared_shares, shared_send, shared_recv)
        line_copies = []

        def to_owners(owner_section, totals):
            line_totals[owner_section] = totals
            turn = (core + owner_section) % 2
            mine = 2 * place + core
            for move in range(4):
                spot = across(place, move)
                copy = remote(line_totals.at[owner_section, spot], pieces.at[mine],
                              line_send.at[owner_section, move], line_recv.at[turn, move],
                              dict(section=owner_section, zhi=spot // 2, zlo=spot % 2))
                line_copies.append((copy, owner_section, move))
                if move:
                    copy.start()
                else:
                    @pl.when(core != owner_section)
                    def give():
                        copy.start()

                    @pl.when(core == owner_section)
                    def keep():
                        pieces[mine] = line_totals[owner_section, place]

    trade.wait()
    for head in range(sizes.heads):
        if last and head == sizes.heads - 1:
            to_owners(1, other_sum.total())
        back_head(sizes.attention, head, mixed, stats, outcome, grads, bias, work)
    weight = qkv_columns(sizes, early, 0)

    def rows_of(piece):
        return pl.ds(pl.multiple_of(piece * span, span), span)

    def piece_back(piece):
        return back_piece(sizes.attention, gathered, rows_of(piece), gain_one, weight, mixed_grad)

    back, gain_total = piece_back(2 * zlo + 1 - core)
    sent[0] = back.astype(BF16)
    back, gain_part = piece_back(2 * (1 - zlo) + 1 - core)
    sent[1] = back.astype(BF16)
    partner_copy = remote(sent, partner_share, pair_send.at[0], pair_recv.at[0], dict(section=1 - core))
    partner_copy.start()
    gain_total = gain_total + gain_part
    leave, gain_part = piece_back(2 * (1 - zlo) + core)
    gain_total = gain_total + gain_part
    partner_copy.wait()
    leaving[...] = (leave + partner_share[1].astype(F32)).astype(BF16)
    stay, gain_part = piece_back(group)
    side_copy = remote(leaving, side_share, pair_send.at[1], pair_recv.at[1], dict(zlo=1 - zlo))
    side_copy.start()
    gain_total = gain_total + gain_part
    kept[...] = stay + partner_share[0].astype(F32)
    columns = qkv_grad.shape[2]
    weights = weight_share(sizes.attention, gathered, gain_one, mixed_grad).astype(BF16)
    extra = extra_columns(sizes.attention, sizes.buckets, features, strips, gain_total)
    by_rank = (sizes.ranks, sizes.shard_rows)
    qkv_grad[:, :, 3 * width :] = jnp.concatenate(
        [extra, jnp.zeros((features, columns - 3 * width - 16), BF16)], axis=1
    ).reshape(*by_rank, columns - 3 * width)
    qkv_grad[:, :, : 3 * width] = weights.reshape(*by_rank, 3 * width)
    if last:
        qkv_sum = PlaneSum(qkv_grad, qkv_shares, plane_send, plane_recv)
        shared_totals[...] = plane_shared.total()
        for move in range(4):
            spot = across(place, move)
            if move:
                copy = remote(shared_totals.at[spot], shared_parts.at[move], spread_send.at[move],
                              spread_recv.at[move], dict(zhi=spot // 2, zlo=spot % 2))
                copy.start()
                line_copies.append((copy, None, move))
            else:
                shared_parts[0] = shared_totals[place]
    side_copy.wait()
    own = gathered[rows_of(group), :].astype(F32)
    back, unused = norm_backward(own, gain_one, kept[...] + side_share[...].astype(F32))
    total = (middle_grad[...] + back).astype(BF16)
    low[...] = total
    if not last:
        spread[...] = spread_values(total.astype(F32), next_aux[...], sizes.slots)
    else:
        homes.send(low, 0)
        to_owners(0, qkv_sum.total())
        for turn in range(2):
            for move in range(4):
                if move or turn:
                    block = pieces.at[2 * across(place, move) + (1 - core if turn else core)]
                    remote(block, block, line_send.at[0, 0], line_recv.at[turn, move], partner).wait_recv()
        for member in range(GROUP):
            owned[member] = pieces[member].astype(F32) + pieces[GROUP + member].astype(F32)
        for copy, owner_section, move in line_copies:
            if owner_section is None:
                copy.wait()
            elif move:
                copy.wait_send()
            else:
                @pl.when(core != owner_section)
                def gone():
                    copy.wait_send()
        owned_shared[...] = sum(shared_parts[move].astype(F32) for move in range(4))
        remote(shared[0], shared_in, in_send, in_recv, partner).wait_send()
    homes.close()


def run_attend_back(section, sizes, operands, picks, collective):
    dma = pltpu.SemaphoreType.DMA
    span, features, width, ranks = sizes.span, sizes.features, sizes.width, sizes.ranks
    rows = sizes.shard_rows
    columns = -(-(3 * width + 16) // 128) * 128
    tail = features + -(-(sizes.experts + 1) // 128) * 128
    block = (span, features)
    last = section == 0
    if last:
        outs = [shape((2, *block), BF16), shape((GROUP, rows, columns), F32), shape((rows, tail), F32)]
    else:
        outs = [shape((features, tail), BF16), shape(block, BF16), shape((ranks, rows, columns), BF16),
                shape((2, *block), BF16), shape((sizes.slots, features), BF16)]
    scratch = [
        pltpu.VMEM((128, 2 * span * GROUP), F32), pltpu.VMEM((sizes.heads * GROUP, span, span), F32),
        pltpu.VMEM((sizes.length, 3 * width), BF16), pltpu.VMEM((GROUP, span, span), F32),
        pltpu.VMEM((sizes.length, sizes.size), F32), pltpu.VMEM((sizes.length, sizes.size), F32),
        pltpu.VMEM((sizes.size, sizes.length), F32), pltpu.VMEM((8, GROUP * 2 * 128), F32),
        pltpu.VMEM((GROUP, width, span), BF16), pltpu.VMEM(block, F32), pltpu.VMEM(block, BF16),
        pltpu.VMEM((2, *block), BF16), pltpu.VMEM((2, *block), BF16), pltpu.VMEM(block, BF16),
        dma((3,)), dma((3,)), dma((2,)), dma((2,)), dma((2,)), dma((2,)),
    ]
    if last:
        scratch += [
            pltpu.VMEM(block, BF16), pltpu.VMEM((ranks, rows, columns), BF16),
            pltpu.VMEM((3, 4, rows, columns), BF16), pltpu.VMEM((3, 4, rows, columns), BF16),
            pltpu.VMEM((ranks, rows, tail), BF16), pltpu.VMEM((ranks, rows, tail), BF16),
            pltpu.VMEM((3, 4, rows, tail), BF16), pltpu.VMEM((2, 4, rows, columns), BF16),
            pltpu.VMEM((2 * GROUP, rows, columns), BF16), pltpu.VMEM((4, rows, tail), BF16),
            pltpu.VMEM((4, rows, tail), BF16),
            dma((3,)), dma((3,)), dma((3,)), dma((3,)), dma, dma, dma((3,)), dma((3,)),
            dma((2, 4)), dma((2, 4)), dma((4,)), dma((4,)),
        ]
    else:
        scratch += [pltpu.VMEM(block, F32), pltpu.VMEM((GROUP, width, span), BF16), pltpu.VMEM(block, BF16)]
    return call(
        functools.partial(attend_back, section, sizes), "attend_back", outs, operands, scratch=scratch,
        flops=10 << 30, collective=collective, picks=picks,
    )


def per_device(inputs, cotangent, qkv_shard, out_shard, router_shard, gain_shard, table_shard,
               w_expert_in, w_expert_out, routes):
    core = lax.axis_index(SECTION)
    zhi = lax.axis_index(ZHI)
    zlo = lax.axis_index(ZLO)
    span, features = inputs.shape[2:]
    ranks = lax.axis_size(RANKS)
    shard_rows = qkv_shard.shape[1]
    experts = router_shard.shape[2]
    table_rows, head_count = table_shard.shape[1:]
    buckets = table_rows * ranks
    heads = head_count // GROUP
    size = features // head_count
    width = heads * size
    spacing = GROUP * span // buckets
    capacity = max(2, 4 * span // experts)
    slots = experts * capacity
    group = 2 * zlo + core
    sizes = (span, heads, size, spacing, ranks)
    ids = jnp.stack([
        group, 2 * zlo + 1 - core, 2 * (1 - zlo) + core, 2 * (1 - zlo) + 1 - core, group,
        group, 2 * (1 - zlo) + core, 2 * zlo + 1 - core, 2 * (1 - zlo) + 1 - core,
    ]).astype(jnp.int32)
    core_id = core.astype(jnp.int32).reshape(1)

    w_in = w_expert_in[0, 0]
    w_down = w_expert_out[0, 0]
    w_in_other = flip(w_in)
    w_down_other = flip(w_down)
    fused = lax.axis_size(EXPERT) == 4 and features == tile_of(w_in.shape[1])
    shared_sizes = Sizes(
        span=span, heads=heads, size=size, spacing=spacing, ranks=ranks, experts=experts, capacity=capacity,
        features=features, buckets=buckets, shard_rows=shard_rows, table_rows=table_rows,
    )

    home_rows = lax.dynamic_index_in_dim(inputs, core, 0, keepdims=False)[0]
    given = to_working(lax.dynamic_index_in_dim(cotangent, core, 0, keepdims=False)[0], 0)
    if not fused:
        own = to_working(home_rows, 0)
        route_parts = [
            to_working(lax.dynamic_index_in_dim(routes[0], core ^ turn, 0, keepdims=False)[0], turn)
            for turn in range(2)
        ]
        section_routes = [
            jnp.where(zhi == section, route_parts[0], route_parts[1]) for section in range(2)
        ]

    small = jnp.concatenate([
        router_shard[0],
        gain_shard[0].T,
        jnp.pad(table_shard[0], ((0, shard_rows - table_rows), (0, 0))),
    ], axis=1)
    by_group = jnp.transpose(
        qkv_shard[0].reshape(shard_rows, 3, GROUP, width), (2, 0, 1, 3)
    ).reshape(GROUP, shard_rows, 3 * width)
    by_group = jnp.concatenate(
        [by_group, jnp.broadcast_to(small[None], (GROUP, *small.shape))], axis=2
    )
    by_group = jnp.pad(by_group, ((0, 0), (0, 0), (0, -by_group.shape[2] % 128)))
    columns = by_group.shape[2]
    if fused:
        home_routes = jnp.pad(
            jnp.swapaxes(routes[0, :, 0], 1, 2).astype(F32), ((0, 0), (0, 6), (0, 0))
        )
        first = run_attend(0, shared_sizes, [home_rows, home_routes, by_group, out_shard[0]], 4)
        early_all, w_out_all, route_all = first[9:]
    else:
        whole_early = lax.all_gather(by_group, RANKS, axis=1, tiled=True)
        kept = lax.dynamic_index_in_dim(whole_early, group, 0, keepdims=False)
        traded = flip(lax.dynamic_index_in_dim(whole_early, 2 * zlo + 1 - core, 0, keepdims=False))
        early = [
            jnp.where(core == section, kept, traded).reshape(features, columns) for section in range(2)
        ]
        w_out_own = lax.all_gather(out_shard[0], RANKS, axis=0, tiled=True)
        w_out_other = flip(w_out_own)
        w_outs = [jnp.where(core == which, w_out_own, w_out_other) for which in range(2)]
    expert_weights = (w_in, w_down, w_in_other, w_down_other)

    def by_rank(block):
        return block.reshape(ranks, capacity, features)

    def by_slot(block):
        return block.reshape(slots, features)

    weights = []
    for section in range(0 if fused else 2):
        is_own = core == section
        others = early[section][:, 3 * width :]
        router = others[:, :experts]
        gains = others[:, experts : experts + 2].T
        table = others[:, experts + 2 : experts + 2 + head_count]
        table = table.reshape(ranks, shard_rows, head_count)[:, :table_rows].reshape(buckets, head_count)
        weights.append((
            early[section], router, gains[0:1], gains[1:2], table,
            jnp.where(is_own, w_in, w_in_other), jnp.where(is_own, w_down, w_down_other),
        ))

    bias_scratch = [
        pltpu.VMEM((-(-head_count // 8) * 8, 2 * span * GROUP), F32),
        pltpu.VMEM((heads * GROUP, span, span), F32),
    ]
    length = GROUP * span
    blocks = span // spacing
    states = []
    results = []
    if fused:
        (outcome, mixed, gathered, stats, outgoing, middle, normed_two, aux, attended) = first[:9]
        returned, arrived, activation, slope = run_expert_layer(FORWARD, 0, expert_weights, [by_rank(outgoing)])
        second = run_attend(
            1, shared_sizes, [by_slot(returned), aux, middle, early_all, w_out_all, route_all, given], 5)
        result, difference, spread = second[9:]
        (outcome, mixed, gathered, stats, outgoing, middle, normed_two, aux, attended) = second[:9]
        returned, returned_grad, grad_in, grad_down = run_expert_layer(
            BOTH, 1, expert_weights, [by_rank(outgoing), by_rank(spread)])
        shared_1, low_1, qkv_1, section_outputs, spread = run_attend_back(
            1, shared_sizes,
            [early_all, mixed, stats, outcome, gathered, by_slot(returned), by_slot(returned_grad), aux, middle,
             given, normed_two, attended, w_out_all, route_all, result, first[7]],
            ((0, 1), (12, 1)), 6)
        returned, grad_in, grad_down = run_expert_layer(
            BACKWARD, 0, expert_weights, [by_rank(spread)], [arrived, activation, slope], [grad_in, grad_down])
        (outcome, mixed, gathered, stats, unused, middle, normed_two, aux, attended) = first[:9]
        pieces = 2 * grad_in.shape[1] // features
        middle_grad, attended_grad, shared_0, grad_in, grad_down = call(
            functools.partial(before_attention_fused, shared_sizes), "before_attention",
            [shape((span, features), F32), shape((GROUP, width, span), BF16), shape(shared_1.shape, BF16),
             shape(grad_in.shape, F32), shape(grad_down.shape, F32)],
            [by_slot(returned), aux, low_1, difference, middle, normed_two, attended, early_all, w_out_all,
             route_all, grad_in, grad_down],
            scratch=[pltpu.VMEM((pieces, features, features), F32),
                     pltpu.SemaphoreType.DMA((pieces,)), pltpu.SemaphoreType.DMA((pieces,))],
            flops=2 << 30, anywhere=(10, 11), out_anywhere=(3, 4), picks=((7, 0), (8, 0)),
        )
        ranked = (ranks, shard_rows, -1)
        home, owned, shared_sum = run_attend_back(
            0, shared_sizes,
            [early_all, mixed, stats, outcome, gathered, middle_grad, attended_grad, low_1,
             shared_0.reshape(ranked), shared_1.reshape(ranked), qkv_1],
            ((0, 0),), 7)
        section_grads, grad_qkv, grad_out, grad_router, grad_gains, grad_table = call(
            functools.partial(unpack, shared_sizes), "unpack",
            [shape(home.shape, F32), shape((shard_rows, 3 * features), F32), shape((shard_rows, features), F32),
             shape((shard_rows, experts), F32), shape((2, shard_rows), F32),
             shape((table_rows, head_count), F32)],
            [home, owned, shared_sum],
        )
    stream = None if fused else own
    for section in range(0 if fused else 2):
        qkv, router, gain_one, gain_two, table, expert_in, expert_down = weights[section]
        route_rows = section_routes[section]
        side = beside(stream)
        pieces = (stream, flip(stream), side, flip(side))
        outcome, mixed, gathered, stats = call(
            functools.partial(attention_forward, sizes), "attention_forward",
            [shape((GROUP, width, span), BF16), shape((length, 3 * width), BF16),
             shape((length, features), BF16), shape((8, length), F32)],
            [*pieces, gain_one, qkv, table], scalars=ids, scratch=bias_scratch, flops=4 << 30,
        )
        attended = regroup(outcome)
        outgoing, middle, normed_two, aux = call(
            functools.partial(after_attention, capacity), "after_attention",
            [shape((slots, features), BF16), shape((span, features), F32),
             shape((span, features), BF16), shape((span, 128), F32)],
            [attended, stream, w_outs[section], gain_two, router, route_rows], flops=1 << 30,
        )
        arrived = exchange(outgoing, experts, capacity)
        activation, slope, produced = run_expert_forward(arrived, expert_in, expert_down)
        returned = exchange(produced, experts, capacity)
        result, difference = call(
            combine, "combine", [shape((span, features), BF16), shape((span, features), F32)],
            [returned, aux, middle], flops=1 << 30,
        )
        states.append((stream, outcome, mixed, gathered, stats, attended, middle, normed_two, aux,
                       arrived, activation, slope, difference))
        results.append(result)
        stream = result

    if not fused:
        section_outputs = home_pair(results, core)

    upstream = given
    shared_grads = [None, None]
    shared_partner = [None, None]
    shared_qkv = [None, None]
    qkv_grads = [None, None]
    expert_states = [None, None]
    partials = [None, None]
    stream_grads = [None, None]
    for section in (() if fused else (1, 0)):
        qkv, router, gain_one, gain_two, table, expert_in, expert_down = weights[section]
        w_out = w_outs[section]
        (stream, outcome, mixed, gathered, stats, attended, middle, normed_two, aux,
         arrived, activation, slope, difference) = states[section]
        route_rows = section_routes[section]
        (spread,) = call(spread_grads, "spread_grads", [shape((slots, features), BF16)],
                         [upstream, aux], flops=1 << 30)
        arrived_grad = exchange(spread, experts, capacity)
        hidden_grad, rows_grad = run_expert_backward(arrived_grad, expert_in, expert_down, slope)
        returned = exchange(rows_grad, experts, capacity)
        expert_states[section] = (arrived, hidden_grad, activation, arrived_grad)
        wanted = (core != section).astype(jnp.int32).reshape(1)
        shares = run_weight_partials(wanted, *expert_states[section])
        partials[section] = [lax.ppermute(part, SECTION, [(1 - section, section)]) for part in shares]
        if section == 0:
            waiting, returned = lax.optimization_barrier((shared_qkv[1], returned))
            qkv_grads[1] = spread_sum(waiting, (EXPERT, ZHI), ranks // 2)
        middle_grad, attended_grad, shared_grads[section] = call(
            before_attention, "before_attention",
            [shape((span, features), F32), shape((GROUP, width, span), BF16),
             shape((features, features + -(-(experts + 1) // 128) * 128), BF16)],
            [returned, aux, upstream, difference, middle, normed_two, attended, gain_two, router, w_out,
             route_rows], flops=2 << 30, after=shares[:1],
        )
        shared_partner[section] = lax.ppermute(shared_grads[section], SECTION, [(1 - section, section)])
        grads = regroup(attended_grad)
        stay, leave, sent, shared_qkv[section] = call(
            functools.partial(attention_backward, sizes), "attention_backward",
            [shape((span, features), BF16), shape((span, features), BF16), shape((2, span, features), BF16),
             shape((features, -(-(3 * width + 16) // 128) * 128), BF16)],
            [mixed, stats, outcome, grads, gathered, gain_one, qkv, table], scalars=ids,
            scratch=[*bias_scratch, pltpu.VMEM((length, 3 * width), BF16),
                     pltpu.VMEM((GROUP, span, span), F32), pltpu.VMEM((length, size), F32),
                     pltpu.VMEM((length, size), F32), pltpu.VMEM((size, length), F32),
                     pltpu.VMEM((8, GROUP * 2 * 128), F32)],
            flops=8 << 30,
        )
        partner = flip(sent)
        leave = leave + partner[1]
        filler = ()
        if section == 0:
            leave, waiting = lax.optimization_barrier((leave, shared_qkv[0]))
            qkv_grads[0] = spread_sum(waiting, (EXPERT, ZHI), ranks // 2)
            grad_in = run_weight_totals(
                core_id, *[(expert_states[which][0], expert_states[which][1], partials[which][0])
                           for which in range(2)], False, sent)
            filler = (grad_in,)
        arrived_share = beside(leave)
        (low,) = call(
            first_norm_grad, "first_norm_grad", [shape((span, features), BF16)],
            [stay, partner, arrived_share, stream, gain_one, middle_grad], after=filler,
        )
        stream_grads[section] = low
        upstream = low

    if not fused:
        shared = jnp.where(
            core == 0,
            shared_grads[0].astype(F32) + shared_partner[0].astype(F32),
            shared_grads[1].astype(F32) + shared_partner[1].astype(F32),
        ).astype(BF16)
        shared = spread_sum(shared, RANKS, ranks)
        grad_out = shared[:, :features]
        grad_router = shared[:, features : features + experts]
        grad_gain_two = shared[:, features + experts]

        columns = qkv_grads[0].shape[1]
        halves = [block.reshape(2, shard_rows, columns) for block in qkv_grads]
        owned = regroup(jnp.stack([halves[0][0], halves[1][0], halves[0][1], halves[1][1]]))
        split = owned[:, :, : 3 * width].reshape(GROUP, shard_rows, 3, width)
        grad_qkv = jnp.transpose(split, (1, 2, 0, 3)).reshape(shard_rows, 3 * features)
        grad_table = jnp.transpose(
            owned[:, :table_rows, 3 * width : 3 * width + heads], (1, 0, 2)
        ).reshape(table_rows, head_count)
        grad_gain_one = jnp.sum(owned[:, :, 3 * width + 8], axis=0)
        grad_gains = jnp.stack([grad_gain_one, grad_gain_two])
        section_grads = home_pair(stream_grads, core).astype(F32)
        grad_down = run_weight_totals(
            core_id, *[(expert_states[which][2], expert_states[which][3], partials[which][1])
                       for which in range(2)], True, stream_grads[0])
    return (
        section_outputs[None, :, None],
        section_grads[None, :, None],
        grad_qkv[None],
        grad_out[None],
        grad_router[None],
        grad_gains[None],
        grad_table[None],
        grad_in[None, None],
        grad_down[None, None],
    )


def solution(mesh):
    sections, ranks, pieces = mesh.devices.shape
    work = Mesh(
        mesh.devices.reshape(sections, ranks, pieces // 2, 2), (SECTION, EXPERT, ZHI, ZLO)
    )
    piece = (ZHI, ZLO)
    in_specs = (
        P(None, EXPERT, piece, None),
        P(None, EXPERT, piece, None),
        P(SECTION, RANKS, None),
        P(SECTION, RANKS, None),
        P(SECTION, RANKS, None),
        P(SECTION, None, RANKS),
        P(SECTION, RANKS, None),
        P(SECTION, RANKS, None, None),
        P(SECTION, RANKS, None, None),
        P(SECTION, None, EXPERT, piece, None),
    )
    out_specs = (
        P(SECTION, None, EXPERT, piece, None),
        P(SECTION, None, EXPERT, piece, None),
        P(SECTION, RANKS, None),
        P(SECTION, RANKS, None),
        P(SECTION, RANKS, None),
        P(SECTION, None, RANKS),
        P(SECTION, RANKS, None),
        P(SECTION, RANKS, None, None),
        P(SECTION, RANKS, None, None),
    )
    return jax.shard_map(per_device, mesh=work, in_specs=in_specs, out_specs=out_specs, check_vma=False)
```

```python
import functools

import jax
import jax.numpy as jnp
from jax import lax
from jax.experimental import pallas as pl
from jax.experimental.pallas import tpu as pltpu
from jax.sharding import Mesh
from jax.sharding import PartitionSpec as P

F32 = jnp.float32
BF16 = jnp.bfloat16
EPS = 1e-06
SECTION, EXPERT, ZHI, ZLO = "section", "expert", "zhi", "zlo"
FORWARD, BACKWARD, BOTH = "forward", "backward", "both"
MASKED = -1e30
GROUP = 4
RANKS = (EXPERT, ZHI, ZLO)
VMEM_LIMIT = 60 << 20

NN = (((1,), (0,)), ((), ()))
NT = (((1,), (1,)), ((), ()))
TN = (((0,), (0,)), ((), ()))


def mm(left, right, dims=NN):
    return lax.dot_general(left, right, dims, preferred_element_type=F32)


def inverse_rms(values):
    return lax.rsqrt(jnp.mean(values * values, axis=-1, keepdims=True) + EPS)


def whole(array):
    rank = len(array.shape)
    return pl.BlockSpec(array.shape, lambda *unused: (0,) * rank)


def ordered(body, skipped):
    def inner(*refs):
        return body(*refs[skipped:])

    return inner if skipped else body


def fetched(body, picked, skipped):
    def inner(*refs):
        refs = list(refs)
        semaphores = refs.pop()
        blocks = refs[-len(picked) :]
        del refs[-len(picked) :]
        copies = []
        for place, index in enumerate(sorted(picked)):
            source = refs[skipped + index].at[pl.ds(picked[index], 1)]
            copy = pltpu.make_async_copy(source, blocks[place], semaphores.at[place])
            copy.start()
            copies.append(copy)
            refs[skipped + index] = blocks[place]
        for copy in copies:
            copy.wait()
        return body(*refs)

    return inner


REMOTE = pl.DeviceIdType.MESH


def remote(source, target, send, recv, peer):
    return pltpu.make_async_remote_copy(
        src_ref=source, dst_ref=target, send_sem=send, recv_sem=recv, device_id=peer, device_id_type=REMOTE
    )


def across(index, step):
    return (index, index + 1 - 2 * (index % 2), (index + 2) % 4, 3 - index)[step]


def greet(peers):
    barrier = pltpu.get_barrier_semaphore()
    for peer in peers:
        pl.semaphore_signal(barrier, inc=1, device_id=peer, device_id_type=REMOTE)
    pl.semaphore_wait(barrier, len(peers))


def call(body, name, outs, args, scalars=None, scratch=(), flops=0, after=(), collective=None, anywhere=(),
         out_anywhere=(), picks=()):
    specs = [pl.BlockSpec(memory_space=pl.ANY)] * len(after)
    specs += [pl.BlockSpec(memory_space=pltpu.SMEM)] if scalars is not None else []
    picked = dict(picks)
    specs += [
        pl.BlockSpec(memory_space=pl.ANY if index in anywhere or index in picked else pltpu.VMEM)
        for index in range(len(args))
    ]
    operands = list(after) + ([scalars] if scalars is not None else []) + list(args)
    moved = sum(a.size * a.dtype.itemsize for a in list(args) + list(outs))
    body = ordered(body, len(after))
    if picked:
        body = fetched(body, picked, int(scalars is not None))
        scratch = list(scratch) + [
            pltpu.VMEM((1, *args[index].shape[1:]), args[index].dtype) for index in sorted(picked)
        ] + [pltpu.SemaphoreType.DMA((len(picked),))]
    return pl.pallas_call(
        body,
        name=name,
        in_specs=specs,
        out_specs=[
            pl.BlockSpec(memory_space=pl.ANY if index in out_anywhere else pltpu.VMEM)
            for index in range(len(outs))
        ],
        out_shape=list(outs),
        scratch_shapes=list(scratch),
        compiler_params=pltpu.CompilerParams(
            vmem_limit_bytes=VMEM_LIMIT, collective_id=collective, has_side_effects=collective is not None
        ),
        cost_estimate=pl.CostEstimate(flops=flops, bytes_accessed=moved, transcendentals=0),
    )(*operands)


def shape(dims, dtype):
    return jax.ShapeDtypeStruct(tuple(dims), dtype)


def bucket_onehot(buckets, span, spacing):
    width = 2 * span * GROUP
    column = lax.broadcasted_iota(jnp.int32, (buckets, width), 1)
    delta = column // (2 * span)
    distance = column - delta * (2 * span) - span + span * delta
    bucket = jnp.where(distance >= 0, distance // spacing, -1)
    row = lax.broadcasted_iota(jnp.int32, (buckets, width), 0)
    return (bucket == row).astype(BF16)


def fill_bias(first_head, heads, table, vectors, bias, span, spacing):
    buckets, head_count = table.shape
    hot = bucket_onehot(buckets, span, spacing)
    rows = mm(table, hot, TN)
    column = lax.broadcasted_iota(jnp.int32, (1, 2 * span * GROUP), 1)
    rows = jnp.where(column < span, MASKED, rows)
    vectors[0:head_count, :] = rows
    for head in range(heads):
        picked = vectors[pl.ds(first_head + head, 1), :]
        for delta in range(GROUP):
            piece = picked[:, delta * 2 * span : (delta + 1) * 2 * span]
            spread = jnp.broadcast_to(piece, (span, 2 * span))
            rolled = pltpu.roll(spread, span, 1, stride=1, stride_axis=0)
            bias[head * GROUP + delta] = rolled[:, :span]


def attention_forward(sizes, ids, own, flip, side, side_flip, gain, weight, table,
                      out, mixed, gathered, stats, vectors, bias):
    span, heads, size, spacing, unused = sizes
    width = heads * size
    fill_bias(ids[4] * heads, heads, table[...], vectors, bias, span, spacing)
    for slot, piece in enumerate((own, flip, side, side_flip)):
        gathered[pl.ds(pl.multiple_of(ids[slot] * span, span), span), :] = piece[...]
    for part in range(GROUP):
        project(gathered, slice(part * span, (part + 1) * span), gain[...], weight[:, : 3 * width], mixed)
    for head in range(heads):
        attend_head(sizes, head, mixed, bias, out, stats)


def project(gathered, rows, gain, weight, mixed):
    values = gathered[rows, :].astype(F32)
    normed = (values * inverse_rms(values) * gain.astype(F32)).astype(BF16)
    mixed[rows, :] = mm(normed, weight).astype(BF16)


def attend_head(sizes, head, mixed, bias, out, stats):
    span, heads, size = sizes[:3]
    width = heads * size
    columns = slice(head * size, (head + 1) * size)
    query_t = (mixed[:, columns].astype(F32) * size ** (-0.5)).T.astype(BF16)
    key = mixed[:, width + head * size : width + (head + 1) * size]
    value_t = mixed[:, 2 * width + head * size : 2 * width + (head + 1) * size].astype(F32).T.astype(BF16)
    for part in range(GROUP):
        mine = slice(part * span, (part + 1) * span)
        blocks = []
        for other in range(part + 1):
            raw = mm(key[other * span : (other + 1) * span], query_t[:, mine])
            blocks.append(raw + bias[head * GROUP + part - other])
        top = functools.reduce(jnp.maximum, [jnp.max(b, axis=0, keepdims=True) for b in blocks])
        total = jnp.zeros_like(top)
        gained = jnp.zeros((size, span), F32)
        for other, block in enumerate(blocks):
            raised = jnp.exp(block - top)
            total = total + jnp.sum(raised, axis=0, keepdims=True)
            gained = gained + mm(value_t[:, other * span : (other + 1) * span], raised.astype(BF16))
        out[part, columns, :] = (gained / total).astype(BF16)
        stats[head : head + 1, mine] = top + jnp.log(total)


def route_masks(columns, experts):
    lane = lax.broadcasted_iota(jnp.int32, (columns[0].shape[0], experts), 1).astype(F32)
    return [(column == lane).astype(F32) for column in columns]


def route_columns(routes):
    return [routes[:, k : k + 1].astype(F32) for k in range(2)]


def slot_places(columns, masks, capacity):
    tokens = columns[0].shape[0]
    members = (masks[0] + masks[1]).astype(BF16)
    row = lax.broadcasted_iota(jnp.int32, (tokens, tokens), 0)
    column = lax.broadcasted_iota(jnp.int32, (tokens, tokens), 1)
    earlier = mm((row > column).astype(BF16), members)
    return [
        columns[k] * capacity + jnp.sum(earlier * masks[k], axis=1, keepdims=True) for k in range(2)
    ]


def dispatch(total, gain, router, masks, places, slots, outgoing, normed_two, aux):
    tokens = total.shape[0]
    normed = (total * inverse_rms(total) * gain.astype(F32)).astype(BF16)
    normed_two[...] = normed
    logits = mm(normed, router)
    chosen = [jnp.sum(logits * mask, axis=1, keepdims=True) for mask in masks]
    first = jax.nn.sigmoid(chosen[0] - chosen[1])
    lane = lax.broadcasted_iota(jnp.int32, (tokens, 128), 1)
    packed = jnp.zeros((tokens, 128), F32)
    for index, entry in enumerate((places[0], places[1], first, 1.0 - first)):
        packed = jnp.where(lane == index, entry, packed)
    aux[...] = packed
    packed_t = packed.T
    hot = fill_slots(packed_t, slots, 0) + fill_slots(packed_t, slots, 1)
    outgoing[...] = mm(hot, normed).astype(BF16)
    return packed


def pick_rows(slot, slots):
    lane = lax.broadcasted_iota(jnp.int32, (slot.shape[0], slots), 1).astype(F32)
    return (lane == slot).astype(BF16)


def fill_slots(aux_t, slots, k):
    row = lax.broadcasted_iota(jnp.int32, (slots, aux_t.shape[1]), 0).astype(F32)
    return (row == aux_t[k : k + 1, :]).astype(BF16)


def after_attention(capacity, attended, own, w_out, gain, router, routes,
                    outgoing, middle, normed_two, aux):
    experts = router.shape[1]
    width = attended.shape[1]
    total = own[...].astype(F32)
    for group in range(GROUP):
        total = total + mm(attended[group], w_out[group * width : (group + 1) * width, :], TN)
    middle[...] = total
    columns = route_columns(routes)
    masks = route_masks(columns, experts)
    places = slot_places(columns, masks, capacity)
    dispatch(total, gain[...], router[...], masks, places, experts * capacity, outgoing, normed_two, aux)


def expert_forward(rows, w_in, w_down, activation, slope, produced, total):
    step = pl.program_id(0)

    @pl.when(step == 0)
    def clear():
        total[...] = jnp.zeros_like(total)

    chunk = rows.shape[0] // 4
    for part in range(4):
        mine = slice(part * chunk, (part + 1) * chunk)
        hidden = mm(rows[mine, :], w_in[...])
        half = 0.5 * (1.0 + lax.erf(hidden * 0.7071067811865476))
        bell = jnp.exp(-0.5 * hidden * hidden) * 0.3989422804014327
        raised = (hidden * half).astype(BF16)
        activation[mine, :] = raised
        slope[mine, :] = (half + hidden * bell).astype(BF16)
        total[mine, :] += mm(raised, w_down[...])

    @pl.when(step == pl.num_programs(0) - 1)
    def finish():
        produced[...] = total[...].astype(BF16)


def expert_backward(arrived_grad, w_in, w_down, slope, hidden_grad, rows_grad, total):
    step = pl.program_id(0)

    @pl.when(step == 0)
    def clear():
        total[...] = jnp.zeros_like(total)

    chunk = arrived_grad.shape[0] // 4
    for part in range(4):
        mine = slice(part * chunk, (part + 1) * chunk)
        lifted = mm(arrived_grad[mine, :], w_down[...], NT) * slope[mine, :].astype(F32)
        lowered = lifted.astype(BF16)
        hidden_grad[mine, :] = lowered
        total[mine, :] += mm(lowered, w_in[...], NT)

    @pl.when(step == pl.num_programs(0) - 1)
    def finish():
        rows_grad[...] = total[...].astype(BF16)


def tile_of(hidden):
    return 768 if hidden % 768 == 0 else hidden


def run_expert_forward(rows, w_in, w_down):
    count, features = rows.shape
    hidden = w_in.shape[1]
    tile = tile_of(hidden)
    return pl.pallas_call(
        expert_forward,
        name="expert_forward",
        grid=(hidden // tile,),
        in_specs=[
            whole(rows),
            pl.BlockSpec((features, tile), lambda j: (0, j)),
            pl.BlockSpec((tile, features), lambda j: (j, 0)),
        ],
        out_specs=[
            pl.BlockSpec((count, tile), lambda j: (0, j)),
            pl.BlockSpec((count, tile), lambda j: (0, j)),
            pl.BlockSpec((count, features), lambda j: (0, 0)),
        ],
        out_shape=[shape((count, hidden), BF16), shape((count, hidden), BF16), shape((count, features), BF16)],
        scratch_shapes=[pltpu.VMEM((count, features), F32)],
        compiler_params=pltpu.CompilerParams(vmem_limit_bytes=VMEM_LIMIT),
        cost_estimate=pl.CostEstimate(
            flops=4 * count * features * hidden, bytes_accessed=30 << 20, transcendentals=2 * count * hidden
        ),
    )(rows, w_in, w_down)


def run_expert_backward(arrived_grad, w_in, w_down, slope):
    count, features = arrived_grad.shape
    hidden = w_in.shape[1]
    tile = tile_of(hidden)
    return pl.pallas_call(
        expert_backward,
        name="expert_backward",
        grid=(hidden // tile,),
        in_specs=[
            whole(arrived_grad),
            pl.BlockSpec((features, tile), lambda j: (0, j)),
            pl.BlockSpec((tile, features), lambda j: (j, 0)),
            pl.BlockSpec((count, tile), lambda j: (0, j)),
        ],
        out_specs=[
            pl.BlockSpec((count, tile), lambda j: (0, j)),
            pl.BlockSpec((count, features), lambda j: (0, 0)),
        ],
        out_shape=[shape((count, hidden), BF16), shape((count, features), BF16)],
        scratch_shapes=[pltpu.VMEM((count, features), F32)],
        compiler_params=pltpu.CompilerParams(vmem_limit_bytes=VMEM_LIMIT),
        cost_estimate=pl.CostEstimate(
            flops=4 * count * features * hidden, bytes_accessed=30 << 20, transcendentals=0
        ),
    )(arrived_grad, w_in, w_down, slope)


def weight_partials(scalars, rows, hidden_grad, activation, arrived_grad, grad_in, grad_down):
    @pl.when(scalars[0] == 1)
    def wanted():
        grad_in[...] = mm(rows[...], hidden_grad[...], TN).astype(BF16)
        grad_down[...] = mm(activation[...], arrived_grad[...], TN).astype(BF16)


def run_weight_partials(wanted, rows, hidden_grad, activation, arrived_grad):
    count, features = rows.shape
    hidden = hidden_grad.shape[1]
    tile = tile_of(hidden)
    return pl.pallas_call(
        weight_partials,
        name="weight_partials",
        grid_spec=pltpu.PrefetchScalarGridSpec(
            num_scalar_prefetch=1,
            grid=(hidden // tile,),
            in_specs=[
                pl.BlockSpec((count, features), lambda j, s: (0, 0)),
                pl.BlockSpec((count, tile), lambda j, s: (0, j * s[0])),
                pl.BlockSpec((count, tile), lambda j, s: (0, j * s[0])),
                pl.BlockSpec((count, features), lambda j, s: (0, 0)),
            ],
            out_specs=[
                pl.BlockSpec((features, tile), lambda j, s: (0, j * s[0])),
                pl.BlockSpec((tile, features), lambda j, s: (j * s[0], 0)),
            ],
        ),
        out_shape=[shape((features, hidden), BF16), shape((hidden, features), BF16)],
        compiler_params=pltpu.CompilerParams(vmem_limit_bytes=VMEM_LIMIT),
        cost_estimate=pl.CostEstimate(
            flops=4 * count * features * hidden, bytes_accessed=30 << 20, transcendentals=0
        ),
    )(wanted, rows, hidden_grad, activation, arrived_grad)


def weight_totals(scalars, left, right, sent, left_1, right_1, sent_1, after, total):
    @pl.when(scalars[0] == 0)
    def first():
        total[...] = mm(left[...], right[...], TN) + sent[...].astype(F32)

    @pl.when(scalars[0] == 1)
    def second():
        total[...] = mm(left_1[...], right_1[...], TN) + sent_1[...].astype(F32)


def run_weight_totals(core, first, second, tiled_left, after):
    count, features = first[1 if tiled_left else 0].shape
    hidden = first[0 if tiled_left else 1].shape[1]
    tile = tile_of(hidden)

    def specs(which):
        def step(j, s):
            return jnp.where(s[0] == which, j, 0)

        full = pl.BlockSpec((count, features), lambda j, s: (0, 0))
        part = pl.BlockSpec((count, tile), lambda j, s: (0, step(j, s)))
        if tiled_left:
            return [part, full, pl.BlockSpec((tile, features), lambda j, s: (step(j, s), 0))]
        return [full, part, pl.BlockSpec((features, tile), lambda j, s: (0, step(j, s)))]

    if tiled_left:
        out_spec = pl.BlockSpec((tile, features), lambda j, s: (j, 0))
        dims = (hidden, features)
    else:
        out_spec = pl.BlockSpec((features, tile), lambda j, s: (0, j))
        dims = (features, hidden)
    return pl.pallas_call(
        weight_totals,
        name="weight_totals",
        grid_spec=pltpu.PrefetchScalarGridSpec(
            num_scalar_prefetch=1, grid=(hidden // tile,),
            in_specs=specs(0) + specs(1) + [pl.BlockSpec(memory_space=pl.ANY)], out_specs=out_spec,
        ),
        out_shape=shape(dims, F32),
        compiler_params=pltpu.CompilerParams(vmem_limit_bytes=VMEM_LIMIT),
        cost_estimate=pl.CostEstimate(
            flops=2 * count * features * hidden, bytes_accessed=30 << 20, transcendentals=0
        ),
    )(core, *first, *second, after)


def combined(returned, packed, middle):
    slots = returned.shape[0]
    outs = [mm(pick_rows(packed[:, k : k + 1], slots), returned) for k in range(2)]
    return middle + packed[:, 2:3] * outs[0] + packed[:, 3:4] * outs[1], outs[0] - outs[1]


def combine(returned, aux, middle, result, difference):
    total, gap = combined(returned[...], aux[...], middle[...])
    result[...] = total.astype(BF16)
    difference[...] = gap


def spread_values(values, packed, slots):
    packed_t = packed.T
    total = jnp.zeros((slots, values.shape[1]), F32)
    for k in range(2):
        total = total + mm(fill_slots(packed_t, slots, k), (values * packed[:, 2 + k : 3 + k]).astype(BF16))
    return total.astype(BF16)


def spread_grads(upstream, aux, outgoing):
    outgoing[...] = spread_values(upstream[...].astype(F32), aux[...], outgoing.shape[0])


def norm_backward(values, gain, grad):
    scale = inverse_rms(values)
    unit = values * scale
    lifted = grad * gain
    back = scale * (lifted - unit * jnp.mean(lifted * unit, axis=-1, keepdims=True))
    return back, jnp.sum(grad * unit, axis=0, keepdims=True)


def publisher(grad_in, grad_down, out_in, out_down, held, wide, in_sem, out_sem):
    tile = held.shape[2]
    tiles = held.shape[0] // 2
    across_tiles = [(slice(None), pl.ds(index * tile, tile)) for index in range(tiles)]
    down_tiles = [pl.ds(index * tile, tile) for index in range(tiles)]
    places = [(grad_in.at[p], out_in.at[p]) for p in across_tiles]
    places += [(grad_down.at[p], out_down.at[p]) for p in down_tiles]
    fetches = [
        pltpu.make_async_copy(pair[0], held.at[index], in_sem.at[index]) for index, pair in enumerate(places)
    ]
    stores = [
        pltpu.make_async_copy(wide.at[index], pair[1], out_sem.at[index]) for index, pair in enumerate(places)
    ]
    for fetch in fetches:
        fetch.start()

    def publish(quarter):
        share = len(fetches) // 4
        for index in range(quarter * share, (quarter + 1) * share):
            fetches[index].wait()
            wide[index] = held[index].astype(F32)
            stores[index].start()

    return publish, stores


def token_backward(returned, packed, flow, difference, middle, normed_two, attended, gain, router, out_block,
                   columns, middle_grad, attended_grad, shared_grad, publish=None, stores=(), hook=None):
    slots, features = returned.shape
    experts = router.shape[1]
    width = attended.shape[1]

    publish = publish or (lambda quarter: None)
    hot = pick_rows(packed[:, 0:1], slots) + pick_rows(packed[:, 1:2], slots)
    token_grad = mm(hot, returned)
    publish(0)
    shift = jnp.sum(flow * difference, axis=1, keepdims=True) * packed[:, 2:3] * packed[:, 3:4]
    masks = route_masks(columns, experts)
    logits_grad = (shift * (masks[0] - masks[1])).astype(BF16)
    token_grad = token_grad + mm(logits_grad, router, NT)
    back, gain_part = norm_backward(middle, gain.astype(F32), token_grad)
    total = flow + back
    middle_grad[...] = total
    branch = total.astype(BF16)
    publish(1)
    for group in range(GROUP):
        attended_grad[group] = mm(out_block(group), branch, NT).astype(BF16)
    publish(2)
    if hook:
        hook()
    for group in range(GROUP):
        mine = slice(group * width, (group + 1) * width)
        shared_grad[mine, :features] = mm(attended[group], branch).astype(BF16)
    publish(3)
    tail = shared_grad.shape[1] - features
    gain_column = jnp.broadcast_to(gain_part, (8, features)).T
    lane = lax.broadcasted_iota(jnp.int32, (features, tail), 1)
    shared_grad[:, features:] = jnp.where(lane == experts, gain_column[:, 0:1], 0.0).astype(BF16)
    shared_grad[:, features : features + experts] = mm(normed_two, logits_grad, TN).astype(BF16)
    for store in stores:
        store.wait()


def before_attention(returned, aux, upstream, difference, middle, normed_two, attended, gain,
                     router, w_out, routes, middle_grad, attended_grad, shared_grad):
    width = attended.shape[1]
    token_backward(
        returned[...], aux[...], upstream[...].astype(F32), difference[...], middle[...], normed_two[...],
        attended, gain[...], router[...], lambda group: w_out[group * width : (group + 1) * width, :],
        route_columns(routes), middle_grad, attended_grad, shared_grad,
    )


def before_attention_fused(sizes, returned, aux, upstream, difference, middle, normed_two, attended,
                           early, w_outs, routes, grad_in, grad_down,
                           middle_grad, attended_grad, shared_grad, out_in, out_down, held, wide, in_sem, out_sem):
    publish, stores = publisher(grad_in, grad_down, out_in, out_down, held, wide, in_sem, out_sem)
    router, unused, gain_two, unused_1 = unpack_small(sizes, early, 0)
    token_backward(
        returned[...], aux[...], upstream[...].astype(F32), difference[...], middle[...], normed_two[...],
        attended, gain_two, router, lambda group: out_rows(sizes, w_outs, 0, group),
        route_columns(routes[0].T), middle_grad, attended_grad, shared_grad, publish, stores,
    )


def back_head(sizes, head, mixed, stats, attended, grads, bias, work):
    mixed_grad, sums, key_total, value_total, turned, strips = work
    span, heads, size, spacing = sizes[:4]
    width = heads * size
    count = span // spacing
    row = lax.broadcasted_iota(jnp.int32, (span, span), 0)
    column = lax.broadcasted_iota(jnp.int32, (span, span), 1)
    later = (column % spacing) >= (row % spacing)
    lane = lax.broadcasted_iota(jnp.int32, (span, 128), 0) // spacing
    backwards = (count - 1 - lane == lax.broadcasted_iota(jnp.int32, (span, 128), 1)).astype(F32)
    columns = slice(head * size, (head + 1) * size)
    key_columns = slice(width + head * size, width + (head + 1) * size)
    value_columns = slice(2 * width + head * size, 2 * width + (head + 1) * size)
    query = (mixed[:, columns].astype(F32) * size ** (-0.5)).astype(BF16)
    query_t = query.astype(F32).T.astype(BF16)
    key = mixed[:, key_columns]
    key_t = key.astype(F32).T.astype(BF16)
    value = mixed[:, value_columns]
    key_total[...] = jnp.zeros_like(key_total)
    value_total[...] = jnp.zeros_like(value_total)
    sums[...] = jnp.zeros_like(sums)
    for part in range(GROUP):
        mine = slice(part * span, (part + 1) * span)
        grad_t = grads[part, columns, :]
        delta_row = jnp.sum(
            grad_t.astype(F32) * attended[part, columns, :].astype(F32), axis=0, keepdims=True
        )
        level = stats[head : head + 1, mine]
        query_total = jnp.zeros((size, span), F32)
        for other in range(part + 1):
            theirs = slice(other * span, (other + 1) * span)
            raw = mm(key[theirs], query_t[:, mine])
            prob = jnp.exp(raw + (bias[head * GROUP + part - other] - level))
            prob_grad = mm(value[theirs], grad_t)
            low = (prob * (prob_grad - delta_row)).astype(BF16)
            sums[part - other] += low.astype(F32)
            query_total = query_total + mm(key_t[:, theirs], low)
            key_total[theirs, :] += mm(low, query[mine])
            value_total[theirs, :] += mm(prob.astype(BF16), grad_t, NT)
        turned[:, mine] = query_total * size ** (-0.5)
    mixed_grad[:, columns] = turned[...].T.astype(BF16)
    mixed_grad[:, key_columns] = key_total[...].astype(BF16)
    mixed_grad[:, value_columns] = value_total[...].astype(BF16)
    for delta in range(GROUP):
        upper = jnp.where(later, sums[delta], 0.0)
        for side, block in enumerate((upper, sums[delta] - upper)):
            tiles = lax.dot_general(
                jnp.sum(block.reshape(count, spacing, span), axis=1), backwards, NN,
                precision=lax.Precision.HIGHEST, preferred_element_type=F32,
            )
            turned_tiles = pltpu.roll(tiles, 0, 1, stride=1, stride_axis=0)
            place = (delta * 2 + side) * 128
            strips[head : head + 1, place : place + 128] = jnp.sum(turned_tiles, axis=0, keepdims=True)


def back_piece(sizes, gathered, rows, gain, weight, mixed_grad):
    values = gathered[rows, :].astype(F32)
    back = mm(mixed_grad[rows, :], weight, NT)
    return back, jnp.sum(back * values * inverse_rms(values), axis=0, keepdims=True)


def weight_share(sizes, gathered, gain, mixed_grad):
    span, heads, size = sizes[:3]
    total = jnp.zeros((gathered.shape[1], 3 * heads * size), F32)
    for part in range(GROUP):
        rows = slice(part * span, (part + 1) * span)
        values = gathered[rows, :].astype(F32)
        normed = (values * inverse_rms(values) * gain.astype(F32)).astype(BF16)
        total = total + mm(normed, mixed_grad[rows, :], TN)
    return total


def extra_columns(sizes, buckets, features, strips, gain_total):
    span, heads, size, spacing, ranks = sizes
    count = span // spacing
    entry = lax.broadcasted_iota(jnp.int32, (GROUP * 2 * 128, 128), 0)
    bucket = (entry // 256) * count + count - 1 - entry % 128 - (entry // 128) % 2
    hot = (bucket == lax.broadcasted_iota(jnp.int32, (GROUP * 2 * 128, 128), 1)) & (entry % 128 < 2 * count)
    table_rows = lax.dot_general(
        strips[...], hot.astype(F32), NN, precision=lax.Precision.HIGHEST, preferred_element_type=F32
    )
    owned = buckets // ranks
    bucket = lax.broadcasted_iota(jnp.int32, (128, features), 0)
    target = (bucket // owned) * (features // ranks) + bucket % owned
    spot = (target == lax.broadcasted_iota(jnp.int32, (128, features), 1)) & (bucket < buckets)
    placed = lax.dot_general(
        table_rows, spot.astype(F32), NN, precision=lax.Precision.HIGHEST, preferred_element_type=F32
    )
    extra = jnp.concatenate([placed, jnp.broadcast_to(gain_total, (8, features))], axis=0)
    return extra.T.astype(BF16)


def attention_backward(sizes, ids, mixed, stats, attended, grads, gathered, gain, weight, table,
                       stay, leave, sent, shared_grad, vectors, bias, *work):
    span, heads, size, spacing, ranks = sizes
    width = heads * size
    mixed_grad, strips = work[0], work[5]
    strips[...] = jnp.zeros_like(strips)
    fill_bias(ids[4] * heads, heads, table[...], vectors, bias, span, spacing)
    for head in range(heads):
        back_head(sizes, head, mixed, stats, attended, grads, bias, work)
    gain_total = 0.0
    for part in range(GROUP):
        rows = pl.ds(pl.multiple_of(ids[5 + part] * span, span), span)
        back, gain_part = back_piece(sizes, gathered, rows, gain[...], weight[:, : 3 * width], mixed_grad)
        gain_total = gain_total + gain_part
        if part == 0:
            stay[...] = back.astype(BF16)
        elif part == 1:
            leave[...] = back.astype(BF16)
        else:
            sent[part - 2] = back.astype(BF16)
    shared_grad[...] = jnp.zeros_like(shared_grad)
    shared_grad[:, : 3 * width] = weight_share(sizes, gathered, gain[...], mixed_grad).astype(BF16)
    shared_grad[:, 3 * width : 3 * width + 16] = extra_columns(
        sizes, table.shape[0], weight.shape[0], strips, gain_total
    )


def first_norm_grad(stay, partner, arrived, own, gain, middle_grad, low):
    grad = stay[...].astype(F32) + partner[0].astype(F32) + arrived[...].astype(F32)
    back, unused = norm_backward(own[...].astype(F32), gain[...].astype(F32), grad)
    low[...] = (middle_grad[...] + back).astype(BF16)


FLIP = [(0, 1), (1, 0)]


def flip(block):
    return lax.ppermute(block, SECTION, FLIP)


def beside(block):
    return lax.ppermute(block, ZLO, FLIP)


def scatter_pairs(turn):
    return [
        (core * 4 + a * 2 + b, b * 4 + (core ^ turn) * 2 + a)
        for core in range(2)
        for a in range(2)
        for b in range(2)
    ]


def to_working(block, turn):
    return lax.ppermute(block, (SECTION, ZHI, ZLO), scatter_pairs(turn))


def to_home(block, section, batch):
    turn = section ^ batch
    pairs = [(after, before) for before, after in scatter_pairs(turn) if before // 4 == section]
    return lax.ppermute(block, (SECTION, ZHI, ZLO), pairs)


def home_pair(blocks, core):
    return jnp.stack([
        jnp.where(core == 0, to_home(blocks[0], 0, batch), to_home(blocks[1], 1, batch))
        for batch in range(2)
    ])


def exchange(block, experts, capacity):
    features = block.shape[-1]
    moved = lax.all_to_all(
        block.reshape(experts, capacity, features), RANKS, split_axis=0, concat_axis=0, tiled=True
    )
    return moved.reshape(experts * capacity, features)


def spread_sum(block, axes, parts):
    rows, columns = block.shape
    moved = lax.all_to_all(
        block.reshape(parts, rows // parts, columns), axes, split_axis=0, concat_axis=0, tiled=True
    )
    return jnp.sum(moved.astype(F32), axis=0)


def regroup(block):
    return lax.all_to_all(block, (ZLO, SECTION), split_axis=0, concat_axis=0, tiled=True)


OFFSETS = [(step, place) for place in (0, 3, 1, 2) for step in range(4)]
SENDS = (12, 13, 14, 15, 4, 5, 6, 7, 8, 9, 10, 11, 1, 2, 3)
BATCH = 4
BATCH_ORDER = (0, 3, 2, 1)


def expert_layer(mode, section, *refs):
    forward = mode != BACKWARD
    backward = mode != FORWARD
    refs = list(refs)

    def take(count):
        taken = refs[:count]
        del refs[:count]
        return taken

    weights = take(4)
    outgoing = take(2 if mode == BOTH else 1)
    if mode == BACKWARD:
        saved_rows, saved_activation, saved_slope, unused, unused_1 = take(5)
    returned = take(len(outgoing))
    if mode == FORWARD:
        kept_rows, kept_activation, kept_slope = take(3)
    else:
        grad_in, grad_down = take(2)
    arrived = take(len(outgoing))
    finished = take(len(outgoing))
    w_in, w_down, activation, slope, totals = take(5)
    send_sem, recv_sem, back_send, back_recv, load_sem = take(5)
    if backward:
        parts, staged, part_send, part_recv, out_sem = take(5)

    core = lax.axis_index(SECTION)
    expert = lax.axis_index(EXPERT)
    place = 2 * lax.axis_index(ZHI) + lax.axis_index(ZLO)
    me = expert * 4 + place
    hidden = w_in.shape[1]
    slot_rows, features = arrived[0].shape[1:]
    rows_in_batch = BATCH * slot_rows
    tile = tile_of(hidden)
    tiles = hidden // tile
    peers = []
    ranks = []
    for step, move in OFFSETS:
        to_expert, to_place = across(expert, step), across(place, move)
        ranks.append(to_expert * 4 + to_place)
        peers.append(dict(expert=to_expert, zhi=to_place // 2, zlo=to_place % 2))

    loads = []

    def load(source, target, index):
        copy = pltpu.make_async_copy(source, target, load_sem.at[index])
        copy.start()
        loads.append(copy)

    @pl.when(core == section)
    def own_weights():
        pltpu.make_async_copy(weights[0], w_in, load_sem.at[0]).start()
        pltpu.make_async_copy(weights[1], w_down, load_sem.at[1]).start()

    @pl.when(core != section)
    def other_weights():
        pltpu.make_async_copy(weights[2], w_in, load_sem.at[0]).start()
        pltpu.make_async_copy(weights[3], w_down, load_sem.at[1]).start()

    if mode == BACKWARD:
        load(saved_activation, activation, 2)
        load(saved_slope, slope, 3)

    greet(peers[1:] + ([dict(section=1 - core)] if backward else []))

    sent = []
    for slot in SENDS:
        for kind, block in enumerate(outgoing):
            copy = remote(block.at[ranks[slot]], arrived[kind].at[slot], send_sem.at[kind, slot],
                          recv_sem.at[kind, slot], peers[slot])
            copy.start()
            sent.append(copy)
    for kind, block in enumerate(outgoing):
        arrived[kind][0] = block[me]

    pltpu.make_async_copy(weights[0], w_in, load_sem.at[0]).wait()
    pltpu.make_async_copy(weights[1], w_down, load_sem.at[1]).wait()
    for copy in loads:
        copy.wait()

    saves = []
    for batch in BATCH_ORDER:
        slots = range(batch * BATCH, (batch + 1) * BATCH)
        mine = slice(batch * rows_in_batch, (batch + 1) * rows_in_batch)
        for slot in slots:
            for kind in range(len(outgoing)):
                if slot:
                    remote(arrived[kind].at[slot], arrived[kind].at[slot], send_sem.at[kind, slot],
                           recv_sem.at[kind, slot], peers[slot]).wait_recv()

        def block_of(kind):
            return arrived[kind][slots[0] : slots[-1] + 1].reshape(rows_in_batch, features)

        def one_tile(index, unused):
            spot = pl.ds(pl.multiple_of(index * tile, tile), tile)
            if forward:
                values = mm(block_of(0), w_in[:, spot])
                half = 0.5 * (1.0 + lax.erf(values * 0.7071067811865476))
                bell = jnp.exp(-0.5 * values * values) * 0.3989422804014327
                raised = (values * half).astype(BF16)
                steep = half + values * bell
                activation[mine, spot] = raised
                if mode == FORWARD:
                    slope[mine, spot] = steep.astype(BF16)
                totals[0] += mm(raised, w_down[spot, :])
            else:
                steep = slope[mine, spot].astype(F32)
            if backward:
                lowered = (mm(block_of(len(outgoing) - 1), w_down[spot, :], NT) * steep).astype(BF16)
                slope[mine, spot] = lowered
                totals[len(outgoing) - 1] += mm(lowered, w_in[:, spot], NT)
            return unused

        totals[...] = jnp.zeros_like(totals)
        lax.fori_loop(0, tiles, one_tile, 0)
        for kind in range(len(outgoing)):
            finished[kind][slots[0] : slots[-1] + 1] = (
                totals[kind].astype(BF16).reshape(BATCH, slot_rows, features)
            )
        for slot in slots:
            for kind in range(len(outgoing)):
                if slot:
                    copy = remote(finished[kind].at[slot], returned[kind].at[me], back_send.at[kind, slot],
                                  back_recv.at[kind, slot], peers[slot])
                    copy.start()
                    sent.append(copy)
                else:
                    returned[kind][me] = finished[kind][0]
        if mode == FORWARD:
            for index, (source, target) in enumerate(((activation, kept_activation), (slope, kept_slope))):
                copy = pltpu.make_async_copy(
                    source.at[mine, :], target.at[mine, :], load_sem.at[2 + 2 * batch + index]
                )
                copy.start()
                saves.append(copy)
    if mode == FORWARD:
        kept_rows[...] = arrived[0][...]

    if backward:
        count = slot_rows * len(OFFSETS)
        grads = arrived[len(outgoing) - 1]
        inputs = arrived[0] if forward else saved_rows
        partner = dict(section=1 - core)

        def share_copy(index):
            return remote(parts.at[index], parts.at[index], part_send.at[index], part_recv.at[index], partner)

        def out_copy(step, kind):
            spot = pl.ds(pl.multiple_of(step * tile, tile), tile)
            target = grad_down.at[spot, :] if kind else grad_in.at[:, spot]
            return pltpu.make_async_copy(staged.at[kind], target, out_sem.at[2 * step + kind])

        def one_step(step, unused):
            spot = pl.ds(pl.multiple_of(step * tile, tile), tile)
            for kind in range(2):
                index = 2 * step + kind
                if kind:
                    value = mm(activation[:, spot], grads[...].reshape(count, features), TN)
                else:
                    value = mm(inputs[...].reshape(count, features), slope[:, spot], TN)

                @pl.when(core != section)
                def give():
                    parts[index] = value.astype(BF16)
                    share_copy(index).start()

                @pl.when(core == section)
                def keep():
                    share_copy(index).wait_recv()

                    @pl.when(step >= 1)
                    def drained():
                        out_copy(step - 1, kind).wait()

                    staged[kind] = (value + parts[index].astype(F32)).astype(BF16)
                    out_copy(step, kind).start()
            return unused

        lax.fori_loop(0, tiles, one_step, 0)

    for slot in range(1, len(OFFSETS)):
        for kind in range(len(outgoing)):
            remote(finished[kind].at[slot], returned[kind].at[ranks[slot]], back_send.at[kind, slot],
                   back_recv.at[kind, slot], peers[slot]).wait_recv()
    for copy in sent:
        copy.wait_send()
    for copy in saves:
        copy.wait()
    if backward:
        @pl.when(core != section)
        def given():
            for index in range(2 * tiles):
                share_copy(index).wait_send()

        @pl.when(core == section)
        def stored():
            for kind in range(2):
                out_copy(tiles - 1, kind).wait()


def run_expert_layer(mode, section, weights, outgoing, saved=(), grads=()):
    ranks, slot_rows, features = outgoing[0].shape
    hidden = weights[0].shape[1]
    count = ranks * slot_rows
    tile = tile_of(hidden)
    kinds = len(outgoing)
    anywhere = pl.BlockSpec(memory_space=pl.ANY)
    local = pl.BlockSpec(memory_space=pltpu.VMEM)
    block = shape((ranks, slot_rows, features), BF16)
    wide = shape((count, hidden), BF16)
    in_specs = [anywhere] * 4 + [local] * kinds
    operands = [*weights, *outgoing]
    out_shape = [block] * kinds
    out_specs = [local] * kinds
    aliases = {}
    if mode == FORWARD:
        out_shape += [block, wide, wide]
        out_specs += [local, anywhere, anywhere]
    else:
        out_shape += [shape((features, hidden), BF16), shape((hidden, features), BF16)]
        out_specs += [anywhere, anywhere]
    if mode == BACKWARD:
        aliases = {len(operands) + 3: kinds, len(operands) + 4: kinds + 1}
        operands += [*saved, *grads]
        in_specs += [local, anywhere, anywhere, anywhere, anywhere]
    scratch = [pltpu.VMEM(block.shape, BF16)] * (2 * kinds) + [
        pltpu.VMEM((features, hidden), BF16), pltpu.VMEM((hidden, features), BF16),
        pltpu.VMEM((count, hidden), BF16), pltpu.VMEM((count, hidden), BF16),
        pltpu.VMEM((kinds, BATCH * slot_rows, features), F32),
        pltpu.SemaphoreType.DMA((kinds, ranks)), pltpu.SemaphoreType.DMA((kinds, ranks)),
        pltpu.SemaphoreType.DMA((kinds, ranks)), pltpu.SemaphoreType.DMA((kinds, ranks)),
        pltpu.SemaphoreType.DMA((10,)),
    ]
    if mode != FORWARD:
        pieces = 2 * hidden // tile
        scratch += [
            pltpu.VMEM((pieces, features, tile), BF16), pltpu.VMEM((2, features, tile), BF16),
            pltpu.SemaphoreType.DMA((pieces,)), pltpu.SemaphoreType.DMA((pieces,)),
            pltpu.SemaphoreType.DMA((pieces,)),
        ]
    return pl.pallas_call(
        functools.partial(expert_layer, mode, section),
        name="expert_layer_" + mode,
        in_specs=in_specs,
        out_specs=out_specs,
        out_shape=out_shape,
        scratch_shapes=scratch,
        input_output_aliases=aliases,
        compiler_params=pltpu.CompilerParams(
            collective_id={FORWARD: 1, BOTH: 2, BACKWARD: 3}[mode], has_side_effects=True,
            vmem_limit_bytes=VMEM_LIMIT,
        ),
        cost_estimate=pl.CostEstimate(
            flops=8 * kinds * count * features * hidden, bytes_accessed=160 << 20, transcendentals=0
        ),
    )(*operands)


class Sizes:
    def __init__(self, **sizes):
        self.__dict__.update(sizes)
        self.width = self.heads * self.size
        self.length = GROUP * self.span
        self.slots = self.experts * self.capacity
        self.attention = (self.span, self.heads, self.size, self.spacing, self.ranks)
        self.base = 3 * self.width // 128 * 128
        self.offset = 3 * self.width - self.base
        self.table_lane = self.offset + self.experts + 2


def unpack_small(sizes, early, section):
    tail = early[section, :, :, sizes.base :]
    tail = tail.reshape(sizes.features, tail.shape[2])
    tail_t = tail.astype(F32).T
    first = sizes.offset + sizes.experts
    bucket = lax.broadcasted_iota(jnp.int32, (sizes.buckets, sizes.features), 0)
    target = bucket // sizes.table_rows * sizes.shard_rows + bucket % sizes.table_rows
    spot = target == lax.broadcasted_iota(jnp.int32, (sizes.buckets, sizes.features), 1)
    table = mm(spot.astype(BF16), tail).astype(BF16)
    router = tail[:, sizes.offset : first]
    return router, tail_t[first : first + 1, :], tail_t[first + 1 : first + 2, :], table


def qkv_columns(sizes, early, section):
    return early[section, :, :, : 3 * sizes.width].reshape(sizes.features, 3 * sizes.width)


def out_rows(sizes, w_outs, section, group):
    per_group = sizes.ranks // GROUP
    rows = w_outs[section, group * per_group : (group + 1) * per_group]
    return rows.reshape(sizes.width, sizes.features)


def whereabouts():
    core, zhi, zlo = (lax.axis_index(name) for name in (SECTION, ZHI, ZLO))
    return core, zhi, zlo, 2 * zhi + zlo, 2 * zlo + core


def line_peers(core, place):
    peers = []
    for move in range(4):
        spot = across(place, move)
        for turn in range(2):
            if move or turn:
                peers.append(dict(section=1 - core if turn else core, zhi=spot // 2, zlo=spot % 2))
    return peers


class Regroup:
    def __init__(self, block, target, send, recv):
        self.block, self.target, self.send, self.recv = block, target, send, recv
        self.core, unused, self.zlo, unused_1, self.mine = whereabouts()
        self.copies = []

    def start(self, rows):
        for turn, move in ((0, 1), (1, 1), (1, 0)):
            to_core = 1 - self.core if turn else self.core
            to_zlo = 1 - self.zlo if move else self.zlo
            index = len(self.copies)
            copy = remote(self.block.at[2 * to_zlo + to_core, rows], self.target.at[self.mine, rows],
                          self.send.at[index], self.recv.at[index], dict(section=to_core, zlo=to_zlo))
            copy.start()
            self.copies.append(copy)
        self.target[self.mine, rows] = self.block[self.mine, rows]

    def wait(self):
        for copy in self.copies:
            copy.wait()


class WeightGather:
    def __init__(self, blocks, shard, early, w_outs, staged, sems):
        (self.early_send, self.early_recv, self.stage_send, self.stage_recv, self.local_sem,
         self.out_send, self.out_recv) = sems
        self.blocks, self.shard, self.early, self.w_outs, self.staged = blocks, shard, early, w_outs, staged
        self.core, unused, self.zlo, self.place, unused_1 = whereabouts()
        self.other = 1 - self.core
        self.expert = lax.axis_index(EXPERT)
        self.beside_x = across(self.expert, 1)
        self.beside_y = across(self.expert, 2)
        self.places = [across(self.place, move) for move in range(4)]
        self.sections = (self.core, self.other)
        self.started = []
        self.early_count = self.out_count = 0

    def at(self, section, owner, spot):
        return self.early.at[section, owner * 4 + spot]

    def send(self, source, section, owner, spot, peer):
        copy = remote(source, self.at(section, owner, spot), self.early_send.at[self.early_count],
                      self.early_recv.at[section, owner * 4 + spot], peer)
        self.early_count += 1
        copy.start()
        self.started.append(copy)

    def arrived(self, section, owner, spot):
        block = self.at(section, owner, spot)
        remote(block, block, self.early_send.at[0], self.early_recv.at[section, owner * 4 + spot],
               dict(section=self.other)).wait_recv()

    def out_at(self, section, owner, spot):
        return self.w_outs.at[section, owner * 4 + spot]

    def send_out(self, source, owner, spot, peer):
        copy = remote(source, self.out_at(self.core, owner, spot), self.out_send.at[self.out_count],
                      self.out_recv.at[self.core, owner * 4 + spot], peer)
        self.out_count += 1
        copy.start()
        self.started.append(copy)

    def out_arrived(self, section, owner, spot):
        block = self.out_at(section, owner, spot)
        remote(block, block, self.out_send.at[0], self.out_recv.at[section, owner * 4 + spot],
               dict(section=self.other)).wait_recv()

    def trade(self):
        self.trades = []
        for parity in range(2):
            copy = remote(self.blocks.at[2 * parity + self.other], self.staged.at[parity],
                          self.stage_send.at[parity], self.stage_recv.at[parity], dict(section=self.other))
            copy.start()
            self.trades.append(copy)

    def start(self):
        for which, section in enumerate(self.sections):
            if which:
                for copy in self.trades:
                    copy.wait()

            def block_for(parity):
                return self.staged.at[parity] if which else self.blocks.at[2 * parity + self.core]

            for spot in self.places[1:]:
                self.send(block_for(spot % 2), section, self.expert, self.place,
                          dict(zhi=spot // 2, zlo=spot % 2))
            for peer in (self.beside_x, self.beside_y):
                self.send(block_for(self.zlo), section, self.expert, self.place, dict(expert=peer))
            local = pltpu.make_async_copy(
                block_for(self.zlo), self.at(section, self.expert, self.place), self.local_sem
            )
            local.start()
            local.wait()

    def along_z(self):
        for spot in self.places[1:]:
            for section in self.sections:
                self.arrived(section, self.expert, spot)
                for peer in (self.beside_x, self.beside_y):
                    self.send(self.at(section, self.expert, spot), section, self.expert, spot, dict(expert=peer))

    def over_plane(self):
        for section in self.sections:
            for step, spot in enumerate(self.places):
                self.arrived(section, self.beside_x, spot)
                self.arrived(section, self.beside_y, spot)
                source, peer = ((self.beside_x, self.beside_y), (self.beside_y, self.beside_x))[step % 2]
                self.send(self.at(section, source, spot), section, source, spot, dict(expert=peer))

    def finish_early(self):
        diagonal = 3 - self.expert
        for section in self.sections:
            for spot in self.places:
                self.arrived(section, diagonal, spot)

    def out_start(self):
        for spot in self.places[1:]:
            self.send_out(self.shard, self.expert, self.place, dict(zhi=spot // 2, zlo=spot % 2))
        for peer in (self.beside_x, self.beside_y):
            self.send_out(self.shard, self.expert, self.place, dict(expert=peer))
        self.send_out(self.shard, self.expert, self.place, dict(section=self.other))
        local = pltpu.make_async_copy(
            self.shard, self.out_at(self.core, self.expert, self.place), self.local_sem
        )
        local.start()
        local.wait()

    def out_pass(self, owner, spot, peers):
        block = self.out_at(self.core, owner, spot)
        self.out_arrived(self.core, owner, spot)
        for peer in peers + [dict(section=self.other)]:
            self.send_out(block, owner, spot, peer)

    def out_along_z(self):
        for spot in self.places[1:]:
            self.out_pass(self.expert, spot, [dict(expert=self.beside_x), dict(expert=self.beside_y)])

    def out_over_plane(self):
        for step, spot in enumerate(self.places):
            self.out_pass(self.beside_x, spot, [dict(expert=self.beside_y)] if step % 2 == 0 else [])
            self.out_pass(self.beside_y, spot, [dict(expert=self.beside_x)] if step % 2 else [])

    def out_finish(self):
        for spot in self.places:
            self.out_pass(3 - self.expert, spot, [])

    def out_all(self):
        for owner in range(4):
            for spot in range(4):
                self.out_arrived(self.other, owner, spot)

    def close(self):
        for copy in self.started:
            copy.wait_send()


def assemble(sizes, route_rows, qkv_shard, router_shard, gain_shard, table_shard, blocks, home_routes):
    rows, features, width = sizes.shard_rows, sizes.features, sizes.width

    def below(block, count):
        return jnp.concatenate([block, jnp.zeros((count - block.shape[0], block.shape[1]), F32)], axis=0)

    small = [
        router_shard[...].astype(F32), below(gain_shard[...].astype(F32), 8).T[:, :2],
        below(table_shard[...].astype(F32), rows),
    ]
    spare = blocks.shape[2] - 3 * width - sum(part.shape[1] for part in small)
    small.append(jnp.zeros((rows, spare), F32))
    for member in range(GROUP):
        parts = [
            qkv_shard[:, part * features + member * width : part * features + (member + 1) * width].astype(F32)
            for part in range(3)
        ]
        blocks[member] = jnp.concatenate(parts + small, axis=1).astype(BF16)
    for batch in range(2):
        wide = jnp.concatenate(
            [route_rows[batch].astype(F32), jnp.zeros((sizes.span, 126), F32)], axis=1
        )
        home_routes[batch] = wide.T[:8, :]


def attend(section, sizes, *refs):
    refs = list(refs)

    def take(count):
        taken = refs[:count]
        del refs[:count]
        return taken

    if section == 0:
        home_inputs, route_rows, qkv_shard, shard, router_shard, gain_shard, table_shard = take(7)
    else:
        returned, aux_before, middle_before, early, w_outs, routes, given = take(7)
    outcome, mixed, gathered, stats, outgoing, middle, normed_two, aux, attended = take(9)
    if section == 0:
        early, w_outs, routes = take(3)
    else:
        result, difference, spread = take(3)
    vectors, bias, pair_send, pair_recv, group_send, group_recv = take(6)
    span = sizes.span
    core, zhi, zlo, place, group = whereabouts()
    expert = lax.axis_index(EXPERT)

    def rows_of(piece):
        return pl.ds(pl.multiple_of(piece * span, span), span)

    if section == 0:
        blocks, home_routes = refs[-2:]
        assemble(sizes, route_rows, qkv_shard, router_shard, gain_shard, table_shard, blocks, home_routes)
    own, flipped = group, 2 * zlo + 1 - core
    side, side_flipped = 2 * (1 - zlo) + core, 2 * (1 - zlo) + 1 - core
    partner, beside_z = dict(section=1 - core), dict(zlo=1 - zlo)
    greet(line_peers(core, place)
          + ([dict(expert=across(expert, 1)), dict(expert=across(expert, 2))] if section == 0 else []))

    pair_copies = []

    def pass_piece(piece, index, peer):
        block = gathered.at[rows_of(piece)]
        copy = remote(block, block, pair_send.at[index], pair_recv.at[index], peer)
        copy.start()
        pair_copies.append(copy)

    def await_piece(piece, index):
        block = gathered.at[rows_of(piece)]
        remote(block, block, pair_send.at[index], pair_recv.at[index], partner).wait_recv()

    if section == 0:
        staged, home_send, home_recv = take(3)
        home_rows = home_inputs.at[core]
        gather = WeightGather(blocks, shard, early, w_outs, staged, take(7))
        gather.trade()
        aligned = (zlo == zhi) & (zlo == core)

        def to_work(source, target, index, slot, turn):
            peer = dict(section=zlo, zhi=1 - core if turn else core, zlo=zhi)
            return remote(source, target, home_send.at[index], home_recv.at[slot], peer)

        rows_copy = to_work(home_rows, gathered.at[rows_of(place)], 0, 0, 0)
        route_copies = [
            to_work(home_routes.at[1 - core if turn else core], routes.at[core], 1 + turn, 1 + core, turn)
            for turn in range(2)
        ]

        @pl.when(aligned)
        def keep():
            gathered[rows_of(place), :] = home_inputs[core]
            routes[core] = home_routes[core]

        @pl.when(jnp.logical_not(aligned))
        def give():
            rows_copy.start()
            route_copies[0].start()

        route_copies[1].start()
        gather.start()

        @pl.when(jnp.logical_not(aligned))
        def landed():
            rows_copy.wait_recv()

        pass_piece(own, 0, beside_z)
        pass_piece(own, 1, partner)
        gather.along_z()
        gather.over_plane()
        gather.out_start()
        await_piece(side, 0)
        pass_piece(side, 2, partner)
        gather.finish_early()
    else:
        total, gap = combined(returned[...], aux_before[...], middle_before[...])
        result[...] = total.astype(BF16)
        gathered[rows_of(own), :] = total.astype(BF16)
        difference[...] = gap
        pass_piece(own, 0, beside_z)
        pass_piece(own, 1, partner)

    router, gain_one, gain_two, table = unpack_small(sizes, early, section)
    fill_bias(group * sizes.heads + sizes.table_lane, sizes.heads, table, vectors, bias, span, sizes.spacing)
    weight = qkv_columns(sizes, early, section)
    project(gathered, rows_of(own), gain_one, weight, mixed)
    await_piece(flipped, 1)
    project(gathered, rows_of(flipped), gain_one, weight, mixed)
    if section:
        await_piece(side, 0)
        pass_piece(side, 2, partner)
    project(gathered, rows_of(side), gain_one, weight, mixed)
    await_piece(side_flipped, 2)
    project(gathered, rows_of(side_flipped), gain_one, weight, mixed)
    trade = Regroup(outcome, attended, group_send, group_recv)
    for head in range(sizes.heads):
        if section == 0 and head < 3:
            (gather.out_along_z, gather.out_over_plane, gather.out_finish)[head]()
        attend_head(sizes.attention, head, mixed, bias, outcome, stats)
        trade.start(slice(head * sizes.size, (head + 1) * sizes.size))
    if section == 0:
        for stage in (gather.out_along_z, gather.out_over_plane, gather.out_finish)[sizes.heads :]:
            stage()
        for which in range(2):
            @pl.when(jnp.logical_not(aligned & (core == which)))
            def routed():
                remote(routes.at[which], routes.at[which], home_send.at[1], home_recv.at[1 + which],
                       partner).wait_recv()
    columns_t = routes[section].T
    columns = [columns_t[:, k : k + 1] for k in range(2)]
    masks = route_masks(columns, sizes.experts)
    places = slot_places(columns, masks, sizes.capacity)
    if section == 0:
        gather.out_all()
    total = gathered[rows_of(own), :].astype(F32)
    trade.wait()
    for member in range(GROUP):
        total = total + mm(attended[member], out_rows(sizes, w_outs, section, member), TN)
    middle[...] = total
    packed = dispatch(total, gain_two, router, masks, places, sizes.slots, outgoing, normed_two, aux)
    if section:
        spread[...] = spread_values(given[...].astype(F32), packed, sizes.slots)
    for copy in pair_copies:
        copy.wait_send()
    if section == 0:
        gather.close()

        @pl.when(jnp.logical_not(aligned))
        def given_away():
            rows_copy.wait_send()
            route_copies[0].wait_send()

        route_copies[1].wait_send()


def run_attend(section, sizes, operands, collective):
    dma = pltpu.SemaphoreType.DMA
    span, features, width = sizes.span, sizes.features, sizes.width
    outs = [
        shape((GROUP, width, span), BF16), shape((sizes.length, 3 * width), BF16),
        shape((sizes.length, features), BF16), shape((8, sizes.length), F32),
        shape((sizes.slots, features), BF16), shape((span, features), F32), shape((span, features), BF16),
        shape((span, 128), F32), shape((GROUP, width, span), BF16),
    ]
    scratch = [
        pltpu.VMEM((128, 2 * span * GROUP), F32), pltpu.VMEM((sizes.heads * GROUP, span, span), F32),
        dma((3,)), dma((3,)), dma((3 * sizes.heads,)), dma((3 * sizes.heads,)),
    ]
    if section == 0:
        rows = sizes.shard_rows
        columns = -(-(3 * width + sizes.experts + 2 + sizes.heads * GROUP) // 128) * 128
        outs += [
            shape((2, sizes.ranks, rows, columns), BF16), shape((2, sizes.ranks, rows, features), BF16),
            shape((2, 8, span), F32),
        ]
        scratch += [
            pltpu.VMEM((2, rows, columns), BF16), dma((3,)), dma((3,)),
            dma((30,)), dma((2, sizes.ranks)), dma((2,)), dma((2,)), dma, dma((34,)), dma((2, sizes.ranks)),
            pltpu.VMEM((GROUP, rows, columns), BF16), pltpu.VMEM((2, 8, span), F32),
        ]
    else:
        outs += [shape((span, features), BF16), shape((span, features), F32), shape((sizes.slots, features), BF16)]
    return call(
        functools.partial(attend, section, sizes), "attend", outs, operands, scratch=scratch,
        flops=6 << 30, collective=collective,
    )


def unpack(sizes, home, owned, shared, outputs, section_outputs, stream_grads, grad_qkv, grad_out, grad_router, grad_gains, grad_table):
    width, features, experts = sizes.width, sizes.features, sizes.experts
    section_outputs[...] = outputs[...]
    stream_grads[...] = home[...].astype(F32)
    grad_qkv[...] = jnp.concatenate(
        [owned[member, :, part * width : (part + 1) * width] for part in range(3) for member in range(GROUP)],
        axis=1,
    )
    grad_out[...] = shared[:, :features]
    tail = shared[:, features:]
    grad_router[...] = tail[:, :experts]
    ends = [owned[member, :, sizes.base :] for member in range(GROUP)]
    grad_table[...] = jnp.concatenate(
        [end[: sizes.table_rows, sizes.offset : sizes.offset + sizes.heads] for end in ends], axis=1
    )
    spot = sizes.offset + 8
    grad_gains[0:1, :] = (ends[0] + ends[1] + ends[2] + ends[3]).T[spot : spot + 1, :]
    grad_gains[1:2, :] = tail.T[experts : experts + 1, :]


class Homes:
    def __init__(self, home, send, recv):
        self.home, self.send_sem, self.recv_sem = home, send, recv
        self.core, self.zhi, self.zlo, unused, unused_1 = whereabouts()
        self.aligned = (self.zlo == self.zhi) & (self.zlo == self.core)
        self.sent = []

    def copy(self, block, section, index):
        return remote(block, self.home.at[self.zhi], self.send_sem.at[index], self.recv_sem.at[self.zhi],
                      dict(section=section, zhi=self.zlo, zlo=self.core))

    def send(self, block, section):
        index = len(self.sent)
        here = self.aligned & (self.core == section)
        self.sent.append((block, section))

        @pl.when(here)
        def keep():
            self.home[self.zhi] = block[...]

        @pl.when(jnp.logical_not(here))
        def give():
            self.copy(block, section, index).start()

    def close(self):
        for batch in range(2):
            @pl.when(jnp.logical_not(self.aligned & (self.zhi == batch)))
            def landed():
                block = self.home.at[batch]
                remote(block, block, self.send_sem.at[0], self.recv_sem.at[batch],
                       dict(section=1 - self.core)).wait_recv()
        for index, (block, section) in enumerate(self.sent):
            @pl.when(jnp.logical_not(self.aligned & (self.core == section)))
            def left():
                self.copy(block, section, index).wait_send()


class PlaneSum:
    def __init__(self, source, shares, send, recv):
        self.source, self.shares = source, shares
        self.expert = lax.axis_index(EXPERT)
        self.copies = []
        for step in range(1, 4):
            spot = across(self.expert, step)
            copy = remote(source.at[pl.ds(4 * spot, 4)], shares.at[step - 1], send.at[step - 1],
                          recv.at[step - 1], dict(expert=spot))
            copy.start()
            self.copies.append(copy)

    def total(self):
        for copy in self.copies:
            copy.wait()
        total = self.source[pl.ds(4 * self.expert, 4)].astype(F32)
        for step in range(3):
            total = total + self.shares[step].astype(F32)
        return total.astype(BF16)


def attend_back(section, sizes, *refs):
    refs = list(refs)

    def take(count):
        taken = refs[:count]
        del refs[:count]
        return taken

    last = section == 0
    early, mixed, stats, outcome, gathered = take(5)
    if last:
        middle_grad, attended_grad, first_low, *shared, other_qkv = take(6)
        home, owned, owned_shared, = take(3)
    else:
        (returned, returned_grad, aux, middle, given, normed_two, attended, w_outs, routes,
         first_result, next_aux) = take(11)
        shared_grad, low, qkv_grad, home, spread = take(5)
    vectors, bias, *work = take(8)
    (grads, kept, leaving, sent, partner_share, side_share, group_send, group_recv, pair_send, pair_recv,
     home_send, home_recv) = take(12)
    mixed_grad, strips = work[0], work[5]
    span, features, width = sizes.span, sizes.features, sizes.width
    core, zhi, zlo, place, group = whereabouts()
    expert = lax.axis_index(EXPERT)
    if last:
        (low, qkv_grad, other_shares, qkv_shares, shared_in, shared_sum, shared_shares, line_totals, pieces,
         shared_totals, shared_parts, other_send, other_recv, plane_send, plane_recv, in_send, in_recv,
         shared_send, shared_recv, line_send, line_recv, spread_send, spread_recv) = take(23)
    else:
        middle_grad, attended_grad, second_result = take(3)
    greet(line_peers(core, place) + ([dict(expert=across(expert, step)) for step in range(1, 4)] if last else []))
    homes = Homes(home, home_send, home_recv)
    router, gain_one, gain_two, table = unpack_small(sizes, early, 0)
    trade = Regroup(attended_grad, grads, group_send, group_recv)
    if not last:
        homes.send(first_result, 0)
        total, difference = combined(returned[...], aux[...], middle[...])
        second_result[...] = total.astype(BF16)
        token_backward(
            returned_grad[...], aux[...], given[...].astype(F32), difference, middle[...], normed_two[...],
            attended, gain_two, router, lambda member: out_rows(sizes, w_outs, 0, member),
            route_columns(routes[section].T), middle_grad, attended_grad, shared_grad,
            hook=lambda: trade.start(slice(None)),
        )
    else:
        trade.start(slice(None))
    if last:
        partner = dict(section=1 - core)
        for which in range(2):
            @pl.when(core != which)
            def pass_share():
                remote(shared[which], shared_in, in_send, in_recv, partner).start()

        other_sum = PlaneSum(other_qkv, other_shares, other_send, other_recv)
        homes.send(first_low, 1)
    else:
        homes.send(second_result, 1)
    strips[...] = jnp.zeros_like(strips)
    fill_bias(group * sizes.heads + sizes.table_lane, sizes.heads, table, vectors, bias, span, sizes.spacing)
    if last:
        remote(shared[0], shared_in, in_send, in_recv, partner).wait_recv()
        for which in range(2):
            @pl.when(core == which)
            def add_share():
                shared_sum[...] = shared[which][...] + shared_in[...]

        plane_shared = PlaneSum(shared_sum, shared_shares, shared_send, shared_recv)
        line_copies = []

        def to_owners(owner_section, totals):
            line_totals[owner_section] = totals
            turn = (core + owner_section) % 2
            mine = 2 * place + core
            for move in range(4):
                spot = across(place, move)
                copy = remote(line_totals.at[owner_section, spot], pieces.at[mine],
                              line_send.at[owner_section, move], line_recv.at[turn, move],
                              dict(section=owner_section, zhi=spot // 2, zlo=spot % 2))
                line_copies.append((copy, owner_section, move))
                if move:
                    copy.start()
                else:
                    @pl.when(core != owner_section)
                    def give():
                        copy.start()

                    @pl.when(core == owner_section)
                    def keep():
                        pieces[mine] = line_totals[owner_section, place]

    trade.wait()
    for head in range(sizes.heads):
        if last and head == sizes.heads - 1:
            to_owners(1, other_sum.total())
        back_head(sizes.attention, head, mixed, stats, outcome, grads, bias, work)
    weight = qkv_columns(sizes, early, 0)

    def rows_of(piece):
        return pl.ds(pl.multiple_of(piece * span, span), span)

    def piece_back(piece):
        return back_piece(sizes.attention, gathered, rows_of(piece), gain_one, weight, mixed_grad)

    back, gain_total = piece_back(2 * zlo + 1 - core)
    sent[0] = back.astype(BF16)
    back, gain_part = piece_back(2 * (1 - zlo) + 1 - core)
    sent[1] = back.astype(BF16)
    partner_copy = remote(sent, partner_share, pair_send.at[0], pair_recv.at[0], dict(section=1 - core))
    partner_copy.start()
    gain_total = gain_total + gain_part
    leave, gain_part = piece_back(2 * (1 - zlo) + core)
    gain_total = gain_total + gain_part
    partner_copy.wait()
    leaving[...] = (leave + partner_share[1].astype(F32)).astype(BF16)
    stay, gain_part = piece_back(group)
    side_copy = remote(leaving, side_share, pair_send.at[1], pair_recv.at[1], dict(zlo=1 - zlo))
    side_copy.start()
    gain_total = gain_total + gain_part
    kept[...] = stay + partner_share[0].astype(F32)
    columns = qkv_grad.shape[2]
    weights = weight_share(sizes.attention, gathered, gain_one, mixed_grad).astype(BF16)
    extra = extra_columns(sizes.attention, sizes.buckets, features, strips, gain_total)
    by_rank = (sizes.ranks, sizes.shard_rows)
    qkv_grad[:, :, 3 * width :] = jnp.concatenate(
        [extra, jnp.zeros((features, columns - 3 * width - 16), BF16)], axis=1
    ).reshape(*by_rank, columns - 3 * width)
    qkv_grad[:, :, : 3 * width] = weights.reshape(*by_rank, 3 * width)
    if last:
        qkv_sum = PlaneSum(qkv_grad, qkv_shares, plane_send, plane_recv)
        shared_totals[...] = plane_shared.total()
        for move in range(4):
            spot = across(place, move)
            if move:
                copy = remote(shared_totals.at[spot], shared_parts.at[move], spread_send.at[move],
                              spread_recv.at[move], dict(zhi=spot // 2, zlo=spot % 2))
                copy.start()
                line_copies.append((copy, None, move))
            else:
                shared_parts[0] = shared_totals[place]
    side_copy.wait()
    own = gathered[rows_of(group), :].astype(F32)
    back, unused = norm_backward(own, gain_one, kept[...] + side_share[...].astype(F32))
    total = (middle_grad[...] + back).astype(BF16)
    low[...] = total
    if not last:
        spread[...] = spread_values(total.astype(F32), next_aux[...], sizes.slots)
    else:
        homes.send(low, 0)
        to_owners(0, qkv_sum.total())
        for turn in range(2):
            for move in range(4):
                if move or turn:
                    block = pieces.at[2 * across(place, move) + (1 - core if turn else core)]
                    remote(block, block, line_send.at[0, 0], line_recv.at[turn, move], partner).wait_recv()
        for member in range(GROUP):
            owned[member] = pieces[member].astype(F32) + pieces[GROUP + member].astype(F32)
        for copy, owner_section, move in line_copies:
            if owner_section is None:
                copy.wait()
            elif move:
                copy.wait_send()
            else:
                @pl.when(core != owner_section)
                def gone():
                    copy.wait_send()
        owned_shared[...] = sum(shared_parts[move].astype(F32) for move in range(4))
        remote(shared[0], shared_in, in_send, in_recv, partner).wait_send()
    homes.close()


def run_attend_back(section, sizes, operands, picks, collective):
    dma = pltpu.SemaphoreType.DMA
    span, features, width, ranks = sizes.span, sizes.features, sizes.width, sizes.ranks
    rows = sizes.shard_rows
    columns = -(-(3 * width + 16) // 128) * 128
    tail = features + -(-(sizes.experts + 1) // 128) * 128
    block = (span, features)
    last = section == 0
    if last:
        outs = [shape((2, *block), BF16), shape((GROUP, rows, columns), F32), shape((rows, tail), F32)]
    else:
        outs = [shape((features, tail), BF16), shape(block, BF16), shape((ranks, rows, columns), BF16),
                shape((2, *block), BF16), shape((sizes.slots, features), BF16)]
    scratch = [
        pltpu.VMEM((128, 2 * span * GROUP), F32), pltpu.VMEM((sizes.heads * GROUP, span, span), F32),
        pltpu.VMEM((sizes.length, 3 * width), BF16), pltpu.VMEM((GROUP, span, span), F32),
        pltpu.VMEM((sizes.length, sizes.size), F32), pltpu.VMEM((sizes.length, sizes.size), F32),
        pltpu.VMEM((sizes.size, sizes.length), F32), pltpu.VMEM((8, GROUP * 2 * 128), F32),
        pltpu.VMEM((GROUP, width, span), BF16), pltpu.VMEM(block, F32), pltpu.VMEM(block, BF16),
        pltpu.VMEM((2, *block), BF16), pltpu.VMEM((2, *block), BF16), pltpu.VMEM(block, BF16),
        dma((3,)), dma((3,)), dma((2,)), dma((2,)), dma((2,)), dma((2,)),
    ]
    if last:
        scratch += [
            pltpu.VMEM(block, BF16), pltpu.VMEM((ranks, rows, columns), BF16),
            pltpu.VMEM((3, 4, rows, columns), BF16), pltpu.VMEM((3, 4, rows, columns), BF16),
            pltpu.VMEM((ranks, rows, tail), BF16), pltpu.VMEM((ranks, rows, tail), BF16),
            pltpu.VMEM((3, 4, rows, tail), BF16), pltpu.VMEM((2, 4, rows, columns), BF16),
            pltpu.VMEM((2 * GROUP, rows, columns), BF16), pltpu.VMEM((4, rows, tail), BF16),
            pltpu.VMEM((4, rows, tail), BF16),
            dma((3,)), dma((3,)), dma((3,)), dma((3,)), dma, dma, dma((3,)), dma((3,)),
            dma((2, 4)), dma((2, 4)), dma((4,)), dma((4,)),
        ]
    else:
        scratch += [pltpu.VMEM(block, F32), pltpu.VMEM((GROUP, width, span), BF16), pltpu.VMEM(block, BF16)]
    return call(
        functools.partial(attend_back, section, sizes), "attend_back", outs, operands, scratch=scratch,
        flops=10 << 30, collective=collective, picks=picks,
    )


def per_device(inputs, cotangent, qkv_shard, out_shard, router_shard, gain_shard, table_shard,
               w_expert_in, w_expert_out, routes):
    core = lax.axis_index(SECTION)
    zhi = lax.axis_index(ZHI)
    zlo = lax.axis_index(ZLO)
    span, features = inputs.shape[2:]
    ranks = lax.axis_size(RANKS)
    shard_rows = qkv_shard.shape[1]
    experts = router_shard.shape[2]
    table_rows, head_count = table_shard.shape[1:]
    buckets = table_rows * ranks
    heads = head_count // GROUP
    size = features // head_count
    width = heads * size
    spacing = GROUP * span // buckets
    capacity = max(2, 4 * span // experts)
    slots = experts * capacity
    group = 2 * zlo + core
    sizes = (span, heads, size, spacing, ranks)
    ids = jnp.stack([
        group, 2 * zlo + 1 - core, 2 * (1 - zlo) + core, 2 * (1 - zlo) + 1 - core, group,
        group, 2 * (1 - zlo) + core, 2 * zlo + 1 - core, 2 * (1 - zlo) + 1 - core,
    ]).astype(jnp.int32)
    core_id = core.astype(jnp.int32).reshape(1)

    w_in = w_expert_in[0, 0]
    w_down = w_expert_out[0, 0]
    w_in_other = flip(w_in)
    w_down_other = flip(w_down)
    fused = lax.axis_size(EXPERT) == 4 and features == tile_of(w_in.shape[1])
    shared_sizes = Sizes(
        span=span, heads=heads, size=size, spacing=spacing, ranks=ranks, experts=experts, capacity=capacity,
        features=features, buckets=buckets, shard_rows=shard_rows, table_rows=table_rows,
    )

    home_rows = lax.dynamic_index_in_dim(inputs, core, 0, keepdims=False)[0]
    given = to_working(lax.dynamic_index_in_dim(cotangent, core, 0, keepdims=False)[0], 0)
    if not fused:
        own = to_working(home_rows, 0)
        route_parts = [
            to_working(lax.dynamic_index_in_dim(routes[0], core ^ turn, 0, keepdims=False)[0], turn)
            for turn in range(2)
        ]
        section_routes = [
            jnp.where(zhi == section, route_parts[0], route_parts[1]) for section in range(2)
        ]

    if fused:
        first = run_attend(
            0, shared_sizes,
            [inputs[:, 0], routes[0, :, 0], qkv_shard[0], out_shard[0], router_shard[0], gain_shard[0],
             table_shard[0]], 4)
        early_all, w_out_all, route_all = first[9:]
    else:
        small = jnp.concatenate([
            router_shard[0],
            gain_shard[0].T,
            jnp.pad(table_shard[0], ((0, shard_rows - table_rows), (0, 0))),
        ], axis=1)
        by_group = jnp.transpose(
            qkv_shard[0].reshape(shard_rows, 3, GROUP, width), (2, 0, 1, 3)
        ).reshape(GROUP, shard_rows, 3 * width)
        by_group = jnp.concatenate(
            [by_group, jnp.broadcast_to(small[None], (GROUP, *small.shape))], axis=2
        )
        by_group = jnp.pad(by_group, ((0, 0), (0, 0), (0, -by_group.shape[2] % 128)))
        columns = by_group.shape[2]
        whole_early = lax.all_gather(by_group, RANKS, axis=1, tiled=True)
        kept = lax.dynamic_index_in_dim(whole_early, group, 0, keepdims=False)
        traded = flip(lax.dynamic_index_in_dim(whole_early, 2 * zlo + 1 - core, 0, keepdims=False))
        early = [
            jnp.where(core == section, kept, traded).reshape(features, columns) for section in range(2)
        ]
        w_out_own = lax.all_gather(out_shard[0], RANKS, axis=0, tiled=True)
        w_out_other = flip(w_out_own)
        w_outs = [jnp.where(core == which, w_out_own, w_out_other) for which in range(2)]
    expert_weights = (w_in, w_down, w_in_other, w_down_other)

    def by_rank(block):
        return block.reshape(ranks, capacity, features)

    def by_slot(block):
        return block.reshape(slots, features)

    weights = []
    for section in range(0 if fused else 2):
        is_own = core == section
        others = early[section][:, 3 * width :]
        router = others[:, :experts]
        gains = others[:, experts : experts + 2].T
        table = others[:, experts + 2 : experts + 2 + head_count]
        table = table.reshape(ranks, shard_rows, head_count)[:, :table_rows].reshape(buckets, head_count)
        weights.append((
            early[section], router, gains[0:1], gains[1:2], table,
            jnp.where(is_own, w_in, w_in_other), jnp.where(is_own, w_down, w_down_other),
        ))

    bias_scratch = [
        pltpu.VMEM((-(-head_count // 8) * 8, 2 * span * GROUP), F32),
        pltpu.VMEM((heads * GROUP, span, span), F32),
    ]
    length = GROUP * span
    blocks = span // spacing
    states = []
    results = []
    if fused:
        (outcome, mixed, gathered, stats, outgoing, middle, normed_two, aux, attended) = first[:9]
        returned, arrived, activation, slope = run_expert_layer(FORWARD, 0, expert_weights, [by_rank(outgoing)])
        second = run_attend(
            1, shared_sizes, [by_slot(returned), aux, middle, early_all, w_out_all, route_all, given], 5)
        result, difference, spread = second[9:]
        (outcome, mixed, gathered, stats, outgoing, middle, normed_two, aux, attended) = second[:9]
        returned, returned_grad, grad_in, grad_down = run_expert_layer(
            BOTH, 1, expert_weights, [by_rank(outgoing), by_rank(spread)])
        shared_1, low_1, qkv_1, section_outputs, spread = run_attend_back(
            1, shared_sizes,
            [early_all, mixed, stats, outcome, gathered, by_slot(returned), by_slot(returned_grad), aux, middle,
             given, normed_two, attended, w_out_all, route_all, result, first[7]],
            ((0, 1), (12, 1)), 6)
        returned, grad_in, grad_down = run_expert_layer(
            BACKWARD, 0, expert_weights, [by_rank(spread)], [arrived, activation, slope], [grad_in, grad_down])
        (outcome, mixed, gathered, stats, unused, middle, normed_two, aux, attended) = first[:9]
        pieces = 2 * grad_in.shape[1] // features
        middle_grad, attended_grad, shared_0, grad_in, grad_down = call(
            functools.partial(before_attention_fused, shared_sizes), "before_attention",
            [shape((span, features), F32), shape((GROUP, width, span), BF16), shape(shared_1.shape, BF16),
             shape(grad_in.shape, F32), shape(grad_down.shape, F32)],
            [by_slot(returned), aux, low_1, difference, middle, normed_two, attended, early_all, w_out_all,
             route_all, grad_in, grad_down],
            scratch=[pltpu.VMEM((pieces, features, features), BF16), pltpu.VMEM((pieces, features, features), F32),
                     pltpu.SemaphoreType.DMA((pieces,)), pltpu.SemaphoreType.DMA((pieces,))],
            flops=2 << 30, anywhere=(10, 11), out_anywhere=(3, 4), picks=((7, 0), (8, 0)),
        )
        ranked = (ranks, shard_rows, -1)
        home, owned, shared_sum = run_attend_back(
            0, shared_sizes,
            [early_all, mixed, stats, outcome, gathered, middle_grad, attended_grad, low_1,
             shared_0.reshape(ranked), shared_1.reshape(ranked), qkv_1],
            ((0, 0),), 7)
        section_outputs, section_grads, grad_qkv, grad_out, grad_router, grad_gains, grad_table = call(
            functools.partial(unpack, shared_sizes), "unpack",
            [shape(home.shape, BF16), shape(home.shape, F32), shape((shard_rows, 3 * features), F32), shape((shard_rows, features), F32),
             shape((shard_rows, experts), F32), shape((2, shard_rows), F32),
             shape((table_rows, head_count), F32)],
            [home, owned, shared_sum, section_outputs],
        )
    stream = None if fused else own
    for section in range(0 if fused else 2):
        qkv, router, gain_one, gain_two, table, expert_in, expert_down = weights[section]
        route_rows = section_routes[section]
        side = beside(stream)
        pieces = (stream, flip(stream), side, flip(side))
        outcome, mixed, gathered, stats = call(
            functools.partial(attention_forward, sizes), "attention_forward",
            [shape((GROUP, width, span), BF16), shape((length, 3 * width), BF16),
             shape((length, features), BF16), shape((8, length), F32)],
            [*pieces, gain_one, qkv, table], scalars=ids, scratch=bias_scratch, flops=4 << 30,
        )
        attended = regroup(outcome)
        outgoing, middle, normed_two, aux = call(
            functools.partial(after_attention, capacity), "after_attention",
            [shape((slots, features), BF16), shape((span, features), F32),
             shape((span, features), BF16), shape((span, 128), F32)],
            [attended, stream, w_outs[section], gain_two, router, route_rows], flops=1 << 30,
        )
        arrived = exchange(outgoing, experts, capacity)
        activation, slope, produced = run_expert_forward(arrived, expert_in, expert_down)
        returned = exchange(produced, experts, capacity)
        result, difference = call(
            combine, "combine", [shape((span, features), BF16), shape((span, features), F32)],
            [returned, aux, middle], flops=1 << 30,
        )
        states.append((stream, outcome, mixed, gathered, stats, attended, middle, normed_two, aux,
                       arrived, activation, slope, difference))
        results.append(result)
        stream = result

    if not fused:
        section_outputs = home_pair(results, core)

    upstream = given
    shared_grads = [None, None]
    shared_partner = [None, None]
    shared_qkv = [None, None]
    qkv_grads = [None, None]
    expert_states = [None, None]
    partials = [None, None]
    stream_grads = [None, None]
    for section in (() if fused else (1, 0)):
        qkv, router, gain_one, gain_two, table, expert_in, expert_down = weights[section]
        w_out = w_outs[section]
        (stream, outcome, mixed, gathered, stats, attended, middle, normed_two, aux,
         arrived, activation, slope, difference) = states[section]
        route_rows = section_routes[section]
        (spread,) = call(spread_grads, "spread_grads", [shape((slots, features), BF16)],
                         [upstream, aux], flops=1 << 30)
        arrived_grad = exchange(spread, experts, capacity)
        hidden_grad, rows_grad = run_expert_backward(arrived_grad, expert_in, expert_down, slope)
        returned = exchange(rows_grad, experts, capacity)
        expert_states[section] = (arrived, hidden_grad, activation, arrived_grad)
        wanted = (core != section).astype(jnp.int32).reshape(1)
        shares = run_weight_partials(wanted, *expert_states[section])
        partials[section] = [lax.ppermute(part, SECTION, [(1 - section, section)]) for part in shares]
        if section == 0:
            waiting, returned = lax.optimization_barrier((shared_qkv[1], returned))
            qkv_grads[1] = spread_sum(waiting, (EXPERT, ZHI), ranks // 2)
        middle_grad, attended_grad, shared_grads[section] = call(
            before_attention, "before_attention",
            [shape((span, features), F32), shape((GROUP, width, span), BF16),
             shape((features, features + -(-(experts + 1) // 128) * 128), BF16)],
            [returned, aux, upstream, difference, middle, normed_two, attended, gain_two, router, w_out,
             route_rows], flops=2 << 30, after=shares[:1],
        )
        shared_partner[section] = lax.ppermute(shared_grads[section], SECTION, [(1 - section, section)])
        grads = regroup(attended_grad)
        stay, leave, sent, shared_qkv[section] = call(
            functools.partial(attention_backward, sizes), "attention_backward",
            [shape((span, features), BF16), shape((span, features), BF16), shape((2, span, features), BF16),
             shape((features, -(-(3 * width + 16) // 128) * 128), BF16)],
            [mixed, stats, outcome, grads, gathered, gain_one, qkv, table], scalars=ids,
            scratch=[*bias_scratch, pltpu.VMEM((length, 3 * width), BF16),
                     pltpu.VMEM((GROUP, span, span), F32), pltpu.VMEM((length, size), F32),
                     pltpu.VMEM((length, size), F32), pltpu.VMEM((size, length), F32),
                     pltpu.VMEM((8, GROUP * 2 * 128), F32)],
            flops=8 << 30,
        )
        partner = flip(sent)
        leave = leave + partner[1]
        filler = ()
        if section == 0:
            leave, waiting = lax.optimization_barrier((leave, shared_qkv[0]))
            qkv_grads[0] = spread_sum(waiting, (EXPERT, ZHI), ranks // 2)
            grad_in = run_weight_totals(
                core_id, *[(expert_states[which][0], expert_states[which][1], partials[which][0])
                           for which in range(2)], False, sent)
            filler = (grad_in,)
        arrived_share = beside(leave)
        (low,) = call(
            first_norm_grad, "first_norm_grad", [shape((span, features), BF16)],
            [stay, partner, arrived_share, stream, gain_one, middle_grad], after=filler,
        )
        stream_grads[section] = low
        upstream = low

    if not fused:
        shared = jnp.where(
            core == 0,
            shared_grads[0].astype(F32) + shared_partner[0].astype(F32),
            shared_grads[1].astype(F32) + shared_partner[1].astype(F32),
        ).astype(BF16)
        shared = spread_sum(shared, RANKS, ranks)
        grad_out = shared[:, :features]
        grad_router = shared[:, features : features + experts]
        grad_gain_two = shared[:, features + experts]

        columns = qkv_grads[0].shape[1]
        halves = [block.reshape(2, shard_rows, columns) for block in qkv_grads]
        owned = regroup(jnp.stack([halves[0][0], halves[1][0], halves[0][1], halves[1][1]]))
        split = owned[:, :, : 3 * width].reshape(GROUP, shard_rows, 3, width)
        grad_qkv = jnp.transpose(split, (1, 2, 0, 3)).reshape(shard_rows, 3 * features)
        grad_table = jnp.transpose(
            owned[:, :table_rows, 3 * width : 3 * width + heads], (1, 0, 2)
        ).reshape(table_rows, head_count)
        grad_gain_one = jnp.sum(owned[:, :, 3 * width + 8], axis=0)
        grad_gains = jnp.stack([grad_gain_one, grad_gain_two])
        section_grads = home_pair(stream_grads, core).astype(F32)
        grad_down = run_weight_totals(
            core_id, *[(expert_states[which][2], expert_states[which][3], partials[which][1])
                       for which in range(2)], True, stream_grads[0])
    return (
        section_outputs[None, :, None],
        section_grads[None, :, None],
        grad_qkv[None],
        grad_out[None],
        grad_router[None],
        grad_gains[None],
        grad_table[None],
        grad_in[None, None],
        grad_down[None, None],
    )


def solution(mesh):
    sections, ranks, pieces = mesh.devices.shape
    work = Mesh(
        mesh.devices.reshape(sections, ranks, pieces // 2, 2), (SECTION, EXPERT, ZHI, ZLO)
    )
    piece = (ZHI, ZLO)
    in_specs = (
        P(None, EXPERT, piece, None),
        P(None, EXPERT, piece, None),
        P(SECTION, RANKS, None),
        P(SECTION, RANKS, None),
        P(SECTION, RANKS, None),
        P(SECTION, None, RANKS),
        P(SECTION, RANKS, None),
        P(SECTION, RANKS, None, None),
        P(SECTION, RANKS, None, None),
        P(SECTION, None, EXPERT, piece, None),
    )
    out_specs = (
        P(SECTION, None, EXPERT, piece, None),
        P(SECTION, None, EXPERT, piece, None),
        P(SECTION, RANKS, None),
        P(SECTION, RANKS, None),
        P(SECTION, RANKS, None),
        P(SECTION, None, RANKS),
        P(SECTION, RANKS, None),
        P(SECTION, RANKS, None, None),
        P(SECTION, RANKS, None, None),
    )
    return jax.shard_map(per_device, mesh=work, in_specs=in_specs, out_specs=out_specs, check_vma=False)
```

```python
import functools

import jax
import jax.numpy as jnp
from jax import lax
from jax.experimental import pallas as pl
from jax.experimental.pallas import tpu as pltpu
from jax.sharding import Mesh
from jax.sharding import PartitionSpec as P

F32 = jnp.float32
BF16 = jnp.bfloat16
EPS = 1e-06
SECTION, EXPERT, ZHI, ZLO = "section", "expert", "zhi", "zlo"
FORWARD, BACKWARD, BOTH = "forward", "backward", "both"
MASKED = -1e30
GROUP = 4
RANKS = (EXPERT, ZHI, ZLO)
VMEM_LIMIT = 60 << 20

NN = (((1,), (0,)), ((), ()))
NT = (((1,), (1,)), ((), ()))
TN = (((0,), (0,)), ((), ()))


def mm(left, right, dims=NN):
    return lax.dot_general(left, right, dims, preferred_element_type=F32)


def inverse_rms(values):
    return lax.rsqrt(jnp.mean(values * values, axis=-1, keepdims=True) + EPS)


def whole(array):
    rank = len(array.shape)
    return pl.BlockSpec(array.shape, lambda *unused: (0,) * rank)


def ordered(body, skipped):
    def inner(*refs):
        return body(*refs[skipped:])

    return inner if skipped else body


def fetched(body, picked, skipped):
    def inner(*refs):
        refs = list(refs)
        semaphores = refs.pop()
        blocks = refs[-len(picked) :]
        del refs[-len(picked) :]
        copies = []
        for place, index in enumerate(sorted(picked)):
            source = refs[skipped + index].at[pl.ds(picked[index], 1)]
            copy = pltpu.make_async_copy(source, blocks[place], semaphores.at[place])
            copy.start()
            copies.append(copy)
            refs[skipped + index] = blocks[place]
        for copy in copies:
            copy.wait()
        return body(*refs)

    return inner


REMOTE = pl.DeviceIdType.MESH


def remote(source, target, send, recv, peer):
    return pltpu.make_async_remote_copy(
        src_ref=source, dst_ref=target, send_sem=send, recv_sem=recv, device_id=peer, device_id_type=REMOTE
    )


def across(index, step):
    return (index, index + 1 - 2 * (index % 2), (index + 2) % 4, 3 - index)[step]


def greet(peers):
    barrier = pltpu.get_barrier_semaphore()
    for peer in peers:
        pl.semaphore_signal(barrier, inc=1, device_id=peer, device_id_type=REMOTE)
    pl.semaphore_wait(barrier, len(peers))


def call(body, name, outs, args, scalars=None, scratch=(), flops=0, after=(), collective=None, anywhere=(),
         out_anywhere=(), picks=()):
    specs = [pl.BlockSpec(memory_space=pl.ANY)] * len(after)
    specs += [pl.BlockSpec(memory_space=pltpu.SMEM)] if scalars is not None else []
    picked = dict(picks)
    specs += [
        pl.BlockSpec(memory_space=pl.ANY if index in anywhere or index in picked else pltpu.VMEM)
        for index in range(len(args))
    ]
    operands = list(after) + ([scalars] if scalars is not None else []) + list(args)
    moved = sum(a.size * a.dtype.itemsize for a in list(args) + list(outs))
    body = ordered(body, len(after))
    if picked:
        body = fetched(body, picked, int(scalars is not None))
        scratch = list(scratch) + [
            pltpu.VMEM((1, *args[index].shape[1:]), args[index].dtype) for index in sorted(picked)
        ] + [pltpu.SemaphoreType.DMA((len(picked),))]
    return pl.pallas_call(
        body,
        name=name,
        in_specs=specs,
        out_specs=[
            pl.BlockSpec(memory_space=pl.ANY if index in out_anywhere else pltpu.VMEM)
            for index in range(len(outs))
        ],
        out_shape=list(outs),
        scratch_shapes=list(scratch),
        compiler_params=pltpu.CompilerParams(
            vmem_limit_bytes=VMEM_LIMIT, collective_id=collective, has_side_effects=collective is not None
        ),
        cost_estimate=pl.CostEstimate(flops=flops, bytes_accessed=moved, transcendentals=0),
    )(*operands)


def shape(dims, dtype):
    return jax.ShapeDtypeStruct(tuple(dims), dtype)


def bucket_onehot(buckets, span, spacing):
    width = 2 * span * GROUP
    column = lax.broadcasted_iota(jnp.int32, (buckets, width), 1)
    delta = column // (2 * span)
    distance = column - delta * (2 * span) - span + span * delta
    bucket = jnp.where(distance >= 0, distance // spacing, -1)
    row = lax.broadcasted_iota(jnp.int32, (buckets, width), 0)
    return (bucket == row).astype(BF16)


def fill_bias(first_head, heads, table, vectors, bias, span, spacing):
    buckets, head_count = table.shape
    hot = bucket_onehot(buckets, span, spacing)
    rows = mm(table, hot, TN)
    column = lax.broadcasted_iota(jnp.int32, (1, 2 * span * GROUP), 1)
    rows = jnp.where(column < span, MASKED, rows)
    vectors[0:head_count, :] = rows
    for head in range(heads):
        picked = vectors[pl.ds(first_head + head, 1), :]
        for delta in range(GROUP):
            piece = picked[:, delta * 2 * span : (delta + 1) * 2 * span]
            spread = jnp.broadcast_to(piece, (span, 2 * span))
            rolled = pltpu.roll(spread, span, 1, stride=1, stride_axis=0)
            bias[head * GROUP + delta] = rolled[:, :span]


def attention_forward(sizes, ids, own, flip, side, side_flip, gain, weight, table,
                      out, mixed, gathered, stats, vectors, bias):
    span, heads, size, spacing, unused = sizes
    width = heads * size
    fill_bias(ids[4] * heads, heads, table[...], vectors, bias, span, spacing)
    for slot, piece in enumerate((own, flip, side, side_flip)):
        gathered[pl.ds(pl.multiple_of(ids[slot] * span, span), span), :] = piece[...]
    for part in range(GROUP):
        project(gathered, slice(part * span, (part + 1) * span), gain[...], weight[:, : 3 * width], mixed)
    for head in range(heads):
        attend_head(sizes, head, mixed, bias, out, stats)


def project(gathered, rows, gain, weight, mixed):
    values = gathered[rows, :].astype(F32)
    normed = (values * inverse_rms(values) * gain.astype(F32)).astype(BF16)
    mixed[rows, :] = mm(normed, weight).astype(BF16)


def attend_head(sizes, head, mixed, bias, out, stats):
    span, heads, size = sizes[:3]
    width = heads * size
    columns = slice(head * size, (head + 1) * size)
    query_t = (mixed[:, columns].astype(F32) * size ** (-0.5)).T.astype(BF16)
    key = mixed[:, width + head * size : width + (head + 1) * size]
    value_t = mixed[:, 2 * width + head * size : 2 * width + (head + 1) * size].astype(F32).T.astype(BF16)
    for part in range(GROUP):
        mine = slice(part * span, (part + 1) * span)
        blocks = []
        for other in range(part + 1):
            raw = mm(key[other * span : (other + 1) * span], query_t[:, mine])
            blocks.append(raw + bias[head * GROUP + part - other])
        top = functools.reduce(jnp.maximum, [jnp.max(b, axis=0, keepdims=True) for b in blocks])
        total = jnp.zeros_like(top)
        gained = jnp.zeros((size, span), F32)
        for other, block in enumerate(blocks):
            raised = jnp.exp(block - top)
            total = total + jnp.sum(raised, axis=0, keepdims=True)
            gained = gained + mm(value_t[:, other * span : (other + 1) * span], raised.astype(BF16))
        out[part, columns, :] = (gained / total).astype(BF16)
        stats[head : head + 1, mine] = top + jnp.log(total)


def route_masks(columns, experts):
    lane = lax.broadcasted_iota(jnp.int32, (columns[0].shape[0], experts), 1).astype(F32)
    return [(column == lane).astype(F32) for column in columns]


def route_columns(routes):
    return [routes[:, k : k + 1].astype(F32) for k in range(2)]


def slot_places(columns, masks, capacity):
    tokens = columns[0].shape[0]
    members = (masks[0] + masks[1]).astype(BF16)
    row = lax.broadcasted_iota(jnp.int32, (tokens, tokens), 0)
    column = lax.broadcasted_iota(jnp.int32, (tokens, tokens), 1)
    earlier = mm((row > column).astype(BF16), members)
    return [
        columns[k] * capacity + jnp.sum(earlier * masks[k], axis=1, keepdims=True) for k in range(2)
    ]


def dispatch(total, gain, router, masks, places, slots, outgoing, normed_two, aux):
    tokens = total.shape[0]
    normed = (total * inverse_rms(total) * gain.astype(F32)).astype(BF16)
    normed_two[...] = normed
    logits = mm(normed, router)
    chosen = [jnp.sum(logits * mask, axis=1, keepdims=True) for mask in masks]
    first = jax.nn.sigmoid(chosen[0] - chosen[1])
    lane = lax.broadcasted_iota(jnp.int32, (tokens, 128), 1)
    packed = jnp.zeros((tokens, 128), F32)
    for index, entry in enumerate((places[0], places[1], first, 1.0 - first)):
        packed = jnp.where(lane == index, entry, packed)
    aux[...] = packed
    packed_t = packed.T
    hot = [fill_slots(packed_t, slots, k) for k in range(2)]
    outgoing[...] = mm(hot[0] + hot[1], normed).astype(BF16)
    return packed, hot


def pick_rows(slot, slots):
    lane = lax.broadcasted_iota(jnp.int32, (slot.shape[0], slots), 1).astype(F32)
    return (lane == slot).astype(BF16)


def fill_slots(aux_t, slots, k):
    row = lax.broadcasted_iota(jnp.int32, (slots, aux_t.shape[1]), 0).astype(F32)
    return (row == aux_t[k : k + 1, :]).astype(BF16)


def after_attention(capacity, attended, own, w_out, gain, router, routes,
                    outgoing, middle, normed_two, aux):
    experts = router.shape[1]
    width = attended.shape[1]
    total = own[...].astype(F32)
    for group in range(GROUP):
        total = total + mm(attended[group], w_out[group * width : (group + 1) * width, :], TN)
    middle[...] = total
    columns = route_columns(routes)
    masks = route_masks(columns, experts)
    places = slot_places(columns, masks, capacity)
    dispatch(total, gain[...], router[...], masks, places, experts * capacity, outgoing, normed_two, aux)


def expert_forward(rows, w_in, w_down, activation, slope, produced, total):
    step = pl.program_id(0)

    @pl.when(step == 0)
    def clear():
        total[...] = jnp.zeros_like(total)

    chunk = rows.shape[0] // 4
    for part in range(4):
        mine = slice(part * chunk, (part + 1) * chunk)
        hidden = mm(rows[mine, :], w_in[...])
        half = 0.5 * (1.0 + lax.erf(hidden * 0.7071067811865476))
        bell = jnp.exp(-0.5 * hidden * hidden) * 0.3989422804014327
        raised = (hidden * half).astype(BF16)
        activation[mine, :] = raised
        slope[mine, :] = (half + hidden * bell).astype(BF16)
        total[mine, :] += mm(raised, w_down[...])

    @pl.when(step == pl.num_programs(0) - 1)
    def finish():
        produced[...] = total[...].astype(BF16)


def expert_backward(arrived_grad, w_in, w_down, slope, hidden_grad, rows_grad, total):
    step = pl.program_id(0)

    @pl.when(step == 0)
    def clear():
        total[...] = jnp.zeros_like(total)

    chunk = arrived_grad.shape[0] // 4
    for part in range(4):
        mine = slice(part * chunk, (part + 1) * chunk)
        lifted = mm(arrived_grad[mine, :], w_down[...], NT) * slope[mine, :].astype(F32)
        lowered = lifted.astype(BF16)
        hidden_grad[mine, :] = lowered
        total[mine, :] += mm(lowered, w_in[...], NT)

    @pl.when(step == pl.num_programs(0) - 1)
    def finish():
        rows_grad[...] = total[...].astype(BF16)


def tile_of(hidden):
    return 768 if hidden % 768 == 0 else hidden


def run_expert_forward(rows, w_in, w_down):
    count, features = rows.shape
    hidden = w_in.shape[1]
    tile = tile_of(hidden)
    return pl.pallas_call(
        expert_forward,
        name="expert_forward",
        grid=(hidden // tile,),
        in_specs=[
            whole(rows),
            pl.BlockSpec((features, tile), lambda j: (0, j)),
            pl.BlockSpec((tile, features), lambda j: (j, 0)),
        ],
        out_specs=[
            pl.BlockSpec((count, tile), lambda j: (0, j)),
            pl.BlockSpec((count, tile), lambda j: (0, j)),
            pl.BlockSpec((count, features), lambda j: (0, 0)),
        ],
        out_shape=[shape((count, hidden), BF16), shape((count, hidden), BF16), shape((count, features), BF16)],
        scratch_shapes=[pltpu.VMEM((count, features), F32)],
        compiler_params=pltpu.CompilerParams(vmem_limit_bytes=VMEM_LIMIT),
        cost_estimate=pl.CostEstimate(
            flops=4 * count * features * hidden, bytes_accessed=30 << 20, transcendentals=2 * count * hidden
        ),
    )(rows, w_in, w_down)


def run_expert_backward(arrived_grad, w_in, w_down, slope):
    count, features = arrived_grad.shape
    hidden = w_in.shape[1]
    tile = tile_of(hidden)
    return pl.pallas_call(
        expert_backward,
        name="expert_backward",
        grid=(hidden // tile,),
        in_specs=[
            whole(arrived_grad),
            pl.BlockSpec((features, tile), lambda j: (0, j)),
            pl.BlockSpec((tile, features), lambda j: (j, 0)),
            pl.BlockSpec((count, tile), lambda j: (0, j)),
        ],
        out_specs=[
            pl.BlockSpec((count, tile), lambda j: (0, j)),
            pl.BlockSpec((count, features), lambda j: (0, 0)),
        ],
        out_shape=[shape((count, hidden), BF16), shape((count, features), BF16)],
        scratch_shapes=[pltpu.VMEM((count, features), F32)],
        compiler_params=pltpu.CompilerParams(vmem_limit_bytes=VMEM_LIMIT),
        cost_estimate=pl.CostEstimate(
            flops=4 * count * features * hidden, bytes_accessed=30 << 20, transcendentals=0
        ),
    )(arrived_grad, w_in, w_down, slope)


def weight_partials(scalars, rows, hidden_grad, activation, arrived_grad, grad_in, grad_down):
    @pl.when(scalars[0] == 1)
    def wanted():
        grad_in[...] = mm(rows[...], hidden_grad[...], TN).astype(BF16)
        grad_down[...] = mm(activation[...], arrived_grad[...], TN).astype(BF16)


def run_weight_partials(wanted, rows, hidden_grad, activation, arrived_grad):
    count, features = rows.shape
    hidden = hidden_grad.shape[1]
    tile = tile_of(hidden)
    return pl.pallas_call(
        weight_partials,
        name="weight_partials",
        grid_spec=pltpu.PrefetchScalarGridSpec(
            num_scalar_prefetch=1,
            grid=(hidden // tile,),
            in_specs=[
                pl.BlockSpec((count, features), lambda j, s: (0, 0)),
                pl.BlockSpec((count, tile), lambda j, s: (0, j * s[0])),
                pl.BlockSpec((count, tile), lambda j, s: (0, j * s[0])),
                pl.BlockSpec((count, features), lambda j, s: (0, 0)),
            ],
            out_specs=[
                pl.BlockSpec((features, tile), lambda j, s: (0, j * s[0])),
                pl.BlockSpec((tile, features), lambda j, s: (j * s[0], 0)),
            ],
        ),
        out_shape=[shape((features, hidden), BF16), shape((hidden, features), BF16)],
        compiler_params=pltpu.CompilerParams(vmem_limit_bytes=VMEM_LIMIT),
        cost_estimate=pl.CostEstimate(
            flops=4 * count * features * hidden, bytes_accessed=30 << 20, transcendentals=0
        ),
    )(wanted, rows, hidden_grad, activation, arrived_grad)


def weight_totals(scalars, left, right, sent, left_1, right_1, sent_1, after, total):
    @pl.when(scalars[0] == 0)
    def first():
        total[...] = mm(left[...], right[...], TN) + sent[...].astype(F32)

    @pl.when(scalars[0] == 1)
    def second():
        total[...] = mm(left_1[...], right_1[...], TN) + sent_1[...].astype(F32)


def run_weight_totals(core, first, second, tiled_left, after):
    count, features = first[1 if tiled_left else 0].shape
    hidden = first[0 if tiled_left else 1].shape[1]
    tile = tile_of(hidden)

    def specs(which):
        def step(j, s):
            return jnp.where(s[0] == which, j, 0)

        full = pl.BlockSpec((count, features), lambda j, s: (0, 0))
        part = pl.BlockSpec((count, tile), lambda j, s: (0, step(j, s)))
        if tiled_left:
            return [part, full, pl.BlockSpec((tile, features), lambda j, s: (step(j, s), 0))]
        return [full, part, pl.BlockSpec((features, tile), lambda j, s: (0, step(j, s)))]

    if tiled_left:
        out_spec = pl.BlockSpec((tile, features), lambda j, s: (j, 0))
        dims = (hidden, features)
    else:
        out_spec = pl.BlockSpec((features, tile), lambda j, s: (0, j))
        dims = (features, hidden)
    return pl.pallas_call(
        weight_totals,
        name="weight_totals",
        grid_spec=pltpu.PrefetchScalarGridSpec(
            num_scalar_prefetch=1, grid=(hidden // tile,),
            in_specs=specs(0) + specs(1) + [pl.BlockSpec(memory_space=pl.ANY)], out_specs=out_spec,
        ),
        out_shape=shape(dims, F32),
        compiler_params=pltpu.CompilerParams(vmem_limit_bytes=VMEM_LIMIT),
        cost_estimate=pl.CostEstimate(
            flops=2 * count * features * hidden, bytes_accessed=30 << 20, transcendentals=0
        ),
    )(core, *first, *second, after)


def combined(returned, packed, middle):
    slots = returned.shape[0]
    outs = [mm(pick_rows(packed[:, k : k + 1], slots), returned) for k in range(2)]
    return middle + packed[:, 2:3] * outs[0] + packed[:, 3:4] * outs[1], outs[0] - outs[1]


def combine(returned, aux, middle, result, difference):
    total, gap = combined(returned[...], aux[...], middle[...])
    result[...] = total.astype(BF16)
    difference[...] = gap


def spread_values(values, packed, slots, hot=None):
    packed_t = packed.T
    total = jnp.zeros((slots, values.shape[1]), F32)
    for k in range(2):
        select = hot[k] if hot else fill_slots(packed_t, slots, k)
        total = total + mm(select, (values * packed[:, 2 + k : 3 + k]).astype(BF16))
    return total.astype(BF16)


def spread_grads(upstream, aux, outgoing):
    outgoing[...] = spread_values(upstream[...].astype(F32), aux[...], outgoing.shape[0])


def norm_backward(values, gain, grad):
    scale = inverse_rms(values)
    unit = values * scale
    lifted = grad * gain
    back = scale * (lifted - unit * jnp.mean(lifted * unit, axis=-1, keepdims=True))
    return back, jnp.sum(grad * unit, axis=0, keepdims=True)


def publisher(grad_in, grad_down, out_in, out_down, held, wide, in_sem, out_sem):
    tile = held.shape[2]
    tiles = held.shape[0] // 2
    across_tiles = [(slice(None), pl.ds(index * tile, tile)) for index in range(tiles)]
    down_tiles = [pl.ds(index * tile, tile) for index in range(tiles)]
    places = [(grad_in.at[p], out_in.at[p]) for p in across_tiles]
    places += [(grad_down.at[p], out_down.at[p]) for p in down_tiles]
    fetches = [
        pltpu.make_async_copy(pair[0], held.at[index], in_sem.at[index]) for index, pair in enumerate(places)
    ]
    stores = [
        pltpu.make_async_copy(wide.at[index], pair[1], out_sem.at[index]) for index, pair in enumerate(places)
    ]
    for fetch in fetches:
        fetch.start()

    def publish(quarter):
        share = len(fetches) // 4
        for index in range(quarter * share, (quarter + 1) * share):
            fetches[index].wait()
            wide[index] = held[index].astype(F32)
            stores[index].start()

    return publish, stores


def token_backward(returned, packed, flow, difference, middle, normed_two, attended, gain, router, out_block,
                   columns, middle_grad, attended_grad, shared_grad, publish=None, stores=(), hook=None):
    slots, features = returned.shape
    experts = router.shape[1]
    width = attended.shape[1]

    publish = publish or (lambda quarter: None)
    hot = pick_rows(packed[:, 0:1], slots) + pick_rows(packed[:, 1:2], slots)
    token_grad = mm(hot, returned)
    publish(0)
    shift = jnp.sum(flow * difference, axis=1, keepdims=True) * packed[:, 2:3] * packed[:, 3:4]
    masks = route_masks(columns, experts)
    logits_grad = (shift * (masks[0] - masks[1])).astype(BF16)
    token_grad = token_grad + mm(logits_grad, router, NT)
    back, gain_part = norm_backward(middle, gain.astype(F32), token_grad)
    total = flow + back
    middle_grad[...] = total
    branch = total.astype(BF16)
    publish(1)
    for group in range(GROUP):
        attended_grad[group] = mm(out_block(group), branch, NT).astype(BF16)
    publish(2)
    if hook:
        hook()
    for group in range(GROUP):
        mine = slice(group * width, (group + 1) * width)
        shared_grad[mine, :features] = mm(attended[group], branch).astype(BF16)
    publish(3)
    tail = shared_grad.shape[1] - features
    gain_column = jnp.broadcast_to(gain_part, (8, features)).T
    lane = lax.broadcasted_iota(jnp.int32, (features, tail), 1)
    shared_grad[:, features:] = jnp.where(lane == experts, gain_column[:, 0:1], 0.0).astype(BF16)
    shared_grad[:, features : features + experts] = mm(normed_two, logits_grad, TN).astype(BF16)
    for store in stores:
        store.wait()


def before_attention(returned, aux, upstream, difference, middle, normed_two, attended, gain,
                     router, w_out, routes, middle_grad, attended_grad, shared_grad):
    width = attended.shape[1]
    token_backward(
        returned[...], aux[...], upstream[...].astype(F32), difference[...], middle[...], normed_two[...],
        attended, gain[...], router[...], lambda group: w_out[group * width : (group + 1) * width, :],
        route_columns(routes), middle_grad, attended_grad, shared_grad,
    )


def before_attention_fused(sizes, returned, aux, upstream, difference, middle, normed_two, attended,
                           early, w_outs, routes, grad_in, grad_down,
                           middle_grad, attended_grad, shared_grad, out_in, out_down, held, wide, in_sem, out_sem):
    publish, stores = publisher(grad_in, grad_down, out_in, out_down, held, wide, in_sem, out_sem)
    router, unused, gain_two, unused_1 = unpack_small(sizes, early, 0)
    token_backward(
        returned[...], aux[...], upstream[...].astype(F32), difference[...], middle[...], normed_two[...],
        attended, gain_two, router, lambda group: out_rows(sizes, w_outs, 0, group),
        route_columns(routes[0].T), middle_grad, attended_grad, shared_grad, publish, stores,
    )


def back_head(sizes, head, mixed, stats, attended, grads, bias, work):
    mixed_grad, sums, key_total, value_total, turned, strips = work
    span, heads, size, spacing = sizes[:4]
    width = heads * size
    count = span // spacing
    row = lax.broadcasted_iota(jnp.int32, (span, span), 0)
    column = lax.broadcasted_iota(jnp.int32, (span, span), 1)
    later = (column % spacing) >= (row % spacing)
    lane = lax.broadcasted_iota(jnp.int32, (span, 128), 0) // spacing
    backwards = (count - 1 - lane == lax.broadcasted_iota(jnp.int32, (span, 128), 1)).astype(F32)
    columns = slice(head * size, (head + 1) * size)
    key_columns = slice(width + head * size, width + (head + 1) * size)
    value_columns = slice(2 * width + head * size, 2 * width + (head + 1) * size)
    query = (mixed[:, columns].astype(F32) * size ** (-0.5)).astype(BF16)
    query_t = query.astype(F32).T.astype(BF16)
    key = mixed[:, key_columns]
    key_t = key.astype(F32).T.astype(BF16)
    value = mixed[:, value_columns]
    key_total[...] = jnp.zeros_like(key_total)
    value_total[...] = jnp.zeros_like(value_total)
    sums[...] = jnp.zeros_like(sums)
    for part in range(GROUP):
        mine = slice(part * span, (part + 1) * span)
        grad_t = grads[part, columns, :]
        delta_row = jnp.sum(
            grad_t.astype(F32) * attended[part, columns, :].astype(F32), axis=0, keepdims=True
        )
        level = stats[head : head + 1, mine]
        query_total = jnp.zeros((size, span), F32)
        for other in range(part + 1):
            theirs = slice(other * span, (other + 1) * span)
            raw = mm(key[theirs], query_t[:, mine])
            prob = jnp.exp(raw + (bias[head * GROUP + part - other] - level))
            prob_grad = mm(value[theirs], grad_t)
            low = (prob * (prob_grad - delta_row)).astype(BF16)
            sums[part - other] += low.astype(F32)
            query_total = query_total + mm(key_t[:, theirs], low)
            key_total[theirs, :] += mm(low, query[mine])
            value_total[theirs, :] += mm(prob.astype(BF16), grad_t, NT)
        turned[:, mine] = query_total * size ** (-0.5)
    mixed_grad[:, columns] = turned[...].T.astype(BF16)
    mixed_grad[:, key_columns] = key_total[...].astype(BF16)
    mixed_grad[:, value_columns] = value_total[...].astype(BF16)
    for delta in range(GROUP):
        upper = jnp.where(later, sums[delta], 0.0)
        for side, block in enumerate((upper, sums[delta] - upper)):
            tiles = lax.dot_general(
                jnp.sum(block.reshape(count, spacing, span), axis=1), backwards, NN,
                precision=lax.Precision.HIGHEST, preferred_element_type=F32,
            )
            turned_tiles = pltpu.roll(tiles, 0, 1, stride=1, stride_axis=0)
            place = (delta * 2 + side) * 128
            strips[head : head + 1, place : place + 128] = jnp.sum(turned_tiles, axis=0, keepdims=True)


def back_piece(sizes, gathered, rows, gain, weight, mixed_grad):
    values = gathered[rows, :].astype(F32)
    back = mm(mixed_grad[rows, :], weight, NT)
    return back, jnp.sum(back * values * inverse_rms(values), axis=0, keepdims=True)


def weight_share(sizes, gathered, gain, mixed_grad):
    span, heads, size = sizes[:3]
    total = jnp.zeros((gathered.shape[1], 3 * heads * size), F32)
    for part in range(GROUP):
        rows = slice(part * span, (part + 1) * span)
        values = gathered[rows, :].astype(F32)
        normed = (values * inverse_rms(values) * gain.astype(F32)).astype(BF16)
        total = total + mm(normed, mixed_grad[rows, :], TN)
    return total


def extra_columns(sizes, buckets, features, strips, gain_total):
    span, heads, size, spacing, ranks = sizes
    count = span // spacing
    entry = lax.broadcasted_iota(jnp.int32, (GROUP * 2 * 128, 128), 0)
    bucket = (entry // 256) * count + count - 1 - entry % 128 - (entry // 128) % 2
    hot = (bucket == lax.broadcasted_iota(jnp.int32, (GROUP * 2 * 128, 128), 1)) & (entry % 128 < 2 * count)
    table_rows = lax.dot_general(
        strips[...], hot.astype(F32), NN, precision=lax.Precision.HIGHEST, preferred_element_type=F32
    )
    owned = buckets // ranks
    bucket = lax.broadcasted_iota(jnp.int32, (128, features), 0)
    target = (bucket // owned) * (features // ranks) + bucket % owned
    spot = (target == lax.broadcasted_iota(jnp.int32, (128, features), 1)) & (bucket < buckets)
    placed = lax.dot_general(
        table_rows, spot.astype(F32), NN, precision=lax.Precision.HIGHEST, preferred_element_type=F32
    )
    extra = jnp.concatenate([placed, jnp.broadcast_to(gain_total, (8, features))], axis=0)
    return extra.T.astype(BF16)


def attention_backward(sizes, ids, mixed, stats, attended, grads, gathered, gain, weight, table,
                       stay, leave, sent, shared_grad, vectors, bias, *work):
    span, heads, size, spacing, ranks = sizes
    width = heads * size
    mixed_grad, strips = work[0], work[5]
    strips[...] = jnp.zeros_like(strips)
    fill_bias(ids[4] * heads, heads, table[...], vectors, bias, span, spacing)
    for head in range(heads):
        back_head(sizes, head, mixed, stats, attended, grads, bias, work)
    gain_total = 0.0
    for part in range(GROUP):
        rows = pl.ds(pl.multiple_of(ids[5 + part] * span, span), span)
        back, gain_part = back_piece(sizes, gathered, rows, gain[...], weight[:, : 3 * width], mixed_grad)
        gain_total = gain_total + gain_part
        if part == 0:
            stay[...] = back.astype(BF16)
        elif part == 1:
            leave[...] = back.astype(BF16)
        else:
            sent[part - 2] = back.astype(BF16)
    shared_grad[...] = jnp.zeros_like(shared_grad)
    shared_grad[:, : 3 * width] = weight_share(sizes, gathered, gain[...], mixed_grad).astype(BF16)
    shared_grad[:, 3 * width : 3 * width + 16] = extra_columns(
        sizes, table.shape[0], weight.shape[0], strips, gain_total
    )


def first_norm_grad(stay, partner, arrived, own, gain, middle_grad, low):
    grad = stay[...].astype(F32) + partner[0].astype(F32) + arrived[...].astype(F32)
    back, unused = norm_backward(own[...].astype(F32), gain[...].astype(F32), grad)
    low[...] = (middle_grad[...] + back).astype(BF16)


FLIP = [(0, 1), (1, 0)]


def flip(block):
    return lax.ppermute(block, SECTION, FLIP)


def beside(block):
    return lax.ppermute(block, ZLO, FLIP)


def scatter_pairs(turn):
    return [
        (core * 4 + a * 2 + b, b * 4 + (core ^ turn) * 2 + a)
        for core in range(2)
        for a in range(2)
        for b in range(2)
    ]


def to_working(block, turn):
    return lax.ppermute(block, (SECTION, ZHI, ZLO), scatter_pairs(turn))


def to_home(block, section, batch):
    turn = section ^ batch
    pairs = [(after, before) for before, after in scatter_pairs(turn) if before // 4 == section]
    return lax.ppermute(block, (SECTION, ZHI, ZLO), pairs)


def home_pair(blocks, core):
    return jnp.stack([
        jnp.where(core == 0, to_home(blocks[0], 0, batch), to_home(blocks[1], 1, batch))
        for batch in range(2)
    ])


def exchange(block, experts, capacity):
    features = block.shape[-1]
    moved = lax.all_to_all(
        block.reshape(experts, capacity, features), RANKS, split_axis=0, concat_axis=0, tiled=True
    )
    return moved.reshape(experts * capacity, features)


def spread_sum(block, axes, parts):
    rows, columns = block.shape
    moved = lax.all_to_all(
        block.reshape(parts, rows // parts, columns), axes, split_axis=0, concat_axis=0, tiled=True
    )
    return jnp.sum(moved.astype(F32), axis=0)


def regroup(block):
    return lax.all_to_all(block, (ZLO, SECTION), split_axis=0, concat_axis=0, tiled=True)


OFFSETS = [(step, place) for place in (0, 3, 1, 2) for step in range(4)]
SENDS = (12, 13, 14, 15, 4, 5, 6, 7, 8, 9, 10, 11, 1, 2, 3)
BATCH = 4
BATCH_ORDER = (0, 3, 2, 1)


def expert_layer(mode, section, *refs):
    forward = mode != BACKWARD
    backward = mode != FORWARD
    refs = list(refs)

    def take(count):
        taken = refs[:count]
        del refs[:count]
        return taken

    weights = take(4)
    outgoing = take(2 if mode == BOTH else 1)
    if mode == BACKWARD:
        saved_rows, saved_activation, saved_slope, unused, unused_1 = take(5)
    returned = take(len(outgoing))
    if mode == FORWARD:
        kept_rows, kept_activation, kept_slope = take(3)
    else:
        grad_in, grad_down = take(2)
    arrived = take(len(outgoing))
    finished = take(len(outgoing))
    w_in, w_down, activation, slope, totals = take(5)
    send_sem, recv_sem, back_send, back_recv, load_sem = take(5)
    if backward:
        parts, staged, part_send, part_recv, out_sem = take(5)

    core = lax.axis_index(SECTION)
    expert = lax.axis_index(EXPERT)
    place = 2 * lax.axis_index(ZHI) + lax.axis_index(ZLO)
    me = expert * 4 + place
    hidden = w_in.shape[1]
    slot_rows, features = arrived[0].shape[1:]
    rows_in_batch = BATCH * slot_rows
    tile = tile_of(hidden)
    tiles = hidden // tile
    peers = []
    ranks = []
    for step, move in OFFSETS:
        to_expert, to_place = across(expert, step), across(place, move)
        ranks.append(to_expert * 4 + to_place)
        peers.append(dict(expert=to_expert, zhi=to_place // 2, zlo=to_place % 2))

    loads = []

    def load(source, target, index):
        copy = pltpu.make_async_copy(source, target, load_sem.at[index])
        copy.start()
        loads.append(copy)

    @pl.when(core == section)
    def own_weights():
        pltpu.make_async_copy(weights[0], w_in, load_sem.at[0]).start()
        pltpu.make_async_copy(weights[1], w_down, load_sem.at[1]).start()

    @pl.when(core != section)
    def other_weights():
        pltpu.make_async_copy(weights[2], w_in, load_sem.at[0]).start()
        pltpu.make_async_copy(weights[3], w_down, load_sem.at[1]).start()

    if mode == BACKWARD:
        load(saved_activation, activation, 2)
        load(saved_slope, slope, 3)

    greet(peers[1:] + ([dict(section=1 - core)] if backward else []))

    sent = []
    for slot in SENDS:
        for kind, block in enumerate(outgoing):
            copy = remote(block.at[ranks[slot]], arrived[kind].at[slot], send_sem.at[kind, slot],
                          recv_sem.at[kind, slot], peers[slot])
            copy.start()
            sent.append(copy)
    for kind, block in enumerate(outgoing):
        arrived[kind][0] = block[me]

    pltpu.make_async_copy(weights[0], w_in, load_sem.at[0]).wait()
    pltpu.make_async_copy(weights[1], w_down, load_sem.at[1]).wait()
    for copy in loads:
        copy.wait()

    saves = []
    for batch in BATCH_ORDER:
        slots = range(batch * BATCH, (batch + 1) * BATCH)
        mine = slice(batch * rows_in_batch, (batch + 1) * rows_in_batch)
        for slot in slots:
            for kind in range(len(outgoing)):
                if slot:
                    remote(arrived[kind].at[slot], arrived[kind].at[slot], send_sem.at[kind, slot],
                           recv_sem.at[kind, slot], peers[slot]).wait_recv()

        def block_of(kind):
            return arrived[kind][slots[0] : slots[-1] + 1].reshape(rows_in_batch, features)

        def one_tile(index, unused):
            spot = pl.ds(pl.multiple_of(index * tile, tile), tile)
            if forward:
                values = mm(block_of(0), w_in[:, spot])
                half = 0.5 * (1.0 + lax.erf(values * 0.7071067811865476))
                bell = jnp.exp(-0.5 * values * values) * 0.3989422804014327
                raised = (values * half).astype(BF16)
                steep = half + values * bell
                activation[mine, spot] = raised
                if mode == FORWARD:
                    slope[mine, spot] = steep.astype(BF16)
                totals[0] += mm(raised, w_down[spot, :])
            else:
                steep = slope[mine, spot].astype(F32)
            if backward:
                lowered = (mm(block_of(len(outgoing) - 1), w_down[spot, :], NT) * steep).astype(BF16)
                slope[mine, spot] = lowered
                totals[len(outgoing) - 1] += mm(lowered, w_in[:, spot], NT)
            return unused

        totals[...] = jnp.zeros_like(totals)
        lax.fori_loop(0, tiles, one_tile, 0)
        for kind in range(len(outgoing)):
            finished[kind][slots[0] : slots[-1] + 1] = (
                totals[kind].astype(BF16).reshape(BATCH, slot_rows, features)
            )
        for slot in slots:
            for kind in range(len(outgoing)):
                if slot:
                    copy = remote(finished[kind].at[slot], returned[kind].at[me], back_send.at[kind, slot],
                                  back_recv.at[kind, slot], peers[slot])
                    copy.start()
                    sent.append(copy)
                else:
                    returned[kind][me] = finished[kind][0]
        if mode == FORWARD:
            for index, (source, target) in enumerate(((activation, kept_activation), (slope, kept_slope))):
                copy = pltpu.make_async_copy(
                    source.at[mine, :], target.at[mine, :], load_sem.at[2 + 2 * batch + index]
                )
                copy.start()
                saves.append(copy)
    if mode == FORWARD:
        kept_rows[...] = arrived[0][...]

    if backward:
        count = slot_rows * len(OFFSETS)
        grads = arrived[len(outgoing) - 1]
        inputs = arrived[0] if forward else saved_rows
        partner = dict(section=1 - core)

        def share_copy(index):
            return remote(parts.at[index], parts.at[index], part_send.at[index], part_recv.at[index], partner)

        def out_copy(step, kind):
            spot = pl.ds(pl.multiple_of(step * tile, tile), tile)
            target = grad_down.at[spot, :] if kind else grad_in.at[:, spot]
            return pltpu.make_async_copy(staged.at[kind], target, out_sem.at[2 * step + kind])

        def one_step(step, unused):
            spot = pl.ds(pl.multiple_of(step * tile, tile), tile)
            for kind in range(2):
                index = 2 * step + kind
                if kind:
                    value = mm(activation[:, spot], grads[...].reshape(count, features), TN)
                else:
                    value = mm(inputs[...].reshape(count, features), slope[:, spot], TN)

                @pl.when(core != section)
                def give():
                    parts[index] = value.astype(BF16)
                    share_copy(index).start()

                @pl.when(core == section)
                def keep():
                    share_copy(index).wait_recv()

                    @pl.when(step >= 1)
                    def drained():
                        out_copy(step - 1, kind).wait()

                    staged[kind] = (value + parts[index].astype(F32)).astype(BF16)
                    out_copy(step, kind).start()
            return unused

        lax.fori_loop(0, tiles, one_step, 0)

    for slot in range(1, len(OFFSETS)):
        for kind in range(len(outgoing)):
            remote(finished[kind].at[slot], returned[kind].at[ranks[slot]], back_send.at[kind, slot],
                   back_recv.at[kind, slot], peers[slot]).wait_recv()
    for copy in sent:
        copy.wait_send()
    for copy in saves:
        copy.wait()
    if backward:
        @pl.when(core != section)
        def given():
            for index in range(2 * tiles):
                share_copy(index).wait_send()

        @pl.when(core == section)
        def stored():
            for kind in range(2):
                out_copy(tiles - 1, kind).wait()


def run_expert_layer(mode, section, weights, outgoing, saved=(), grads=()):
    ranks, slot_rows, features = outgoing[0].shape
    hidden = weights[0].shape[1]
    count = ranks * slot_rows
    tile = tile_of(hidden)
    kinds = len(outgoing)
    anywhere = pl.BlockSpec(memory_space=pl.ANY)
    local = pl.BlockSpec(memory_space=pltpu.VMEM)
    block = shape((ranks, slot_rows, features), BF16)
    wide = shape((count, hidden), BF16)
    in_specs = [anywhere] * 4 + [local] * kinds
    operands = [*weights, *outgoing]
    out_shape = [block] * kinds
    out_specs = [local] * kinds
    aliases = {}
    if mode == FORWARD:
        out_shape += [block, wide, wide]
        out_specs += [local, anywhere, anywhere]
    else:
        out_shape += [shape((features, hidden), BF16), shape((hidden, features), BF16)]
        out_specs += [anywhere, anywhere]
    if mode == BACKWARD:
        aliases = {len(operands) + 3: kinds, len(operands) + 4: kinds + 1}
        operands += [*saved, *grads]
        in_specs += [local, anywhere, anywhere, anywhere, anywhere]
    scratch = [pltpu.VMEM(block.shape, BF16)] * (2 * kinds) + [
        pltpu.VMEM((features, hidden), BF16), pltpu.VMEM((hidden, features), BF16),
        pltpu.VMEM((count, hidden), BF16), pltpu.VMEM((count, hidden), BF16),
        pltpu.VMEM((kinds, BATCH * slot_rows, features), F32),
        pltpu.SemaphoreType.DMA((kinds, ranks)), pltpu.SemaphoreType.DMA((kinds, ranks)),
        pltpu.SemaphoreType.DMA((kinds, ranks)), pltpu.SemaphoreType.DMA((kinds, ranks)),
        pltpu.SemaphoreType.DMA((10,)),
    ]
    if mode != FORWARD:
        pieces = 2 * hidden // tile
        scratch += [
            pltpu.VMEM((pieces, features, tile), BF16), pltpu.VMEM((2, features, tile), BF16),
            pltpu.SemaphoreType.DMA((pieces,)), pltpu.SemaphoreType.DMA((pieces,)),
            pltpu.SemaphoreType.DMA((pieces,)),
        ]
    return pl.pallas_call(
        functools.partial(expert_layer, mode, section),
        name="expert_layer_" + mode,
        in_specs=in_specs,
        out_specs=out_specs,
        out_shape=out_shape,
        scratch_shapes=scratch,
        input_output_aliases=aliases,
        compiler_params=pltpu.CompilerParams(
            collective_id={FORWARD: 1, BOTH: 2, BACKWARD: 3}[mode], has_side_effects=True,
            vmem_limit_bytes=VMEM_LIMIT,
        ),
        cost_estimate=pl.CostEstimate(
            flops=8 * kinds * count * features * hidden, bytes_accessed=160 << 20, transcendentals=0
        ),
    )(*operands)


class Sizes:
    def __init__(self, **sizes):
        self.__dict__.update(sizes)
        self.width = self.heads * self.size
        self.length = GROUP * self.span
        self.slots = self.experts * self.capacity
        self.attention = (self.span, self.heads, self.size, self.spacing, self.ranks)
        self.base = 3 * self.width // 128 * 128
        self.offset = 3 * self.width - self.base
        self.table_lane = self.offset + self.experts + 2


def unpack_small(sizes, early, section):
    tail = early[section, :, :, sizes.base :]
    tail = tail.reshape(sizes.features, tail.shape[2])
    tail_t = tail.astype(F32).T
    first = sizes.offset + sizes.experts
    bucket = lax.broadcasted_iota(jnp.int32, (sizes.buckets, sizes.features), 0)
    target = bucket // sizes.table_rows * sizes.shard_rows + bucket % sizes.table_rows
    spot = target == lax.broadcasted_iota(jnp.int32, (sizes.buckets, sizes.features), 1)
    table = mm(spot.astype(BF16), tail).astype(BF16)
    router = tail[:, sizes.offset : first]
    return router, tail_t[first : first + 1, :], tail_t[first + 1 : first + 2, :], table


def qkv_columns(sizes, early, section):
    return early[section, :, :, : 3 * sizes.width].reshape(sizes.features, 3 * sizes.width)


def out_rows(sizes, w_outs, section, group):
    per_group = sizes.ranks // GROUP
    rows = w_outs[section, group * per_group : (group + 1) * per_group]
    return rows.reshape(sizes.width, sizes.features)


def whereabouts():
    core, zhi, zlo = (lax.axis_index(name) for name in (SECTION, ZHI, ZLO))
    return core, zhi, zlo, 2 * zhi + zlo, 2 * zlo + core


def line_peers(core, place):
    peers = []
    for move in range(4):
        spot = across(place, move)
        for turn in range(2):
            if move or turn:
                peers.append(dict(section=1 - core if turn else core, zhi=spot // 2, zlo=spot % 2))
    return peers


class Regroup:
    def __init__(self, block, target, send, recv):
        self.block, self.target, self.send, self.recv = block, target, send, recv
        self.core, unused, self.zlo, unused_1, self.mine = whereabouts()
        self.copies = []

    def start(self, rows):
        for turn, move in ((0, 1), (1, 1), (1, 0)):
            to_core = 1 - self.core if turn else self.core
            to_zlo = 1 - self.zlo if move else self.zlo
            index = len(self.copies)
            copy = remote(self.block.at[2 * to_zlo + to_core, rows], self.target.at[self.mine, rows],
                          self.send.at[index], self.recv.at[index], dict(section=to_core, zlo=to_zlo))
            copy.start()
            self.copies.append(copy)
        self.target[self.mine, rows] = self.block[self.mine, rows]

    def wait(self):
        for copy in self.copies:
            copy.wait()


class WeightGather:
    def __init__(self, blocks, shard, early, w_outs, staged, sems):
        (self.early_send, self.early_recv, self.stage_send, self.stage_recv, self.local_sem,
         self.out_send, self.out_recv) = sems
        self.blocks, self.shard, self.early, self.w_outs, self.staged = blocks, shard, early, w_outs, staged
        self.core, unused, self.zlo, self.place, unused_1 = whereabouts()
        self.other = 1 - self.core
        self.expert = lax.axis_index(EXPERT)
        self.beside_x = across(self.expert, 1)
        self.beside_y = across(self.expert, 2)
        self.places = [across(self.place, move) for move in range(4)]
        self.sections = (self.core, self.other)
        self.started = []
        self.early_count = self.out_count = 0

    def at(self, section, owner, spot):
        return self.early.at[section, owner * 4 + spot]

    def send(self, source, section, owner, spot, peer):
        copy = remote(source, self.at(section, owner, spot), self.early_send.at[self.early_count],
                      self.early_recv.at[section, owner * 4 + spot], peer)
        self.early_count += 1
        copy.start()
        self.started.append(copy)

    def arrived(self, section, owner, spot):
        block = self.at(section, owner, spot)
        remote(block, block, self.early_send.at[0], self.early_recv.at[section, owner * 4 + spot],
               dict(section=self.other)).wait_recv()

    def out_at(self, section, owner, spot):
        return self.w_outs.at[section, owner * 4 + spot]

    def send_out(self, source, owner, spot, peer):
        copy = remote(source, self.out_at(self.core, owner, spot), self.out_send.at[self.out_count],
                      self.out_recv.at[self.core, owner * 4 + spot], peer)
        self.out_count += 1
        copy.start()
        self.started.append(copy)

    def out_arrived(self, section, owner, spot):
        block = self.out_at(section, owner, spot)
        remote(block, block, self.out_send.at[0], self.out_recv.at[section, owner * 4 + spot],
               dict(section=self.other)).wait_recv()

    def trade(self):
        self.trades = []
        for parity in range(2):
            copy = remote(self.blocks.at[2 * parity + self.other], self.staged.at[parity],
                          self.stage_send.at[parity], self.stage_recv.at[parity], dict(section=self.other))
            copy.start()
            self.trades.append(copy)

    def start(self):
        for which, section in enumerate(self.sections):
            if which:
                for copy in self.trades:
                    copy.wait()

            def block_for(parity):
                return self.staged.at[parity] if which else self.blocks.at[2 * parity + self.core]

            for spot in self.places[1:]:
                self.send(block_for(spot % 2), section, self.expert, self.place,
                          dict(zhi=spot // 2, zlo=spot % 2))
            for peer in (self.beside_x, self.beside_y):
                self.send(block_for(self.zlo), section, self.expert, self.place, dict(expert=peer))
            local = pltpu.make_async_copy(
                block_for(self.zlo), self.at(section, self.expert, self.place), self.local_sem
            )
            local.start()
            local.wait()

    def along_z(self):
        for spot in self.places[1:]:
            for section in self.sections:
                self.arrived(section, self.expert, spot)
                for peer in (self.beside_x, self.beside_y):
                    self.send(self.at(section, self.expert, spot), section, self.expert, spot, dict(expert=peer))

    def over_plane(self):
        for section in self.sections:
            for step, spot in enumerate(self.places):
                self.arrived(section, self.beside_x, spot)
                self.arrived(section, self.beside_y, spot)
                source, peer = ((self.beside_x, self.beside_y), (self.beside_y, self.beside_x))[step % 2]
                self.send(self.at(section, source, spot), section, source, spot, dict(expert=peer))

    def finish_early(self):
        diagonal = 3 - self.expert
        for section in self.sections:
            for spot in self.places:
                self.arrived(section, diagonal, spot)

    def out_start(self):
        for spot in self.places[1:]:
            self.send_out(self.shard, self.expert, self.place, dict(zhi=spot // 2, zlo=spot % 2))
        for peer in (self.beside_x, self.beside_y):
            self.send_out(self.shard, self.expert, self.place, dict(expert=peer))
        self.send_out(self.shard, self.expert, self.place, dict(section=self.other))
        local = pltpu.make_async_copy(
            self.shard, self.out_at(self.core, self.expert, self.place), self.local_sem
        )
        local.start()
        local.wait()

    def out_pass(self, owner, spot, peers):
        block = self.out_at(self.core, owner, spot)
        self.out_arrived(self.core, owner, spot)
        for peer in peers + [dict(section=self.other)]:
            self.send_out(block, owner, spot, peer)

    def out_along_z(self):
        for spot in self.places[1:]:
            self.out_pass(self.expert, spot, [dict(expert=self.beside_x), dict(expert=self.beside_y)])

    def out_over_plane(self):
        for step, spot in enumerate(self.places):
            self.out_pass(self.beside_x, spot, [dict(expert=self.beside_y)] if step % 2 == 0 else [])
            self.out_pass(self.beside_y, spot, [dict(expert=self.beside_x)] if step % 2 else [])

    def out_finish(self):
        for spot in self.places:
            self.out_pass(3 - self.expert, spot, [])

    def out_all(self):
        for owner in range(4):
            for spot in range(4):
                self.out_arrived(self.other, owner, spot)

    def close(self):
        for copy in self.started:
            copy.wait_send()


def assemble(sizes, route_rows, qkv_shard, router_shard, gain_shard, table_shard, blocks, home_routes):
    rows, features, width = sizes.shard_rows, sizes.features, sizes.width

    def below(block, count):
        return jnp.concatenate([block, jnp.zeros((count - block.shape[0], block.shape[1]), F32)], axis=0)

    small = [
        router_shard[...].astype(F32).T, below(gain_shard[...].astype(F32), 8).T[:, :2],
        below(table_shard[...].astype(F32), rows),
    ]
    spare = blocks.shape[2] - 3 * width - sum(part.shape[1] for part in small)
    small.append(jnp.zeros((rows, spare), F32))
    for member in range(GROUP):
        parts = [
            qkv_shard[:, part * features + member * width : part * features + (member + 1) * width].astype(F32)
            for part in range(3)
        ]
        blocks[member] = jnp.concatenate(parts + small, axis=1).astype(BF16)
    for batch in range(2):
        home_routes[batch] = below(route_rows[batch].astype(F32), 8)


def attend(section, sizes, *refs):
    refs = list(refs)

    def take(count):
        taken = refs[:count]
        del refs[:count]
        return taken

    if section == 0:
        home_inputs, route_rows, qkv_shard, shard, router_shard, gain_shard, table_shard = take(7)
    else:
        returned, aux_before, middle_before, early, w_outs, routes, given = take(7)
    outcome, mixed, gathered, stats, outgoing, middle, normed_two, aux, attended = take(9)
    if section == 0:
        early, w_outs, routes = take(3)
    else:
        result, difference, spread = take(3)
    vectors, bias, pair_send, pair_recv, group_send, group_recv = take(6)
    span = sizes.span
    core, zhi, zlo, place, group = whereabouts()
    expert = lax.axis_index(EXPERT)

    def rows_of(piece):
        return pl.ds(pl.multiple_of(piece * span, span), span)

    if section == 0:
        blocks, home_routes = refs[-2:]
        assemble(sizes, route_rows, qkv_shard, router_shard, gain_shard, table_shard, blocks, home_routes)
    own, flipped = group, 2 * zlo + 1 - core
    side, side_flipped = 2 * (1 - zlo) + core, 2 * (1 - zlo) + 1 - core
    partner, beside_z = dict(section=1 - core), dict(zlo=1 - zlo)
    greet(line_peers(core, place)
          + ([dict(expert=across(expert, 1)), dict(expert=across(expert, 2))] if section == 0 else []))

    pair_copies = []

    def pass_piece(piece, index, peer):
        block = gathered.at[rows_of(piece)]
        copy = remote(block, block, pair_send.at[index], pair_recv.at[index], peer)
        copy.start()
        pair_copies.append(copy)

    def half_of(piece, part):
        return pl.ds(pl.multiple_of(piece * span + part * (span // 2), span // 2), span // 2)

    def pass_half(part, values):
        gathered[half_of(own, part), :] = values
        block = gathered.at[half_of(own, part)]
        copy = remote(block, block, pair_send.at[3 * part], pair_recv.at[3 * part], beside_z)
        copy.start()
        pair_copies.append(copy)

    def await_side():
        if section == 0:
            await_piece(side, 0)
            return
        for part in range(2):
            block = gathered.at[half_of(side, part)]
            remote(block, block, pair_send.at[3 * part], pair_recv.at[3 * part], partner).wait_recv()

    def await_piece(piece, index):
        block = gathered.at[rows_of(piece)]
        remote(block, block, pair_send.at[index], pair_recv.at[index], partner).wait_recv()

    if section == 0:
        staged, home_send, home_recv = take(3)
        home_rows = home_inputs.at[core]
        gather = WeightGather(blocks, shard, early, w_outs, staged, take(7))
        gather.trade()
        aligned = (zlo == zhi) & (zlo == core)

        def to_work(source, target, index, slot, turn):
            peer = dict(section=zlo, zhi=1 - core if turn else core, zlo=zhi)
            return remote(source, target, home_send.at[index], home_recv.at[slot], peer)

        rows_copy = to_work(home_rows, gathered.at[rows_of(place)], 0, 0, 0)
        route_copies = [
            to_work(home_routes.at[1 - core if turn else core], routes.at[core], 1 + turn, 1 + core, turn)
            for turn in range(2)
        ]

        @pl.when(aligned)
        def keep():
            gathered[rows_of(place), :] = home_inputs[core]
            routes[core] = home_routes[core]

        @pl.when(jnp.logical_not(aligned))
        def give():
            rows_copy.start()
            route_copies[0].start()

        route_copies[1].start()
        gather.start()

        @pl.when(jnp.logical_not(aligned))
        def landed():
            rows_copy.wait_recv()

        pass_piece(own, 0, beside_z)
        pass_piece(own, 1, partner)
        gather.along_z()
        gather.over_plane()
        gather.out_start()
        await_side()
        pass_piece(side, 2, partner)
        gather.finish_early()
    else:
        for part in range(2):
            some = slice(part * span // 2, (part + 1) * span // 2)
            total, gap = combined(returned[...], aux_before[some, :], middle_before[some, :])
            result[some, :] = total.astype(BF16)
            difference[some, :] = gap
            pass_half(part, total.astype(BF16))
        pass_piece(own, 1, partner)

    router, gain_one, gain_two, table = unpack_small(sizes, early, section)
    fill_bias(group * sizes.heads + sizes.table_lane, sizes.heads, table, vectors, bias, span, sizes.spacing)
    weight = qkv_columns(sizes, early, section)
    project(gathered, rows_of(own), gain_one, weight, mixed)
    await_piece(flipped, 1)
    project(gathered, rows_of(flipped), gain_one, weight, mixed)
    if section:
        await_side()
        pass_piece(side, 2, partner)
    project(gathered, rows_of(side), gain_one, weight, mixed)
    await_piece(side_flipped, 2)
    project(gathered, rows_of(side_flipped), gain_one, weight, mixed)
    trade = Regroup(outcome, attended, group_send, group_recv)
    for head in range(sizes.heads):
        if section == 0 and 0 < head < 3:
            (gather.out_along_z, gather.out_over_plane)[head - 1]()
        attend_head(sizes.attention, head, mixed, bias, outcome, stats)
        trade.start(slice(head * sizes.size, (head + 1) * sizes.size))
    if section == 0:
        for stage in (gather.out_along_z, gather.out_over_plane)[max(sizes.heads - 1, 0) :]:
            stage()
        gather.out_finish()
        for which in range(2):
            @pl.when(jnp.logical_not(aligned & (core == which)))
            def routed():
                remote(routes.at[which], routes.at[which], home_send.at[1], home_recv.at[1 + which],
                       partner).wait_recv()
    columns_t = routes[section].T
    columns = [columns_t[:, k : k + 1] for k in range(2)]
    masks = route_masks(columns, sizes.experts)
    places = slot_places(columns, masks, sizes.capacity)
    if section == 0:
        gather.out_all()
    total = gathered[rows_of(own), :].astype(F32)
    trade.wait()
    for member in range(GROUP):
        total = total + mm(attended[member], out_rows(sizes, w_outs, section, member), TN)
    middle[...] = total
    packed, hot = dispatch(total, gain_two, router, masks, places, sizes.slots, outgoing, normed_two, aux)
    if section:
        spread[...] = spread_values(given[...].astype(F32), packed, sizes.slots, hot)
    for copy in pair_copies:
        copy.wait_send()
    if section == 0:
        gather.close()

        @pl.when(jnp.logical_not(aligned))
        def given_away():
            rows_copy.wait_send()
            route_copies[0].wait_send()

        route_copies[1].wait_send()


def run_attend(section, sizes, operands, collective):
    dma = pltpu.SemaphoreType.DMA
    span, features, width = sizes.span, sizes.features, sizes.width
    outs = [
        shape((GROUP, width, span), BF16), shape((sizes.length, 3 * width), BF16),
        shape((sizes.length, features), BF16), shape((8, sizes.length), F32),
        shape((sizes.slots, features), BF16), shape((span, features), F32), shape((span, features), BF16),
        shape((span, 128), F32), shape((GROUP, width, span), BF16),
    ]
    scratch = [
        pltpu.VMEM((128, 2 * span * GROUP), F32), pltpu.VMEM((sizes.heads * GROUP, span, span), F32),
        dma((4,)), dma((4,)), dma((3 * sizes.heads,)), dma((3 * sizes.heads,)),
    ]
    if section == 0:
        rows = sizes.shard_rows
        columns = -(-(3 * width + sizes.experts + 2 + sizes.heads * GROUP) // 128) * 128
        outs += [
            shape((2, sizes.ranks, rows, columns), BF16), shape((2, sizes.ranks, rows, features), BF16),
            shape((2, 8, span), F32),
        ]
        scratch += [
            pltpu.VMEM((2, rows, columns), BF16), dma((3,)), dma((3,)),
            dma((30,)), dma((2, sizes.ranks)), dma((2,)), dma((2,)), dma, dma((34,)), dma((2, sizes.ranks)),
            pltpu.VMEM((GROUP, rows, columns), BF16), pltpu.VMEM((2, 8, span), F32),
        ]
    else:
        outs += [shape((span, features), BF16), shape((span, features), F32), shape((sizes.slots, features), BF16)]
    return call(
        functools.partial(attend, section, sizes), "attend", outs, operands, scratch=scratch,
        flops=6 << 30, collective=collective,
    )


def unpack(sizes, home, owned, shared, outputs, section_outputs, stream_grads, grad_qkv, grad_out, grad_router, grad_gains, grad_table):
    width, features, experts = sizes.width, sizes.features, sizes.experts
    section_outputs[...] = outputs[...]
    stream_grads[...] = home[...].astype(F32)
    grad_qkv[...] = jnp.concatenate(
        [owned[member, :, part * width : (part + 1) * width] for part in range(3) for member in range(GROUP)],
        axis=1,
    )
    grad_out[...] = shared[:, :features]
    tail = shared[:, features:]
    grad_router[...] = tail.T[:experts, :]
    ends = [owned[member, :, sizes.base :] for member in range(GROUP)]
    grad_table[...] = jnp.concatenate(
        [end[: sizes.table_rows, sizes.offset : sizes.offset + sizes.heads] for end in ends], axis=1
    )
    spot = sizes.offset + 8
    grad_gains[0:1, :] = (ends[0] + ends[1] + ends[2] + ends[3]).T[spot : spot + 1, :]
    grad_gains[1:2, :] = tail.T[experts : experts + 1, :]


class Homes:
    def __init__(self, home, send, recv):
        self.home, self.send_sem, self.recv_sem = home, send, recv
        self.core, self.zhi, self.zlo, unused, unused_1 = whereabouts()
        self.aligned = (self.zlo == self.zhi) & (self.zlo == self.core)
        self.sent = []

    def copy(self, block, section, index):
        return remote(block, self.home.at[self.zhi], self.send_sem.at[index], self.recv_sem.at[self.zhi],
                      dict(section=section, zhi=self.zlo, zlo=self.core))

    def send(self, block, section):
        index = len(self.sent)
        here = self.aligned & (self.core == section)
        self.sent.append((block, section))

        @pl.when(here)
        def keep():
            self.home[self.zhi] = block[...]

        @pl.when(jnp.logical_not(here))
        def give():
            self.copy(block, section, index).start()

    def close(self):
        for batch in range(2):
            @pl.when(jnp.logical_not(self.aligned & (self.zhi == batch)))
            def landed():
                block = self.home.at[batch]
                remote(block, block, self.send_sem.at[0], self.recv_sem.at[batch],
                       dict(section=1 - self.core)).wait_recv()
        for index, (block, section) in enumerate(self.sent):
            @pl.when(jnp.logical_not(self.aligned & (self.core == section)))
            def left():
                self.copy(block, section, index).wait_send()


class PlaneSum:
    def __init__(self, source, shares, send, recv):
        self.source, self.shares = source, shares
        self.expert = lax.axis_index(EXPERT)
        self.copies = []
        for step in range(1, 4):
            spot = across(self.expert, step)
            copy = remote(source.at[pl.ds(4 * spot, 4)], shares.at[step - 1], send.at[step - 1],
                          recv.at[step - 1], dict(expert=spot))
            copy.start()
            self.copies.append(copy)

    def total(self):
        for copy in self.copies:
            copy.wait()
        total = self.source[pl.ds(4 * self.expert, 4)].astype(F32)
        for step in range(3):
            total = total + self.shares[step].astype(F32)
        return total.astype(BF16)


def attend_back(section, sizes, *refs):
    refs = list(refs)

    def take(count):
        taken = refs[:count]
        del refs[:count]
        return taken

    last = section == 0
    early, mixed, stats, outcome, gathered = take(5)
    if last:
        middle_grad, attended_grad, first_low, *shared, other_qkv = take(6)
        home, owned, owned_shared, = take(3)
    else:
        (returned, returned_grad, aux, middle, given, normed_two, attended, w_outs, routes,
         first_result, next_aux) = take(11)
        shared_grad, low, qkv_grad, home, spread = take(5)
    vectors, bias, *work = take(8)
    (grads, kept, leaving, sent, partner_share, side_share, group_send, group_recv, pair_send, pair_recv,
     home_send, home_recv) = take(12)
    mixed_grad, strips = work[0], work[5]
    span, features, width = sizes.span, sizes.features, sizes.width
    core, zhi, zlo, place, group = whereabouts()
    expert = lax.axis_index(EXPERT)
    if last:
        (low, qkv_grad, other_shares, qkv_shares, shared_in, shared_sum, shared_shares, line_totals, pieces,
         shared_totals, shared_parts, other_send, other_recv, plane_send, plane_recv, in_send, in_recv,
         shared_send, shared_recv, line_send, line_recv, spread_send, spread_recv) = take(23)
    else:
        middle_grad, attended_grad, second_result = take(3)
    greet(line_peers(core, place) + ([dict(expert=across(expert, step)) for step in range(1, 4)] if last else []))
    homes = Homes(home, home_send, home_recv)
    router, gain_one, gain_two, table = unpack_small(sizes, early, 0)
    trade = Regroup(attended_grad, grads, group_send, group_recv)
    if not last:
        homes.send(first_result, 0)
        total, difference = combined(returned[...], aux[...], middle[...])
        second_result[...] = total.astype(BF16)
        token_backward(
            returned_grad[...], aux[...], given[...].astype(F32), difference, middle[...], normed_two[...],
            attended, gain_two, router, lambda member: out_rows(sizes, w_outs, 0, member),
            route_columns(routes[section].T), middle_grad, attended_grad, shared_grad,
            hook=lambda: trade.start(slice(None)),
        )
    else:
        trade.start(slice(None))
    if last:
        partner = dict(section=1 - core)
        for which in range(2):
            @pl.when(core != which)
            def pass_share():
                remote(shared[which], shared_in, in_send, in_recv, partner).start()

        other_sum = PlaneSum(other_qkv, other_shares, other_send, other_recv)
        homes.send(first_low, 1)
    else:
        homes.send(second_result, 1)
    strips[...] = jnp.zeros_like(strips)
    fill_bias(group * sizes.heads + sizes.table_lane, sizes.heads, table, vectors, bias, span, sizes.spacing)
    if last:
        remote(shared[0], shared_in, in_send, in_recv, partner).wait_recv()
        for which in range(2):
            @pl.when(core == which)
            def add_share():
                shared_sum[...] = shared[which][...] + shared_in[...]

        plane_shared = PlaneSum(shared_sum, shared_shares, shared_send, shared_recv)
        line_copies = []

        def to_owners(owner_section, totals):
            line_totals[owner_section] = totals
            turn = (core + owner_section) % 2
            mine = 2 * place + core
            for move in range(4):
                spot = across(place, move)
                copy = remote(line_totals.at[owner_section, spot], pieces.at[mine],
                              line_send.at[owner_section, move], line_recv.at[turn, move],
                              dict(section=owner_section, zhi=spot // 2, zlo=spot % 2))
                line_copies.append((copy, owner_section, move))
                if move:
                    copy.start()
                else:
                    @pl.when(core != owner_section)
                    def give():
                        copy.start()

                    @pl.when(core == owner_section)
                    def keep():
                        pieces[mine] = line_totals[owner_section, place]

    trade.wait()
    for head in range(sizes.heads):
        if last and head == sizes.heads - 1:
            to_owners(1, other_sum.total())
        back_head(sizes.attention, head, mixed, stats, outcome, grads, bias, work)
    weight = qkv_columns(sizes, early, 0)

    def rows_of(piece):
        return pl.ds(pl.multiple_of(piece * span, span), span)

    def piece_back(piece):
        return back_piece(sizes.attention, gathered, rows_of(piece), gain_one, weight, mixed_grad)

    back, gain_total = piece_back(2 * zlo + 1 - core)
    sent[0] = back.astype(BF16)
    back, gain_part = piece_back(2 * (1 - zlo) + 1 - core)
    sent[1] = back.astype(BF16)
    partner_copy = remote(sent, partner_share, pair_send.at[0], pair_recv.at[0], dict(section=1 - core))
    partner_copy.start()
    gain_total = gain_total + gain_part
    leave, gain_part = piece_back(2 * (1 - zlo) + core)
    gain_total = gain_total + gain_part
    partner_copy.wait()
    leaving[...] = (leave + partner_share[1].astype(F32)).astype(BF16)
    stay, gain_part = piece_back(group)
    side_copy = remote(leaving, side_share, pair_send.at[1], pair_recv.at[1], dict(zlo=1 - zlo))
    side_copy.start()
    gain_total = gain_total + gain_part
    kept[...] = stay + partner_share[0].astype(F32)
    columns = qkv_grad.shape[2]
    weights = weight_share(sizes.attention, gathered, gain_one, mixed_grad).astype(BF16)
    extra = extra_columns(sizes.attention, sizes.buckets, features, strips, gain_total)
    by_rank = (sizes.ranks, sizes.shard_rows)
    qkv_grad[:, :, 3 * width :] = jnp.concatenate(
        [extra, jnp.zeros((features, columns - 3 * width - 16), BF16)], axis=1
    ).reshape(*by_rank, columns - 3 * width)
    qkv_grad[:, :, : 3 * width] = weights.reshape(*by_rank, 3 * width)
    if last:
        qkv_sum = PlaneSum(qkv_grad, qkv_shares, plane_send, plane_recv)
        shared_totals[...] = plane_shared.total()
        for move in range(4):
            spot = across(place, move)
            if move:
                copy = remote(shared_totals.at[spot], shared_parts.at[move], spread_send.at[move],
                              spread_recv.at[move], dict(zhi=spot // 2, zlo=spot % 2))
                copy.start()
                line_copies.append((copy, None, move))
            else:
                shared_parts[0] = shared_totals[place]
    side_copy.wait()
    own = gathered[rows_of(group), :].astype(F32)
    back, unused = norm_backward(own, gain_one, kept[...] + side_share[...].astype(F32))
    total = (middle_grad[...] + back).astype(BF16)
    low[...] = total
    if not last:
        spread[...] = spread_values(total.astype(F32), next_aux[...], sizes.slots)
    else:
        homes.send(low, 0)
        to_owners(0, qkv_sum.total())
        for turn in range(2):
            for move in range(4):
                if move or turn:
                    block = pieces.at[2 * across(place, move) + (1 - core if turn else core)]
                    remote(block, block, line_send.at[0, 0], line_recv.at[turn, move], partner).wait_recv()
        for member in range(GROUP):
            owned[member] = pieces[member].astype(F32) + pieces[GROUP + member].astype(F32)
        for copy, owner_section, move in line_copies:
            if owner_section is None:
                copy.wait()
            elif move:
                copy.wait_send()
            else:
                @pl.when(core != owner_section)
                def gone():
                    copy.wait_send()
        owned_shared[...] = sum(shared_parts[move].astype(F32) for move in range(4))
        remote(shared[0], shared_in, in_send, in_recv, partner).wait_send()
    homes.close()


def run_attend_back(section, sizes, operands, picks, collective):
    dma = pltpu.SemaphoreType.DMA
    span, features, width, ranks = sizes.span, sizes.features, sizes.width, sizes.ranks
    rows = sizes.shard_rows
    columns = -(-(3 * width + 16) // 128) * 128
    tail = features + -(-(sizes.experts + 1) // 128) * 128
    block = (span, features)
    last = section == 0
    if last:
        outs = [shape((2, *block), BF16), shape((GROUP, rows, columns), F32), shape((rows, tail), F32)]
    else:
        outs = [shape((features, tail), BF16), shape(block, BF16), shape((ranks, rows, columns), BF16),
                shape((2, *block), BF16), shape((sizes.slots, features), BF16)]
    scratch = [
        pltpu.VMEM((128, 2 * span * GROUP), F32), pltpu.VMEM((sizes.heads * GROUP, span, span), F32),
        pltpu.VMEM((sizes.length, 3 * width), BF16), pltpu.VMEM((GROUP, span, span), F32),
        pltpu.VMEM((sizes.length, sizes.size), F32), pltpu.VMEM((sizes.length, sizes.size), F32),
        pltpu.VMEM((sizes.size, sizes.length), F32), pltpu.VMEM((8, GROUP * 2 * 128), F32),
        pltpu.VMEM((GROUP, width, span), BF16), pltpu.VMEM(block, F32), pltpu.VMEM(block, BF16),
        pltpu.VMEM((2, *block), BF16), pltpu.VMEM((2, *block), BF16), pltpu.VMEM(block, BF16),
        dma((3,)), dma((3,)), dma((2,)), dma((2,)), dma((2,)), dma((2,)),
    ]
    if last:
        scratch += [
            pltpu.VMEM(block, BF16), pltpu.VMEM((ranks, rows, columns), BF16),
            pltpu.VMEM((3, 4, rows, columns), BF16), pltpu.VMEM((3, 4, rows, columns), BF16),
            pltpu.VMEM((ranks, rows, tail), BF16), pltpu.VMEM((ranks, rows, tail), BF16),
            pltpu.VMEM((3, 4, rows, tail), BF16), pltpu.VMEM((2, 4, rows, columns), BF16),
            pltpu.VMEM((2 * GROUP, rows, columns), BF16), pltpu.VMEM((4, rows, tail), BF16),
            pltpu.VMEM((4, rows, tail), BF16),
            dma((3,)), dma((3,)), dma((3,)), dma((3,)), dma, dma, dma((3,)), dma((3,)),
            dma((2, 4)), dma((2, 4)), dma((4,)), dma((4,)),
        ]
    else:
        scratch += [pltpu.VMEM(block, F32), pltpu.VMEM((GROUP, width, span), BF16), pltpu.VMEM(block, BF16)]
    return call(
        functools.partial(attend_back, section, sizes), "attend_back", outs, operands, scratch=scratch,
        flops=10 << 30, collective=collective, picks=picks,
    )


def per_device(inputs, cotangent, qkv_shard, out_shard, router_shard, gain_shard, table_shard,
               w_expert_in, w_expert_out, routes):
    core = lax.axis_index(SECTION)
    zhi = lax.axis_index(ZHI)
    zlo = lax.axis_index(ZLO)
    span, features = inputs.shape[2:]
    ranks = lax.axis_size(RANKS)
    shard_rows = qkv_shard.shape[1]
    experts = router_shard.shape[2]
    table_rows, head_count = table_shard.shape[1:]
    buckets = table_rows * ranks
    heads = head_count // GROUP
    size = features // head_count
    width = heads * size
    spacing = GROUP * span // buckets
    capacity = max(2, 4 * span // experts)
    slots = experts * capacity
    group = 2 * zlo + core
    sizes = (span, heads, size, spacing, ranks)
    ids = jnp.stack([
        group, 2 * zlo + 1 - core, 2 * (1 - zlo) + core, 2 * (1 - zlo) + 1 - core, group,
        group, 2 * (1 - zlo) + core, 2 * zlo + 1 - core, 2 * (1 - zlo) + 1 - core,
    ]).astype(jnp.int32)
    core_id = core.astype(jnp.int32).reshape(1)

    w_in = w_expert_in[0, 0]
    w_down = w_expert_out[0, 0]
    w_in_other = flip(w_in)
    w_down_other = flip(w_down)
    fused = lax.axis_size(EXPERT) == 4 and features == tile_of(w_in.shape[1])
    shared_sizes = Sizes(
        span=span, heads=heads, size=size, spacing=spacing, ranks=ranks, experts=experts, capacity=capacity,
        features=features, buckets=buckets, shard_rows=shard_rows, table_rows=table_rows,
    )

    home_rows = lax.dynamic_index_in_dim(inputs, core, 0, keepdims=False)[0]
    given = to_working(lax.dynamic_index_in_dim(cotangent, core, 0, keepdims=False)[0], 0)
    if not fused:
        own = to_working(home_rows, 0)
        route_parts = [
            to_working(lax.dynamic_index_in_dim(routes[0], core ^ turn, 0, keepdims=False)[0], turn)
            for turn in range(2)
        ]
        section_routes = [
            jnp.where(zhi == section, route_parts[0], route_parts[1]) for section in range(2)
        ]

    if fused:
        first = run_attend(
            0, shared_sizes,
            [inputs[:, 0], jnp.swapaxes(routes[0, :, 0], 1, 2), qkv_shard[0], out_shard[0],
             router_shard[0].T, gain_shard[0],
             table_shard[0]], 4)
        early_all, w_out_all, route_all = first[9:]
    else:
        small = jnp.concatenate([
            router_shard[0],
            gain_shard[0].T,
            jnp.pad(table_shard[0], ((0, shard_rows - table_rows), (0, 0))),
        ], axis=1)
        by_group = jnp.transpose(
            qkv_shard[0].reshape(shard_rows, 3, GROUP, width), (2, 0, 1, 3)
        ).reshape(GROUP, shard_rows, 3 * width)
        by_group = jnp.concatenate(
            [by_group, jnp.broadcast_to(small[None], (GROUP, *small.shape))], axis=2
        )
        by_group = jnp.pad(by_group, ((0, 0), (0, 0), (0, -by_group.shape[2] % 128)))
        columns = by_group.shape[2]
        whole_early = lax.all_gather(by_group, RANKS, axis=1, tiled=True)
        kept = lax.dynamic_index_in_dim(whole_early, group, 0, keepdims=False)
        traded = flip(lax.dynamic_index_in_dim(whole_early, 2 * zlo + 1 - core, 0, keepdims=False))
        early = [
            jnp.where(core == section, kept, traded).reshape(features, columns) for section in range(2)
        ]
        w_out_own = lax.all_gather(out_shard[0], RANKS, axis=0, tiled=True)
        w_out_other = flip(w_out_own)
        w_outs = [jnp.where(core == which, w_out_own, w_out_other) for which in range(2)]
    expert_weights = (w_in, w_down, w_in_other, w_down_other)

    def by_rank(block):
        return block.reshape(ranks, capacity, features)

    def by_slot(block):
        return block.reshape(slots, features)

    weights = []
    for section in range(0 if fused else 2):
        is_own = core == section
        others = early[section][:, 3 * width :]
        router = others[:, :experts]
        gains = others[:, experts : experts + 2].T
        table = others[:, experts + 2 : experts + 2 + head_count]
        table = table.reshape(ranks, shard_rows, head_count)[:, :table_rows].reshape(buckets, head_count)
        weights.append((
            early[section], router, gains[0:1], gains[1:2], table,
            jnp.where(is_own, w_in, w_in_other), jnp.where(is_own, w_down, w_down_other),
        ))

    bias_scratch = [
        pltpu.VMEM((-(-head_count // 8) * 8, 2 * span * GROUP), F32),
        pltpu.VMEM((heads * GROUP, span, span), F32),
    ]
    length = GROUP * span
    blocks = span // spacing
    states = []
    results = []
    if fused:
        (outcome, mixed, gathered, stats, outgoing, middle, normed_two, aux, attended) = first[:9]
        returned, arrived, activation, slope = run_expert_layer(FORWARD, 0, expert_weights, [by_rank(outgoing)])
        second = run_attend(
            1, shared_sizes, [by_slot(returned), aux, middle, early_all, w_out_all, route_all, given], 5)
        result, difference, spread = second[9:]
        (outcome, mixed, gathered, stats, outgoing, middle, normed_two, aux, attended) = second[:9]
        returned, returned_grad, grad_in, grad_down = run_expert_layer(
            BOTH, 1, expert_weights, [by_rank(outgoing), by_rank(spread)])
        shared_1, low_1, qkv_1, section_outputs, spread = run_attend_back(
            1, shared_sizes,
            [early_all, mixed, stats, outcome, gathered, by_slot(returned), by_slot(returned_grad), aux, middle,
             given, normed_two, attended, w_out_all, route_all, result, first[7]],
            ((0, 1), (12, 1)), 6)
        returned, grad_in, grad_down = run_expert_layer(
            BACKWARD, 0, expert_weights, [by_rank(spread)], [arrived, activation, slope], [grad_in, grad_down])
        (outcome, mixed, gathered, stats, unused, middle, normed_two, aux, attended) = first[:9]
        pieces = 2 * grad_in.shape[1] // features
        middle_grad, attended_grad, shared_0, grad_in, grad_down = call(
            functools.partial(before_attention_fused, shared_sizes), "before_attention",
            [shape((span, features), F32), shape((GROUP, width, span), BF16), shape(shared_1.shape, BF16),
             shape(grad_in.shape, F32), shape(grad_down.shape, F32)],
            [by_slot(returned), aux, low_1, difference, middle, normed_two, attended, early_all, w_out_all,
             route_all, grad_in, grad_down],
            scratch=[pltpu.VMEM((pieces, features, features), BF16), pltpu.VMEM((pieces, features, features), F32),
                     pltpu.SemaphoreType.DMA((pieces,)), pltpu.SemaphoreType.DMA((pieces,))],
            flops=2 << 30, anywhere=(10, 11), out_anywhere=(3, 4), picks=((7, 0), (8, 0)),
        )
        ranked = (ranks, shard_rows, -1)
        home, owned, shared_sum = run_attend_back(
            0, shared_sizes,
            [early_all, mixed, stats, outcome, gathered, middle_grad, attended_grad, low_1,
             shared_0.reshape(ranked), shared_1.reshape(ranked), qkv_1],
            ((0, 0),), 7)
        section_outputs, section_grads, grad_qkv, grad_out, grad_router, grad_gains, grad_table = call(
            functools.partial(unpack, shared_sizes), "unpack",
            [shape(home.shape, BF16), shape(home.shape, F32), shape((shard_rows, 3 * features), F32), shape((shard_rows, features), F32),
             shape((experts, shard_rows), F32), shape((2, shard_rows), F32),
             shape((table_rows, head_count), F32)],
            [home, owned, shared_sum, section_outputs],
        )
        grad_router = grad_router.T
    stream = None if fused else own
    for section in range(0 if fused else 2):
        qkv, router, gain_one, gain_two, table, expert_in, expert_down = weights[section]
        route_rows = section_routes[section]
        side = beside(stream)
        pieces = (stream, flip(stream), side, flip(side))
        outcome, mixed, gathered, stats = call(
            functools.partial(attention_forward, sizes), "attention_forward",
            [shape((GROUP, width, span), BF16), shape((length, 3 * width), BF16),
             shape((length, features), BF16), shape((8, length), F32)],
            [*pieces, gain_one, qkv, table], scalars=ids, scratch=bias_scratch, flops=4 << 30,
        )
        attended = regroup(outcome)
        outgoing, middle, normed_two, aux = call(
            functools.partial(after_attention, capacity), "after_attention",
            [shape((slots, features), BF16), shape((span, features), F32),
             shape((span, features), BF16), shape((span, 128), F32)],
            [attended, stream, w_outs[section], gain_two, router, route_rows], flops=1 << 30,
        )
        arrived = exchange(outgoing, experts, capacity)
        activation, slope, produced = run_expert_forward(arrived, expert_in, expert_down)
        returned = exchange(produced, experts, capacity)
        result, difference = call(
            combine, "combine", [shape((span, features), BF16), shape((span, features), F32)],
            [returned, aux, middle], flops=1 << 30,
        )
        states.append((stream, outcome, mixed, gathered, stats, attended, middle, normed_two, aux,
                       arrived, activation, slope, difference))
        results.append(result)
        stream = result

    if not fused:
        section_outputs = home_pair(results, core)

    upstream = given
    shared_grads = [None, None]
    shared_partner = [None, None]
    shared_qkv = [None, None]
    qkv_grads = [None, None]
    expert_states = [None, None]
    partials = [None, None]
    stream_grads = [None, None]
    for section in (() if fused else (1, 0)):
        qkv, router, gain_one, gain_two, table, expert_in, expert_down = weights[section]
        w_out = w_outs[section]
        (stream, outcome, mixed, gathered, stats, attended, middle, normed_two, aux,
         arrived, activation, slope, difference) = states[section]
        route_rows = section_routes[section]
        (spread,) = call(spread_grads, "spread_grads", [shape((slots, features), BF16)],
                         [upstream, aux], flops=1 << 30)
        arrived_grad = exchange(spread, experts, capacity)
        hidden_grad, rows_grad = run_expert_backward(arrived_grad, expert_in, expert_down, slope)
        returned = exchange(rows_grad, experts, capacity)
        expert_states[section] = (arrived, hidden_grad, activation, arrived_grad)
        wanted = (core != section).astype(jnp.int32).reshape(1)
        shares = run_weight_partials(wanted, *expert_states[section])
        partials[section] = [lax.ppermute(part, SECTION, [(1 - section, section)]) for part in shares]
        if section == 0:
            waiting, returned = lax.optimization_barrier((shared_qkv[1], returned))
            qkv_grads[1] = spread_sum(waiting, (EXPERT, ZHI), ranks // 2)
        middle_grad, attended_grad, shared_grads[section] = call(
            before_attention, "before_attention",
            [shape((span, features), F32), shape((GROUP, width, span), BF16),
             shape((features, features + -(-(experts + 1) // 128) * 128), BF16)],
            [returned, aux, upstream, difference, middle, normed_two, attended, gain_two, router, w_out,
             route_rows], flops=2 << 30, after=shares[:1],
        )
        shared_partner[section] = lax.ppermute(shared_grads[section], SECTION, [(1 - section, section)])
        grads = regroup(attended_grad)
        stay, leave, sent, shared_qkv[section] = call(
            functools.partial(attention_backward, sizes), "attention_backward",
            [shape((span, features), BF16), shape((span, features), BF16), shape((2, span, features), BF16),
             shape((features, -(-(3 * width + 16) // 128) * 128), BF16)],
            [mixed, stats, outcome, grads, gathered, gain_one, qkv, table], scalars=ids,
            scratch=[*bias_scratch, pltpu.VMEM((length, 3 * width), BF16),
                     pltpu.VMEM((GROUP, span, span), F32), pltpu.VMEM((length, size), F32),
                     pltpu.VMEM((length, size), F32), pltpu.VMEM((size, length), F32),
                     pltpu.VMEM((8, GROUP * 2 * 128), F32)],
            flops=8 << 30,
        )
        partner = flip(sent)
        leave = leave + partner[1]
        filler = ()
        if section == 0:
            leave, waiting = lax.optimization_barrier((leave, shared_qkv[0]))
            qkv_grads[0] = spread_sum(waiting, (EXPERT, ZHI), ranks // 2)
            grad_in = run_weight_totals(
                core_id, *[(expert_states[which][0], expert_states[which][1], partials[which][0])
                           for which in range(2)], False, sent)
            filler = (grad_in,)
        arrived_share = beside(leave)
        (low,) = call(
            first_norm_grad, "first_norm_grad", [shape((span, features), BF16)],
            [stay, partner, arrived_share, stream, gain_one, middle_grad], after=filler,
        )
        stream_grads[section] = low
        upstream = low

    if not fused:
        shared = jnp.where(
            core == 0,
            shared_grads[0].astype(F32) + shared_partner[0].astype(F32),
            shared_grads[1].astype(F32) + shared_partner[1].astype(F32),
        ).astype(BF16)
        shared = spread_sum(shared, RANKS, ranks)
        grad_out = shared[:, :features]
        grad_router = shared[:, features : features + experts]
        grad_gain_two = shared[:, features + experts]

        columns = qkv_grads[0].shape[1]
        halves = [block.reshape(2, shard_rows, columns) for block in qkv_grads]
        owned = regroup(jnp.stack([halves[0][0], halves[1][0], halves[0][1], halves[1][1]]))
        split = owned[:, :, : 3 * width].reshape(GROUP, shard_rows, 3, width)
        grad_qkv = jnp.transpose(split, (1, 2, 0, 3)).reshape(shard_rows, 3 * features)
        grad_table = jnp.transpose(
            owned[:, :table_rows, 3 * width : 3 * width + heads], (1, 0, 2)
        ).reshape(table_rows, head_count)
        grad_gain_one = jnp.sum(owned[:, :, 3 * width + 8], axis=0)
        grad_gains = jnp.stack([grad_gain_one, grad_gain_two])
        section_grads = home_pair(stream_grads, core).astype(F32)
        grad_down = run_weight_totals(
            core_id, *[(expert_states[which][2], expert_states[which][3], partials[which][1])
                       for which in range(2)], True, stream_grads[0])
    return (
        section_outputs[None, :, None],
        section_grads[None, :, None],
        grad_qkv[None],
        grad_out[None],
        grad_router[None],
        grad_gains[None],
        grad_table[None],
        grad_in[None, None],
        grad_down[None, None],
    )


def solution(mesh):
    sections, ranks, pieces = mesh.devices.shape
    work = Mesh(
        mesh.devices.reshape(sections, ranks, pieces // 2, 2), (SECTION, EXPERT, ZHI, ZLO)
    )
    piece = (ZHI, ZLO)
    in_specs = (
        P(None, EXPERT, piece, None),
        P(None, EXPERT, piece, None),
        P(SECTION, RANKS, None),
        P(SECTION, RANKS, None),
        P(SECTION, RANKS, None),
        P(SECTION, None, RANKS),
        P(SECTION, RANKS, None),
        P(SECTION, RANKS, None, None),
        P(SECTION, RANKS, None, None),
        P(SECTION, None, EXPERT, piece, None),
    )
    out_specs = (
        P(SECTION, None, EXPERT, piece, None),
        P(SECTION, None, EXPERT, piece, None),
        P(SECTION, RANKS, None),
        P(SECTION, RANKS, None),
        P(SECTION, RANKS, None),
        P(SECTION, None, RANKS),
        P(SECTION, RANKS, None),
        P(SECTION, RANKS, None, None),
        P(SECTION, RANKS, None, None),
    )
    return jax.shard_map(per_device, mesh=work, in_specs=in_specs, out_specs=out_specs, check_vma=False)
```
